32 devices in a mesh: group: 2 (over core), replica: 16 (over z, y, x).
Axes of the slice: x: 2, y: 2, z: 4, core: 2. Of those that a mesh axis runs over, the one named last changes fastest.
Arguments:
- tokens: bfloat16 [32768, 1152], P(('group', 'replica')), may hold values from -6 to 6
- out_grad: bfloat16 [32768, 1152], P(('group', 'replica')), may hold values from -6 to 6
- ln1_gain: bfloat16 [1152], P('group'), may hold values from 0.5 to 1.5
- ln1_bias: bfloat16 [1152], P('group'), may hold values from -3 to 3
- q_weight: bfloat16 [1152, 1152], P('group'), may hold values from -0.1875 to 0.1875
- q_bias: bfloat16 [1152], P('group'), may hold values from -3 to 3
- k_weight: bfloat16 [1152, 1152], P('group'), may hold values from -0.1875 to 0.1875
- v_weight: bfloat16 [1152, 1152], P('group'), may hold values from -0.1875 to 0.1875
- v_bias: bfloat16 [1152], P('group'), may hold values from -3 to 3
- o_weight: bfloat16 [1152, 1152], P('group'), may hold values from -2 to 2
- o_bias: bfloat16 [1152], P('group'), may hold values from -3 to 3
- ln2_gain: bfloat16 [1152], P('group'), may hold values from 0.5 to 1.5
- ln2_bias: bfloat16 [1152], P('group'), may hold values from -3 to 3
- up_weight: bfloat16 [1152, 4304], P('group'), may hold values from -0.1875 to 0.1875
- up_bias: bfloat16 [4304], P('group'), may hold values from -3 to 3
- down_weight: bfloat16 [4304, 1152], P('group'), may hold values from -0.09375 to 0.09375
- down_bias: bfloat16 [1152], P('group'), may hold values from -3 to 3
Outputs:
- activations: bfloat16 [32768, 1152], P(('group', 'replica'))
- input_grad: bfloat16 [32768, 1152], P(('group', 'replica'))
- ln1_gain_grad: float32 [1152], P('group')
- ln1_bias_grad: float32 [1152], P('group')
- q_weight_grad: float32 [1152, 1152], P('group')
- q_bias_grad: float32 [1152], P('group')
- k_weight_grad: float32 [1152, 1152], P('group')
- v_weight_grad: float32 [1152, 1152], P('group')
- v_bias_grad: float32 [1152], P('group')
- o_weight_grad: float32 [1152, 1152], P('group')
- o_bias_grad: float32 [1152], P('group')
- ln2_gain_grad: float32 [1152], P('group')
- ln2_bias_grad: float32 [1152], P('group')
- up_weight_grad: float32 [1152, 4304], P('group')
- up_bias_grad: float32 [4304], P('group')
- down_weight_grad: float32 [4304, 1152], P('group')
- down_bias_grad: float32 [1152], P('group')
The draws below stay inside these ranges and needn't reach their ends.
All inputs are finite; a program needn't handle non-finite values.
Results may differ from the reference program's by a relative error of at most 0.018.
Values may be sent and summed in bfloat16 or wider, within the bound.
A program may use at most 256 MiB of HBM per device.

```python
import math
import jax
import jax.numpy as jnp
from jax import lax

D = 1152
HEADS = 16
HEAD_DIM = 72
FF = 4304
PATCHES = 128
TOKENS = 32768


def block_scale(key, extent, shards, smallest, largest):
    loudness, own = 1.0, jax.random.fold_in(key, 6)
    for axis_at, shards_of in shards:
        steps = jnp.exp(jax.random.uniform(jax.random.fold_in(own, axis_at), (shards_of,), jnp.float32, smallest / len(shards), largest / len(shards)))
        loudness = loudness * jnp.repeat(steps, extent[axis_at] // shards_of).reshape([-1 if axis == axis_at else 1 for axis in range(len(extent))])
    return loudness


def gaussian(key, dims, width, bound, cuts=(), held_as=jnp.bfloat16):
    drawn = width * jax.random.normal(key, dims, jnp.float32)
    if cuts:
        drawn = drawn * block_scale(key, dims, cuts, -0.22, 0.18)
    return jnp.clip(drawn, -bound, bound).astype(held_as)


def setup_inputs(seed: int = 0) -> dict:
    key_of = jax.random.split(jax.random.key(seed), 18)
    tokens = gaussian(key_of[0], (TOKENS, D), 1.0, 6.0, ((0, 32),))
    out_grad = gaussian(key_of[1], (TOKENS, D), 1.0, 6.0, ((0, 32),))
    ln1_gain = jnp.clip(1.0 + 0.1 * jax.random.normal(key_of[2], (D,), jnp.float32), 0.5, 1.5).astype(jnp.bfloat16)
    ln1_bias = gaussian(key_of[3], (D,), 0.5, 3.0, ((0, 2),))
    q_weight = gaussian(key_of[4], (D, D), D ** -0.5, 0.1875, ((0, 2),))
    q_bias = gaussian(key_of[5], (D,), 0.5, 3.0, ((0, 2),))
    k_weight = gaussian(key_of[6], (D, D), D ** -0.5, 0.1875, ((0, 2),))
    v_weight = gaussian(key_of[7], (D, D), D ** -0.5, 0.1875, ((0, 2),))
    v_bias = gaussian(key_of[8], (D,), 0.5, 3.0, ((0, 2),))
    o_weight = gaussian(key_of[9], (D, D), (max(D // PATCHES, 1)) ** -0.5, 2.0, ((0, 2),))
    o_bias = gaussian(key_of[10], (D,), 0.5, 3.0, ((0, 2),))
    ln2_gain = jnp.clip(1.0 + 0.1 * jax.random.normal(key_of[11], (D,), jnp.float32), 0.5, 1.5).astype(jnp.bfloat16)
    ln2_bias = gaussian(key_of[12], (D,), 0.5, 3.0, ((0, 2),))
    up_weight = gaussian(key_of[13], (D, FF), D ** -0.5, 0.1875, ((0, 2),))
    up_bias = gaussian(key_of[14], (FF,), 0.5, 3.0, ((0, 2),))
    down_weight = gaussian(key_of[15], (FF, D), FF ** -0.5, 0.09375, ((0, 2),))
    down_bias = gaussian(key_of[16], (D,), 0.5, 3.0, ((0, 2),))
    return {"tokens": tokens, "out_grad": out_grad, "ln1_gain": ln1_gain, "ln1_bias": ln1_bias, "q_weight": q_weight, "q_bias": q_bias, "k_weight": k_weight, "v_weight": v_weight, "v_bias": v_bias, "o_weight": o_weight, "o_bias": o_bias, "ln2_gain": ln2_gain, "ln2_bias": ln2_bias, "up_weight": up_weight, "up_bias": up_bias, "down_weight": down_weight, "down_bias": down_bias}


@jax.custom_vjp
def low(v):
    return lax.optimization_barrier(v.astype(jnp.bfloat16)).astype(jnp.float32)

@jax.custom_vjp
def low_back(v):
    return v

def low_keep(v):
    return (low(v), None)

def low_pass(kept, grad):
    return (grad,)

def back_keep(v):
    return (v, None)

def back_low(kept, grad):
    return (low(grad),)
low.defvjp(low_keep, low_pass)
low_back.defvjp(back_keep, back_low)

def layer_norm(values, gain, shift):
    center = values - lax.optimization_barrier(jnp.mean(values, axis=-1, keepdims=True))
    spread = lax.optimization_barrier(jnp.mean(center * center, axis=-1, keepdims=True))
    return center * lax.rsqrt(spread + 1e-06) * gain + shift

def matmul_high(left, right):
    return jnp.dot(left, right, precision=lax.Precision.HIGHEST)

def forward(values, params):
    gain_one, shift_one, wq_full, bq_full, wk_full, wv_full, bv_full, wo_full, bo_full, gain_two, shift_two, wup_full, bup_full, wdown_full, bdown_full = params
    normed1 = low(layer_norm(values, gain_one, shift_one))
    query = low(low_back(matmul_high(normed1, wq_full) + bq_full))
    key_rows = low(low_back(matmul_high(normed1, wk_full)))
    value_rows = low(low_back(matmul_high(normed1, wv_full) + bv_full))
    factor = HEAD_DIM ** (-0.5)
    query_h = query.reshape(-1, PATCHES, HEADS, HEAD_DIM)
    key_h = key_rows.reshape(-1, PATCHES, HEADS, HEAD_DIM)
    value_h = value_rows.reshape(-1, PATCHES, HEADS, HEAD_DIM)
    logits = low_back(jnp.einsum('isha,itha->ihst', query_h, key_h, precision=lax.Precision.HIGHEST) * factor)
    weights = jax.nn.softmax(logits, axis=-1)
    mixed = jnp.einsum('ihst,itha->isha', low(weights), value_h, precision=lax.Precision.HIGHEST)
    attn_in = low(low_back(mixed.reshape(values.shape)))
    residual = values + low_back(matmul_high(attn_in, wo_full) + bo_full)
    normed2 = low(layer_norm(residual, gain_two, shift_two))
    pre_act = low_back(matmul_high(normed2, wup_full) + bup_full)
    hidden = low(jax.nn.gelu(pre_act, approximate=True))
    return residual + low_back(matmul_high(hidden, wdown_full) + bdown_full)

def reference(tokens, out_grad, ln1_gain, ln1_bias, q_weight, q_bias, k_weight, v_weight, v_bias, o_weight, o_bias, ln2_gain, ln2_bias, up_weight, up_bias, down_weight, down_bias):
    params = tuple((param.astype(jnp.float32) for param in (ln1_gain, ln1_bias, q_weight, q_bias, k_weight, v_weight, v_bias, o_weight, o_bias, ln2_gain, ln2_bias, up_weight, up_bias, down_weight, down_bias)))
    total_rows = tokens.shape[0]
    block_rows = math.gcd(total_rows, 4096)
    inputs = tokens.astype(jnp.float32).reshape(-1, block_rows, D)
    cotangents = out_grad.astype(jnp.float32).reshape(-1, block_rows, D)

    def step(totals, pair):
        block_in, block_cot = pair
        block_out, backward = jax.vjp(forward, block_in, params)
        d_block, d_params = backward(block_cot)
        totals = tuple((older + newer for older, newer in zip(totals, d_params)))
        return (totals, (block_out, d_block))
    start = tuple((jnp.zeros_like(param) for param in params))
    totals, (outputs, d_inputs) = lax.scan(step, start, (inputs, cotangents))
    return (outputs.reshape(total_rows, D).astype(jnp.bfloat16), d_inputs.reshape(total_rows, D).astype(jnp.bfloat16), totals[0], totals[1], totals[2], totals[3], totals[4], totals[5], totals[6], totals[7], totals[8], totals[9], totals[10], totals[11], totals[12], totals[13], totals[14])
```

```python
import functools

import jax
import jax.numpy as jnp
from jax import lax
from jax.experimental import pallas as pl
from jax.experimental.pallas import tpu as pltpu
from jax.sharding import PartitionSpec as P

HEADS = 16
PATCHES = 128


def layer_norm(values, gain, shift):
    center = values - jnp.mean(values, axis=-1, keepdims=True)
    spread = jnp.mean(center * center, axis=-1, keepdims=True)
    return center * lax.rsqrt(spread + 1e-06) * gain + shift


def gelu_tanh(values):
    return jax.nn.gelu(values, approximate=True)


def split_heads(rows):
    return rows.reshape(-1, PATCHES, HEADS, rows.shape[-1] // HEADS)


def head_logits(query, key_rows):
    factor = (query.shape[-1] // HEADS) ** (-0.5)
    query_h = split_heads(query)
    key_h = split_heads(key_rows)
    logits = (
        jnp.einsum("isha,itha->ihst", query_h, key_h, preferred_element_type=jnp.float32) * factor
    )
    return (logits, query_h, key_h, factor)


def attend(query, key_rows, value_rows):
    logits, query_h, key_h, factor = head_logits(query, key_rows)
    peak = jnp.max(logits, axis=-1, keepdims=True)
    log_total = peak + jnp.log(jnp.sum(jnp.exp(logits - peak), axis=-1, keepdims=True))
    weights_low = jnp.exp(logits - log_total).astype(jnp.bfloat16)
    mixed = jnp.einsum(
        "ihst,itha->isha", weights_low, split_heads(value_rows), preferred_element_type=jnp.float32
    )
    return (mixed.reshape(query.shape), log_total)


def attend_back(query, key_rows, value_rows, log_total, d_mixed):
    logits, query_h, key_h, factor = head_logits(query, key_rows)
    weights = jnp.exp(logits - log_total)
    weights_low = weights.astype(jnp.bfloat16)
    value_h = split_heads(value_rows)
    d_mix_h = split_heads(d_mixed)
    d_weights = jnp.einsum("isha,itha->ihst", d_mix_h, value_h, preferred_element_type=jnp.float32)
    d_logits = weights * (d_weights - jnp.sum(weights * d_weights, axis=-1, keepdims=True))
    d_low = d_logits.astype(jnp.bfloat16)
    d_query = (
        jnp.einsum("ihst,itha->isha", d_low, key_h, preferred_element_type=jnp.float32) * factor
    ).astype(jnp.bfloat16)
    d_key = (
        jnp.einsum("ihst,isha->itha", d_low, query_h, preferred_element_type=jnp.float32) * factor
    ).astype(jnp.bfloat16)
    d_value = jnp.einsum(
        "ihst,isha->itha", weights_low, d_mix_h, preferred_element_type=jnp.float32
    ).astype(jnp.bfloat16)
    return (d_query.reshape(query.shape), d_key.reshape(query.shape), d_value.reshape(query.shape))


def outer_rows(left, right):
    return jnp.einsum("ra,rb->ab", left, right, preferred_element_type=jnp.float32)


def back_rows(grads, weight):
    return jnp.einsum("rb,ab->ra", grads, weight, preferred_element_type=jnp.float32)


def column_sums(grads):
    return jnp.sum(grads.astype(jnp.float32), axis=0)


def shards(
    tokens,
    out_grad,
    ln1_gain,
    ln1_bias,
    q_weight,
    q_bias,
    k_weight,
    v_weight,
    v_bias,
    o_weight,
    o_bias,
    ln2_gain,
    ln2_bias,
    up_weight,
    up_bias,
    down_weight,
    down_bias,
):
    attn_full = (
        lax.all_gather(ln1_gain, "group", axis=0, tiled=True),
        lax.all_gather(ln1_bias, "group", axis=0, tiled=True),
        lax.all_gather(q_weight, "group", axis=0, tiled=True),
        lax.all_gather(q_bias, "group", axis=0, tiled=True),
        lax.all_gather(k_weight, "group", axis=0, tiled=True),
        lax.all_gather(v_weight, "group", axis=0, tiled=True),
        lax.all_gather(v_bias, "group", axis=0, tiled=True),
        lax.all_gather(o_weight, "group", axis=0, tiled=True),
        lax.all_gather(o_bias, "group", axis=0, tiled=True),
    )
    gain_one, shift_one, wq_full, bq_full, wk_full, wv_full, bv_full, wo_full, bo_full = attn_full
    input_f = tokens.astype(jnp.float32)
    gain_one_f = gain_one.astype(jnp.float32)
    shift_one_f = shift_one.astype(jnp.float32)
    normed1 = layer_norm(input_f, gain_one_f, shift_one_f).astype(jnp.bfloat16)
    query = (
        jnp.dot(normed1, wq_full, preferred_element_type=jnp.float32) + bq_full.astype(jnp.float32)
    ).astype(jnp.bfloat16)
    key_rows = jnp.dot(normed1, wk_full, preferred_element_type=jnp.float32).astype(jnp.bfloat16)
    value_rows = (
        jnp.dot(normed1, wv_full, preferred_element_type=jnp.float32) + bv_full.astype(jnp.float32)
    ).astype(jnp.bfloat16)
    mixed, log_total = attend(query, key_rows, value_rows)
    attn_in = mixed.astype(jnp.bfloat16)
    residual = (
        input_f
        + jnp.dot(attn_in, wo_full, preferred_element_type=jnp.float32)
        + bo_full.astype(jnp.float32)
    )
    mlp_full = (
        lax.all_gather(ln2_gain, "group", axis=0, tiled=True),
        lax.all_gather(ln2_bias, "group", axis=0, tiled=True),
        lax.all_gather(up_weight, "group", axis=0, tiled=True),
        lax.all_gather(up_bias, "group", axis=0, tiled=True),
        lax.all_gather(down_weight, "group", axis=0, tiled=True),
        lax.all_gather(down_bias, "group", axis=0, tiled=True),
    )
    gain_two, shift_two, wup_full, bup_full, wdown_full, bdown_full = mlp_full
    gain_two_f = gain_two.astype(jnp.float32)
    shift_two_f = shift_two.astype(jnp.float32)
    normed2 = layer_norm(residual, gain_two_f, shift_two_f).astype(jnp.bfloat16)
    pre_act = jnp.dot(normed2, wup_full, preferred_element_type=jnp.float32) + bup_full.astype(
        jnp.float32
    )
    hidden = gelu_tanh(pre_act).astype(jnp.bfloat16)
    output = (
        residual
        + jnp.dot(hidden, wdown_full, preferred_element_type=jnp.float32)
        + bdown_full.astype(jnp.float32)
    )
    mlp_back = (
        lax.all_gather(ln2_gain, "group", axis=0, tiled=True),
        lax.all_gather(ln2_bias, "group", axis=0, tiled=True),
        lax.all_gather(up_weight, "group", axis=0, tiled=True),
        lax.all_gather(up_bias, "group", axis=0, tiled=True),
        lax.all_gather(down_weight, "group", axis=0, tiled=True),
        lax.all_gather(down_bias, "group", axis=0, tiled=True),
    )
    wup_back = mlp_back[2]
    wdown_back = mlp_back[4]
    grad_out = out_grad.astype(jnp.float32)
    d_wdown = outer_rows(hidden, out_grad)
    d_bdown = column_sums(out_grad)
    d_hidden = back_rows(out_grad, wdown_back)
    unused_act, gelu_back = jax.vjp(gelu_tanh, pre_act)
    d_pre = gelu_back(d_hidden)[0].astype(jnp.bfloat16)
    d_wup = outer_rows(normed2, d_pre)
    d_bup = column_sums(d_pre)
    d_normed2 = back_rows(d_pre, wup_back)
    unused_two, norm_back_two = jax.vjp(layer_norm, residual, gain_two_f, shift_two_f)
    d_res_norm, d_gain_two, d_shift_two = norm_back_two(d_normed2)
    d_residual = grad_out + d_res_norm
    mlp_grads = (
        lax.psum_scatter(
            d_gain_two.astype(jnp.bfloat16), "group", scatter_dimension=0, tiled=True
        ).astype(jnp.float32),
        lax.psum_scatter(
            d_shift_two.astype(jnp.bfloat16), "group", scatter_dimension=0, tiled=True
        ).astype(jnp.float32),
        lax.psum_scatter(
            d_wup.astype(jnp.bfloat16), "group", scatter_dimension=0, tiled=True
        ).astype(jnp.float32),
        lax.psum_scatter(
            d_bup.astype(jnp.bfloat16), "group", scatter_dimension=0, tiled=True
        ).astype(jnp.float32),
        lax.psum_scatter(
            d_wdown.astype(jnp.bfloat16), "group", scatter_dimension=0, tiled=True
        ).astype(jnp.float32),
        lax.psum_scatter(
            d_bdown.astype(jnp.bfloat16), "group", scatter_dimension=0, tiled=True
        ).astype(jnp.float32),
    )
    attn_back = (
        lax.all_gather(ln1_gain, "group", axis=0, tiled=True),
        lax.all_gather(ln1_bias, "group", axis=0, tiled=True),
        lax.all_gather(q_weight, "group", axis=0, tiled=True),
        lax.all_gather(q_bias, "group", axis=0, tiled=True),
        lax.all_gather(k_weight, "group", axis=0, tiled=True),
        lax.all_gather(v_weight, "group", axis=0, tiled=True),
        lax.all_gather(v_bias, "group", axis=0, tiled=True),
        lax.all_gather(o_weight, "group", axis=0, tiled=True),
        lax.all_gather(o_bias, "group", axis=0, tiled=True),
    )
    wq_back = attn_back[2]
    wk_back = attn_back[4]
    wv_back = attn_back[5]
    wo_back = attn_back[7]
    d_attn = d_residual.astype(jnp.bfloat16)
    d_wout = outer_rows(attn_in, d_attn)
    d_bout = column_sums(d_attn)
    d_mixed = back_rows(d_attn, wo_back).astype(jnp.bfloat16)
    d_query, d_key, d_value = attend_back(query, key_rows, value_rows, log_total, d_mixed)
    d_wquery = outer_rows(normed1, d_query)
    d_bquery = column_sums(d_query)
    d_wkey = outer_rows(normed1, d_key)
    d_wvalue = outer_rows(normed1, d_value)
    d_bvalue = column_sums(d_value)
    d_normed1 = (
        back_rows(d_query, wq_back) + back_rows(d_key, wk_back) + back_rows(d_value, wv_back)
    )
    unused_one, norm_back_one = jax.vjp(layer_norm, input_f, gain_one_f, shift_one_f)
    d_in_norm, d_gain_one, d_shift_one = norm_back_one(d_normed1)
    d_input = (d_residual + d_in_norm).astype(jnp.bfloat16)
    attn_grads = (
        lax.psum_scatter(
            d_gain_one.astype(jnp.bfloat16), "group", scatter_dimension=0, tiled=True
        ).astype(jnp.float32),
        lax.psum_scatter(
            d_shift_one.astype(jnp.bfloat16), "group", scatter_dimension=0, tiled=True
        ).astype(jnp.float32),
        lax.psum_scatter(
            d_wquery.astype(jnp.bfloat16), "group", scatter_dimension=0, tiled=True
        ).astype(jnp.float32),
        lax.psum_scatter(
            d_bquery.astype(jnp.bfloat16), "group", scatter_dimension=0, tiled=True
        ).astype(jnp.float32),
        lax.psum_scatter(
            d_wkey.astype(jnp.bfloat16), "group", scatter_dimension=0, tiled=True
        ).astype(jnp.float32),
        lax.psum_scatter(
            d_wvalue.astype(jnp.bfloat16), "group", scatter_dimension=0, tiled=True
        ).astype(jnp.float32),
        lax.psum_scatter(
            d_bvalue.astype(jnp.bfloat16), "group", scatter_dimension=0, tiled=True
        ).astype(jnp.float32),
        lax.psum_scatter(
            d_wout.astype(jnp.bfloat16), "group", scatter_dimension=0, tiled=True
        ).astype(jnp.float32),
        lax.psum_scatter(
            d_bout.astype(jnp.bfloat16), "group", scatter_dimension=0, tiled=True
        ).astype(jnp.float32),
    )
    summed = (
        lax.psum(attn_grads[0].astype(jnp.bfloat16), "replica").astype(jnp.float32),
        lax.psum(attn_grads[1].astype(jnp.bfloat16), "replica").astype(jnp.float32),
        lax.psum(attn_grads[2].astype(jnp.bfloat16), "replica").astype(jnp.float32),
        lax.psum(attn_grads[3].astype(jnp.bfloat16), "replica").astype(jnp.float32),
        lax.psum(attn_grads[4].astype(jnp.bfloat16), "replica").astype(jnp.float32),
        lax.psum(attn_grads[5].astype(jnp.bfloat16), "replica").astype(jnp.float32),
        lax.psum(attn_grads[6].astype(jnp.bfloat16), "replica").astype(jnp.float32),
        lax.psum(attn_grads[7].astype(jnp.bfloat16), "replica").astype(jnp.float32),
        lax.psum(attn_grads[8].astype(jnp.bfloat16), "replica").astype(jnp.float32),
        lax.psum(mlp_grads[0].astype(jnp.bfloat16), "replica").astype(jnp.float32),
        lax.psum(mlp_grads[1].astype(jnp.bfloat16), "replica").astype(jnp.float32),
        lax.psum(mlp_grads[2].astype(jnp.bfloat16), "replica").astype(jnp.float32),
        lax.psum(mlp_grads[3].astype(jnp.bfloat16), "replica").astype(jnp.float32),
        lax.psum(mlp_grads[4].astype(jnp.bfloat16), "replica").astype(jnp.float32),
        lax.psum(mlp_grads[5].astype(jnp.bfloat16), "replica").astype(jnp.float32),
    )
    attn_grads = tuple(summed[:9])
    mlp_grads = tuple(summed[9:])
    return (output.astype(jnp.bfloat16), d_input) + tuple(attn_grads) + tuple(mlp_grads)


MESH = pl.DeviceIdType.MESH
bf16 = jnp.bfloat16
f32 = jnp.float32
ANY = pl.BlockSpec(memory_space=pl.ANY)
WIDTH = 1152
HALF = 576
FF = 4304
FF_HALF = 2152
TILES = 17
TILE = 128
FF_PAD = 2 * TILES * TILE
FIRST = 320
SECOND = 256


class Place:
    def __init__(self):
        self.core = lax.axis_index("group")
        chip = lax.axis_index("replica")
        self.chip = chip
        self.x = lax.rem(chip, 2)
        self.y = lax.rem(chip // 2, 2)
        self.z = chip // 4
        self.x_pair = chip + 1 - 2 * self.x
        self.y_pair = chip + 2 - 4 * self.y
        self.z_pair = chip + 4 - 8 * lax.rem(self.z, 2)
        self.inner = (self.z == 1) | (self.z == 2)
        self.outer = jnp.logical_not(self.inner)
        self.mid_pair = jnp.where(self.inner, chip + 12 - 8 * self.z, chip)
        self.z_half = lax.rem(self.z // 2, 2)

    def barrier(self):
        sem = pltpu.get_barrier_semaphore()

        def greet(core, chip):
            pl.semaphore_signal(sem, inc=1, device_id=(core, chip), device_id_type=MESH)

        greet(1 - self.core, self.chip)
        greet(self.core, self.x_pair)
        greet(self.core, self.y_pair)
        greet(self.core, self.z_pair)

        @pl.when(self.inner)
        def _():
            greet(self.core, self.mid_pair)
            pl.semaphore_wait(sem, 5)

        @pl.when(self.outer)
        def _():
            pl.semaphore_wait(sem, 4)

    def copy(self, source, target, sent, got, chip):
        return pltpu.make_async_remote_copy(
            source, target, sent, got, device_id=(self.core, chip), device_id_type=MESH
        )

    def copy_sibling(self, source, target, sent, got):
        return pltpu.make_async_remote_copy(
            source, target, sent, got, device_id=(1 - self.core, self.chip), device_id_type=MESH
        )


def aligned(value, unit):
    return pl.multiple_of(value, unit)


def add_rows(total, landed, chunk, start, count):
    rows = pl.ds(start, count)
    total[chunk, rows, :] = (
        total[chunk, rows, :].astype(f32) + landed.astype(f32)
    ).astype(bf16)


class TreeFirst:
    steps = 9

    def __init__(self, place, total, final, landing, sent, got, kept):
        self.at = place
        self.total = total
        self.final = final
        self.kept = kept
        self.land = landing
        self.sent = sent
        self.got = got
        n = total.shape[1]
        self.n = n
        p = place
        self.own = [
            (0, n),
            (aligned(p.z_half * (n // 2), n // 2), n // 2),
        ]
        self.other = [None, (aligned((1 - p.z_half) * (n // 2), n // 2), n // 2)]
        for bit, part in ((p.y, n // 4), (p.x, n // 8)):
            base = self.own[-1][0]
            self.own.append((aligned(base + bit * part, part), part))
            self.other.append((aligned(base + (1 - bit) * part, part), part))
        self.peer = [p.z_pair, p.mid_pair, p.y_pair, p.x_pair]

    def rows(self, chunk, span):
        return self.total.at[chunk, pl.ds(span[0], span[1]), :]

    def ends(self, chunk, span):
        return self.final.at[chunk, pl.ds(span[0], span[1]), :]

    def send(self, k, chunk):
        sent, got = self.sent.at[k, chunk], self.got.at[k, chunk]
        if k < 4:
            span = self.own[0] if k == 0 else self.other[k]
            return self.at.copy(
                self.rows(chunk, span), self.land[k].at[chunk], sent, got, self.peer[k]
            )
        level = 7 - k
        target = self.ends(chunk, self.own[level])
        source = self.rows(chunk, self.own[3]) if k == 4 else target
        return self.at.copy(source, target, sent, got, self.peer[level])

    def keep(self, chunk):
        return pltpu.make_async_copy(
            self.rows(chunk, self.own[3]), self.ends(chunk, self.own[3]), self.kept.at[chunk]
        )

    def arrive(self, k, chunk):
        if k < 4:
            landed = self.land[k].at[chunk]
        else:
            level = 7 - k
            landed = self.ends(chunk, self.own[0] if level == 0 else self.other[level])
        self.at.copy(
            landed, landed, self.sent.at[k, chunk], self.got.at[k, chunk], self.at.z_pair
        ).wait_recv()

    def step(self, k, chunk):
        at = self.at
        if k == 0:

            @pl.when(at.outer)
            def _():
                self.send(0, chunk).start()

        elif k <= 7:

            @pl.when(at.inner)
            def _():
                self.arrive(k - 1, chunk)
                if k <= 4:
                    add_rows(self.total, self.land[k - 1][chunk], chunk, *self.own[k - 1])
                if k == 4:
                    self.keep(chunk).start()
                if k == 5:
                    self.keep(chunk).wait()
                self.send(k, chunk).start()

        else:

            @pl.when(at.inner)
            def _():
                for j in range(1, 8):
                    self.send(j, chunk).wait_send()

            @pl.when(at.outer)
            def _():
                self.arrive(7, chunk)
                self.send(0, chunk).wait_send()


class PlaneFirst:
    steps = 8

    def __init__(self, place, total, final, base, n, x_first, landing, sent, got, kept):
        self.at = place
        self.total = total
        self.final = final
        self.kept = kept
        self.land = landing
        self.sent = sent
        self.got = got
        p = place
        if x_first:
            one, two = (p.x, p.x_pair), (p.y, p.y_pair)
        else:
            one, two = (p.y, p.y_pair), (p.x, p.x_pair)
        self.peer_one, self.peer_two = one[1], two[1]
        start = aligned(base + one[0] * (n // 2), 16)
        self.half = (start, n // 2)
        self.half_other = (aligned(base + (1 - one[0]) * (n // 2), 16), n // 2)
        self.quarter = (aligned(start + two[0] * (n // 4), 16), n // 4)
        self.quarter_other = (aligned(start + (1 - two[0]) * (n // 4), 16), n // 4)

    def rows(self, chunk, span):
        return self.total.at[chunk, pl.ds(span[0], span[1]), :]

    def ends(self, chunk, span):
        return self.final.at[chunk, pl.ds(span[0], span[1]), :]

    def keep(self, chunk):
        return pltpu.make_async_copy(
            self.rows(chunk, self.quarter), self.ends(chunk, self.quarter), self.kept.at[chunk]
        )

    def send(self, k, chunk):
        at = self.at
        quarter = self.rows(chunk, self.quarter)
        quarter_end = self.ends(chunk, self.quarter)
        half_end = self.ends(chunk, self.half)
        source, target, peer = (
            (self.rows(chunk, self.half_other), self.land[0].at[chunk], self.peer_one),
            (self.rows(chunk, self.quarter_other), self.land[1].at[chunk], self.peer_two),
            (quarter, self.land[2].at[chunk], at.z_pair),
            (quarter, self.land[3].at[chunk], at.mid_pair),
            (quarter, quarter_end, at.z_pair),
            (quarter_end, quarter_end, self.peer_two),
            (half_end, half_end, self.peer_one),
        )[k]
        return at.copy(source, target, self.sent.at[k, chunk], self.got.at[k, chunk], peer)

    def arrive(self, k, chunk):
        if k < 4:
            landed = self.land[k].at[chunk]
        else:
            landed = self.ends(
                chunk, (self.quarter, self.quarter_other, self.half_other)[k - 4]
            )
        self.at.copy(
            landed, landed, self.sent.at[k, chunk], self.got.at[k, chunk], self.at.z_pair
        ).wait_recv()

    def step(self, k, chunk):
        at = self.at
        if k == 0:
            self.send(0, chunk).start()
        elif k == 1:
            self.arrive(0, chunk)
            add_rows(self.total, self.land[0][chunk], chunk, *self.half)
            self.send(1, chunk).start()
        elif k == 2:
            self.arrive(1, chunk)
            add_rows(self.total, self.land[1][chunk], chunk, *self.quarter)

            @pl.when(at.outer)
            def _():
                self.send(2, chunk).start()

        elif k == 3:

            @pl.when(at.inner)
            def _():
                self.arrive(2, chunk)
                add_rows(self.total, self.land[2][chunk], chunk, *self.quarter)
                self.send(3, chunk).start()

        elif k == 4:

            @pl.when(at.inner)
            def _():
                self.arrive(3, chunk)
                self.send(3, chunk).wait_send()
                add_rows(self.total, self.land[3][chunk], chunk, *self.quarter)
                self.send(4, chunk).start()
                self.keep(chunk).start()

        elif k == 5:

            @pl.when(at.inner)
            def _():
                self.keep(chunk).wait()

            @pl.when(at.outer)
            def _():
                self.arrive(4, chunk)

            self.send(5, chunk).start()
        elif k == 6:
            self.arrive(5, chunk)
            self.send(6, chunk).start()
        else:
            self.arrive(6, chunk)
            for j in (0, 1, 5, 6):
                self.send(j, chunk).wait_send()

            @pl.when(at.inner)
            def _():
                self.send(4, chunk).wait_send()

            @pl.when(at.outer)
            def _():
                self.send(2, chunk).wait_send()


def tree_scratch(count, n, width):
    return [pltpu.VMEM((count, n // part, width), bf16) for part in (1, 2, 4, 8)] + [
        pltpu.SemaphoreType.DMA((8, count)),
        pltpu.SemaphoreType.DMA((8, count)),
        pltpu.SemaphoreType.DMA((count,)),
    ]


def plane_scratch(count, n, width):
    return [pltpu.VMEM((count, n // part, width), bf16) for part in (2, 4, 4, 4)] + [
        pltpu.SemaphoreType.DMA((7, count)),
        pltpu.SemaphoreType.DMA((7, count)),
        pltpu.SemaphoreType.DMA((count,)),
    ]


def advance(tick, count, sums):
    for k in reversed(range(max(s.steps for s in sums))):
        chunk = tick - k

        @pl.when((chunk >= 0) & (chunk < count))
        def _():
            for s in sums:
                if k < s.steps:
                    s.step(k, chunk)


def dot(left, right, contract):
    return lax.dot_general(left, right, (contract, ((), ())), preferred_element_type=f32)


NN = ((1,), (0,))
NT = ((1,), (1,))
TN = ((0,), (0,))


def gelu_and_slope(u):
    c = 0.7978845608028654
    square = u * u
    t = jnp.tanh(c * u * (1.0 + 0.044715 * square))
    half = 0.5 * (1.0 + t)
    slope = half + 0.5 * u * (1.0 - t * t) * (c * (1.0 + 3 * 0.044715 * square))
    return u * half, slope


def ff_kernel(
    h2_ref,
    x2_ref,
    og_ref,
    wup_ref,
    wdown_ref,
    bup_ref,
    bdown_ref,
    out_ref,
    dh2_ref,
    g1_ref,
    g2_ref,
    dbup_ref,
    h2,
    h2t,
    og,
    out,
    dh2,
    wu,
    wd,
    bup,
    bdown,
    dbup,
    out16,
    mine1,
    mine2,
    sib1,
    sib2,
    sum1,
    sum2,
    *rest,
):
    rest = list(rest)
    local, wsem, gsent, ggot = rest[:4]
    tree, plane1, plane2 = rest[4:11], rest[11:18], rest[18:25]
    at = Place()
    loads = [
        pltpu.make_async_copy(s, d, local.at[j])
        for j, (s, d) in enumerate(
            ((h2_ref, h2), (og_ref, og), (x2_ref, out), (bup_ref, bup), (bdown_ref, bdown))
        )
    ]
    for load in loads:
        load.start()

    def weights(i, slot):
        cols = [pl.ds(aligned(h * TILES * TILE + i * TILE, TILE), TILE) for h in (0, 1)]
        parts = []
        for h in (0, 1):
            here = pl.ds(h * TILE, TILE)
            parts.append(
                pltpu.make_async_copy(
                    wup_ref.at[:, cols[h]], wu.at[slot, :, here], wsem.at[h, slot]
                )
            )
            parts.append(
                pltpu.make_async_copy(
                    wdown_ref.at[cols[h], :], wd.at[slot, here, :], wsem.at[2 + h, slot]
                )
            )
        return parts

    for part in weights(0, 0):
        part.start()
    at.barrier()
    for load in loads:
        load.wait()
    for b in range(8):
        rows = pl.ds(b * 128, 128)
        h2t[:, rows] = h2[rows, :].T
    out[...] = out[...] + bdown[...].astype(f32)
    dh2[...] = jnp.zeros_like(dh2)

    sums = [
        TreeFirst(at, sum1, g1_ref, tree[:4], *tree[4:]),
        PlaneFirst(at, sum2, g2_ref, 0, FIRST, True, plane1[:4], *plane1[4:]),
        PlaneFirst(at, sum2, g2_ref, FIRST, SECOND, False, plane2[:4], *plane2[4:]),
    ]

    def to_sibling(slot):
        return (
            at.copy_sibling(
                mine1.at[slot, 1 - at.core], sib1.at[slot], gsent.at[0, slot], ggot.at[0, slot]
            ),
            at.copy_sibling(
                mine2.at[slot, 1 - at.core], sib2.at[slot], gsent.at[1, slot], ggot.at[1, slot]
            ),
        )

    def meet(i):
        slot = lax.rem(i, 2)
        for copy in to_sibling(slot):
            copy.wait()
        sum1[i] = (mine1[slot, at.core].astype(f32) + sib1[slot].astype(f32)).astype(bf16)
        sum2[i] = (mine2[slot, at.core].astype(f32) + sib2[slot].astype(f32)).astype(bf16)

    def compute(i):
        slot = lax.rem(i, 2)
        for part in weights(i, slot):
            part.wait()

        @pl.when(i + 1 < TILES)
        def _():
            for part in weights(i + 1, 1 - slot):
                part.start()

        bias = bup[i].astype(f32)
        u = dot(h2[...], wu[slot], NN) + bias
        a, slope = gelu_and_slope(u)
        a = a.astype(bf16)
        out[...] += dot(a, wd[slot], NN)
        d_wd = dot(a, og[...], TN).astype(bf16)
        mine1[slot, 0] = d_wd[:TILE]
        mine1[slot, 1] = d_wd[TILE:]
        du = (dot(og[...], wd[slot], NT) * slope).astype(bf16)
        d_wu = dot(h2t[...], du, NN).astype(bf16)
        mine2[slot, 0] = d_wu[:HALF]
        mine2[slot, 1] = d_wu[HALF:]
        for copy in to_sibling(slot):
            copy.start()
        dh2[...] += dot(du, wu[slot], NT)
        dbup[i] = jnp.sum(du.astype(f32), axis=0, keepdims=True)

    def body(i, carry):
        @pl.when((i >= 1) & (i <= TILES))
        def _():
            meet(i - 1)

        advance(i - 1, TILES, sums)

        @pl.when(i < TILES)
        def _():
            compute(i)

        @pl.when(i == TILES)
        def _():
            out16[...] = out[...].astype(bf16)
            pltpu.make_async_copy(out16, out_ref, local.at[0]).start()
            pltpu.make_async_copy(dh2, dh2_ref, local.at[1]).start()
            pltpu.make_async_copy(dbup, dbup_ref, local.at[2]).start()

        return carry

    lax.fori_loop(0, TILES + 1 + 8, body, 0)
    pltpu.make_async_copy(out16, out_ref, local.at[0]).wait()
    pltpu.make_async_copy(dh2, dh2_ref, local.at[1]).wait()
    pltpu.make_async_copy(dbup, dbup_ref, local.at[2]).wait()

def feed_forward(h2, x2, og, wup, wdown, bup, bdown):
    rows = h2.shape[0]
    return pl.pallas_call(
        ff_kernel,
        out_shape=(
            jax.ShapeDtypeStruct((rows, WIDTH), bf16),
            jax.ShapeDtypeStruct((rows, WIDTH), f32),
            jax.ShapeDtypeStruct((TILES, TILE, WIDTH), bf16),
            jax.ShapeDtypeStruct((TILES, HALF, 2 * TILE), bf16),
            jax.ShapeDtypeStruct((TILES, 1, 2 * TILE), f32),
        ),
        in_specs=[ANY] * 7,
        out_specs=[ANY] * 5,
        scratch_shapes=[
            pltpu.VMEM((rows, WIDTH), bf16),
            pltpu.VMEM((WIDTH, rows), bf16),
            pltpu.VMEM((rows, WIDTH), bf16),
            pltpu.VMEM((rows, WIDTH), f32),
            pltpu.VMEM((rows, WIDTH), f32),
            pltpu.VMEM((2, WIDTH, 2 * TILE), bf16),
            pltpu.VMEM((2, 2 * TILE, WIDTH), bf16),
            pltpu.VMEM((TILES, 1, 2 * TILE), bf16),
            pltpu.VMEM((1, WIDTH), bf16),
            pltpu.VMEM((TILES, 1, 2 * TILE), f32),
            pltpu.VMEM((rows, WIDTH), bf16),
            pltpu.VMEM((2, 2, TILE, WIDTH), bf16),
            pltpu.VMEM((2, 2, HALF, 2 * TILE), bf16),
            pltpu.VMEM((2, TILE, WIDTH), bf16),
            pltpu.VMEM((2, HALF, 2 * TILE), bf16),
            pltpu.VMEM((TILES, TILE, WIDTH), bf16),
            pltpu.VMEM((TILES, HALF, 2 * TILE), bf16),
            pltpu.SemaphoreType.DMA((5,)),
            pltpu.SemaphoreType.DMA((4, 2)),
            pltpu.SemaphoreType.DMA((2, 2)),
            pltpu.SemaphoreType.DMA((2, 2)),
        ]
        + tree_scratch(TILES, TILE, WIDTH)
        + plane_scratch(TILES, FIRST, 2 * TILE)
        + plane_scratch(TILES, SECOND, 2 * TILE),
        compiler_params=pltpu.CompilerParams(
            collective_id=1, has_side_effects=True, vmem_limit_bytes=62 * 2**20
        ),
        name="feed_forward",
    )(h2, x2, og, wup, wdown, bup, bdown)


CHUNKS = 9


def attention_sum_kernel(grad_ref, out_ref, sum1, sum2, sib1, sib2, *rest):
    rest = list(rest)
    local, gsent, ggot = rest[:3]
    tree, plane1, plane2 = rest[3:10], rest[10:17], rest[17:24]
    at = Place()
    own = [
        pltpu.make_async_copy(grad_ref.at[at.core, j], s, local.at[j])
        for j, s in ((0, sum1), (1, sum2))
    ]
    for load in own:
        load.start()
    at.barrier()

    def sibling(j, chunk):
        return at.copy_sibling(
            grad_ref.at[1 - at.core, j, chunk],
            (sib1, sib2)[j].at[chunk],
            gsent.at[j, chunk],
            ggot.at[j, chunk],
        )

    for chunk in range(CHUNKS):
        sibling(0, chunk).start()
        sibling(1, chunk).start()
    for load in own:
        load.wait()
    sums = [
        TreeFirst(at, sum1, out_ref.at[0], tree[:4], *tree[4:]),
        PlaneFirst(at, sum2, out_ref.at[1], 0, TILE // 2, True, plane1[:4], *plane1[4:]),
        PlaneFirst(
            at, sum2, out_ref.at[1], TILE // 2, TILE // 2, False, plane2[:4], *plane2[4:]
        ),
    ]

    def body(i, carry):
        @pl.when(i < CHUNKS)
        def _():
            sibling(0, i).wait()
            sibling(1, i).wait()
            sum1[i] = (sum1[i].astype(f32) + sib1[i].astype(f32)).astype(bf16)
            sum2[i] = (sum2[i].astype(f32) + sib2[i].astype(f32)).astype(bf16)

        advance(i, CHUNKS, sums)
        return carry

    lax.fori_loop(0, CHUNKS + 8, body, 0)

def attention_sum(grads):
    return pl.pallas_call(
        attention_sum_kernel,
        out_shape=jax.ShapeDtypeStruct((2, CHUNKS, TILE, WIDTH), bf16),
        in_specs=[ANY],
        out_specs=ANY,
        scratch_shapes=[pltpu.VMEM((CHUNKS, TILE, WIDTH), bf16)] * 4
        + [
            pltpu.SemaphoreType.DMA((2,)),
            pltpu.SemaphoreType.DMA((2, CHUNKS)),
            pltpu.SemaphoreType.DMA((2, CHUNKS)),
        ]
        + tree_scratch(CHUNKS, TILE, WIDTH)
        + plane_scratch(CHUNKS, TILE // 2, WIDTH)
        + plane_scratch(CHUNKS, TILE // 2, WIDTH),
        compiler_params=pltpu.CompilerParams(
            collective_id=2, has_side_effects=True, vmem_limit_bytes=62 * 2**20
        ),
        name="attention_sum",
    )(grads)


def gather(value):
    return lax.all_gather(value, "group", axis=0, tiled=True)


def fast_shards(
    tokens,
    out_grad,
    ln1_gain,
    ln1_bias,
    q_weight,
    q_bias,
    k_weight,
    v_weight,
    v_bias,
    o_weight,
    o_bias,
    ln2_gain,
    ln2_bias,
    up_weight,
    up_bias,
    down_weight,
    down_bias,
):
    gap = TILES * TILE - FF_HALF
    gain_one, shift_one, wq, bq, wk, wv, bv, wo, bo, gain_two, shift_two, bdown = [
        gather(v)
        for v in (
            ln1_gain,
            ln1_bias,
            q_weight,
            q_bias,
            k_weight,
            v_weight,
            v_bias,
            o_weight,
            o_bias,
            ln2_gain,
            ln2_bias,
            down_bias,
        )
    ]
    up_parts = jnp.pad(up_weight.reshape(HALF, 2, FF_HALF), ((0, 0), (0, 0), (0, gap)))
    wup = gather(up_parts.reshape(HALF, FF_PAD))
    wdown = gather(jnp.pad(down_weight, ((0, gap), (0, 0))))
    bup = gather(jnp.pad(up_bias, (0, gap)))
    bup = bup.reshape(2, TILES, TILE).transpose(1, 0, 2).reshape(TILES, 1, 2 * TILE)

    input_f = tokens.astype(f32)
    gain_one, shift_one = gain_one.astype(f32), shift_one.astype(f32)
    gain_two, shift_two = gain_two.astype(f32), shift_two.astype(f32)
    normed1 = layer_norm(input_f, gain_one, shift_one).astype(bf16)
    query = (jnp.dot(normed1, wq, preferred_element_type=f32) + bq.astype(f32)).astype(bf16)
    key_rows = jnp.dot(normed1, wk, preferred_element_type=f32).astype(bf16)
    value_rows = (jnp.dot(normed1, wv, preferred_element_type=f32) + bv.astype(f32)).astype(bf16)
    mixed, log_total = attend(query, key_rows, value_rows)
    attn_in = mixed.astype(bf16)
    residual = input_f + jnp.dot(attn_in, wo, preferred_element_type=f32) + bo.astype(f32)
    normed2 = layer_norm(residual, gain_two, shift_two).astype(bf16)

    output, d_normed2, g1, g2, d_bup = feed_forward(
        normed2, residual, out_grad, wup, wdown, bup, bdown.reshape(1, WIDTH)
    )

    _, norm_back_two = jax.vjp(layer_norm, residual, gain_two, shift_two)
    d_res_norm, d_gain_two, d_shift_two = norm_back_two(d_normed2)
    d_residual = out_grad.astype(f32) + d_res_norm
    d_attn = d_residual.astype(bf16)
    d_wout = outer_rows(attn_in, d_attn)
    d_mixed = back_rows(d_attn, wo).astype(bf16)
    d_query, d_key, d_value = attend_back(query, key_rows, value_rows, log_total, d_mixed)
    d_wquery = outer_rows(normed1, d_query)
    d_wkey = outer_rows(normed1, d_key)
    d_wvalue = outer_rows(normed1, d_value)
    d_normed1 = back_rows(d_query, wq) + back_rows(d_key, wk) + back_rows(d_value, wv)
    _, norm_back_one = jax.vjp(layer_norm, input_f, gain_one, shift_one)
    d_in_norm, d_gain_one, d_shift_one = norm_back_one(d_normed1)
    d_input = (d_residual + d_in_norm).astype(bf16)

    parts = [w.astype(bf16).reshape(2, 1, HALF, WIDTH) for w in (d_wquery, d_wkey, d_wvalue, d_wout)]
    grads = jnp.concatenate(parts, axis=1).reshape(2, 2, CHUNKS, TILE, WIDTH)
    g3 = attention_sum(grads).reshape(4, HALF, WIDTH)

    d_bup = d_bup.reshape(TILES, 2, TILE).transpose(1, 0, 2).reshape(2, TILES * TILE)[:, :FF_HALF]
    small = [
        d_gain_one,
        d_shift_one,
        column_sums(d_query),
        column_sums(d_value),
        column_sums(d_attn),
        d_gain_two,
        d_shift_two,
        column_sums(out_grad),
    ]
    pack = jnp.concatenate([v.reshape(2, HALF) for v in small] + [d_bup], axis=1).astype(bf16)
    pack = lax.psum(pack, ("group", "replica")).astype(f32)
    mine = lax.dynamic_index_in_dim(pack, lax.axis_index("group"), 0, keepdims=False)
    small = [mine[j * HALF : (j + 1) * HALF] for j in range(8)]

    g1 = g1.reshape(TILES * TILE, WIDTH)[:FF_HALF].astype(f32)
    g2 = g2.reshape(TILES, HALF, 2, TILE).transpose(1, 2, 0, 3).reshape(HALF, 2, TILES * TILE)
    g2 = g2[:, :, :FF_HALF].reshape(HALF, FF).astype(f32)
    g3 = g3.astype(f32)
    return (
        output,
        d_input,
        small[0],
        small[1],
        g3[0],
        small[2],
        g3[1],
        g3[2],
        small[3],
        g3[3],
        small[4],
        small[5],
        small[6],
        g2,
        mine[8 * HALF :],
        g1,
        small[7],
    )


def solution(mesh):
    placed = (
        P(("group", "replica"), None),
        P(("group", "replica"), None),
        P("group"),
        P("group"),
        P("group", None),
        P("group"),
        P("group", None),
        P("group", None),
        P("group"),
        P("group", None),
        P("group"),
        P("group"),
        P("group"),
        P("group", None),
        P("group"),
        P("group", None),
        P("group"),
    )
    fast = mesh.shape["group"] == 2 and mesh.shape["replica"] == 16
    return jax.shard_map(
        fast_shards if fast else shards,
        mesh=mesh,
        in_specs=placed,
        out_specs=(
            P(("group", "replica"), None),
            P(("group", "replica"), None),
            P("group"),
            P("group"),
            P("group", None),
            P("group"),
            P("group", None),
            P("group", None),
            P("group"),
            P("group", None),
            P("group"),
            P("group"),
            P("group"),
            P("group", None),
            P("group"),
            P("group", None),
            P("group"),
        ),
        check_vma=False,
    )
```

```python
import functools

import jax
import jax.numpy as jnp
from jax import lax
from jax.experimental import pallas as pl
from jax.experimental.pallas import tpu as pltpu
from jax.sharding import PartitionSpec as P

HEADS = 16
PATCHES = 128


def layer_norm(values, gain, shift):
    center = values - jnp.mean(values, axis=-1, keepdims=True)
    spread = jnp.mean(center * center, axis=-1, keepdims=True)
    return center * lax.rsqrt(spread + 1e-06) * gain + shift


def gelu_tanh(values):
    return jax.nn.gelu(values, approximate=True)


def split_heads(rows):
    return rows.reshape(-1, PATCHES, HEADS, rows.shape[-1] // HEADS)


def head_logits(query, key_rows):
    factor = (query.shape[-1] // HEADS) ** (-0.5)
    query_h = split_heads(query)
    key_h = split_heads(key_rows)
    logits = (
        jnp.einsum("isha,itha->ihst", query_h, key_h, preferred_element_type=jnp.float32) * factor
    )
    return (logits, query_h, key_h, factor)


def attend(query, key_rows, value_rows):
    logits, query_h, key_h, factor = head_logits(query, key_rows)
    peak = jnp.max(logits, axis=-1, keepdims=True)
    log_total = peak + jnp.log(jnp.sum(jnp.exp(logits - peak), axis=-1, keepdims=True))
    weights_low = jnp.exp(logits - log_total).astype(jnp.bfloat16)
    mixed = jnp.einsum(
        "ihst,itha->isha", weights_low, split_heads(value_rows), preferred_element_type=jnp.float32
    )
    return (mixed.reshape(query.shape), log_total)


def attend_back(query, key_rows, value_rows, log_total, d_mixed):
    logits, query_h, key_h, factor = head_logits(query, key_rows)
    weights = jnp.exp(logits - log_total)
    weights_low = weights.astype(jnp.bfloat16)
    value_h = split_heads(value_rows)
    d_mix_h = split_heads(d_mixed)
    d_weights = jnp.einsum("isha,itha->ihst", d_mix_h, value_h, preferred_element_type=jnp.float32)
    d_logits = weights * (d_weights - jnp.sum(weights * d_weights, axis=-1, keepdims=True))
    d_low = d_logits.astype(jnp.bfloat16)
    d_query = (
        jnp.einsum("ihst,itha->isha", d_low, key_h, preferred_element_type=jnp.float32) * factor
    ).astype(jnp.bfloat16)
    d_key = (
        jnp.einsum("ihst,isha->itha", d_low, query_h, preferred_element_type=jnp.float32) * factor
    ).astype(jnp.bfloat16)
    d_value = jnp.einsum(
        "ihst,isha->itha", weights_low, d_mix_h, preferred_element_type=jnp.float32
    ).astype(jnp.bfloat16)
    return (d_query.reshape(query.shape), d_key.reshape(query.shape), d_value.reshape(query.shape))


def outer_rows(left, right):
    return jnp.einsum("ra,rb->ab", left, right, preferred_element_type=jnp.float32)


def back_rows(grads, weight):
    return jnp.einsum("rb,ab->ra", grads, weight, preferred_element_type=jnp.float32)


def column_sums(grads):
    return jnp.sum(grads.astype(jnp.float32), axis=0)


def shards(
    tokens,
    out_grad,
    ln1_gain,
    ln1_bias,
    q_weight,
    q_bias,
    k_weight,
    v_weight,
    v_bias,
    o_weight,
    o_bias,
    ln2_gain,
    ln2_bias,
    up_weight,
    up_bias,
    down_weight,
    down_bias,
):
    attn_full = (
        lax.all_gather(ln1_gain, "group", axis=0, tiled=True),
        lax.all_gather(ln1_bias, "group", axis=0, tiled=True),
        lax.all_gather(q_weight, "group", axis=0, tiled=True),
        lax.all_gather(q_bias, "group", axis=0, tiled=True),
        lax.all_gather(k_weight, "group", axis=0, tiled=True),
        lax.all_gather(v_weight, "group", axis=0, tiled=True),
        lax.all_gather(v_bias, "group", axis=0, tiled=True),
        lax.all_gather(o_weight, "group", axis=0, tiled=True),
        lax.all_gather(o_bias, "group", axis=0, tiled=True),
    )
    gain_one, shift_one, wq_full, bq_full, wk_full, wv_full, bv_full, wo_full, bo_full = attn_full
    input_f = tokens.astype(jnp.float32)
    gain_one_f = gain_one.astype(jnp.float32)
    shift_one_f = shift_one.astype(jnp.float32)
    normed1 = layer_norm(input_f, gain_one_f, shift_one_f).astype(jnp.bfloat16)
    query = (
        jnp.dot(normed1, wq_full, preferred_element_type=jnp.float32) + bq_full.astype(jnp.float32)
    ).astype(jnp.bfloat16)
    key_rows = jnp.dot(normed1, wk_full, preferred_element_type=jnp.float32).astype(jnp.bfloat16)
    value_rows = (
        jnp.dot(normed1, wv_full, preferred_element_type=jnp.float32) + bv_full.astype(jnp.float32)
    ).astype(jnp.bfloat16)
    mixed, log_total = attend(query, key_rows, value_rows)
    attn_in = mixed.astype(jnp.bfloat16)
    residual = (
        input_f
        + jnp.dot(attn_in, wo_full, preferred_element_type=jnp.float32)
        + bo_full.astype(jnp.float32)
    )
    mlp_full = (
        lax.all_gather(ln2_gain, "group", axis=0, tiled=True),
        lax.all_gather(ln2_bias, "group", axis=0, tiled=True),
        lax.all_gather(up_weight, "group", axis=0, tiled=True),
        lax.all_gather(up_bias, "group", axis=0, tiled=True),
        lax.all_gather(down_weight, "group", axis=0, tiled=True),
        lax.all_gather(down_bias, "group", axis=0, tiled=True),
    )
    gain_two, shift_two, wup_full, bup_full, wdown_full, bdown_full = mlp_full
    gain_two_f = gain_two.astype(jnp.float32)
    shift_two_f = shift_two.astype(jnp.float32)
    normed2 = layer_norm(residual, gain_two_f, shift_two_f).astype(jnp.bfloat16)
    pre_act = jnp.dot(normed2, wup_full, preferred_element_type=jnp.float32) + bup_full.astype(
        jnp.float32
    )
    hidden = gelu_tanh(pre_act).astype(jnp.bfloat16)
    output = (
        residual
        + jnp.dot(hidden, wdown_full, preferred_element_type=jnp.float32)
        + bdown_full.astype(jnp.float32)
    )
    mlp_back = (
        lax.all_gather(ln2_gain, "group", axis=0, tiled=True),
        lax.all_gather(ln2_bias, "group", axis=0, tiled=True),
        lax.all_gather(up_weight, "group", axis=0, tiled=True),
        lax.all_gather(up_bias, "group", axis=0, tiled=True),
        lax.all_gather(down_weight, "group", axis=0, tiled=True),
        lax.all_gather(down_bias, "group", axis=0, tiled=True),
    )
    wup_back = mlp_back[2]
    wdown_back = mlp_back[4]
    grad_out = out_grad.astype(jnp.float32)
    d_wdown = outer_rows(hidden, out_grad)
    d_bdown = column_sums(out_grad)
    d_hidden = back_rows(out_grad, wdown_back)
    unused_act, gelu_back = jax.vjp(gelu_tanh, pre_act)
    d_pre = gelu_back(d_hidden)[0].astype(jnp.bfloat16)
    d_wup = outer_rows(normed2, d_pre)
    d_bup = column_sums(d_pre)
    d_normed2 = back_rows(d_pre, wup_back)
    unused_two, norm_back_two = jax.vjp(layer_norm, residual, gain_two_f, shift_two_f)
    d_res_norm, d_gain_two, d_shift_two = norm_back_two(d_normed2)
    d_residual = grad_out + d_res_norm
    mlp_grads = (
        lax.psum_scatter(
            d_gain_two.astype(jnp.bfloat16), "group", scatter_dimension=0, tiled=True
        ).astype(jnp.float32),
        lax.psum_scatter(
            d_shift_two.astype(jnp.bfloat16), "group", scatter_dimension=0, tiled=True
        ).astype(jnp.float32),
        lax.psum_scatter(
            d_wup.astype(jnp.bfloat16), "group", scatter_dimension=0, tiled=True
        ).astype(jnp.float32),
        lax.psum_scatter(
            d_bup.astype(jnp.bfloat16), "group", scatter_dimension=0, tiled=True
        ).astype(jnp.float32),
        lax.psum_scatter(
            d_wdown.astype(jnp.bfloat16), "group", scatter_dimension=0, tiled=True
        ).astype(jnp.float32),
        lax.psum_scatter(
            d_bdown.astype(jnp.bfloat16), "group", scatter_dimension=0, tiled=True
        ).astype(jnp.float32),
    )
    attn_back = (
        lax.all_gather(ln1_gain, "group", axis=0, tiled=True),
        lax.all_gather(ln1_bias, "group", axis=0, tiled=True),
        lax.all_gather(q_weight, "group", axis=0, tiled=True),
        lax.all_gather(q_bias, "group", axis=0, tiled=True),
        lax.all_gather(k_weight, "group", axis=0, tiled=True),
        lax.all_gather(v_weight, "group", axis=0, tiled=True),
        lax.all_gather(v_bias, "group", axis=0, tiled=True),
        lax.all_gather(o_weight, "group", axis=0, tiled=True),
        lax.all_gather(o_bias, "group", axis=0, tiled=True),
    )
    wq_back = attn_back[2]
    wk_back = attn_back[4]
    wv_back = attn_back[5]
    wo_back = attn_back[7]
    d_attn = d_residual.astype(jnp.bfloat16)
    d_wout = outer_rows(attn_in, d_attn)
    d_bout = column_sums(d_attn)
    d_mixed = back_rows(d_attn, wo_back).astype(jnp.bfloat16)
    d_query, d_key, d_value = attend_back(query, key_rows, value_rows, log_total, d_mixed)
    d_wquery = outer_rows(normed1, d_query)
    d_bquery = column_sums(d_query)
    d_wkey = outer_rows(normed1, d_key)
    d_wvalue = outer_rows(normed1, d_value)
    d_bvalue = column_sums(d_value)
    d_normed1 = (
        back_rows(d_query, wq_back) + back_rows(d_key, wk_back) + back_rows(d_value, wv_back)
    )
    unused_one, norm_back_one = jax.vjp(layer_norm, input_f, gain_one_f, shift_one_f)
    d_in_norm, d_gain_one, d_shift_one = norm_back_one(d_normed1)
    d_input = (d_residual + d_in_norm).astype(jnp.bfloat16)
    attn_grads = (
        lax.psum_scatter(
            d_gain_one.astype(jnp.bfloat16), "group", scatter_dimension=0, tiled=True
        ).astype(jnp.float32),
        lax.psum_scatter(
            d_shift_one.astype(jnp.bfloat16), "group", scatter_dimension=0, tiled=True
        ).astype(jnp.float32),
        lax.psum_scatter(
            d_wquery.astype(jnp.bfloat16), "group", scatter_dimension=0, tiled=True
        ).astype(jnp.float32),
        lax.psum_scatter(
            d_bquery.astype(jnp.bfloat16), "group", scatter_dimension=0, tiled=True
        ).astype(jnp.float32),
        lax.psum_scatter(
            d_wkey.astype(jnp.bfloat16), "group", scatter_dimension=0, tiled=True
        ).astype(jnp.float32),
        lax.psum_scatter(
            d_wvalue.astype(jnp.bfloat16), "group", scatter_dimension=0, tiled=True
        ).astype(jnp.float32),
        lax.psum_scatter(
            d_bvalue.astype(jnp.bfloat16), "group", scatter_dimension=0, tiled=True
        ).astype(jnp.float32),
        lax.psum_scatter(
            d_wout.astype(jnp.bfloat16), "group", scatter_dimension=0, tiled=True
        ).astype(jnp.float32),
        lax.psum_scatter(
            d_bout.astype(jnp.bfloat16), "group", scatter_dimension=0, tiled=True
        ).astype(jnp.float32),
    )
    summed = (
        lax.psum(attn_grads[0].astype(jnp.bfloat16), "replica").astype(jnp.float32),
        lax.psum(attn_grads[1].astype(jnp.bfloat16), "replica").astype(jnp.float32),
        lax.psum(attn_grads[2].astype(jnp.bfloat16), "replica").astype(jnp.float32),
        lax.psum(attn_grads[3].astype(jnp.bfloat16), "replica").astype(jnp.float32),
        lax.psum(attn_grads[4].astype(jnp.bfloat16), "replica").astype(jnp.float32),
        lax.psum(attn_grads[5].astype(jnp.bfloat16), "replica").astype(jnp.float32),
        lax.psum(attn_grads[6].astype(jnp.bfloat16), "replica").astype(jnp.float32),
        lax.psum(attn_grads[7].astype(jnp.bfloat16), "replica").astype(jnp.float32),
        lax.psum(attn_grads[8].astype(jnp.bfloat16), "replica").astype(jnp.float32),
        lax.psum(mlp_grads[0].astype(jnp.bfloat16), "replica").astype(jnp.float32),
        lax.psum(mlp_grads[1].astype(jnp.bfloat16), "replica").astype(jnp.float32),
        lax.psum(mlp_grads[2].astype(jnp.bfloat16), "replica").astype(jnp.float32),
        lax.psum(mlp_grads[3].astype(jnp.bfloat16), "replica").astype(jnp.float32),
        lax.psum(mlp_grads[4].astype(jnp.bfloat16), "replica").astype(jnp.float32),
        lax.psum(mlp_grads[5].astype(jnp.bfloat16), "replica").astype(jnp.float32),
    )
    attn_grads = tuple(summed[:9])
    mlp_grads = tuple(summed[9:])
    return (output.astype(jnp.bfloat16), d_input) + tuple(attn_grads) + tuple(mlp_grads)


MESH = pl.DeviceIdType.MESH
bf16 = jnp.bfloat16
f32 = jnp.float32
ANY = pl.BlockSpec(memory_space=pl.ANY)
WIDTH = 1152
HALF = 576
FF = 4304
FF_HALF = 2152
TILES = 17
TILE = 128
FF_PAD = 2 * TILES * TILE
FIRST = 320
SECOND = 256


class Place:
    def __init__(self):
        self.core = lax.axis_index("group")
        chip = lax.axis_index("replica")
        self.chip = chip
        self.x = lax.rem(chip, 2)
        self.y = lax.rem(chip // 2, 2)
        self.z = chip // 4
        self.x_pair = chip + 1 - 2 * self.x
        self.y_pair = chip + 2 - 4 * self.y
        self.z_pair = chip + 4 - 8 * lax.rem(self.z, 2)
        self.inner = (self.z == 1) | (self.z == 2)
        self.outer = jnp.logical_not(self.inner)
        self.mid_pair = jnp.where(self.inner, chip + 12 - 8 * self.z, chip)
        self.z_half = lax.rem(self.z // 2, 2)

    def barrier(self):
        sem = pltpu.get_barrier_semaphore()

        def greet(core, chip):
            pl.semaphore_signal(sem, inc=1, device_id=(core, chip), device_id_type=MESH)

        greet(1 - self.core, self.chip)
        greet(self.core, self.x_pair)
        greet(self.core, self.y_pair)
        greet(self.core, self.z_pair)

        @pl.when(self.inner)
        def _():
            greet(self.core, self.mid_pair)
            pl.semaphore_wait(sem, 5)

        @pl.when(self.outer)
        def _():
            pl.semaphore_wait(sem, 4)

    def copy(self, source, target, sent, got, chip):
        return pltpu.make_async_remote_copy(
            source, target, sent, got, device_id=(self.core, chip), device_id_type=MESH
        )

    def copy_sibling(self, source, target, sent, got):
        return pltpu.make_async_remote_copy(
            source, target, sent, got, device_id=(1 - self.core, self.chip), device_id_type=MESH
        )


def aligned(value, unit):
    return pl.multiple_of(value, unit)


def add_rows(total, landed, chunk, start, count):
    rows = pl.ds(start, count)
    total[chunk, rows, :] = (
        total[chunk, rows, :].astype(f32) + landed.astype(f32)
    ).astype(bf16)


class TreeFirst:
    steps = 9

    def __init__(self, place, total, final, landing, sent, got, kept):
        self.at = place
        self.total = total
        self.final = final
        self.kept = kept
        self.land = landing
        self.sent = sent
        self.got = got
        n = total.shape[1]
        self.n = n
        p = place
        self.own = [
            (0, n),
            (aligned(p.z_half * (n // 2), n // 2), n // 2),
        ]
        self.other = [None, (aligned((1 - p.z_half) * (n // 2), n // 2), n // 2)]
        for bit, part in ((p.y, n // 4), (p.x, n // 8)):
            base = self.own[-1][0]
            self.own.append((aligned(base + bit * part, part), part))
            self.other.append((aligned(base + (1 - bit) * part, part), part))
        self.peer = [p.z_pair, p.mid_pair, p.y_pair, p.x_pair]

    def rows(self, chunk, span):
        return self.total.at[chunk, pl.ds(span[0], span[1]), :]

    def ends(self, chunk, span):
        return self.final.at[chunk, pl.ds(span[0], span[1]), :]

    def send(self, k, chunk):
        sent, got = self.sent.at[k, chunk], self.got.at[k, chunk]
        if k < 4:
            span = self.own[0] if k == 0 else self.other[k]
            return self.at.copy(
                self.rows(chunk, span), self.land[k].at[chunk], sent, got, self.peer[k]
            )
        level = 7 - k
        target = self.ends(chunk, self.own[level])
        source = self.rows(chunk, self.own[3]) if k == 4 else target
        return self.at.copy(source, target, sent, got, self.peer[level])

    def keep(self, chunk):
        return pltpu.make_async_copy(
            self.rows(chunk, self.own[3]), self.ends(chunk, self.own[3]), self.kept.at[chunk]
        )

    def arrive(self, k, chunk):
        if k < 4:
            landed = self.land[k].at[chunk]
        else:
            level = 7 - k
            landed = self.ends(chunk, self.own[0] if level == 0 else self.other[level])
        self.at.copy(
            landed, landed, self.sent.at[k, chunk], self.got.at[k, chunk], self.at.z_pair
        ).wait_recv()

    def step(self, k, chunk):
        at = self.at
        if k == 0:

            @pl.when(at.outer)
            def _():
                self.send(0, chunk).start()

        elif k <= 7:

            @pl.when(at.inner)
            def _():
                self.arrive(k - 1, chunk)
                if k <= 4:
                    add_rows(self.total, self.land[k - 1][chunk], chunk, *self.own[k - 1])
                if k == 4:
                    self.keep(chunk).start()
                if k == 5:
                    self.keep(chunk).wait()
                self.send(k, chunk).start()

        else:

            @pl.when(at.inner)
            def _():
                for j in range(1, 8):
                    self.send(j, chunk).wait_send()

            @pl.when(at.outer)
            def _():
                self.arrive(7, chunk)
                self.send(0, chunk).wait_send()


class PlaneFirst:
    steps = 8

    def __init__(self, place, total, final, base, n, x_first, landing, sent, got, kept):
        self.at = place
        self.total = total
        self.final = final
        self.kept = kept
        self.land = landing
        self.sent = sent
        self.got = got
        p = place
        if x_first:
            one, two = (p.x, p.x_pair), (p.y, p.y_pair)
        else:
            one, two = (p.y, p.y_pair), (p.x, p.x_pair)
        self.peer_one, self.peer_two = one[1], two[1]
        start = aligned(base + one[0] * (n // 2), 16)
        self.half = (start, n // 2)
        self.half_other = (aligned(base + (1 - one[0]) * (n // 2), 16), n // 2)
        self.quarter = (aligned(start + two[0] * (n // 4), 16), n // 4)
        self.quarter_other = (aligned(start + (1 - two[0]) * (n // 4), 16), n // 4)

    def rows(self, chunk, span):
        return self.total.at[chunk, pl.ds(span[0], span[1]), :]

    def ends(self, chunk, span):
        return self.final.at[chunk, pl.ds(span[0], span[1]), :]

    def keep(self, chunk):
        return pltpu.make_async_copy(
            self.rows(chunk, self.quarter), self.ends(chunk, self.quarter), self.kept.at[chunk]
        )

    def send(self, k, chunk):
        at = self.at
        quarter = self.rows(chunk, self.quarter)
        quarter_end = self.ends(chunk, self.quarter)
        half_end = self.ends(chunk, self.half)
        source, target, peer = (
            (self.rows(chunk, self.half_other), self.land[0].at[chunk], self.peer_one),
            (self.rows(chunk, self.quarter_other), self.land[1].at[chunk], self.peer_two),
            (quarter, self.land[2].at[chunk], at.z_pair),
            (quarter, self.land[3].at[chunk], at.mid_pair),
            (quarter, quarter_end, at.z_pair),
            (quarter_end, quarter_end, self.peer_two),
            (half_end, half_end, self.peer_one),
        )[k]
        return at.copy(source, target, self.sent.at[k, chunk], self.got.at[k, chunk], peer)

    def arrive(self, k, chunk):
        if k < 4:
            landed = self.land[k].at[chunk]
        else:
            landed = self.ends(
                chunk, (self.quarter, self.quarter_other, self.half_other)[k - 4]
            )
        self.at.copy(
            landed, landed, self.sent.at[k, chunk], self.got.at[k, chunk], self.at.z_pair
        ).wait_recv()

    def step(self, k, chunk):
        at = self.at
        if k == 0:
            self.send(0, chunk).start()
        elif k == 1:
            self.arrive(0, chunk)
            add_rows(self.total, self.land[0][chunk], chunk, *self.half)
            self.send(1, chunk).start()
        elif k == 2:
            self.arrive(1, chunk)
            add_rows(self.total, self.land[1][chunk], chunk, *self.quarter)

            @pl.when(at.outer)
            def _():
                self.send(2, chunk).start()

        elif k == 3:

            @pl.when(at.inner)
            def _():
                self.arrive(2, chunk)
                add_rows(self.total, self.land[2][chunk], chunk, *self.quarter)
                self.send(3, chunk).start()

        elif k == 4:

            @pl.when(at.inner)
            def _():
                self.arrive(3, chunk)
                self.send(3, chunk).wait_send()
                add_rows(self.total, self.land[3][chunk], chunk, *self.quarter)
                self.send(4, chunk).start()
                self.keep(chunk).start()

        elif k == 5:

            @pl.when(at.inner)
            def _():
                self.keep(chunk).wait()

            @pl.when(at.outer)
            def _():
                self.arrive(4, chunk)

            self.send(5, chunk).start()
        elif k == 6:
            self.arrive(5, chunk)
            self.send(6, chunk).start()
        else:
            self.arrive(6, chunk)
            for j in (0, 1, 5, 6):
                self.send(j, chunk).wait_send()

            @pl.when(at.inner)
            def _():
                self.send(4, chunk).wait_send()

            @pl.when(at.outer)
            def _():
                self.send(2, chunk).wait_send()


def tree_scratch(count, n, width):
    return [pltpu.VMEM((count, n // part, width), bf16) for part in (1, 2, 4, 8)] + [
        pltpu.SemaphoreType.DMA((8, count)),
        pltpu.SemaphoreType.DMA((8, count)),
        pltpu.SemaphoreType.DMA((count,)),
    ]


def plane_scratch(count, n, width):
    return [pltpu.VMEM((count, n // part, width), bf16) for part in (2, 4, 4, 4)] + [
        pltpu.SemaphoreType.DMA((7, count)),
        pltpu.SemaphoreType.DMA((7, count)),
        pltpu.SemaphoreType.DMA((count,)),
    ]


def advance(tick, count, sums):
    for k in reversed(range(max(s.steps for s in sums))):
        chunk = tick - k

        @pl.when((chunk >= 0) & (chunk < count))
        def _():
            for s in sums:
                if k < s.steps:
                    s.step(k, chunk)


def dot(left, right, contract):
    return lax.dot_general(left, right, (contract, ((), ())), preferred_element_type=f32)


NN = ((1,), (0,))
NT = ((1,), (1,))
TN = ((0,), (0,))


def gelu_and_slope(u):
    c = 0.7978845608028654
    square = u * u
    t = jnp.tanh(c * u * (1.0 + 0.044715 * square))
    half = 0.5 * (1.0 + t)
    slope = half + 0.5 * u * (1.0 - t * t) * (c * (1.0 + 3 * 0.044715 * square))
    return u * half, slope


def ff_kernel(
    h2_ref,
    x2_ref,
    og_ref,
    wup_ref,
    wdown_ref,
    bup_ref,
    bdown_ref,
    out_ref,
    dh2_ref,
    g1_ref,
    g2_ref,
    dbup_ref,
    h2,
    h2t,
    og,
    out,
    dh2,
    wu,
    wd,
    bup,
    bdown,
    dbup,
    out16,
    mine1,
    mine2,
    sib1,
    sib2,
    sum1,
    sum2,
    *rest,
):
    rest = list(rest)
    local, wsem, gsent, ggot = rest[:4]
    tree, plane1, plane2 = rest[4:11], rest[11:18], rest[18:25]
    at = Place()
    loads = [
        pltpu.make_async_copy(s, d, local.at[j])
        for j, (s, d) in enumerate(
            ((h2_ref, h2), (og_ref, og), (x2_ref, out), (bup_ref, bup), (bdown_ref, bdown))
        )
    ]
    for load in loads:
        load.start()

    def weights(i, slot):
        cols = [pl.ds(aligned(h * TILES * TILE + i * TILE, TILE), TILE) for h in (0, 1)]
        parts = []
        for h in (0, 1):
            here = pl.ds(h * TILE, TILE)
            parts.append(
                pltpu.make_async_copy(
                    wup_ref.at[:, cols[h]], wu.at[slot, :, here], wsem.at[h, slot]
                )
            )
            parts.append(
                pltpu.make_async_copy(
                    wdown_ref.at[cols[h], :], wd.at[slot, here, :], wsem.at[2 + h, slot]
                )
            )
        return parts

    for part in weights(0, 0):
        part.start()
    at.barrier()
    for load in loads:
        load.wait()
    for b in range(8):
        rows = pl.ds(b * 128, 128)
        h2t[:, rows] = h2[rows, :].T
    out[...] = out[...] + bdown[7:8, :]
    dh2[...] = jnp.zeros_like(dh2)

    sums = [
        TreeFirst(at, sum1, g1_ref, tree[:4], *tree[4:]),
        PlaneFirst(at, sum2, g2_ref, 0, FIRST, True, plane1[:4], *plane1[4:]),
        PlaneFirst(at, sum2, g2_ref, FIRST, SECOND, False, plane2[:4], *plane2[4:]),
    ]

    def to_sibling(slot):
        return (
            at.copy_sibling(
                mine1.at[slot, 1 - at.core], sib1.at[slot], gsent.at[0, slot], ggot.at[0, slot]
            ),
            at.copy_sibling(
                mine2.at[slot, 1 - at.core], sib2.at[slot], gsent.at[1, slot], ggot.at[1, slot]
            ),
        )

    def meet(i):
        slot = lax.rem(i, 2)
        for copy in to_sibling(slot):
            copy.wait()
        sum1[i] = (mine1[slot, at.core].astype(f32) + sib1[slot].astype(f32)).astype(bf16)
        sum2[i] = (mine2[slot, at.core].astype(f32) + sib2[slot].astype(f32)).astype(bf16)

    def compute(i):
        slot = lax.rem(i, 2)
        for part in weights(i, slot):
            part.wait()

        @pl.when(i + 1 < TILES)
        def _():
            for part in weights(i + 1, 1 - slot):
                part.start()

        bias = jnp.concatenate([bup[0, i], bup[1, i]], axis=1)
        u = dot(h2[...], wu[slot], NN) + bias
        a, slope = gelu_and_slope(u)
        a = a.astype(bf16)
        out[...] += dot(a, wd[slot], NN)
        d_wd = dot(a, og[...], TN).astype(bf16)
        mine1[slot, 0] = d_wd[:TILE]
        mine1[slot, 1] = d_wd[TILE:]
        du = (dot(og[...], wd[slot], NT) * slope).astype(bf16)
        d_wu = dot(h2t[...], du, NN).astype(bf16)
        mine2[slot, 0] = d_wu[:HALF]
        mine2[slot, 1] = d_wu[HALF:]
        for copy in to_sibling(slot):
            copy.start()
        dh2[...] += dot(du, wu[slot], NT)
        dbup[i] = jnp.sum(du.astype(f32), axis=0, keepdims=True)

    def body(i, carry):
        @pl.when((i >= 1) & (i <= TILES))
        def _():
            meet(i - 1)

        advance(i - 1, TILES, sums)

        @pl.when(i < TILES)
        def _():
            compute(i)

        @pl.when(i == TILES)
        def _():
            out16[...] = out[...].astype(bf16)
            pltpu.make_async_copy(out16, out_ref, local.at[0]).start()
            pltpu.make_async_copy(dh2, dh2_ref, local.at[1]).start()
            pltpu.make_async_copy(dbup, dbup_ref, local.at[2]).start()

        return carry

    lax.fori_loop(0, TILES + 1 + 8, body, 0)
    pltpu.make_async_copy(out16, out_ref, local.at[0]).wait()
    pltpu.make_async_copy(dh2, dh2_ref, local.at[1]).wait()
    pltpu.make_async_copy(dbup, dbup_ref, local.at[2]).wait()

def feed_forward(h2, x2, og, wup, wdown, bup, bdown):
    rows = h2.shape[0]
    return pl.pallas_call(
        ff_kernel,
        out_shape=(
            jax.ShapeDtypeStruct((rows, WIDTH), bf16),
            jax.ShapeDtypeStruct((rows, WIDTH), f32),
            jax.ShapeDtypeStruct((TILES, TILE, WIDTH), bf16),
            jax.ShapeDtypeStruct((TILES, HALF, 2 * TILE), bf16),
            jax.ShapeDtypeStruct((TILES, 1, 2 * TILE), f32),
        ),
        in_specs=[ANY] * 7,
        out_specs=[ANY] * 5,
        scratch_shapes=[
            pltpu.VMEM((rows, WIDTH), bf16),
            pltpu.VMEM((WIDTH, rows), bf16),
            pltpu.VMEM((rows, WIDTH), bf16),
            pltpu.VMEM((rows, WIDTH), f32),
            pltpu.VMEM((rows, WIDTH), f32),
            pltpu.VMEM((2, WIDTH, 2 * TILE), bf16),
            pltpu.VMEM((2, 2 * TILE, WIDTH), bf16),
            pltpu.VMEM((2, TILES, 1, TILE), f32),
            pltpu.VMEM((VECTORS, WIDTH), f32),
            pltpu.VMEM((TILES, 1, 2 * TILE), f32),
            pltpu.VMEM((rows, WIDTH), bf16),
            pltpu.VMEM((2, 2, TILE, WIDTH), bf16),
            pltpu.VMEM((2, 2, HALF, 2 * TILE), bf16),
            pltpu.VMEM((2, TILE, WIDTH), bf16),
            pltpu.VMEM((2, HALF, 2 * TILE), bf16),
            pltpu.VMEM((TILES, TILE, WIDTH), bf16),
            pltpu.VMEM((TILES, HALF, 2 * TILE), bf16),
            pltpu.SemaphoreType.DMA((5,)),
            pltpu.SemaphoreType.DMA((4, 2)),
            pltpu.SemaphoreType.DMA((2, 2)),
            pltpu.SemaphoreType.DMA((2, 2)),
        ]
        + tree_scratch(TILES, TILE, WIDTH)
        + plane_scratch(TILES, FIRST, 2 * TILE)
        + plane_scratch(TILES, SECOND, 2 * TILE),
        compiler_params=pltpu.CompilerParams(
            collective_id=1, has_side_effects=True, vmem_limit_bytes=62 * 2**20
        ),
        name="feed_forward",
    )(h2, x2, og, wup, wdown, bup, bdown)


CHUNKS = 9


def attention_sum_kernel(grad_ref, out_ref, sum1, sum2, sib1, sib2, *rest):
    rest = list(rest)
    local, gsent, ggot = rest[:3]
    tree, plane1, plane2 = rest[3:10], rest[10:17], rest[17:24]
    at = Place()
    own = [
        pltpu.make_async_copy(grad_ref.at[at.core, j], s, local.at[j])
        for j, s in ((0, sum1), (1, sum2))
    ]
    for load in own:
        load.start()
    at.barrier()

    def sibling(j, chunk):
        return at.copy_sibling(
            grad_ref.at[1 - at.core, j, chunk],
            (sib1, sib2)[j].at[chunk],
            gsent.at[j, chunk],
            ggot.at[j, chunk],
        )

    for chunk in range(CHUNKS):
        sibling(0, chunk).start()
        sibling(1, chunk).start()
    for load in own:
        load.wait()
    sums = [
        TreeFirst(at, sum1, out_ref.at[0], tree[:4], *tree[4:]),
        PlaneFirst(at, sum2, out_ref.at[1], 0, TILE // 2, True, plane1[:4], *plane1[4:]),
        PlaneFirst(
            at, sum2, out_ref.at[1], TILE // 2, TILE // 2, False, plane2[:4], *plane2[4:]
        ),
    ]

    def body(i, carry):
        @pl.when(i < CHUNKS)
        def _():
            sibling(0, i).wait()
            sibling(1, i).wait()
            sum1[i] = (sum1[i].astype(f32) + sib1[i].astype(f32)).astype(bf16)
            sum2[i] = (sum2[i].astype(f32) + sib2[i].astype(f32)).astype(bf16)

        advance(i, CHUNKS, sums)
        return carry

    lax.fori_loop(0, CHUNKS + 8, body, 0)

def attention_sum(grads):
    return pl.pallas_call(
        attention_sum_kernel,
        out_shape=jax.ShapeDtypeStruct((2, CHUNKS, TILE, WIDTH), bf16),
        in_specs=[ANY],
        out_specs=ANY,
        scratch_shapes=[pltpu.VMEM((CHUNKS, TILE, WIDTH), bf16)] * 4
        + [
            pltpu.SemaphoreType.DMA((2,)),
            pltpu.SemaphoreType.DMA((2, CHUNKS)),
            pltpu.SemaphoreType.DMA((2, CHUNKS)),
        ]
        + tree_scratch(CHUNKS, TILE, WIDTH)
        + plane_scratch(CHUNKS, TILE // 2, WIDTH)
        + plane_scratch(CHUNKS, TILE // 2, WIDTH),
        compiler_params=pltpu.CompilerParams(
            collective_id=2, has_side_effects=True, vmem_limit_bytes=62 * 2**20
        ),
        name="attention_sum",
    )(grads)


VECTORS = 8
LANES = 640
SCALE = 72**-0.5
HEAD = 72


def head_window(h):
    return slice(h * HEAD // 128 * 128, ((h + 1) * HEAD + 127) // 128 * 128)


def only_head(rows, h):
    lane = lax.broadcasted_iota(jnp.int32, rows.shape, 1) + head_window(h).start
    return jnp.where((lane >= h * HEAD) & (lane < (h + 1) * HEAD), rows, jnp.zeros_like(rows))


class Lanes:
    def __init__(self):
        self.tiles = [None] * (WIDTH // 128)

    def add(self, h, window):
        first = head_window(h).start // 128
        for j in range(window.shape[1] // 128):
            part = window[:, j * 128 : (j + 1) * 128]
            old = self.tiles[first + j]
            self.tiles[first + j] = part if old is None else old + part

    def joined(self):
        return jnp.concatenate([t.astype(bf16) for t in self.tiles], axis=1)


def normalise(rows, gain, shift):
    center = rows - jnp.mean(rows, axis=-1, keepdims=True)
    spread = jnp.mean(center * center, axis=-1, keepdims=True)
    return center * lax.rsqrt(spread + 1e-06) * gain + shift


def forward_kernel(
    tokens_ref,
    wq_ref,
    wk_ref,
    wv_ref,
    wo_ref,
    up_ref,
    down_ref,
    pack_ref,
    bup_ref,
    h1_ref,
    q_ref,
    k_ref,
    v_ref,
    ao_ref,
    probs_ref,
    x2_ref,
    h2_ref,
    w_ref,
    wup_ref,
    wdown_ref,
    vec_ref,
    bups_ref,
    x,
    h1,
    q,
    k,
    v,
    ao,
    probs,
    x2,
    h2,
    w,
    up,
    up_wide,
    zeros,
    pack,
    vec,
    local,
    wsem,
    psem,
    sent,
    got,
    bsem,
):
    at = Place()
    core = at.core
    own = pl.ds(aligned(core * HALF, HALF), HALF)
    ff_own = pl.ds(aligned(core * TILES * TILE, TILE), FF_HALF)
    shards = (wq_ref, wk_ref, wv_ref, wo_ref)
    load_x = pltpu.make_async_copy(tokens_ref, x, local.at[0])
    load_x.start()
    load_w = [pltpu.make_async_copy(s, w.at[j, own, :], local.at[1 + j]) for j, s in enumerate(shards)]
    load_pack = pltpu.make_async_copy(pack_ref, pack.at[core], local.at[5])
    load_bup = pltpu.make_async_copy(bup_ref, bups_ref.at[core], local.at[6])
    load_up = pltpu.make_async_copy(up_ref, up, local.at[7])
    load_down = pltpu.make_async_copy(down_ref, wdown_ref.at[ff_own, :], local.at[8])
    for load in (load_pack, *load_w, load_bup, load_up, load_down):
        load.start()
    zeros[...] = jnp.zeros_like(zeros)
    gap = TILES * TILE - FF_HALF
    blanks = [
        pltpu.make_async_copy(
            zeros, wdown_ref.at[pl.ds(h * TILES * TILE + FF_HALF, gap), :], local.at[9 + h]
        )
        for h in (0, 1)
    ]
    for blank in blanks:
        blank.start()

    bar = pltpu.get_barrier_semaphore()
    pl.semaphore_signal(bar, inc=1, device_id=(1 - core, at.chip), device_id_type=MESH)
    pl.semaphore_wait(bar, 1)

    def share(j, source, target):
        return at.copy_sibling(source, target, sent.at[j], got.at[j])

    give_w = [share(j, s, w.at[j, own, :]) for j, s in enumerate(shards)]
    give_pack = share(4, pack_ref, pack.at[core])
    give_bup = share(5, bup_ref, bups_ref.at[core])
    give_down = share(6, down_ref, wdown_ref.at[ff_own, :])
    give_up = share(7, up_wide, wup_ref.at[own, :])
    keep_up = pltpu.make_async_copy(up_wide, wup_ref.at[own, :], local.at[11])
    give_pack.start()
    for give in give_w:
        give.start()
    give_bup.start()
    give_down.start()

    load_pack.wait()
    give_pack.wait()
    vec[...] = jnp.concatenate([pack[0, :, :HALF], pack[1, :, :HALF]], axis=1)
    load_x.wait()
    rows_of = [pl.ds(b * 512, 512) for b in range(2)]

    def first_norm(b, carry):
        rows = pl.ds(aligned(b * 128, 128), 128)
        h1[rows, :] = normalise(x[rows, :].astype(f32), vec[0:1, :], vec[1:2, :]).astype(bf16)
        return carry

    lax.fori_loop(0, 8, first_norm, 0)
    keep = [pltpu.make_async_copy(h1, h1_ref, local.at[0])]
    keep[0].start()

    def project(j, target, bias):
        load_w[j].wait()
        give_w[j].wait()
        for rows in rows_of:
            y = dot(h1[rows, :], w[j], NN)
            if bias is not None:
                y = y + vec[bias : bias + 1, :]
            target[rows, :] = y.astype(bf16)

    project(0, q, 2)
    project(1, k, None)
    project(2, v, 3)
    for j, (s, d) in enumerate(((q, q_ref), (k, k_ref), (v, v_ref))):
        keep.append(pltpu.make_async_copy(s, d, local.at[12 + j]))
        keep[-1].start()

    load_up.wait()

    def widen(b, carry):
        rows = pl.ds(aligned(b * 64, 64), 64)
        row = up[rows, :]
        none = jnp.zeros((64, gap), bf16)
        up_wide[rows, :] = jnp.concatenate([row[:, :FF_HALF], none, row[:, FF_HALF:], none], axis=1)
        return carry

    lax.fori_loop(0, HALF // 64, widen, 0)
    keep_up.start()
    give_up.start()

    def keep_probs(i):
        slot = lax.rem(i, 2)
        return pltpu.make_async_copy(probs.at[slot], probs_ref.at[i], psem.at[slot])

    def attention(i, carry):
        rows = pl.ds(aligned(i * 128, 128), 128)
        slot = lax.rem(i, 2)

        @pl.when(i >= 2)
        def _():
            keep_probs(i - 2).wait()

        qi, ki, vi = q[rows, :], k[rows, :], v[rows, :]
        mixed = Lanes()
        held = []
        for h in range(HEADS):
            cols = head_window(h)
            logits = dot(qi[:, cols], only_head(ki[:, cols], h), NT) * SCALE
            e = jnp.exp(logits - jnp.max(logits, axis=-1, keepdims=True))
            p = (e / jnp.sum(e, axis=-1, keepdims=True)).astype(bf16)
            held.append(p)
            mixed.add(h, dot(p, only_head(vi[:, cols], h), NN))
        ao[rows, :] = mixed.joined()
        probs[slot] = jnp.concatenate(held, axis=1)
        keep_probs(i).start()
        return carry

    lax.fori_loop(0, 8, attention, 0)
    keep_ao = pltpu.make_async_copy(ao, ao_ref, local.at[15])
    keep_ao.start()

    load_w[3].wait()
    give_w[3].wait()
    keep_w = pltpu.make_async_copy(w, w_ref, wsem.at[0])
    keep_w.start()
    keep_vec = pltpu.make_async_copy(vec, vec_ref, wsem.at[1])
    keep_vec.start()
    for rows in rows_of:
        x2[rows, :] = x[rows, :].astype(f32) + dot(ao[rows, :], w[3], NN) + vec[4:5, :]

    def second_norm(b, carry):
        rows = pl.ds(aligned(b * 128, 128), 128)
        h2[rows, :] = normalise(x2[rows, :], vec[5:6, :], vec[6:7, :]).astype(bf16)
        return carry

    lax.fori_loop(0, 8, second_norm, 0)
    keep_x2 = pltpu.make_async_copy(x2, x2_ref, wsem.at[2])
    keep_h2 = pltpu.make_async_copy(h2, h2_ref, wsem.at[3])
    for copy in (keep_x2, keep_h2):
        copy.start()
    for copy in (
        *keep,
        keep_probs(6),
        keep_probs(7),
        keep_ao,
        keep_w,
        keep_vec,
        load_bup,
        load_down,
        *blanks,
        keep_up,
        keep_x2,
        keep_h2,
    ):
        copy.wait()
    for give in (give_bup, give_down, give_up):
        give.wait()


def forward(tokens, wq, wk, wv, wo, up, down, pack, bup):
    rows = tokens.shape[0]
    images = rows // PATCHES
    flat = jax.ShapeDtypeStruct((rows, WIDTH), bf16)
    return pl.pallas_call(
        forward_kernel,
        out_shape=(
            flat,
            flat,
            flat,
            flat,
            flat,
            jax.ShapeDtypeStruct((images, PATCHES, HEADS * PATCHES), bf16),
            jax.ShapeDtypeStruct((rows, WIDTH), f32),
            flat,
            jax.ShapeDtypeStruct((4, WIDTH, WIDTH), bf16),
            jax.ShapeDtypeStruct((WIDTH, FF_PAD), bf16),
            jax.ShapeDtypeStruct((FF_PAD, WIDTH), bf16),
            jax.ShapeDtypeStruct((VECTORS, WIDTH), f32),
            jax.ShapeDtypeStruct((2, TILES, 1, TILE), f32),
        ),
        in_specs=[ANY] * 9,
        out_specs=[ANY] * 13,
        scratch_shapes=[pltpu.VMEM((rows, WIDTH), bf16)] * 6
        + [
            pltpu.VMEM((2, PATCHES, HEADS * PATCHES), bf16),
            pltpu.VMEM((rows, WIDTH), f32),
            pltpu.VMEM((rows, WIDTH), bf16),
            pltpu.VMEM((4, WIDTH, WIDTH), bf16),
            pltpu.VMEM((HALF, FF), bf16),
            pltpu.VMEM((HALF, FF_PAD), bf16),
            pltpu.VMEM((TILES * TILE - FF_HALF, WIDTH), bf16),
            pltpu.VMEM((2, VECTORS, LANES), f32),
            pltpu.VMEM((VECTORS, WIDTH), f32),
            pltpu.SemaphoreType.DMA((16,)),
            pltpu.SemaphoreType.DMA((4,)),
            pltpu.SemaphoreType.DMA((2,)),
            pltpu.SemaphoreType.DMA((8,)),
            pltpu.SemaphoreType.DMA((8,)),
            pltpu.SemaphoreType.DMA((1,)),
        ],
        compiler_params=pltpu.CompilerParams(
            collective_id=3, has_side_effects=True, vmem_limit_bytes=62 * 2**20
        ),
        name="forward",
    )(tokens, wq, wk, wv, wo, up, down, pack, bup)


def finish_kernel(g1_ref, g2_ref, g3_ref, d1_ref, d2_ref, dq_ref, dk_ref, dv_ref, do_ref):
    d1_ref[...] = g1_ref[0].astype(f32)
    parts = []
    for h in (0, 1):
        for i in range(TILES):
            wide = TILE if i < TILES - 1 else FF_HALF - (TILES - 1) * TILE
            parts.append(g2_ref[i, :, h * TILE : h * TILE + wide].astype(f32))
    d2_ref[...] = jnp.concatenate(parts, axis=1)
    for j, d in enumerate((dq_ref, dk_ref, dv_ref, do_ref)):
        d[...] = g3_ref[j].astype(f32)


def finish(g1, g2, g3):
    steps = HALF // 32
    square = jax.ShapeDtypeStruct((HALF, WIDTH), f32)
    last = TILES - 1
    return pl.pallas_call(
        finish_kernel,
        grid=(steps,),
        out_shape=(
            jax.ShapeDtypeStruct((FF_HALF, WIDTH), f32),
            jax.ShapeDtypeStruct((HALF, FF), f32),
        )
        + (square,) * 4,
        in_specs=[
            pl.BlockSpec((1, TILE, WIDTH), lambda i: (jnp.minimum(i, last), 0, 0)),
            pl.BlockSpec((TILES, 32, 2 * TILE), lambda i: (0, i, 0)),
            pl.BlockSpec((4, 32, WIDTH), lambda i: (0, i, 0)),
        ],
        out_specs=[
            pl.BlockSpec((TILE, WIDTH), lambda i: (jnp.minimum(i, last), 0)),
            pl.BlockSpec((32, FF), lambda i: (i, 0)),
        ]
        + [pl.BlockSpec((32, WIDTH), lambda i: (i, 0))] * 4,
        compiler_params=pltpu.CompilerParams(vmem_limit_bytes=48 * 2**20),
        name="finish",
    )(g1, g2, g3)


def fast_shards(
    tokens,
    out_grad,
    ln1_gain,
    ln1_bias,
    q_weight,
    q_bias,
    k_weight,
    v_weight,
    v_bias,
    o_weight,
    o_bias,
    ln2_gain,
    ln2_bias,
    up_weight,
    up_bias,
    down_weight,
    down_bias,
):
    small = [ln1_gain, ln1_bias, q_bias, v_bias, o_bias, ln2_gain, ln2_bias, down_bias]
    pack = jnp.pad(jnp.stack(small).astype(f32), ((0, 0), (0, LANES - HALF)))
    gap = TILES * TILE - FF_HALF
    bup = jnp.pad(up_bias.astype(f32), (0, gap)).reshape(TILES, 1, TILE)
    normed1, query, key_rows, value_rows, attn_in, probs, residual, normed2, w, wup, wdown, vec, bup = (
        forward(tokens, q_weight, k_weight, v_weight, o_weight, up_weight, down_weight, pack, bup)
    )
    wq, wk, wv, wo = w[0], w[1], w[2], w[3]
    input_f = tokens.astype(f32)
    gain_one, shift_one, gain_two, shift_two = vec[0], vec[1], vec[5], vec[6]
    log_total = attend(query, key_rows, value_rows)[1]

    output, d_normed2, g1, g2, d_bup = feed_forward(
        normed2, residual, out_grad, wup, wdown, bup, vec
    )

    _, norm_back_two = jax.vjp(layer_norm, residual, gain_two, shift_two)
    d_res_norm, d_gain_two, d_shift_two = norm_back_two(d_normed2)
    d_residual = out_grad.astype(f32) + d_res_norm
    d_attn = d_residual.astype(bf16)
    d_wout = outer_rows(attn_in, d_attn)
    d_mixed = back_rows(d_attn, wo).astype(bf16)
    d_query, d_key, d_value = attend_back(query, key_rows, value_rows, log_total, d_mixed)
    d_wquery = outer_rows(normed1, d_query)
    d_wkey = outer_rows(normed1, d_key)
    d_wvalue = outer_rows(normed1, d_value)
    d_normed1 = back_rows(d_query, wq) + back_rows(d_key, wk) + back_rows(d_value, wv)
    _, norm_back_one = jax.vjp(layer_norm, input_f, gain_one, shift_one)
    d_in_norm, d_gain_one, d_shift_one = norm_back_one(d_normed1)
    d_input = (d_residual + d_in_norm).astype(bf16)

    parts = [w.astype(bf16).reshape(2, 1, HALF, WIDTH) for w in (d_wquery, d_wkey, d_wvalue, d_wout)]
    grads = jnp.concatenate(parts, axis=1).reshape(2, 2, CHUNKS, TILE, WIDTH)
    g3 = attention_sum(grads).reshape(4, HALF, WIDTH)

    d_bup = d_bup.reshape(TILES, 2, TILE).transpose(1, 0, 2).reshape(2, TILES * TILE)[:, :FF_HALF]
    small = [
        d_gain_one,
        d_shift_one,
        column_sums(d_query),
        column_sums(d_value),
        column_sums(d_attn),
        d_gain_two,
        d_shift_two,
        column_sums(out_grad),
    ]
    pack = jnp.concatenate([v.reshape(2, HALF) for v in small] + [d_bup], axis=1).astype(bf16)
    pack = lax.psum(pack, ("group", "replica")).astype(f32)
    mine = lax.dynamic_index_in_dim(pack, lax.axis_index("group"), 0, keepdims=False)
    small = [mine[j * HALF : (j + 1) * HALF] for j in range(8)]

    g1, g2, gq, gk, gv, go = finish(g1, g2, g3)
    return (
        output,
        d_input,
        small[0],
        small[1],
        gq,
        small[2],
        gk,
        gv,
        small[3],
        go,
        small[4],
        small[5],
        small[6],
        g2,
        mine[8 * HALF :],
        g1,
        small[7],
    )


def solution(mesh):
    placed = (
        P(("group", "replica"), None),
        P(("group", "replica"), None),
        P("group"),
        P("group"),
        P("group", None),
        P("group"),
        P("group", None),
        P("group", None),
        P("group"),
        P("group", None),
        P("group"),
        P("group"),
        P("group"),
        P("group", None),
        P("group"),
        P("group", None),
        P("group"),
    )
    fast = mesh.shape["group"] == 2 and mesh.shape["replica"] == 16
    return jax.shard_map(
        fast_shards if fast else shards,
        mesh=mesh,
        in_specs=placed,
        out_specs=(
            P(("group", "replica"), None),
            P(("group", "replica"), None),
            P("group"),
            P("group"),
            P("group", None),
            P("group"),
            P("group", None),
            P("group", None),
            P("group"),
            P("group", None),
            P("group"),
            P("group"),
            P("group"),
            P("group", None),
            P("group"),
            P("group", None),
            P("group"),
        ),
        check_vma=False,
    )
```

```python
import functools

import jax
import jax.numpy as jnp
from jax import lax
from jax.experimental import pallas as pl
from jax.experimental.pallas import tpu as pltpu
from jax.sharding import PartitionSpec as P

HEADS = 16
PATCHES = 128


def layer_norm(values, gain, shift):
    center = values - jnp.mean(values, axis=-1, keepdims=True)
    spread = jnp.mean(center * center, axis=-1, keepdims=True)
    return center * lax.rsqrt(spread + 1e-06) * gain + shift


def gelu_tanh(values):
    return jax.nn.gelu(values, approximate=True)


def split_heads(rows):
    return rows.reshape(-1, PATCHES, HEADS, rows.shape[-1] // HEADS)


def head_logits(query, key_rows):
    factor = (query.shape[-1] // HEADS) ** (-0.5)
    query_h = split_heads(query)
    key_h = split_heads(key_rows)
    logits = (
        jnp.einsum("isha,itha->ihst", query_h, key_h, preferred_element_type=jnp.float32) * factor
    )
    return (logits, query_h, key_h, factor)


def attend(query, key_rows, value_rows):
    logits, query_h, key_h, factor = head_logits(query, key_rows)
    peak = jnp.max(logits, axis=-1, keepdims=True)
    log_total = peak + jnp.log(jnp.sum(jnp.exp(logits - peak), axis=-1, keepdims=True))
    weights_low = jnp.exp(logits - log_total).astype(jnp.bfloat16)
    mixed = jnp.einsum(
        "ihst,itha->isha", weights_low, split_heads(value_rows), preferred_element_type=jnp.float32
    )
    return (mixed.reshape(query.shape), log_total)


def attend_back(query, key_rows, value_rows, log_total, d_mixed):
    logits, query_h, key_h, factor = head_logits(query, key_rows)
    weights = jnp.exp(logits - log_total)
    weights_low = weights.astype(jnp.bfloat16)
    value_h = split_heads(value_rows)
    d_mix_h = split_heads(d_mixed)
    d_weights = jnp.einsum("isha,itha->ihst", d_mix_h, value_h, preferred_element_type=jnp.float32)
    d_logits = weights * (d_weights - jnp.sum(weights * d_weights, axis=-1, keepdims=True))
    d_low = d_logits.astype(jnp.bfloat16)
    d_query = (
        jnp.einsum("ihst,itha->isha", d_low, key_h, preferred_element_type=jnp.float32) * factor
    ).astype(jnp.bfloat16)
    d_key = (
        jnp.einsum("ihst,isha->itha", d_low, query_h, preferred_element_type=jnp.float32) * factor
    ).astype(jnp.bfloat16)
    d_value = jnp.einsum(
        "ihst,isha->itha", weights_low, d_mix_h, preferred_element_type=jnp.float32
    ).astype(jnp.bfloat16)
    return (d_query.reshape(query.shape), d_key.reshape(query.shape), d_value.reshape(query.shape))


def outer_rows(left, right):
    return jnp.einsum("ra,rb->ab", left, right, preferred_element_type=jnp.float32)


def back_rows(grads, weight):
    return jnp.einsum("rb,ab->ra", grads, weight, preferred_element_type=jnp.float32)


def column_sums(grads):
    return jnp.sum(grads.astype(jnp.float32), axis=0)


def shards(
    tokens,
    out_grad,
    ln1_gain,
    ln1_bias,
    q_weight,
    q_bias,
    k_weight,
    v_weight,
    v_bias,
    o_weight,
    o_bias,
    ln2_gain,
    ln2_bias,
    up_weight,
    up_bias,
    down_weight,
    down_bias,
):
    attn_full = (
        lax.all_gather(ln1_gain, "group", axis=0, tiled=True),
        lax.all_gather(ln1_bias, "group", axis=0, tiled=True),
        lax.all_gather(q_weight, "group", axis=0, tiled=True),
        lax.all_gather(q_bias, "group", axis=0, tiled=True),
        lax.all_gather(k_weight, "group", axis=0, tiled=True),
        lax.all_gather(v_weight, "group", axis=0, tiled=True),
        lax.all_gather(v_bias, "group", axis=0, tiled=True),
        lax.all_gather(o_weight, "group", axis=0, tiled=True),
        lax.all_gather(o_bias, "group", axis=0, tiled=True),
    )
    gain_one, shift_one, wq_full, bq_full, wk_full, wv_full, bv_full, wo_full, bo_full = attn_full
    input_f = tokens.astype(jnp.float32)
    gain_one_f = gain_one.astype(jnp.float32)
    shift_one_f = shift_one.astype(jnp.float32)
    normed1 = layer_norm(input_f, gain_one_f, shift_one_f).astype(jnp.bfloat16)
    query = (
        jnp.dot(normed1, wq_full, preferred_element_type=jnp.float32) + bq_full.astype(jnp.float32)
    ).astype(jnp.bfloat16)
    key_rows = jnp.dot(normed1, wk_full, preferred_element_type=jnp.float32).astype(jnp.bfloat16)
    value_rows = (
        jnp.dot(normed1, wv_full, preferred_element_type=jnp.float32) + bv_full.astype(jnp.float32)
    ).astype(jnp.bfloat16)
    mixed, log_total = attend(query, key_rows, value_rows)
    attn_in = mixed.astype(jnp.bfloat16)
    residual = (
        input_f
        + jnp.dot(attn_in, wo_full, preferred_element_type=jnp.float32)
        + bo_full.astype(jnp.float32)
    )
    mlp_full = (
        lax.all_gather(ln2_gain, "group", axis=0, tiled=True),
        lax.all_gather(ln2_bias, "group", axis=0, tiled=True),
        lax.all_gather(up_weight, "group", axis=0, tiled=True),
        lax.all_gather(up_bias, "group", axis=0, tiled=True),
        lax.all_gather(down_weight, "group", axis=0, tiled=True),
        lax.all_gather(down_bias, "group", axis=0, tiled=True),
    )
    gain_two, shift_two, wup_full, bup_full, wdown_full, bdown_full = mlp_full
    gain_two_f = gain_two.astype(jnp.float32)
    shift_two_f = shift_two.astype(jnp.float32)
    normed2 = layer_norm(residual, gain_two_f, shift_two_f).astype(jnp.bfloat16)
    pre_act = jnp.dot(normed2, wup_full, preferred_element_type=jnp.float32) + bup_full.astype(
        jnp.float32
    )
    hidden = gelu_tanh(pre_act).astype(jnp.bfloat16)
    output = (
        residual
        + jnp.dot(hidden, wdown_full, preferred_element_type=jnp.float32)
        + bdown_full.astype(jnp.float32)
    )
    mlp_back = (
        lax.all_gather(ln2_gain, "group", axis=0, tiled=True),
        lax.all_gather(ln2_bias, "group", axis=0, tiled=True),
        lax.all_gather(up_weight, "group", axis=0, tiled=True),
        lax.all_gather(up_bias, "group", axis=0, tiled=True),
        lax.all_gather(down_weight, "group", axis=0, tiled=True),
        lax.all_gather(down_bias, "group", axis=0, tiled=True),
    )
    wup_back = mlp_back[2]
    wdown_back = mlp_back[4]
    grad_out = out_grad.astype(jnp.float32)
    d_wdown = outer_rows(hidden, out_grad)
    d_bdown = column_sums(out_grad)
    d_hidden = back_rows(out_grad, wdown_back)
    unused_act, gelu_back = jax.vjp(gelu_tanh, pre_act)
    d_pre = gelu_back(d_hidden)[0].astype(jnp.bfloat16)
    d_wup = outer_rows(normed2, d_pre)
    d_bup = column_sums(d_pre)
    d_normed2 = back_rows(d_pre, wup_back)
    unused_two, norm_back_two = jax.vjp(layer_norm, residual, gain_two_f, shift_two_f)
    d_res_norm, d_gain_two, d_shift_two = norm_back_two(d_normed2)
    d_residual = grad_out + d_res_norm
    mlp_grads = (
        lax.psum_scatter(
            d_gain_two.astype(jnp.bfloat16), "group", scatter_dimension=0, tiled=True
        ).astype(jnp.float32),
        lax.psum_scatter(
            d_shift_two.astype(jnp.bfloat16), "group", scatter_dimension=0, tiled=True
        ).astype(jnp.float32),
        lax.psum_scatter(
            d_wup.astype(jnp.bfloat16), "group", scatter_dimension=0, tiled=True
        ).astype(jnp.float32),
        lax.psum_scatter(
            d_bup.astype(jnp.bfloat16), "group", scatter_dimension=0, tiled=True
        ).astype(jnp.float32),
        lax.psum_scatter(
            d_wdown.astype(jnp.bfloat16), "group", scatter_dimension=0, tiled=True
        ).astype(jnp.float32),
        lax.psum_scatter(
            d_bdown.astype(jnp.bfloat16), "group", scatter_dimension=0, tiled=True
        ).astype(jnp.float32),
    )
    attn_back = (
        lax.all_gather(ln1_gain, "group", axis=0, tiled=True),
        lax.all_gather(ln1_bias, "group", axis=0, tiled=True),
        lax.all_gather(q_weight, "group", axis=0, tiled=True),
        lax.all_gather(q_bias, "group", axis=0, tiled=True),
        lax.all_gather(k_weight, "group", axis=0, tiled=True),
        lax.all_gather(v_weight, "group", axis=0, tiled=True),
        lax.all_gather(v_bias, "group", axis=0, tiled=True),
        lax.all_gather(o_weight, "group", axis=0, tiled=True),
        lax.all_gather(o_bias, "group", axis=0, tiled=True),
    )
    wq_back = attn_back[2]
    wk_back = attn_back[4]
    wv_back = attn_back[5]
    wo_back = attn_back[7]
    d_attn = d_residual.astype(jnp.bfloat16)
    d_wout = outer_rows(attn_in, d_attn)
    d_bout = column_sums(d_attn)
    d_mixed = back_rows(d_attn, wo_back).astype(jnp.bfloat16)
    d_query, d_key, d_value = attend_back(query, key_rows, value_rows, log_total, d_mixed)
    d_wquery = outer_rows(normed1, d_query)
    d_bquery = column_sums(d_query)
    d_wkey = outer_rows(normed1, d_key)
    d_wvalue = outer_rows(normed1, d_value)
    d_bvalue = column_sums(d_value)
    d_normed1 = (
        back_rows(d_query, wq_back) + back_rows(d_key, wk_back) + back_rows(d_value, wv_back)
    )
    unused_one, norm_back_one = jax.vjp(layer_norm, input_f, gain_one_f, shift_one_f)
    d_in_norm, d_gain_one, d_shift_one = norm_back_one(d_normed1)
    d_input = (d_residual + d_in_norm).astype(jnp.bfloat16)
    attn_grads = (
        lax.psum_scatter(
            d_gain_one.astype(jnp.bfloat16), "group", scatter_dimension=0, tiled=True
        ).astype(jnp.float32),
        lax.psum_scatter(
            d_shift_one.astype(jnp.bfloat16), "group", scatter_dimension=0, tiled=True
        ).astype(jnp.float32),
        lax.psum_scatter(
            d_wquery.astype(jnp.bfloat16), "group", scatter_dimension=0, tiled=True
        ).astype(jnp.float32),
        lax.psum_scatter(
            d_bquery.astype(jnp.bfloat16), "group", scatter_dimension=0, tiled=True
        ).astype(jnp.float32),
        lax.psum_scatter(
            d_wkey.astype(jnp.bfloat16), "group", scatter_dimension=0, tiled=True
        ).astype(jnp.float32),
        lax.psum_scatter(
            d_wvalue.astype(jnp.bfloat16), "group", scatter_dimension=0, tiled=True
        ).astype(jnp.float32),
        lax.psum_scatter(
            d_bvalue.astype(jnp.bfloat16), "group", scatter_dimension=0, tiled=True
        ).astype(jnp.float32),
        lax.psum_scatter(
            d_wout.astype(jnp.bfloat16), "group", scatter_dimension=0, tiled=True
        ).astype(jnp.float32),
        lax.psum_scatter(
            d_bout.astype(jnp.bfloat16), "group", scatter_dimension=0, tiled=True
        ).astype(jnp.float32),
    )
    summed = (
        lax.psum(attn_grads[0].astype(jnp.bfloat16), "replica").astype(jnp.float32),
        lax.psum(attn_grads[1].astype(jnp.bfloat16), "replica").astype(jnp.float32),
        lax.psum(attn_grads[2].astype(jnp.bfloat16), "replica").astype(jnp.float32),
        lax.psum(attn_grads[3].astype(jnp.bfloat16), "replica").astype(jnp.float32),
        lax.psum(attn_grads[4].astype(jnp.bfloat16), "replica").astype(jnp.float32),
        lax.psum(attn_grads[5].astype(jnp.bfloat16), "replica").astype(jnp.float32),
        lax.psum(attn_grads[6].astype(jnp.bfloat16), "replica").astype(jnp.float32),
        lax.psum(attn_grads[7].astype(jnp.bfloat16), "replica").astype(jnp.float32),
        lax.psum(attn_grads[8].astype(jnp.bfloat16), "replica").astype(jnp.float32),
        lax.psum(mlp_grads[0].astype(jnp.bfloat16), "replica").astype(jnp.float32),
        lax.psum(mlp_grads[1].astype(jnp.bfloat16), "replica").astype(jnp.float32),
        lax.psum(mlp_grads[2].astype(jnp.bfloat16), "replica").astype(jnp.float32),
        lax.psum(mlp_grads[3].astype(jnp.bfloat16), "replica").astype(jnp.float32),
        lax.psum(mlp_grads[4].astype(jnp.bfloat16), "replica").astype(jnp.float32),
        lax.psum(mlp_grads[5].astype(jnp.bfloat16), "replica").astype(jnp.float32),
    )
    attn_grads = tuple(summed[:9])
    mlp_grads = tuple(summed[9:])
    return (output.astype(jnp.bfloat16), d_input) + tuple(attn_grads) + tuple(mlp_grads)


MESH = pl.DeviceIdType.MESH
bf16 = jnp.bfloat16
f32 = jnp.float32
ANY = pl.BlockSpec(memory_space=pl.ANY)
WIDTH = 1152
HALF = 576
FF = 4304
FF_HALF = 2152
TILES = 17
TILE = 128
FF_PAD = 2 * TILES * TILE
FIRST = 320
SECOND = 256


class Place:
    def __init__(self):
        self.core = lax.axis_index("group")
        chip = lax.axis_index("replica")
        self.chip = chip
        self.x = lax.rem(chip, 2)
        self.y = lax.rem(chip // 2, 2)
        self.z = chip // 4
        self.x_pair = chip + 1 - 2 * self.x
        self.y_pair = chip + 2 - 4 * self.y
        self.z_pair = chip + 4 - 8 * lax.rem(self.z, 2)
        self.inner = (self.z == 1) | (self.z == 2)
        self.outer = jnp.logical_not(self.inner)
        self.mid_pair = jnp.where(self.inner, chip + 12 - 8 * self.z, chip)
        self.z_half = lax.rem(self.z // 2, 2)

    def barrier(self):
        sem = pltpu.get_barrier_semaphore()

        def greet(core, chip):
            pl.semaphore_signal(sem, inc=1, device_id=(core, chip), device_id_type=MESH)

        greet(1 - self.core, self.chip)
        greet(self.core, self.x_pair)
        greet(self.core, self.y_pair)
        greet(self.core, self.z_pair)

        @pl.when(self.inner)
        def _():
            greet(self.core, self.mid_pair)
            pl.semaphore_wait(sem, 5)

        @pl.when(self.outer)
        def _():
            pl.semaphore_wait(sem, 4)

    def copy(self, source, target, sent, got, chip):
        return pltpu.make_async_remote_copy(
            source, target, sent, got, device_id=(self.core, chip), device_id_type=MESH
        )

    def copy_sibling(self, source, target, sent, got):
        return pltpu.make_async_remote_copy(
            source, target, sent, got, device_id=(1 - self.core, self.chip), device_id_type=MESH
        )


def aligned(value, unit):
    return pl.multiple_of(value, unit)


def add_rows(total, landed, chunk, start, count):
    rows = pl.ds(start, count)
    total[chunk, rows, :] = (
        total[chunk, rows, :].astype(f32) + landed.astype(f32)
    ).astype(bf16)


class TreeFirst:
    steps = 9

    def __init__(self, place, total, final, landing, sent, got, kept):
        self.at = place
        self.total = total
        self.final = final
        self.kept = kept
        self.land = landing
        self.sent = sent
        self.got = got
        n = total.shape[1]
        self.n = n
        p = place
        self.own = [
            (0, n),
            (aligned(p.z_half * (n // 2), n // 2), n // 2),
        ]
        self.other = [None, (aligned((1 - p.z_half) * (n // 2), n // 2), n // 2)]
        for bit, part in ((p.y, n // 4), (p.x, n // 8)):
            base = self.own[-1][0]
            self.own.append((aligned(base + bit * part, part), part))
            self.other.append((aligned(base + (1 - bit) * part, part), part))
        self.peer = [p.z_pair, p.mid_pair, p.y_pair, p.x_pair]

    def rows(self, chunk, span):
        return self.total.at[chunk, pl.ds(span[0], span[1]), :]

    def ends(self, chunk, span):
        return self.final.at[chunk, pl.ds(span[0], span[1]), :]

    def send(self, k, chunk):
        sent, got = self.sent.at[k, chunk], self.got.at[k, chunk]
        if k < 4:
            span = self.own[0] if k == 0 else self.other[k]
            return self.at.copy(
                self.rows(chunk, span), self.land[k].at[chunk], sent, got, self.peer[k]
            )
        level = 7 - k
        target = self.ends(chunk, self.own[level])
        source = self.rows(chunk, self.own[3]) if k == 4 else target
        return self.at.copy(source, target, sent, got, self.peer[level])

    def keep(self, chunk):
        return pltpu.make_async_copy(
            self.rows(chunk, self.own[3]), self.ends(chunk, self.own[3]), self.kept.at[chunk]
        )

    def arrive(self, k, chunk):
        if k < 4:
            landed = self.land[k].at[chunk]
        else:
            level = 7 - k
            landed = self.ends(chunk, self.own[0] if level == 0 else self.other[level])
        self.at.copy(
            landed, landed, self.sent.at[k, chunk], self.got.at[k, chunk], self.at.z_pair
        ).wait_recv()

    def step(self, k, chunk):
        at = self.at
        if k == 0:

            @pl.when(at.outer)
            def _():
                self.send(0, chunk).start()

        elif k <= 7:

            @pl.when(at.inner)
            def _():
                self.arrive(k - 1, chunk)
                if k <= 4:
                    add_rows(self.total, self.land[k - 1][chunk], chunk, *self.own[k - 1])
                if k == 4:
                    self.keep(chunk).start()
                if k == 5:
                    self.keep(chunk).wait()
                self.send(k, chunk).start()

        else:

            @pl.when(at.inner)
            def _():
                for j in range(1, 8):
                    self.send(j, chunk).wait_send()

            @pl.when(at.outer)
            def _():
                self.arrive(7, chunk)
                self.send(0, chunk).wait_send()


class PlaneFirst:
    steps = 8

    def __init__(self, place, total, final, base, n, x_first, landing, sent, got, kept):
        self.at = place
        self.total = total
        self.final = final
        self.kept = kept
        self.land = landing
        self.sent = sent
        self.got = got
        p = place
        if x_first:
            one, two = (p.x, p.x_pair), (p.y, p.y_pair)
        else:
            one, two = (p.y, p.y_pair), (p.x, p.x_pair)
        self.peer_one, self.peer_two = one[1], two[1]
        start = aligned(base + one[0] * (n // 2), 16)
        self.half = (start, n // 2)
        self.half_other = (aligned(base + (1 - one[0]) * (n // 2), 16), n // 2)
        self.quarter = (aligned(start + two[0] * (n // 4), 16), n // 4)
        self.quarter_other = (aligned(start + (1 - two[0]) * (n // 4), 16), n // 4)

    def rows(self, chunk, span):
        return self.total.at[chunk, pl.ds(span[0], span[1]), :]

    def ends(self, chunk, span):
        return self.final.at[chunk, pl.ds(span[0], span[1]), :]

    def keep(self, chunk):
        return pltpu.make_async_copy(
            self.rows(chunk, self.quarter), self.ends(chunk, self.quarter), self.kept.at[chunk]
        )

    def send(self, k, chunk):
        at = self.at
        quarter = self.rows(chunk, self.quarter)
        quarter_end = self.ends(chunk, self.quarter)
        half_end = self.ends(chunk, self.half)
        source, target, peer = (
            (self.rows(chunk, self.half_other), self.land[0].at[chunk], self.peer_one),
            (self.rows(chunk, self.quarter_other), self.land[1].at[chunk], self.peer_two),
            (quarter, self.land[2].at[chunk], at.z_pair),
            (quarter, self.land[3].at[chunk], at.mid_pair),
            (quarter, quarter_end, at.z_pair),
            (quarter_end, quarter_end, self.peer_two),
            (half_end, half_end, self.peer_one),
        )[k]
        return at.copy(source, target, self.sent.at[k, chunk], self.got.at[k, chunk], peer)

    def arrive(self, k, chunk):
        if k < 4:
            landed = self.land[k].at[chunk]
        else:
            landed = self.ends(
                chunk, (self.quarter, self.quarter_other, self.half_other)[k - 4]
            )
        self.at.copy(
            landed, landed, self.sent.at[k, chunk], self.got.at[k, chunk], self.at.z_pair
        ).wait_recv()

    def step(self, k, chunk):
        at = self.at
        if k == 0:
            self.send(0, chunk).start()
        elif k == 1:
            self.arrive(0, chunk)
            add_rows(self.total, self.land[0][chunk], chunk, *self.half)
            self.send(1, chunk).start()
        elif k == 2:
            self.arrive(1, chunk)
            add_rows(self.total, self.land[1][chunk], chunk, *self.quarter)

            @pl.when(at.outer)
            def _():
                self.send(2, chunk).start()

        elif k == 3:

            @pl.when(at.inner)
            def _():
                self.arrive(2, chunk)
                add_rows(self.total, self.land[2][chunk], chunk, *self.quarter)
                self.send(3, chunk).start()

        elif k == 4:

            @pl.when(at.inner)
            def _():
                self.arrive(3, chunk)
                self.send(3, chunk).wait_send()
                add_rows(self.total, self.land[3][chunk], chunk, *self.quarter)
                self.send(4, chunk).start()
                self.keep(chunk).start()

        elif k == 5:

            @pl.when(at.inner)
            def _():
                self.keep(chunk).wait()

            @pl.when(at.outer)
            def _():
                self.arrive(4, chunk)

            self.send(5, chunk).start()
        elif k == 6:
            self.arrive(5, chunk)
            self.send(6, chunk).start()
        else:
            self.arrive(6, chunk)
            for j in (0, 1, 5, 6):
                self.send(j, chunk).wait_send()

            @pl.when(at.inner)
            def _():
                self.send(4, chunk).wait_send()

            @pl.when(at.outer)
            def _():
                self.send(2, chunk).wait_send()


def tree_scratch(count, n, width):
    return [pltpu.VMEM((count, n // part, width), bf16) for part in (1, 2, 4, 8)] + [
        pltpu.SemaphoreType.DMA((8, count)),
        pltpu.SemaphoreType.DMA((8, count)),
        pltpu.SemaphoreType.DMA((count,)),
    ]


def plane_scratch(count, n, width):
    return [pltpu.VMEM((count, n // part, width), bf16) for part in (2, 4, 4, 4)] + [
        pltpu.SemaphoreType.DMA((7, count)),
        pltpu.SemaphoreType.DMA((7, count)),
        pltpu.SemaphoreType.DMA((count,)),
    ]


def advance(tick, count, sums):
    for k in reversed(range(max(s.steps for s in sums))):
        chunk = tick - k

        @pl.when((chunk >= 0) & (chunk < count))
        def _():
            for s in sums:
                if k < s.steps:
                    s.step(k, chunk)


def dot(left, right, contract):
    return lax.dot_general(left, right, (contract, ((), ())), preferred_element_type=f32)


NN = ((1,), (0,))
NT = ((1,), (1,))
TN = ((0,), (0,))


def gelu_and_slope(u):
    c = 0.7978845608028654
    square = u * u
    t = jnp.tanh(c * u * (1.0 + 0.044715 * square))
    half = 0.5 * (1.0 + t)
    slope = half + 0.5 * u * (1.0 - t * t) * (c * (1.0 + 3 * 0.044715 * square))
    return u * half, slope


def ff_kernel(
    h2_ref,
    x2_ref,
    og_ref,
    wup_ref,
    wdown_ref,
    bup_ref,
    bdown_ref,
    out_ref,
    dh2_ref,
    g1_ref,
    g2_ref,
    dbup_ref,
    h2,
    h2t,
    og,
    out,
    dh2,
    wu,
    wd,
    bup,
    bdown,
    dbup,
    out16,
    mine1,
    mine2,
    sib1,
    sib2,
    sum1,
    sum2,
    *rest,
):
    rest = list(rest)
    local, wsem, gsent, ggot = rest[:4]
    tree, plane1, plane2 = rest[4:11], rest[11:18], rest[18:25]
    at = Place()
    loads = [
        pltpu.make_async_copy(s, d, local.at[j])
        for j, (s, d) in enumerate(
            ((h2_ref, h2), (og_ref, og), (x2_ref, out), (bup_ref, bup), (bdown_ref, bdown))
        )
    ]
    for load in loads:
        load.start()

    def weights(i, slot):
        cols = [pl.ds(aligned(h * TILES * TILE + i * TILE, TILE), TILE) for h in (0, 1)]
        parts = []
        for h in (0, 1):
            here = pl.ds(h * TILE, TILE)
            parts.append(
                pltpu.make_async_copy(
                    wup_ref.at[:, cols[h]], wu.at[slot, :, here], wsem.at[h, slot]
                )
            )
            parts.append(
                pltpu.make_async_copy(
                    wdown_ref.at[cols[h], :], wd.at[slot, here, :], wsem.at[2 + h, slot]
                )
            )
        return parts

    for part in weights(0, 0):
        part.start()
    at.barrier()
    for load in loads:
        load.wait()
    for b in range(8):
        rows = pl.ds(b * 128, 128)
        h2t[:, rows] = h2[rows, :].T
    out[...] = out[...] + bdown[7:8, :]
    dh2[...] = jnp.zeros_like(dh2)

    sums = [
        TreeFirst(at, sum1, g1_ref, tree[:4], *tree[4:]),
        PlaneFirst(at, sum2, g2_ref, 0, FIRST, True, plane1[:4], *plane1[4:]),
        PlaneFirst(at, sum2, g2_ref, FIRST, SECOND, False, plane2[:4], *plane2[4:]),
    ]

    def to_sibling(slot):
        return (
            at.copy_sibling(
                mine1.at[slot, 1 - at.core], sib1.at[slot], gsent.at[0, slot], ggot.at[0, slot]
            ),
            at.copy_sibling(
                mine2.at[slot, 1 - at.core], sib2.at[slot], gsent.at[1, slot], ggot.at[1, slot]
            ),
        )

    def meet(i):
        slot = lax.rem(i, 2)
        for copy in to_sibling(slot):
            copy.wait()
        sum1[i] = (mine1[slot, at.core].astype(f32) + sib1[slot].astype(f32)).astype(bf16)
        sum2[i] = (mine2[slot, at.core].astype(f32) + sib2[slot].astype(f32)).astype(bf16)

    def compute(i):
        slot = lax.rem(i, 2)
        for part in weights(i, slot):
            part.wait()

        @pl.when(i + 1 < TILES)
        def _():
            for part in weights(i + 1, 1 - slot):
                part.start()

        bias = jnp.concatenate([bup[0, i], bup[1, i]], axis=1)
        u = dot(h2[...], wu[slot], NN) + bias
        a, slope = gelu_and_slope(u)
        a = a.astype(bf16)
        out[...] += dot(a, wd[slot], NN)
        d_wd = dot(a, og[...], TN).astype(bf16)
        mine1[slot, 0] = d_wd[:TILE]
        mine1[slot, 1] = d_wd[TILE:]
        du = (dot(og[...], wd[slot], NT) * slope).astype(bf16)
        d_wu = dot(h2t[...], du, NN).astype(bf16)
        mine2[slot, 0] = d_wu[:HALF]
        mine2[slot, 1] = d_wu[HALF:]
        for copy in to_sibling(slot):
            copy.start()
        dh2[...] += dot(du, wu[slot], NT)
        dbup[i] = jnp.sum(du.astype(f32), axis=0, keepdims=True)

    def body(i, carry):
        @pl.when((i >= 1) & (i <= TILES))
        def _():
            meet(i - 1)

        advance(i - 1, TILES, sums)

        @pl.when(i < TILES)
        def _():
            compute(i)

        @pl.when(i == TILES)
        def _():
            out16[...] = out[...].astype(bf16)
            pltpu.make_async_copy(out16, out_ref, local.at[0]).start()
            pltpu.make_async_copy(dh2, dh2_ref, local.at[1]).start()
            pltpu.make_async_copy(dbup, dbup_ref, local.at[2]).start()

        return carry

    lax.fori_loop(0, TILES + 1 + 8, body, 0)
    pltpu.make_async_copy(out16, out_ref, local.at[0]).wait()
    pltpu.make_async_copy(dh2, dh2_ref, local.at[1]).wait()
    pltpu.make_async_copy(dbup, dbup_ref, local.at[2]).wait()

def feed_forward(h2, x2, og, wup, wdown, bup, bdown):
    rows = h2.shape[0]
    return pl.pallas_call(
        ff_kernel,
        out_shape=(
            jax.ShapeDtypeStruct((rows, WIDTH), bf16),
            jax.ShapeDtypeStruct((rows, WIDTH), f32),
            jax.ShapeDtypeStruct((TILES, TILE, WIDTH), bf16),
            jax.ShapeDtypeStruct((TILES, HALF, 2 * TILE), bf16),
            jax.ShapeDtypeStruct((TILES, 1, 2 * TILE), f32),
        ),
        in_specs=[ANY] * 7,
        out_specs=[ANY] * 5,
        scratch_shapes=[
            pltpu.VMEM((rows, WIDTH), bf16),
            pltpu.VMEM((WIDTH, rows), bf16),
            pltpu.VMEM((rows, WIDTH), bf16),
            pltpu.VMEM((rows, WIDTH), f32),
            pltpu.VMEM((rows, WIDTH), f32),
            pltpu.VMEM((2, WIDTH, 2 * TILE), bf16),
            pltpu.VMEM((2, 2 * TILE, WIDTH), bf16),
            pltpu.VMEM((2, TILES, 1, TILE), f32),
            pltpu.VMEM((VECTORS, WIDTH), f32),
            pltpu.VMEM((TILES, 1, 2 * TILE), f32),
            pltpu.VMEM((rows, WIDTH), bf16),
            pltpu.VMEM((2, 2, TILE, WIDTH), bf16),
            pltpu.VMEM((2, 2, HALF, 2 * TILE), bf16),
            pltpu.VMEM((2, TILE, WIDTH), bf16),
            pltpu.VMEM((2, HALF, 2 * TILE), bf16),
            pltpu.VMEM((TILES, TILE, WIDTH), bf16),
            pltpu.VMEM((TILES, HALF, 2 * TILE), bf16),
            pltpu.SemaphoreType.DMA((5,)),
            pltpu.SemaphoreType.DMA((4, 2)),
            pltpu.SemaphoreType.DMA((2, 2)),
            pltpu.SemaphoreType.DMA((2, 2)),
        ]
        + tree_scratch(TILES, TILE, WIDTH)
        + plane_scratch(TILES, FIRST, 2 * TILE)
        + plane_scratch(TILES, SECOND, 2 * TILE),
        compiler_params=pltpu.CompilerParams(
            collective_id=1, has_side_effects=True, vmem_limit_bytes=62 * 2**20
        ),
        name="feed_forward",
    )(h2, x2, og, wup, wdown, bup, bdown)


CHUNKS = 9


def attention_sum_kernel(grad_ref, out_ref, sum1, sum2, sib1, sib2, *rest):
    rest = list(rest)
    local, gsent, ggot = rest[:3]
    tree, plane1, plane2 = rest[3:10], rest[10:17], rest[17:24]
    at = Place()
    own = [
        pltpu.make_async_copy(grad_ref.at[at.core, j], s, local.at[j])
        for j, s in ((0, sum1), (1, sum2))
    ]
    for load in own:
        load.start()
    at.barrier()

    def sibling(j, chunk):
        return at.copy_sibling(
            grad_ref.at[1 - at.core, j, chunk],
            (sib1, sib2)[j].at[chunk],
            gsent.at[j, chunk],
            ggot.at[j, chunk],
        )

    for chunk in range(CHUNKS):
        sibling(0, chunk).start()
        sibling(1, chunk).start()
    for load in own:
        load.wait()
    sums = [
        TreeFirst(at, sum1, out_ref.at[0], tree[:4], *tree[4:]),
        PlaneFirst(at, sum2, out_ref.at[1], 0, TILE // 2, True, plane1[:4], *plane1[4:]),
        PlaneFirst(
            at, sum2, out_ref.at[1], TILE // 2, TILE // 2, False, plane2[:4], *plane2[4:]
        ),
    ]

    def body(i, carry):
        @pl.when(i < CHUNKS)
        def _():
            sibling(0, i).wait()
            sibling(1, i).wait()
            sum1[i] = (sum1[i].astype(f32) + sib1[i].astype(f32)).astype(bf16)
            sum2[i] = (sum2[i].astype(f32) + sib2[i].astype(f32)).astype(bf16)

        advance(i, CHUNKS, sums)
        return carry

    lax.fori_loop(0, CHUNKS + 8, body, 0)

def attention_sum(grads):
    return pl.pallas_call(
        attention_sum_kernel,
        out_shape=jax.ShapeDtypeStruct((2, CHUNKS, TILE, WIDTH), bf16),
        in_specs=[ANY],
        out_specs=ANY,
        scratch_shapes=[pltpu.VMEM((CHUNKS, TILE, WIDTH), bf16)] * 4
        + [
            pltpu.SemaphoreType.DMA((2,)),
            pltpu.SemaphoreType.DMA((2, CHUNKS)),
            pltpu.SemaphoreType.DMA((2, CHUNKS)),
        ]
        + tree_scratch(CHUNKS, TILE, WIDTH)
        + plane_scratch(CHUNKS, TILE // 2, WIDTH)
        + plane_scratch(CHUNKS, TILE // 2, WIDTH),
        compiler_params=pltpu.CompilerParams(
            collective_id=2, has_side_effects=True, vmem_limit_bytes=62 * 2**20
        ),
        name="attention_sum",
    )(grads)


VECTORS = 8
LANES = 640
SCALE = 72**-0.5
HEAD = 72


def head_window(h):
    return slice(h * HEAD // 128 * 128, ((h + 1) * HEAD + 127) // 128 * 128)


def only_head(rows, h):
    lane = lax.broadcasted_iota(jnp.int32, rows.shape, 1) + head_window(h).start
    return jnp.where((lane >= h * HEAD) & (lane < (h + 1) * HEAD), rows, jnp.zeros_like(rows))


class Lanes:
    def __init__(self):
        self.tiles = [None] * (WIDTH // 128)

    def add(self, h, window):
        first = head_window(h).start // 128
        for j in range(window.shape[1] // 128):
            part = window[:, j * 128 : (j + 1) * 128]
            old = self.tiles[first + j]
            self.tiles[first + j] = part if old is None else old + part

    def joined(self):
        return jnp.concatenate([t.astype(bf16) for t in self.tiles], axis=1)


def normalise(rows, gain, shift):
    center = rows - jnp.mean(rows, axis=-1, keepdims=True)
    spread = jnp.mean(center * center, axis=-1, keepdims=True)
    return center * lax.rsqrt(spread + 1e-06) * gain + shift


def forward_kernel(
    tokens_ref,
    wq_ref,
    wk_ref,
    wv_ref,
    wo_ref,
    up_ref,
    down_ref,
    pack_ref,
    bup_ref,
    h1_ref,
    q_ref,
    k_ref,
    v_ref,
    ao_ref,
    probs_ref,
    x2_ref,
    h2_ref,
    w_ref,
    wup_ref,
    wdown_ref,
    vec_ref,
    bups_ref,
    x,
    h1,
    q,
    k,
    v,
    ao,
    probs,
    x2,
    h2,
    w,
    up,
    up_wide,
    down,
    zeros,
    pack,
    vec,
    local,
    wsem,
    psem,
    sent,
    got,
    bsem,
):
    at = Place()
    core = at.core
    own = pl.ds(aligned(core * HALF, HALF), HALF)
    ff_own = pl.ds(aligned(core * TILES * TILE, TILE), FF_HALF)
    shards = (wq_ref, wk_ref, wv_ref, wo_ref)
    load_x = pltpu.make_async_copy(tokens_ref, x, local.at[0])
    load_x.start()
    load_w = [pltpu.make_async_copy(s, w.at[j, own, :], local.at[1 + j]) for j, s in enumerate(shards)]
    load_pack = pltpu.make_async_copy(pack_ref, pack.at[core], local.at[5])
    load_bup = pltpu.make_async_copy(bup_ref, bups_ref.at[core], local.at[6])
    load_up = pltpu.make_async_copy(up_ref, up, local.at[7])
    load_down = pltpu.make_async_copy(down_ref, down, local.at[8])
    keep_down = pltpu.make_async_copy(down, wdown_ref.at[ff_own, :], wsem.at[4])
    for load in (load_pack, *load_w, load_bup, load_up, load_down):
        load.start()
    zeros[...] = jnp.zeros_like(zeros)
    gap = TILES * TILE - FF_HALF
    blanks = [
        pltpu.make_async_copy(
            zeros, wdown_ref.at[pl.ds(h * TILES * TILE + FF_HALF, gap), :], local.at[9 + h]
        )
        for h in (0, 1)
    ]
    for blank in blanks:
        blank.start()

    bar = pltpu.get_barrier_semaphore()
    pl.semaphore_signal(bar, inc=1, device_id=(1 - core, at.chip), device_id_type=MESH)
    pl.semaphore_wait(bar, 1)

    def share(j, source, target):
        return at.copy_sibling(source, target, sent.at[j], got.at[j])

    give_w = [share(j, s, w.at[j, own, :]) for j, s in enumerate(shards)]
    give_pack = share(4, pack_ref, pack.at[core])
    give_bup = share(5, bup_ref, bups_ref.at[core])
    give_down = share(6, down_ref, wdown_ref.at[ff_own, :])
    give_up = share(7, up_wide, wup_ref.at[own, :])
    keep_up = pltpu.make_async_copy(up_wide, wup_ref.at[own, :], local.at[11])
    give_pack.start()
    for give in give_w:
        give.start()
    give_bup.start()
    give_down.start()

    load_pack.wait()
    give_pack.wait()
    vec[...] = jnp.concatenate([pack[0, :, :HALF], pack[1, :, :HALF]], axis=1)
    load_x.wait()
    rows_of = [pl.ds(b * 512, 512) for b in range(2)]

    def first_norm(b, carry):
        rows = pl.ds(aligned(b * 128, 128), 128)
        h1[rows, :] = normalise(x[rows, :].astype(f32), vec[0:1, :], vec[1:2, :]).astype(bf16)
        return carry

    lax.fori_loop(0, 8, first_norm, 0)
    keep = [pltpu.make_async_copy(h1, h1_ref, local.at[0])]
    keep[0].start()

    def project(j, target, bias):
        load_w[j].wait()
        give_w[j].wait()
        for rows in rows_of:
            y = dot(h1[rows, :], w[j], NN)
            if bias is not None:
                y = y + vec[bias : bias + 1, :]
            target[rows, :] = y.astype(bf16)

    project(0, q, 2)
    project(1, k, None)
    project(2, v, 3)
    for j, (s, d) in enumerate(((q, q_ref), (k, k_ref), (v, v_ref))):
        keep.append(pltpu.make_async_copy(s, d, local.at[12 + j]))
        keep[-1].start()

    load_down.wait()
    keep_down.start()
    load_up.wait()

    def widen(b, carry):
        rows = pl.ds(aligned(b * 64, 64), 64)
        row = up[rows, :]
        none = jnp.zeros((64, gap), bf16)
        up_wide[rows, :] = jnp.concatenate([row[:, :FF_HALF], none, row[:, FF_HALF:], none], axis=1)
        return carry

    lax.fori_loop(0, HALF // 64, widen, 0)
    keep_up.start()
    give_up.start()

    def keep_probs(i):
        slot = lax.rem(i, 2)
        return pltpu.make_async_copy(probs.at[slot], probs_ref.at[i], psem.at[slot])

    def attention(i, carry):
        rows = pl.ds(aligned(i * 128, 128), 128)
        slot = lax.rem(i, 2)

        @pl.when(i >= 2)
        def _():
            keep_probs(i - 2).wait()

        qi, ki, vi = q[rows, :], k[rows, :], v[rows, :]
        mixed = Lanes()
        held = []
        for h in range(HEADS):
            cols = head_window(h)
            logits = dot(qi[:, cols], only_head(ki[:, cols], h), NT) * SCALE
            e = jnp.exp(logits - jnp.max(logits, axis=-1, keepdims=True))
            p = (e / jnp.sum(e, axis=-1, keepdims=True)).astype(bf16)
            held.append(p)
            mixed.add(h, dot(p, only_head(vi[:, cols], h), NN))
        ao[rows, :] = mixed.joined()
        probs[slot] = jnp.concatenate(held, axis=1)
        keep_probs(i).start()
        return carry

    lax.fori_loop(0, 8, attention, 0)
    keep_ao = pltpu.make_async_copy(ao, ao_ref, local.at[15])
    keep_ao.start()

    load_w[3].wait()
    give_w[3].wait()
    keep_w = pltpu.make_async_copy(w, w_ref, wsem.at[0])
    keep_w.start()
    keep_vec = pltpu.make_async_copy(vec, vec_ref, wsem.at[1])
    keep_vec.start()
    for rows in rows_of:
        x2[rows, :] = x[rows, :].astype(f32) + dot(ao[rows, :], w[3], NN) + vec[4:5, :]

    def second_norm(b, carry):
        rows = pl.ds(aligned(b * 128, 128), 128)
        h2[rows, :] = normalise(x2[rows, :], vec[5:6, :], vec[6:7, :]).astype(bf16)
        return carry

    lax.fori_loop(0, 8, second_norm, 0)
    keep_x2 = pltpu.make_async_copy(x2, x2_ref, wsem.at[2])
    keep_h2 = pltpu.make_async_copy(h2, h2_ref, wsem.at[3])
    for copy in (keep_x2, keep_h2):
        copy.start()
    for copy in (
        *keep,
        keep_probs(6),
        keep_probs(7),
        keep_ao,
        keep_w,
        keep_vec,
        load_bup,
        keep_down,
        *blanks,
        keep_up,
        keep_x2,
        keep_h2,
    ):
        copy.wait()
    for give in (give_bup, give_down, give_up):
        give.wait()


def forward(tokens, wq, wk, wv, wo, up, down, pack, bup):
    rows = tokens.shape[0]
    images = rows // PATCHES
    flat = jax.ShapeDtypeStruct((rows, WIDTH), bf16)
    return pl.pallas_call(
        forward_kernel,
        out_shape=(
            flat,
            flat,
            flat,
            flat,
            flat,
            jax.ShapeDtypeStruct((images, PATCHES, HEADS * PATCHES), bf16),
            jax.ShapeDtypeStruct((rows, WIDTH), f32),
            flat,
            jax.ShapeDtypeStruct((4, WIDTH, WIDTH), bf16),
            jax.ShapeDtypeStruct((WIDTH, FF_PAD), bf16),
            jax.ShapeDtypeStruct((FF_PAD, WIDTH), bf16),
            jax.ShapeDtypeStruct((VECTORS, WIDTH), f32),
            jax.ShapeDtypeStruct((2, TILES, 1, TILE), f32),
        ),
        in_specs=[ANY] * 9,
        out_specs=[ANY] * 13,
        scratch_shapes=[pltpu.VMEM((rows, WIDTH), bf16)] * 6
        + [
            pltpu.VMEM((2, PATCHES, HEADS * PATCHES), bf16),
            pltpu.VMEM((rows, WIDTH), f32),
            pltpu.VMEM((rows, WIDTH), bf16),
            pltpu.VMEM((4, WIDTH, WIDTH), bf16),
            pltpu.VMEM((HALF, FF), bf16),
            pltpu.VMEM((HALF, FF_PAD), bf16),
            pltpu.VMEM((FF_HALF, WIDTH), bf16),
            pltpu.VMEM((TILES * TILE - FF_HALF, WIDTH), bf16),
            pltpu.VMEM((2, VECTORS, LANES), f32),
            pltpu.VMEM((VECTORS, WIDTH), f32),
            pltpu.SemaphoreType.DMA((16,)),
            pltpu.SemaphoreType.DMA((5,)),
            pltpu.SemaphoreType.DMA((2,)),
            pltpu.SemaphoreType.DMA((8,)),
            pltpu.SemaphoreType.DMA((8,)),
            pltpu.SemaphoreType.DMA((1,)),
        ],
        compiler_params=pltpu.CompilerParams(
            collective_id=3, has_side_effects=True, vmem_limit_bytes=62 * 2**20
        ),
        name="forward",
    )(tokens, wq, wk, wv, wo, up, down, pack, bup)


def finish_kernel(g1_ref, g2_ref, g3_ref, d1_ref, d2_ref, dq_ref, dk_ref, dv_ref, do_ref):
    d1_ref[...] = g1_ref[0].astype(f32)
    parts = []
    for h in (0, 1):
        for i in range(TILES):
            wide = TILE if i < TILES - 1 else FF_HALF - (TILES - 1) * TILE
            parts.append(g2_ref[i, :, h * TILE : h * TILE + wide].astype(f32))
    d2_ref[...] = jnp.concatenate(parts, axis=1)
    for j, d in enumerate((dq_ref, dk_ref, dv_ref, do_ref)):
        d[...] = g3_ref[j].astype(f32)


def finish(g1, g2, g3):
    steps = HALF // 32
    square = jax.ShapeDtypeStruct((HALF, WIDTH), f32)
    last = TILES - 1
    return pl.pallas_call(
        finish_kernel,
        grid=(steps,),
        out_shape=(
            jax.ShapeDtypeStruct((FF_HALF, WIDTH), f32),
            jax.ShapeDtypeStruct((HALF, FF), f32),
        )
        + (square,) * 4,
        in_specs=[
            pl.BlockSpec((1, TILE, WIDTH), lambda i: (jnp.minimum(i, last), 0, 0)),
            pl.BlockSpec((TILES, 32, 2 * TILE), lambda i: (0, i, 0)),
            pl.BlockSpec((4, 32, WIDTH), lambda i: (0, i, 0)),
        ],
        out_specs=[
            pl.BlockSpec((TILE, WIDTH), lambda i: (jnp.minimum(i, last), 0)),
            pl.BlockSpec((32, FF), lambda i: (i, 0)),
        ]
        + [pl.BlockSpec((32, WIDTH), lambda i: (i, 0))] * 4,
        compiler_params=pltpu.CompilerParams(vmem_limit_bytes=48 * 2**20),
        name="finish",
    )(g1, g2, g3)


def fast_shards(
    tokens,
    out_grad,
    ln1_gain,
    ln1_bias,
    q_weight,
    q_bias,
    k_weight,
    v_weight,
    v_bias,
    o_weight,
    o_bias,
    ln2_gain,
    ln2_bias,
    up_weight,
    up_bias,
    down_weight,
    down_bias,
):
    small = [ln1_gain, ln1_bias, q_bias, v_bias, o_bias, ln2_gain, ln2_bias, down_bias]
    pack = jnp.pad(jnp.stack(small).astype(f32), ((0, 0), (0, LANES - HALF)))
    gap = TILES * TILE - FF_HALF
    bup = jnp.pad(up_bias.astype(f32), (0, gap)).reshape(TILES, 1, TILE)
    normed1, query, key_rows, value_rows, attn_in, probs, residual, normed2, w, wup, wdown, vec, bup = (
        forward(tokens, q_weight, k_weight, v_weight, o_weight, up_weight, down_weight, pack, bup)
    )
    wq, wk, wv, wo = w[0], w[1], w[2], w[3]
    input_f = tokens.astype(f32)
    gain_one, shift_one, gain_two, shift_two = vec[0], vec[1], vec[5], vec[6]
    log_total = attend(query, key_rows, value_rows)[1]

    output, d_normed2, g1, g2, d_bup = feed_forward(
        normed2, residual, out_grad, wup, wdown, bup, vec
    )

    _, norm_back_two = jax.vjp(layer_norm, residual, gain_two, shift_two)
    d_res_norm, d_gain_two, d_shift_two = norm_back_two(d_normed2)
    d_residual = out_grad.astype(f32) + d_res_norm
    d_attn = d_residual.astype(bf16)
    d_wout = outer_rows(attn_in, d_attn)
    d_mixed = back_rows(d_attn, wo).astype(bf16)
    d_query, d_key, d_value = attend_back(query, key_rows, value_rows, log_total, d_mixed)
    d_wquery = outer_rows(normed1, d_query)
    d_wkey = outer_rows(normed1, d_key)
    d_wvalue = outer_rows(normed1, d_value)
    d_normed1 = back_rows(d_query, wq) + back_rows(d_key, wk) + back_rows(d_value, wv)
    _, norm_back_one = jax.vjp(layer_norm, input_f, gain_one, shift_one)
    d_in_norm, d_gain_one, d_shift_one = norm_back_one(d_normed1)
    d_input = (d_residual + d_in_norm).astype(bf16)

    parts = [w.astype(bf16).reshape(2, 1, HALF, WIDTH) for w in (d_wquery, d_wkey, d_wvalue, d_wout)]
    grads = jnp.concatenate(parts, axis=1).reshape(2, 2, CHUNKS, TILE, WIDTH)
    g3 = attention_sum(grads).reshape(4, HALF, WIDTH)

    d_bup = d_bup.reshape(TILES, 2, TILE).transpose(1, 0, 2).reshape(2, TILES * TILE)[:, :FF_HALF]
    small = [
        d_gain_one,
        d_shift_one,
        column_sums(d_query),
        column_sums(d_value),
        column_sums(d_attn),
        d_gain_two,
        d_shift_two,
        column_sums(out_grad),
    ]
    pack = jnp.concatenate([v.reshape(2, HALF) for v in small] + [d_bup], axis=1).astype(bf16)
    pack = lax.psum(pack, ("group", "replica")).astype(f32)
    mine = lax.dynamic_index_in_dim(pack, lax.axis_index("group"), 0, keepdims=False)
    small = [mine[j * HALF : (j + 1) * HALF] for j in range(8)]

    g1, g2, gq, gk, gv, go = finish(g1, g2, g3)
    return (
        output,
        d_input,
        small[0],
        small[1],
        gq,
        small[2],
        gk,
        gv,
        small[3],
        go,
        small[4],
        small[5],
        small[6],
        g2,
        mine[8 * HALF :],
        g1,
        small[7],
    )


def solution(mesh):
    placed = (
        P(("group", "replica"), None),
        P(("group", "replica"), None),
        P("group"),
        P("group"),
        P("group", None),
        P("group"),
        P("group", None),
        P("group", None),
        P("group"),
        P("group", None),
        P("group"),
        P("group"),
        P("group"),
        P("group", None),
        P("group"),
        P("group", None),
        P("group"),
    )
    fast = mesh.shape["group"] == 2 and mesh.shape["replica"] == 16
    return jax.shard_map(
        fast_shards if fast else shards,
        mesh=mesh,
        in_specs=placed,
        out_specs=(
            P(("group", "replica"), None),
            P(("group", "replica"), None),
            P("group"),
            P("group"),
            P("group", None),
            P("group"),
            P("group", None),
            P("group", None),
            P("group"),
            P("group", None),
            P("group"),
            P("group"),
            P("group"),
            P("group", None),
            P("group"),
            P("group", None),
            P("group"),
        ),
        check_vma=False,
    )
```

```python
import functools

import jax
import jax.numpy as jnp
from jax import lax
from jax.experimental import pallas as pl
from jax.experimental.pallas import tpu as pltpu
from jax.sharding import PartitionSpec as P

HEADS = 16
PATCHES = 128


def layer_norm(values, gain, shift):
    center = values - jnp.mean(values, axis=-1, keepdims=True)
    spread = jnp.mean(center * center, axis=-1, keepdims=True)
    return center * lax.rsqrt(spread + 1e-06) * gain + shift


def gelu_tanh(values):
    return jax.nn.gelu(values, approximate=True)


def split_heads(rows):
    return rows.reshape(-1, PATCHES, HEADS, rows.shape[-1] // HEADS)


def head_logits(query, key_rows):
    factor = (query.shape[-1] // HEADS) ** (-0.5)
    query_h = split_heads(query)
    key_h = split_heads(key_rows)
    logits = (
        jnp.einsum("isha,itha->ihst", query_h, key_h, preferred_element_type=jnp.float32) * factor
    )
    return (logits, query_h, key_h, factor)


def attend(query, key_rows, value_rows):
    logits, query_h, key_h, factor = head_logits(query, key_rows)
    peak = jnp.max(logits, axis=-1, keepdims=True)
    log_total = peak + jnp.log(jnp.sum(jnp.exp(logits - peak), axis=-1, keepdims=True))
    weights_low = jnp.exp(logits - log_total).astype(jnp.bfloat16)
    mixed = jnp.einsum(
        "ihst,itha->isha", weights_low, split_heads(value_rows), preferred_element_type=jnp.float32
    )
    return (mixed.reshape(query.shape), log_total)


def attend_back(query, key_rows, value_rows, log_total, d_mixed):
    logits, query_h, key_h, factor = head_logits(query, key_rows)
    weights = jnp.exp(logits - log_total)
    weights_low = weights.astype(jnp.bfloat16)
    value_h = split_heads(value_rows)
    d_mix_h = split_heads(d_mixed)
    d_weights = jnp.einsum("isha,itha->ihst", d_mix_h, value_h, preferred_element_type=jnp.float32)
    d_logits = weights * (d_weights - jnp.sum(weights * d_weights, axis=-1, keepdims=True))
    d_low = d_logits.astype(jnp.bfloat16)
    d_query = (
        jnp.einsum("ihst,itha->isha", d_low, key_h, preferred_element_type=jnp.float32) * factor
    ).astype(jnp.bfloat16)
    d_key = (
        jnp.einsum("ihst,isha->itha", d_low, query_h, preferred_element_type=jnp.float32) * factor
    ).astype(jnp.bfloat16)
    d_value = jnp.einsum(
        "ihst,isha->itha", weights_low, d_mix_h, preferred_element_type=jnp.float32
    ).astype(jnp.bfloat16)
    return (d_query.reshape(query.shape), d_key.reshape(query.shape), d_value.reshape(query.shape))


def outer_rows(left, right):
    return jnp.einsum("ra,rb->ab", left, right, preferred_element_type=jnp.float32)


def back_rows(grads, weight):
    return jnp.einsum("rb,ab->ra", grads, weight, preferred_element_type=jnp.float32)


def column_sums(grads):
    return jnp.sum(grads.astype(jnp.float32), axis=0)


def shards(
    tokens,
    out_grad,
    ln1_gain,
    ln1_bias,
    q_weight,
    q_bias,
    k_weight,
    v_weight,
    v_bias,
    o_weight,
    o_bias,
    ln2_gain,
    ln2_bias,
    up_weight,
    up_bias,
    down_weight,
    down_bias,
):
    attn_full = tuple(lax.all_gather(v, "group", axis=0, tiled=True) for v in (
        ln1_gain, ln1_bias, q_weight, q_bias, k_weight, v_weight, v_bias, o_weight, o_bias,
    ))
    gain_one, shift_one, wq_full, bq_full, wk_full, wv_full, bv_full, wo_full, bo_full = attn_full
    input_f = tokens.astype(jnp.float32)
    gain_one_f = gain_one.astype(jnp.float32)
    shift_one_f = shift_one.astype(jnp.float32)
    normed1 = layer_norm(input_f, gain_one_f, shift_one_f).astype(jnp.bfloat16)
    query = (
        jnp.dot(normed1, wq_full, preferred_element_type=jnp.float32) + bq_full.astype(jnp.float32)
    ).astype(jnp.bfloat16)
    key_rows = jnp.dot(normed1, wk_full, preferred_element_type=jnp.float32).astype(jnp.bfloat16)
    value_rows = (
        jnp.dot(normed1, wv_full, preferred_element_type=jnp.float32) + bv_full.astype(jnp.float32)
    ).astype(jnp.bfloat16)
    mixed, log_total = attend(query, key_rows, value_rows)
    attn_in = mixed.astype(jnp.bfloat16)
    residual = (
        input_f
        + jnp.dot(attn_in, wo_full, preferred_element_type=jnp.float32)
        + bo_full.astype(jnp.float32)
    )
    mlp_full = tuple(lax.all_gather(v, "group", axis=0, tiled=True) for v in (
        ln2_gain, ln2_bias, up_weight, up_bias, down_weight, down_bias,
    ))
    gain_two, shift_two, wup_full, bup_full, wdown_full, bdown_full = mlp_full
    gain_two_f = gain_two.astype(jnp.float32)
    shift_two_f = shift_two.astype(jnp.float32)
    normed2 = layer_norm(residual, gain_two_f, shift_two_f).astype(jnp.bfloat16)
    pre_act = jnp.dot(normed2, wup_full, preferred_element_type=jnp.float32) + bup_full.astype(
        jnp.float32
    )
    hidden = gelu_tanh(pre_act).astype(jnp.bfloat16)
    output = (
        residual
        + jnp.dot(hidden, wdown_full, preferred_element_type=jnp.float32)
        + bdown_full.astype(jnp.float32)
    )
    mlp_back = tuple(lax.all_gather(v, "group", axis=0, tiled=True) for v in (
        ln2_gain, ln2_bias, up_weight, up_bias, down_weight, down_bias,
    ))
    wup_back = mlp_back[2]
    wdown_back = mlp_back[4]
    grad_out = out_grad.astype(jnp.float32)
    d_wdown = outer_rows(hidden, out_grad)
    d_bdown = column_sums(out_grad)
    d_hidden = back_rows(out_grad, wdown_back)
    unused_act, gelu_back = jax.vjp(gelu_tanh, pre_act)
    d_pre = gelu_back(d_hidden)[0].astype(jnp.bfloat16)
    d_wup = outer_rows(normed2, d_pre)
    d_bup = column_sums(d_pre)
    d_normed2 = back_rows(d_pre, wup_back)
    unused_two, norm_back_two = jax.vjp(layer_norm, residual, gain_two_f, shift_two_f)
    d_res_norm, d_gain_two, d_shift_two = norm_back_two(d_normed2)
    d_residual = grad_out + d_res_norm
    mlp_grads = tuple(
        lax.psum_scatter(v.astype(jnp.bfloat16), "group", scatter_dimension=0, tiled=True).astype(jnp.float32)
        for v in (d_gain_two, d_shift_two, d_wup, d_bup, d_wdown, d_bdown)
    )
    attn_back = tuple(lax.all_gather(v, "group", axis=0, tiled=True) for v in (
        ln1_gain, ln1_bias, q_weight, q_bias, k_weight, v_weight, v_bias, o_weight, o_bias,
    ))
    wq_back = attn_back[2]
    wk_back = attn_back[4]
    wv_back = attn_back[5]
    wo_back = attn_back[7]
    d_attn = d_residual.astype(jnp.bfloat16)
    d_wout = outer_rows(attn_in, d_attn)
    d_bout = column_sums(d_attn)
    d_mixed = back_rows(d_attn, wo_back).astype(jnp.bfloat16)
    d_query, d_key, d_value = attend_back(query, key_rows, value_rows, log_total, d_mixed)
    d_wquery = outer_rows(normed1, d_query)
    d_bquery = column_sums(d_query)
    d_wkey = outer_rows(normed1, d_key)
    d_wvalue = outer_rows(normed1, d_value)
    d_bvalue = column_sums(d_value)
    d_normed1 = (
        back_rows(d_query, wq_back) + back_rows(d_key, wk_back) + back_rows(d_value, wv_back)
    )
    unused_one, norm_back_one = jax.vjp(layer_norm, input_f, gain_one_f, shift_one_f)
    d_in_norm, d_gain_one, d_shift_one = norm_back_one(d_normed1)
    d_input = (d_residual + d_in_norm).astype(jnp.bfloat16)
    attn_grads = tuple(
        lax.psum_scatter(v.astype(jnp.bfloat16), "group", scatter_dimension=0, tiled=True).astype(jnp.float32)
        for v in (d_gain_one, d_shift_one, d_wquery, d_bquery, d_wkey, d_wvalue, d_bvalue, d_wout, d_bout)
    )
    summed = tuple(
        lax.psum(v.astype(jnp.bfloat16), "replica").astype(jnp.float32) for v in attn_grads + mlp_grads
    )
    attn_grads = tuple(summed[:9])
    mlp_grads = tuple(summed[9:])
    return (output.astype(jnp.bfloat16), d_input) + tuple(attn_grads) + tuple(mlp_grads)


MESH = pl.DeviceIdType.MESH
bf16 = jnp.bfloat16
f32 = jnp.float32
ANY = pl.BlockSpec(memory_space=pl.ANY)
WIDTH = 1152
HALF = 576
FF = 4304
FF_HALF = 2152
TILES = 17
TILE = 128
FF_PAD = 2 * TILES * TILE
FIRST = 320
SECOND = 256


class Place:
    def __init__(self):
        self.core = lax.axis_index("group")
        chip = lax.axis_index("replica")
        self.chip = chip
        self.x = lax.rem(chip, 2)
        self.y = lax.rem(chip // 2, 2)
        self.z = chip // 4
        self.x_pair = chip + 1 - 2 * self.x
        self.y_pair = chip + 2 - 4 * self.y
        self.z_pair = chip + 4 - 8 * lax.rem(self.z, 2)
        self.inner = (self.z == 1) | (self.z == 2)
        self.outer = jnp.logical_not(self.inner)
        self.mid_pair = jnp.where(self.inner, chip + 12 - 8 * self.z, chip)
        self.z_half = lax.rem(self.z // 2, 2)

    def barrier(self):
        sem = pltpu.get_barrier_semaphore()

        def greet(core, chip):
            pl.semaphore_signal(sem, inc=1, device_id=(core, chip), device_id_type=MESH)

        greet(1 - self.core, self.chip)
        greet(self.core, self.x_pair)
        greet(self.core, self.y_pair)
        greet(self.core, self.z_pair)

        @pl.when(self.inner)
        def _():
            greet(self.core, self.mid_pair)
            pl.semaphore_wait(sem, 5)

        @pl.when(self.outer)
        def _():
            pl.semaphore_wait(sem, 4)

    def copy(self, source, target, sent, got, chip):
        return pltpu.make_async_remote_copy(
            source, target, sent, got, device_id=(self.core, chip), device_id_type=MESH
        )

    def copy_sibling(self, source, target, sent, got):
        return pltpu.make_async_remote_copy(
            source, target, sent, got, device_id=(1 - self.core, self.chip), device_id_type=MESH
        )


def aligned(value, unit):
    return pl.multiple_of(value, unit)


def landing(slots, chunk):
    return slots.at[lax.rem(chunk, slots.shape[0])]


def add_rows(total, landed, chunk, start, count):
    rows = pl.ds(start, count)
    slot = lax.rem(chunk, total.shape[0])
    total[slot, rows, :] = (
        total[slot, rows, :].astype(f32) + landed[...].astype(f32)
    ).astype(bf16)


class TreeFirst:
    steps = 9

    def __init__(self, place, total, final, landing, sent, got, kept):
        self.at = place
        self.total = total
        self.final = final
        self.kept = kept
        self.land = landing
        self.sent = sent
        self.got = got
        n = total.shape[1]
        self.n = n
        p = place
        self.own = [
            (0, n),
            (aligned(p.z_half * (n // 2), n // 2), n // 2),
        ]
        self.other = [None, (aligned((1 - p.z_half) * (n // 2), n // 2), n // 2)]
        for bit, part in ((p.y, n // 4), (p.x, n // 8)):
            base = self.own[-1][0]
            self.own.append((aligned(base + bit * part, part), part))
            self.other.append((aligned(base + (1 - bit) * part, part), part))
        self.peer = [p.z_pair, p.mid_pair, p.y_pair, p.x_pair]

    def rows(self, chunk, span):
        return landing(self.total, chunk).at[pl.ds(span[0], span[1]), :]

    def ends(self, chunk, span):
        return self.final.at[chunk, pl.ds(span[0], span[1]), :]

    def send(self, k, chunk):
        sent, got = self.sent.at[k, chunk], self.got.at[k, chunk]
        if k < 4:
            span = self.own[0] if k == 0 else self.other[k]
            return self.at.copy(
                self.rows(chunk, span), landing(self.land[k], chunk), sent, got, self.peer[k]
            )
        level = 7 - k
        target = self.ends(chunk, self.own[level])
        source = self.rows(chunk, self.own[3]) if k == 4 else target
        return self.at.copy(source, target, sent, got, self.peer[level])

    def keep(self, chunk):
        return pltpu.make_async_copy(
            self.rows(chunk, self.own[3]), self.ends(chunk, self.own[3]), self.kept.at[chunk]
        )

    def arrive(self, k, chunk):
        if k < 4:
            landed = landing(self.land[k], chunk)
        else:
            level = 7 - k
            landed = self.ends(chunk, self.own[0] if level == 0 else self.other[level])
        self.at.copy(
            landed, landed, self.sent.at[k, chunk], self.got.at[k, chunk], self.at.z_pair
        ).wait_recv()

    def step(self, k, chunk):
        at = self.at
        if k == 0:

            @pl.when(at.outer)
            def _():
                self.send(0, chunk).start()

        elif k <= 7:

            @pl.when(at.inner)
            def _():
                self.arrive(k - 1, chunk)
                if k <= 4:
                    add_rows(self.total, landing(self.land[k - 1], chunk), chunk, *self.own[k - 1])
                if k == 4:
                    self.keep(chunk).start()
                if k == 5:
                    self.keep(chunk).wait()
                self.send(k, chunk).start()

        else:

            @pl.when(at.inner)
            def _():
                for j in range(1, 8):
                    self.send(j, chunk).wait_send()

            @pl.when(at.outer)
            def _():
                self.arrive(7, chunk)
                self.send(0, chunk).wait_send()


class PlaneFirst:
    steps = 8

    def __init__(self, place, total, final, base, n, x_first, landing, sent, got, kept):
        self.at = place
        self.total = total
        self.final = final
        self.kept = kept
        self.land = landing
        self.sent = sent
        self.got = got
        p = place
        if x_first:
            one, two = (p.x, p.x_pair), (p.y, p.y_pair)
        else:
            one, two = (p.y, p.y_pair), (p.x, p.x_pair)
        self.peer_one, self.peer_two = one[1], two[1]
        start = aligned(base + one[0] * (n // 2), 16)
        self.half = (start, n // 2)
        self.half_other = (aligned(base + (1 - one[0]) * (n // 2), 16), n // 2)
        self.quarter = (aligned(start + two[0] * (n // 4), 16), n // 4)
        self.quarter_other = (aligned(start + (1 - two[0]) * (n // 4), 16), n // 4)

    def rows(self, chunk, span):
        return landing(self.total, chunk).at[pl.ds(span[0], span[1]), :]

    def ends(self, chunk, span):
        return self.final.at[chunk, pl.ds(span[0], span[1]), :]

    def keep(self, chunk):
        return pltpu.make_async_copy(
            self.rows(chunk, self.quarter), self.ends(chunk, self.quarter), self.kept.at[chunk]
        )

    def send(self, k, chunk):
        at = self.at
        quarter = self.rows(chunk, self.quarter)
        quarter_end = self.ends(chunk, self.quarter)
        half_end = self.ends(chunk, self.half)
        source, target, peer = (
            (self.rows(chunk, self.half_other), landing(self.land[0], chunk), self.peer_one),
            (self.rows(chunk, self.quarter_other), landing(self.land[1], chunk), self.peer_two),
            (quarter, landing(self.land[2], chunk), at.z_pair),
            (quarter, landing(self.land[3], chunk), at.mid_pair),
            (quarter, quarter_end, at.z_pair),
            (quarter_end, quarter_end, self.peer_two),
            (half_end, half_end, self.peer_one),
        )[k]
        return at.copy(source, target, self.sent.at[k, chunk], self.got.at[k, chunk], peer)

    def arrive(self, k, chunk):
        if k < 4:
            landed = landing(self.land[k], chunk)
        else:
            landed = self.ends(
                chunk, (self.quarter, self.quarter_other, self.half_other)[k - 4]
            )
        self.at.copy(
            landed, landed, self.sent.at[k, chunk], self.got.at[k, chunk], self.at.z_pair
        ).wait_recv()

    def step(self, k, chunk):
        at = self.at
        if k == 0:
            self.send(0, chunk).start()
        elif k == 1:
            self.arrive(0, chunk)
            add_rows(self.total, landing(self.land[0], chunk), chunk, *self.half)
            self.send(1, chunk).start()
        elif k == 2:
            self.arrive(1, chunk)
            add_rows(self.total, landing(self.land[1], chunk), chunk, *self.quarter)

            @pl.when(at.outer)
            def _():
                self.send(2, chunk).start()

        elif k == 3:

            @pl.when(at.inner)
            def _():
                self.arrive(2, chunk)
                add_rows(self.total, landing(self.land[2], chunk), chunk, *self.quarter)
                self.send(3, chunk).start()

        elif k == 4:

            @pl.when(at.inner)
            def _():
                self.arrive(3, chunk)
                self.send(3, chunk).wait_send()
                add_rows(self.total, landing(self.land[3], chunk), chunk, *self.quarter)
                self.send(4, chunk).start()
                self.keep(chunk).start()

        elif k == 5:

            @pl.when(at.inner)
            def _():
                self.keep(chunk).wait()

            @pl.when(at.outer)
            def _():
                self.arrive(4, chunk)

            self.send(5, chunk).start()
        elif k == 6:
            self.arrive(5, chunk)
            self.send(6, chunk).start()
        else:
            self.arrive(6, chunk)
            for j in (0, 1, 5, 6):
                self.send(j, chunk).wait_send()

            @pl.when(at.inner)
            def _():
                self.send(4, chunk).wait_send()

            @pl.when(at.outer)
            def _():
                self.send(2, chunk).wait_send()


def tree_scratch(count, n, width):
    return [
        pltpu.VMEM((slots, n // part, width), bf16)
        for slots, part in ((10, 1), (3, 2), (3, 4), (3, 8))
    ] + [
        pltpu.SemaphoreType.DMA((8, count)),
        pltpu.SemaphoreType.DMA((8, count)),
        pltpu.SemaphoreType.DMA((count,)),
    ]


def plane_scratch(count, n, width):
    return [
        pltpu.VMEM((slots, n // part, width), bf16)
        for slots, part in ((3, 2), (3, 4), (4, 4), (3, 4))
    ] + [
        pltpu.SemaphoreType.DMA((7, count)),
        pltpu.SemaphoreType.DMA((7, count)),
        pltpu.SemaphoreType.DMA((count,)),
    ]


def dot(left, right, contract):
    return lax.dot_general(left, right, (contract, ((), ())), preferred_element_type=f32)


NN = ((1,), (0,))
NT = ((1,), (1,))
TN = ((0,), (0,))


def gelu_and_slope(u):
    c = 0.7978845608028654
    square = u * u
    t = jnp.tanh(c * u * (1.0 + 0.044715 * square))
    half = 0.5 * (1.0 + t)
    slope = half + 0.5 * u * (1.0 - t * t) * (c * (1.0 + 3 * 0.044715 * square))
    return u * half, slope


VECTORS = 8
LANES = 640
SCALE = 72**-0.5
HEAD = 72


def head_window(h):
    return slice(h * HEAD // 128 * 128, ((h + 1) * HEAD + 127) // 128 * 128)


def only_head(rows, h):
    lane = lax.broadcasted_iota(jnp.int32, rows.shape, 1) + head_window(h).start
    return jnp.where((lane >= h * HEAD) & (lane < (h + 1) * HEAD), rows, jnp.zeros_like(rows))


class Lanes:
    def __init__(self):
        self.tiles = [None] * (WIDTH // 128)

    def add(self, h, window):
        first = head_window(h).start // 128
        for j in range(window.shape[1] // 128):
            part = window[:, j * 128 : (j + 1) * 128]
            old = self.tiles[first + j]
            self.tiles[first + j] = part if old is None else old + part

    def joined(self, scale=None):
        tiles = self.tiles if scale is None else [t * scale for t in self.tiles]
        return jnp.concatenate([t.astype(bf16) for t in tiles], axis=1)


def normalise(rows, gain, shift):
    center = rows - jnp.mean(rows, axis=-1, keepdims=True)
    spread = jnp.mean(center * center, axis=-1, keepdims=True)
    return center * lax.rsqrt(spread + 1e-06) * gain + shift


def forward_kernel(
    tokens_ref,
    wq_ref,
    wk_ref,
    wv_ref,
    wo_ref,
    up_ref,
    down_ref,
    pack_ref,
    bup_ref,
    h1_ref,
    q_ref,
    k_ref,
    v_ref,
    ao_ref,
    probs_ref,
    x2_ref,
    h2_ref,
    w_ref,
    wup_ref,
    wdown_ref,
    vec_ref,
    bups_ref,
    x,
    h1,
    q,
    k,
    v,
    ao,
    probs,
    x2,
    h2,
    w,
    up,
    up_wide,
    down,
    zeros,
    pack,
    vec,
    local,
    wsem,
    psem,
    sent,
    got,
    bsem,
):
    at = Place()
    core = at.core
    own = pl.ds(aligned(core * HALF, HALF), HALF)
    ff_own = pl.ds(aligned(core * TILES * TILE, TILE), FF_HALF)
    shards = (wq_ref, wk_ref, wv_ref, wo_ref)
    load_x = pltpu.make_async_copy(tokens_ref, x, local.at[0])
    load_x.start()
    load_w = [pltpu.make_async_copy(s, w.at[j, own, :], local.at[1 + j]) for j, s in enumerate(shards)]
    load_pack = pltpu.make_async_copy(pack_ref, pack.at[core], local.at[5])
    load_bup = pltpu.make_async_copy(bup_ref, bups_ref.at[core], local.at[6])
    load_up = pltpu.make_async_copy(up_ref, up, local.at[7])
    load_down = pltpu.make_async_copy(down_ref, down, local.at[8])
    keep_down = pltpu.make_async_copy(down, wdown_ref.at[ff_own, :], wsem.at[4])
    for load in (load_pack, *load_w, load_bup, load_up, load_down):
        load.start()
    zeros[...] = jnp.zeros_like(zeros)
    gap = TILES * TILE - FF_HALF
    blanks = [
        pltpu.make_async_copy(
            zeros, wdown_ref.at[pl.ds(h * TILES * TILE + FF_HALF, gap), :], local.at[9 + h]
        )
        for h in (0, 1)
    ]
    for blank in blanks:
        blank.start()

    bar = pltpu.get_barrier_semaphore()
    pl.semaphore_signal(bar, inc=1, device_id=(1 - core, at.chip), device_id_type=MESH)
    pl.semaphore_wait(bar, 1)

    def share(j, source, target):
        return at.copy_sibling(source, target, sent.at[j], got.at[j])

    give_w = [share(j, s, w.at[j, own, :]) for j, s in enumerate(shards)]
    give_pack = share(4, pack_ref, pack.at[core])
    give_bup = share(5, bup_ref, bups_ref.at[core])
    give_down = share(6, down_ref, wdown_ref.at[ff_own, :])
    give_up = share(7, up_wide, wup_ref.at[own, :])
    keep_up = pltpu.make_async_copy(up_wide, wup_ref.at[own, :], local.at[11])
    give_pack.start()
    for give in give_w:
        give.start()
    give_bup.start()
    give_down.start()

    load_pack.wait()
    give_pack.wait()
    vec[...] = jnp.concatenate([pack[0, :, :HALF], pack[1, :, :HALF]], axis=1)
    load_x.wait()
    rows_of = [pl.ds(b * 512, 512) for b in range(2)]

    def first_norm(b, carry):
        rows = pl.ds(aligned(b * 128, 128), 128)
        h1[rows, :] = normalise(x[rows, :].astype(f32), vec[0:1, :], vec[1:2, :]).astype(bf16)
        return carry

    lax.fori_loop(0, 8, first_norm, 0)
    keep = [pltpu.make_async_copy(h1, h1_ref, local.at[0])]
    keep[0].start()

    def project(j, target, bias):
        load_w[j].wait()
        give_w[j].wait()
        for rows in rows_of:
            y = dot(h1[rows, :], w[j], NN)
            if bias is not None:
                y = y + vec[bias : bias + 1, :]
            target[rows, :] = y.astype(bf16)

    project(0, q, 2)
    project(1, k, None)
    project(2, v, 3)
    for j, (s, d) in enumerate(((q, q_ref), (k, k_ref), (v, v_ref))):
        keep.append(pltpu.make_async_copy(s, d, local.at[12 + j]))
        keep[-1].start()

    load_down.wait()
    keep_down.start()
    load_up.wait()

    def widen(b, carry):
        rows = pl.ds(aligned(b * 64, 64), 64)
        row = up[rows, :]
        none = jnp.zeros((64, gap), bf16)
        up_wide[rows, :] = jnp.concatenate([row[:, :FF_HALF], none, row[:, FF_HALF:], none], axis=1)
        return carry

    lax.fori_loop(0, HALF // 64, widen, 0)
    keep_up.start()
    give_up.start()

    def keep_probs(i):
        slot = lax.rem(i, 2)
        return pltpu.make_async_copy(probs.at[slot], probs_ref.at[i], psem.at[slot])

    def attention(i, carry):
        rows = pl.ds(aligned(i * 128, 128), 128)
        slot = lax.rem(i, 2)

        @pl.when(i >= 2)
        def _():
            keep_probs(i - 2).wait()

        qi, ki, vi = q[rows, :], k[rows, :], v[rows, :]
        mixed = Lanes()
        held = []
        for h in range(HEADS):
            cols = head_window(h)
            logits = dot(qi[:, cols], only_head(ki[:, cols], h), NT) * SCALE
            e = jnp.exp(logits - jnp.max(logits, axis=-1, keepdims=True))
            p = (e / jnp.sum(e, axis=-1, keepdims=True)).astype(bf16)
            held.append(p)
            mixed.add(h, dot(p, only_head(vi[:, cols], h), NN))
        ao[rows, :] = mixed.joined()
        probs[slot] = jnp.concatenate(held, axis=1)
        keep_probs(i).start()
        return carry

    lax.fori_loop(0, 8, attention, 0)
    keep_ao = pltpu.make_async_copy(ao, ao_ref, local.at[15])
    keep_ao.start()

    load_w[3].wait()
    give_w[3].wait()
    keep_w = pltpu.make_async_copy(w, w_ref, wsem.at[0])
    keep_w.start()
    keep_vec = pltpu.make_async_copy(vec, vec_ref, wsem.at[1])
    keep_vec.start()
    for rows in rows_of:
        x2[rows, :] = x[rows, :].astype(f32) + dot(ao[rows, :], w[3], NN) + vec[4:5, :]

    def second_norm(b, carry):
        rows = pl.ds(aligned(b * 128, 128), 128)
        h2[rows, :] = normalise(x2[rows, :], vec[5:6, :], vec[6:7, :]).astype(bf16)
        return carry

    lax.fori_loop(0, 8, second_norm, 0)
    keep_x2 = pltpu.make_async_copy(x2, x2_ref, wsem.at[2])
    keep_h2 = pltpu.make_async_copy(h2, h2_ref, wsem.at[3])
    for copy in (keep_x2, keep_h2):
        copy.start()
    for copy in (
        *keep,
        keep_probs(6),
        keep_probs(7),
        keep_ao,
        keep_w,
        keep_vec,
        load_bup,
        keep_down,
        *blanks,
        keep_up,
        keep_x2,
        keep_h2,
    ):
        copy.wait()
    for give in (give_bup, give_down, give_up):
        give.wait()


def forward(tokens, wq, wk, wv, wo, up, down, pack, bup):
    rows = tokens.shape[0]
    images = rows // PATCHES
    flat = jax.ShapeDtypeStruct((rows, WIDTH), bf16)
    return pl.pallas_call(
        forward_kernel,
        out_shape=(
            flat,
            flat,
            flat,
            flat,
            flat,
            jax.ShapeDtypeStruct((images, PATCHES, HEADS * PATCHES), bf16),
            jax.ShapeDtypeStruct((rows, WIDTH), f32),
            flat,
            jax.ShapeDtypeStruct((4, WIDTH, WIDTH), bf16),
            jax.ShapeDtypeStruct((WIDTH, FF_PAD), bf16),
            jax.ShapeDtypeStruct((FF_PAD, WIDTH), bf16),
            jax.ShapeDtypeStruct((VECTORS, WIDTH), f32),
            jax.ShapeDtypeStruct((2, TILES, 1, TILE), f32),
        ),
        in_specs=[ANY] * 9,
        out_specs=[ANY] * 13,
        scratch_shapes=[pltpu.VMEM((rows, WIDTH), bf16)] * 6
        + [
            pltpu.VMEM((2, PATCHES, HEADS * PATCHES), bf16),
            pltpu.VMEM((rows, WIDTH), f32),
            pltpu.VMEM((rows, WIDTH), bf16),
            pltpu.VMEM((4, WIDTH, WIDTH), bf16),
            pltpu.VMEM((HALF, FF), bf16),
            pltpu.VMEM((HALF, FF_PAD), bf16),
            pltpu.VMEM((FF_HALF, WIDTH), bf16),
            pltpu.VMEM((TILES * TILE - FF_HALF, WIDTH), bf16),
            pltpu.VMEM((2, VECTORS, LANES), f32),
            pltpu.VMEM((VECTORS, WIDTH), f32),
            pltpu.SemaphoreType.DMA((16,)),
            pltpu.SemaphoreType.DMA((5,)),
            pltpu.SemaphoreType.DMA((2,)),
            pltpu.SemaphoreType.DMA((8,)),
            pltpu.SemaphoreType.DMA((8,)),
            pltpu.SemaphoreType.DMA((1,)),
        ],
        compiler_params=pltpu.CompilerParams(
            collective_id=3, has_side_effects=True, vmem_limit_bytes=62 * 2**20
        ),
        name="forward",
    )(tokens, wq, wk, wv, wo, up, down, pack, bup)


CHUNKS = 9
TREE = TILES + CHUNKS
BLOCK = 128


def rest_kernel(
    tokens_ref,
    og_ref,
    h1_ref,
    q_ref,
    k_ref,
    v_ref,
    ao_ref,
    probs_ref,
    x2_ref,
    h2_ref,
    w_ref,
    wup_ref,
    wdown_ref,
    vec_ref,
    bup_ref,
    out_ref,
    din_ref,
    g1_ref,
    g2_ref,
    g3_ref,
    h2,
    h2t,
    og,
    dh2,
    bup,
    vec,
    dbup,
    dvec,
    small,
    sib1,
    sib2,
    sib3,
    sum1,
    sum2,
    sum3,
    local,
    gsent,
    ggot,
    *comm,
):
    at = Place()
    rows_all = h2.shape[0]
    blocks = rows_all // BLOCK
    comm = [comm[j : j + 7] for j in range(0, 35, 7)]
    tree = TreeFirst(at, sum1, g1_ref, comm[0][:4], *comm[0][4:])
    early = [
        PlaneFirst(at, sum2, g2_ref, base, n, first, comm[j][:4], *comm[j][4:])
        for j, base, n, first in ((1, 0, FIRST, True), (2, FIRST, SECOND, False))
    ]
    late = [
        PlaneFirst(at, sum3, g3_ref, base, TILE // 2, first, comm[j][:4], *comm[j][4:])
        for j, base, first in ((3, 0, True), (4, TILE // 2, False))
    ]

    def advance(tick):
        for k in reversed(range(TreeFirst.steps)):
            chunk = tick - k

            @pl.when((chunk >= 0) & (chunk < TREE))
            def _():
                tree.step(k, chunk)

            if k < PlaneFirst.steps:

                @pl.when((chunk >= 0) & (chunk < TILES))
                def _():
                    for part in early:
                        part.step(k, chunk)

                @pl.when((chunk >= TILES) & (chunk <= TREE))
                def _():
                    for part in late:
                        part.step(k, chunk - TILES)

    def block(b):
        return pl.ds(aligned(b * BLOCK, BLOCK), BLOCK)

    loads = [
        pltpu.make_async_copy(s, d, local.at[j])
        for j, (s, d) in enumerate(
            ((h2_ref, h2), (og_ref, og), (bup_ref, bup), (vec_ref, vec))
        )
    ]
    for load in loads:
        load.start()
    dvec[...] = jnp.zeros_like(dvec)

    def feed_forward(out, staged, wu, wd, mine1, mine2, wsem):
        load_x2 = pltpu.make_async_copy(x2_ref, out, local.at[4])
        load_x2.start()

        def weights(i, slot):
            cols = [pl.ds(aligned(h * TILES * TILE + i * TILE, TILE), TILE) for h in (0, 1)]
            parts = []
            for h in (0, 1):
                here = pl.ds(h * TILE, TILE)
                parts.append(
                    pltpu.make_async_copy(
                        wup_ref.at[:, cols[h]], wu.at[slot, :, here], wsem.at[h, slot]
                    )
                )
                parts.append(
                    pltpu.make_async_copy(
                        wdown_ref.at[cols[h], :], wd.at[slot, here, :], wsem.at[2 + h, slot]
                    )
                )
            return parts

        for part in weights(0, 0):
            part.start()
        at.barrier()
        for load in loads:
            load.wait()
        load_x2.wait()
        for b in range(blocks):
            rows = pl.ds(b * BLOCK, BLOCK)
            h2t[:, rows] = h2[rows, :].T
        out[...] = out[...] + vec[7:8, :]
        dh2[...] = jnp.zeros_like(dh2)

        def to_sibling(slot):
            return [
                at.copy_sibling(m.at[slot, 1 - at.core], s.at[slot], gsent.at[j, slot], ggot.at[j, slot])
                for j, (m, s) in enumerate(((mine1, sib1), (mine2, sib2)))
            ]

        def meet(i):
            slot = lax.rem(i, 2)
            for copy in to_sibling(slot):
                copy.wait()
            sum1[i] = (mine1[slot, at.core].astype(f32) + sib1[slot].astype(f32)).astype(bf16)
            sum2[i] = (mine2[slot, at.core].astype(f32) + sib2[slot].astype(f32)).astype(bf16)

        def tile(i, carry):
            slot = lax.rem(i, 2)

            @pl.when(i >= 1)
            def _():
                meet(i - 1)

            @pl.when((i >= 1) & (lax.rem(i, 3) != 0))
            def _():
                advance(i - 1 - i // 3)

            for part in weights(i, slot):
                part.wait()

            @pl.when(i + 1 < TILES)
            def _():
                for part in weights(i + 1, 1 - slot):
                    part.start()

            bias = jnp.concatenate([bup[0, i], bup[1, i]], axis=1)
            u = dot(h2[...], wu[slot], NN) + bias
            a, slope = gelu_and_slope(u)
            a = a.astype(bf16)
            out[...] += dot(a, wd[slot], NN)
            d_wd = dot(a, og[...], TN).astype(bf16)
            mine1[slot, 0] = d_wd[:TILE]
            mine1[slot, 1] = d_wd[TILE:]
            du = (dot(og[...], wd[slot], NT) * slope).astype(bf16)
            d_wu = dot(h2t[...], du, NN).astype(bf16)
            mine2[slot, 0] = d_wu[:HALF]
            mine2[slot, 1] = d_wu[HALF:]
            for copy in to_sibling(slot):
                copy.start()
            dh2[...] += dot(du, wu[slot], NT)
            dbup[i] = jnp.sum(du.astype(f32), axis=0, keepdims=True)
            return carry

        lax.fori_loop(0, TILES, tile, 0)
        meet(TILES - 1)

        def put(b):
            slot = lax.rem(b, 2)
            return pltpu.make_async_copy(staged.at[slot], out_ref.at[block(b), :], local.at[slot])

        def put_rows(b, carry):
            @pl.when(b >= 2)
            def _():
                put(b - 2).wait()

            staged[lax.rem(b, 2)] = out[block(b), :].astype(bf16)
            put(b).start()
            return carry

        lax.fori_loop(0, blocks, put_rows, 0)
        put(blocks - 2).wait()
        put(blocks - 1).wait()

    pl.run_scoped(
        feed_forward,
        pltpu.VMEM((rows_all, WIDTH), f32),
        pltpu.VMEM((2, BLOCK, WIDTH), bf16),
        pltpu.VMEM((2, WIDTH, 2 * TILE), bf16),
        pltpu.VMEM((2, 2 * TILE, WIDTH), bf16),
        pltpu.VMEM((2, 2, TILE, WIDTH), bf16),
        pltpu.VMEM((2, 2, HALF, 2 * TILE), bf16),
        pltpu.SemaphoreType.DMA((4, 2)),
    )

    def attention(aot, dq, dk, dv, w, image, pimage, wide, staged, mine3, wsem, isem):
        load_ao = pltpu.make_async_copy(ao_ref, dq, wsem.at[0])
        load_h1 = pltpu.make_async_copy(h1_ref, dk, wsem.at[1])

        def load_w(j, slot):
            return pltpu.make_async_copy(w_ref.at[j], w.at[slot], wsem.at[2 + slot])

        def load_x2(b):
            slot = lax.rem(b, 2)
            return pltpu.make_async_copy(x2_ref.at[block(b), :], wide.at[slot], isem.at[4, slot])

        def load_x(b):
            slot = lax.rem(b, 2)
            return pltpu.make_async_copy(
                tokens_ref.at[block(b), :], image.at[0, slot], isem.at[0, slot]
            )

        def put(b):
            slot = lax.rem(b, 2)
            return pltpu.make_async_copy(staged.at[slot], din_ref.at[block(b), :], isem.at[4, slot])

        def load_image(i):
            slot = lax.rem(i, 2)
            return [
                pltpu.make_async_copy(s.at[block(i), :], image.at[j, slot], isem.at[j, slot])
                for j, s in enumerate((q_ref, k_ref, v_ref))
            ] + [pltpu.make_async_copy(probs_ref.at[i], pimage.at[slot], isem.at[3, slot])]

        load_x2(0).start()
        load_w(3, 0).start()
        load_ao.start()
        load_h1.start()
        load_w(1, 1).start()
        load_w(2, 2).start()
        for copy in load_image(0):
            copy.start()

        def column_sum(j, value):
            dvec[j : j + 1, :] += jnp.sum(value, axis=0, keepdims=True)

        def norm_back(source, gain, incoming):
            center = source - jnp.mean(source, axis=-1, keepdims=True)
            rate = lax.rsqrt(jnp.mean(center * center, axis=-1, keepdims=True) + 1e-06)
            n = center * rate
            scaled = incoming * gain
            first = jnp.mean(scaled, axis=-1, keepdims=True)
            second = jnp.mean(scaled * n, axis=-1, keepdims=True)
            return n, (scaled - first - n * second) * rate

        def second_norm(b, carry):
            @pl.when((b == 2) | (b == 5))
            def _():
                advance(11 + b // 4)

            load_x2(b).wait()

            @pl.when(b + 1 < blocks)
            def _():
                load_x2(b + 1).start()

            rows = block(b)
            e = dh2[rows, :]
            n, dn = norm_back(wide[lax.rem(b, 2)], vec[5:6, :], e)
            g = og[rows, :].astype(f32)
            dx2 = g + dn
            dt = dx2.astype(bf16)
            dh2[rows, :] = dx2
            h2[rows, :] = dt
            column_sum(5, e * n)
            column_sum(6, e)
            column_sum(7, g)
            column_sum(4, dt.astype(f32))
            return carry

        lax.fori_loop(0, blocks, second_norm, 0)
        load_ao.wait()
        load_h1.wait()
        for b in range(blocks):
            rows = pl.ds(b * BLOCK, BLOCK)
            aot[:, rows] = dq[rows, :].T
            h2t[:, rows] = dk[rows, :].T
        load_w(3, 0).wait()
        for b in range(2):
            rows = pl.ds(b * (rows_all // 2), rows_all // 2)
            og[rows, :] = dot(h2[rows, :], w[0], NT).astype(bf16)
        load_w(0, 0).start()

        def heads(i, carry):
            @pl.when(lax.rem(i, 2) == 1)
            def _():
                advance(13 + i // 2)

            slot = lax.rem(i, 2)
            for copy in load_image(i):
                copy.wait()

            @pl.when(i + 1 < blocks)
            def _():
                for copy in load_image(i + 1):
                    copy.start()

            rows = block(i)
            qi, ki, vi, gi = image[0, slot], image[1, slot], image[2, slot], og[rows, :]
            sums = Lanes(), Lanes(), Lanes()
            for h in range(HEADS):
                cols = head_window(h)
                low = pimage[slot, :, h * PATCHES : (h + 1) * PATCHES]
                p = low.astype(f32)
                dp = dot(gi[:, cols], only_head(vi[:, cols], h), NT)
                ds = (p * (dp - jnp.sum(p * dp, axis=-1, keepdims=True))).astype(bf16)
                sums[0].add(h, dot(ds, only_head(ki[:, cols], h), NN))
                sums[1].add(h, dot(ds, only_head(qi[:, cols], h), TN))
                sums[2].add(h, dot(low, only_head(gi[:, cols], h), TN))
            dqi, dki, dvi = sums[0].joined(SCALE), sums[1].joined(SCALE), sums[2].joined()
            dq[rows, :] = dqi
            dk[rows, :] = dki
            dv[rows, :] = dvi
            column_sum(2, dqi.astype(f32))
            column_sum(3, dvi.astype(f32))
            return carry

        lax.fori_loop(0, blocks, heads, 0)
        for j in range(3):
            load_w(j, j).wait()
        load_x(0).start()

        def to_sibling(slot):
            return [
                at.copy_sibling(
                    mine3.at[slot, j, 1 - at.core],
                    sib3.at[slot, j],
                    gsent.at[2 + j, slot],
                    ggot.at[2 + j, slot],
                )
                for j in (0, 1)
            ]

        def meet(i):
            slot = lax.rem(i, 2)
            for copy in to_sibling(slot):
                copy.wait()
            for j, (s, c) in enumerate(((sum1, i + TILES), (sum3, i))):
                c = lax.rem(c, s.shape[0])
                s[c] = (mine3[slot, j, at.core].astype(f32) + sib3[slot, j].astype(f32)).astype(bf16)

        def weight_gradients(j, carry):
            @pl.when(j >= 1)
            def _():
                meet(j - 1)
                advance(TILES - 1 + j)

            @pl.when(j < CHUNKS)
            def _():
                slot = lax.rem(j, 2)
                here = [pl.ds(aligned(h * HALF + j * 64, 64), 64) for h in (0, 1)]
                left = jnp.concatenate([h2t[r, :] for r in here], axis=0)
                gq = dot(left, dq[...], NN).astype(bf16)
                gk = dot(left, dk[...], NN).astype(bf16)
                gv = dot(left, dv[...], NN).astype(bf16)
                left = jnp.concatenate([aot[r, :] for r in here], axis=0)
                go = dot(left, h2[...], NN).astype(bf16)
                for h in (0, 1):
                    part = slice(h * 64, h * 64 + 64)
                    mine3[slot, 0, h] = jnp.concatenate([gq[part], gk[part]], axis=0)
                    mine3[slot, 1, h] = jnp.concatenate([gv[part], go[part]], axis=0)
                for copy in to_sibling(slot):
                    copy.start()

            @pl.when(j < blocks)
            def _():
                load_x(j).wait()

                @pl.when(j + 1 < blocks)
                def _():
                    load_x(j + 1).start()

                @pl.when(j >= 2)
                def _():
                    put(j - 2).wait()

                rows = block(j)
                e = dot(dq[rows, :], w[0], NT) + dot(dk[rows, :], w[1], NT)
                e = e + dot(dv[rows, :], w[2], NT)
                x = image[0, lax.rem(j, 2)].astype(f32)
                n, dn = norm_back(x, vec[0:1, :], e)
                staged[lax.rem(j, 2)] = (dh2[rows, :] + dn).astype(bf16)
                put(j).start()
                column_sum(0, e * n)
                column_sum(1, e)

            return carry

        lax.fori_loop(0, CHUNKS + 1, weight_gradients, 0)
        put(blocks - 2).wait()
        put(blocks - 1).wait()

        small[...] = jnp.zeros_like(small)
        small[0:VECTORS, :] = dvec[...]
        for i in range(TILES):
            small[VECTORS + i : VECTORS + i + 1, : 2 * TILE] = dbup[i]
        mine3[1, 1, 0] = jnp.concatenate(
            [small[...].astype(bf16), jnp.zeros((TILE - small.shape[0], WIDTH), bf16)], axis=0
        )
        trade = at.copy_sibling(mine3.at[1, 1, 0], sib3.at[1, 1], gsent.at[3, 1], ggot.at[3, 1])
        trade.start()
        trade.wait()
        sum3[CHUNKS] = (mine3[1, 1, 0].astype(f32) + sib3[1, 1].astype(f32)).astype(bf16)

    flat = pltpu.VMEM((rows_all, WIDTH), bf16)
    pl.run_scoped(
        attention,
        pltpu.VMEM((WIDTH, rows_all), bf16),
        flat,
        flat,
        flat,
        pltpu.VMEM((3, WIDTH, WIDTH), bf16),
        pltpu.VMEM((3, 2, BLOCK, WIDTH), bf16),
        pltpu.VMEM((2, PATCHES, HEADS * PATCHES), bf16),
        pltpu.VMEM((2, BLOCK, WIDTH), f32),
        pltpu.VMEM((2, BLOCK, WIDTH), bf16),
        pltpu.VMEM((2, 2, 2, TILE, WIDTH), bf16),
        pltpu.SemaphoreType.DMA((5,)),
        pltpu.SemaphoreType.DMA((5, 2)),
    )

    def drain(tick, carry):
        advance(tick)
        return carry

    lax.fori_loop(TREE, TREE + 8, drain, 0)


def rest_of_layer(tokens, og, h1, q, k, v, ao, probs, x2, h2, w, wup, wdown, vec, bup):
    rows = h2.shape[0]
    flat = jax.ShapeDtypeStruct((rows, WIDTH), bf16)
    return pl.pallas_call(
        rest_kernel,
        out_shape=(
            flat,
            flat,
            jax.ShapeDtypeStruct((TREE, TILE, WIDTH), bf16),
            jax.ShapeDtypeStruct((TILES, HALF, 2 * TILE), bf16),
            jax.ShapeDtypeStruct((CHUNKS + 1, TILE, WIDTH), bf16),
        ),
        in_specs=[ANY] * 15,
        out_specs=[ANY] * 5,
        scratch_shapes=[
            pltpu.VMEM((rows, WIDTH), bf16),
            pltpu.VMEM((WIDTH, rows), bf16),
            pltpu.VMEM((rows, WIDTH), bf16),
            pltpu.VMEM((rows, WIDTH), f32),
            pltpu.VMEM((2, TILES, 1, TILE), f32),
            pltpu.VMEM((VECTORS, WIDTH), f32),
            pltpu.VMEM((TILES, 1, 2 * TILE), f32),
            pltpu.VMEM((VECTORS, WIDTH), f32),
            pltpu.VMEM((32, WIDTH), f32),
            pltpu.VMEM((2, TILE, WIDTH), bf16),
            pltpu.VMEM((2, HALF, 2 * TILE), bf16),
            pltpu.VMEM((2, 2, TILE, WIDTH), bf16),
            pltpu.VMEM((TILES + 1, TILE, WIDTH), bf16),
            pltpu.VMEM((TILES, HALF, 2 * TILE), bf16),
            pltpu.VMEM((CHUNKS + 1, TILE, WIDTH), bf16),
            pltpu.SemaphoreType.DMA((5,)),
            pltpu.SemaphoreType.DMA((4, 2)),
            pltpu.SemaphoreType.DMA((4, 2)),
        ]
        + tree_scratch(TREE, TILE, WIDTH)
        + plane_scratch(TILES, FIRST, 2 * TILE)
        + plane_scratch(TILES, SECOND, 2 * TILE)
        + plane_scratch(CHUNKS + 1, TILE // 2, WIDTH) * 2,
        compiler_params=pltpu.CompilerParams(
            collective_id=1, has_side_effects=True, vmem_limit_bytes=62 * 2**20
        ),
        name="rest_of_layer",
    )(tokens, og, h1, q, k, v, ao, probs, x2, h2, w, wup, wdown, vec, bup)


def finish_kernel(
    g1_ref, q_ref, k_ref, g2_ref, v_ref, o_ref, d1_ref, d2_ref, dq_ref, dk_ref, dv_ref, do_ref
):
    d1_ref[...] = g1_ref[0].astype(f32)
    parts = []
    for h in (0, 1):
        for i in range(TILES):
            wide = TILE if i < TILES - 1 else FF_HALF - (TILES - 1) * TILE
            parts.append(g2_ref[i, :, h * TILE : h * TILE + wide].astype(f32))
    d2_ref[...] = jnp.concatenate(parts, axis=1)
    for s, d in ((q_ref, dq_ref), (k_ref, dk_ref), (v_ref, dv_ref), (o_ref, do_ref)):
        d[...] = s[0].astype(f32)


def finish(g1, g2, g3):
    steps = HALF // 32
    square = jax.ShapeDtypeStruct((HALF, WIDTH), f32)
    last = TILES - 1

    def quarter(first, offset):
        return pl.BlockSpec((1, 32, WIDTH), lambda i: (first + i // 2, offset + i % 2, 0))

    return pl.pallas_call(
        finish_kernel,
        grid=(steps,),
        out_shape=(
            jax.ShapeDtypeStruct((FF_HALF, WIDTH), f32),
            jax.ShapeDtypeStruct((HALF, FF), f32),
        )
        + (square,) * 4,
        in_specs=[
            pl.BlockSpec((1, TILE, WIDTH), lambda i: (jnp.minimum(i, last), 0, 0)),
            quarter(TILES, 0),
            quarter(TILES, 2),
            pl.BlockSpec((TILES, 32, 2 * TILE), lambda i: (0, i, 0)),
            quarter(0, 0),
            quarter(0, 2),
        ],
        out_specs=[
            pl.BlockSpec((TILE, WIDTH), lambda i: (jnp.minimum(i, last), 0)),
            pl.BlockSpec((32, FF), lambda i: (i, 0)),
        ]
        + [pl.BlockSpec((32, WIDTH), lambda i: (i, 0))] * 4,
        compiler_params=pltpu.CompilerParams(vmem_limit_bytes=48 * 2**20),
        name="finish",
    )(g1, g1, g1, g2, g3, g3)


def fast_shards(
    tokens,
    out_grad,
    ln1_gain,
    ln1_bias,
    q_weight,
    q_bias,
    k_weight,
    v_weight,
    v_bias,
    o_weight,
    o_bias,
    ln2_gain,
    ln2_bias,
    up_weight,
    up_bias,
    down_weight,
    down_bias,
):
    small = [ln1_gain, ln1_bias, q_bias, v_bias, o_bias, ln2_gain, ln2_bias, down_bias]
    pack = jnp.pad(jnp.stack(small).astype(f32), ((0, 0), (0, LANES - HALF)))
    gap = TILES * TILE - FF_HALF
    bup = jnp.pad(up_bias.astype(f32), (0, gap)).reshape(TILES, 1, TILE)
    saved = forward(
        tokens, q_weight, k_weight, v_weight, o_weight, up_weight, down_weight, pack, bup
    )
    output, d_input, g1, g2, g3 = rest_of_layer(tokens, out_grad, *saved)
    d_down, d_up, d_q, d_k, d_v, d_o = finish(g1, g2, g3)
    core = lax.axis_index("group")
    vectors = lax.dynamic_slice(g3[CHUNKS, :VECTORS], (0, core * HALF), (VECTORS, HALF)).astype(f32)
    d_bup = lax.dynamic_slice(
        g3[CHUNKS, VECTORS : VECTORS + TILES], (0, core * TILE), (TILES, TILE)
    )
    d_bup = d_bup.reshape(TILES * TILE)[:FF_HALF].astype(f32)
    return (
        output,
        d_input,
        vectors[0],
        vectors[1],
        d_q,
        vectors[2],
        d_k,
        d_v,
        vectors[3],
        d_o,
        vectors[4],
        vectors[5],
        vectors[6],
        d_up,
        d_bup,
        d_down,
        vectors[7],
    )


def solution(mesh):
    placed = (
        P(("group", "replica"), None),
        P(("group", "replica"), None),
        P("group"),
        P("group"),
        P("group", None),
        P("group"),
        P("group", None),
        P("group", None),
        P("group"),
        P("group", None),
        P("group"),
        P("group"),
        P("group"),
        P("group", None),
        P("group"),
        P("group", None),
        P("group"),
    )
    fast = mesh.shape["group"] == 2 and mesh.shape["replica"] == 16
    return jax.shard_map(
        fast_shards if fast else shards,
        mesh=mesh,
        in_specs=placed,
        out_specs=(
            P(("group", "replica"), None),
            P(("group", "replica"), None),
            P("group"),
            P("group"),
            P("group", None),
            P("group"),
            P("group", None),
            P("group", None),
            P("group"),
            P("group", None),
            P("group"),
            P("group"),
            P("group"),
            P("group", None),
            P("group"),
            P("group", None),
            P("group"),
        ),
        check_vma=False,
    )
```

```python
import functools

import jax
import jax.numpy as jnp
from jax import lax
from jax.experimental import pallas as pl
from jax.experimental.pallas import tpu as pltpu
from jax.sharding import PartitionSpec as P

HEADS = 16
PATCHES = 128


def layer_norm(values, gain, shift):
    center = values - jnp.mean(values, axis=-1, keepdims=True)
    spread = jnp.mean(center * center, axis=-1, keepdims=True)
    return center * lax.rsqrt(spread + 1e-06) * gain + shift


def gelu_tanh(values):
    return jax.nn.gelu(values, approximate=True)


def split_heads(rows):
    return rows.reshape(-1, PATCHES, HEADS, rows.shape[-1] // HEADS)


def head_logits(query, key_rows):
    factor = (query.shape[-1] // HEADS) ** (-0.5)
    query_h = split_heads(query)
    key_h = split_heads(key_rows)
    logits = (
        jnp.einsum("isha,itha->ihst", query_h, key_h, preferred_element_type=jnp.float32) * factor
    )
    return (logits, query_h, key_h, factor)


def attend(query, key_rows, value_rows):
    logits, query_h, key_h, factor = head_logits(query, key_rows)
    peak = jnp.max(logits, axis=-1, keepdims=True)
    log_total = peak + jnp.log(jnp.sum(jnp.exp(logits - peak), axis=-1, keepdims=True))
    weights_low = jnp.exp(logits - log_total).astype(jnp.bfloat16)
    mixed = jnp.einsum(
        "ihst,itha->isha", weights_low, split_heads(value_rows), preferred_element_type=jnp.float32
    )
    return (mixed.reshape(query.shape), log_total)


def attend_back(query, key_rows, value_rows, log_total, d_mixed):
    logits, query_h, key_h, factor = head_logits(query, key_rows)
    weights = jnp.exp(logits - log_total)
    weights_low = weights.astype(jnp.bfloat16)
    value_h = split_heads(value_rows)
    d_mix_h = split_heads(d_mixed)
    d_weights = jnp.einsum("isha,itha->ihst", d_mix_h, value_h, preferred_element_type=jnp.float32)
    d_logits = weights * (d_weights - jnp.sum(weights * d_weights, axis=-1, keepdims=True))
    d_low = d_logits.astype(jnp.bfloat16)
    d_query = (
        jnp.einsum("ihst,itha->isha", d_low, key_h, preferred_element_type=jnp.float32) * factor
    ).astype(jnp.bfloat16)
    d_key = (
        jnp.einsum("ihst,isha->itha", d_low, query_h, preferred_element_type=jnp.float32) * factor
    ).astype(jnp.bfloat16)
    d_value = jnp.einsum(
        "ihst,isha->itha", weights_low, d_mix_h, preferred_element_type=jnp.float32
    ).astype(jnp.bfloat16)
    return (d_query.reshape(query.shape), d_key.reshape(query.shape), d_value.reshape(query.shape))


def outer_rows(left, right):
    return jnp.einsum("ra,rb->ab", left, right, preferred_element_type=jnp.float32)


def back_rows(grads, weight):
    return jnp.einsum("rb,ab->ra", grads, weight, preferred_element_type=jnp.float32)


def column_sums(grads):
    return jnp.sum(grads.astype(jnp.float32), axis=0)


def shards(
    tokens,
    out_grad,
    ln1_gain,
    ln1_bias,
    q_weight,
    q_bias,
    k_weight,
    v_weight,
    v_bias,
    o_weight,
    o_bias,
    ln2_gain,
    ln2_bias,
    up_weight,
    up_bias,
    down_weight,
    down_bias,
):
    attn_full = tuple(lax.all_gather(v, "group", axis=0, tiled=True) for v in (
        ln1_gain, ln1_bias, q_weight, q_bias, k_weight, v_weight, v_bias, o_weight, o_bias,
    ))
    gain_one, shift_one, wq_full, bq_full, wk_full, wv_full, bv_full, wo_full, bo_full = attn_full
    input_f = tokens.astype(jnp.float32)
    gain_one_f = gain_one.astype(jnp.float32)
    shift_one_f = shift_one.astype(jnp.float32)
    normed1 = layer_norm(input_f, gain_one_f, shift_one_f).astype(jnp.bfloat16)
    query = (
        jnp.dot(normed1, wq_full, preferred_element_type=jnp.float32) + bq_full.astype(jnp.float32)
    ).astype(jnp.bfloat16)
    key_rows = jnp.dot(normed1, wk_full, preferred_element_type=jnp.float32).astype(jnp.bfloat16)
    value_rows = (
        jnp.dot(normed1, wv_full, preferred_element_type=jnp.float32) + bv_full.astype(jnp.float32)
    ).astype(jnp.bfloat16)
    mixed, log_total = attend(query, key_rows, value_rows)
    attn_in = mixed.astype(jnp.bfloat16)
    residual = (
        input_f
        + jnp.dot(attn_in, wo_full, preferred_element_type=jnp.float32)
        + bo_full.astype(jnp.float32)
    )
    mlp_full = tuple(lax.all_gather(v, "group", axis=0, tiled=True) for v in (
        ln2_gain, ln2_bias, up_weight, up_bias, down_weight, down_bias,
    ))
    gain_two, shift_two, wup_full, bup_full, wdown_full, bdown_full = mlp_full
    gain_two_f = gain_two.astype(jnp.float32)
    shift_two_f = shift_two.astype(jnp.float32)
    normed2 = layer_norm(residual, gain_two_f, shift_two_f).astype(jnp.bfloat16)
    pre_act = jnp.dot(normed2, wup_full, preferred_element_type=jnp.float32) + bup_full.astype(
        jnp.float32
    )
    hidden = gelu_tanh(pre_act).astype(jnp.bfloat16)
    output = (
        residual
        + jnp.dot(hidden, wdown_full, preferred_element_type=jnp.float32)
        + bdown_full.astype(jnp.float32)
    )
    mlp_back = tuple(lax.all_gather(v, "group", axis=0, tiled=True) for v in (
        ln2_gain, ln2_bias, up_weight, up_bias, down_weight, down_bias,
    ))
    wup_back = mlp_back[2]
    wdown_back = mlp_back[4]
    grad_out = out_grad.astype(jnp.float32)
    d_wdown = outer_rows(hidden, out_grad)
    d_bdown = column_sums(out_grad)
    d_hidden = back_rows(out_grad, wdown_back)
    unused_act, gelu_back = jax.vjp(gelu_tanh, pre_act)
    d_pre = gelu_back(d_hidden)[0].astype(jnp.bfloat16)
    d_wup = outer_rows(normed2, d_pre)
    d_bup = column_sums(d_pre)
    d_normed2 = back_rows(d_pre, wup_back)
    unused_two, norm_back_two = jax.vjp(layer_norm, residual, gain_two_f, shift_two_f)
    d_res_norm, d_gain_two, d_shift_two = norm_back_two(d_normed2)
    d_residual = grad_out + d_res_norm
    mlp_grads = tuple(
        lax.psum_scatter(v.astype(jnp.bfloat16), "group", scatter_dimension=0, tiled=True).astype(jnp.float32)
        for v in (d_gain_two, d_shift_two, d_wup, d_bup, d_wdown, d_bdown)
    )
    attn_back = tuple(lax.all_gather(v, "group", axis=0, tiled=True) for v in (
        ln1_gain, ln1_bias, q_weight, q_bias, k_weight, v_weight, v_bias, o_weight, o_bias,
    ))
    wq_back = attn_back[2]
    wk_back = attn_back[4]
    wv_back = attn_back[5]
    wo_back = attn_back[7]
    d_attn = d_residual.astype(jnp.bfloat16)
    d_wout = outer_rows(attn_in, d_attn)
    d_bout = column_sums(d_attn)
    d_mixed = back_rows(d_attn, wo_back).astype(jnp.bfloat16)
    d_query, d_key, d_value = attend_back(query, key_rows, value_rows, log_total, d_mixed)
    d_wquery = outer_rows(normed1, d_query)
    d_bquery = column_sums(d_query)
    d_wkey = outer_rows(normed1, d_key)
    d_wvalue = outer_rows(normed1, d_value)
    d_bvalue = column_sums(d_value)
    d_normed1 = (
        back_rows(d_query, wq_back) + back_rows(d_key, wk_back) + back_rows(d_value, wv_back)
    )
    unused_one, norm_back_one = jax.vjp(layer_norm, input_f, gain_one_f, shift_one_f)
    d_in_norm, d_gain_one, d_shift_one = norm_back_one(d_normed1)
    d_input = (d_residual + d_in_norm).astype(jnp.bfloat16)
    attn_grads = tuple(
        lax.psum_scatter(v.astype(jnp.bfloat16), "group", scatter_dimension=0, tiled=True).astype(jnp.float32)
        for v in (d_gain_one, d_shift_one, d_wquery, d_bquery, d_wkey, d_wvalue, d_bvalue, d_wout, d_bout)
    )
    summed = tuple(
        lax.psum(v.astype(jnp.bfloat16), "replica").astype(jnp.float32) for v in attn_grads + mlp_grads
    )
    attn_grads = tuple(summed[:9])
    mlp_grads = tuple(summed[9:])
    return (output.astype(jnp.bfloat16), d_input) + tuple(attn_grads) + tuple(mlp_grads)


MESH = pl.DeviceIdType.MESH
bf16 = jnp.bfloat16
f32 = jnp.float32
ANY = pl.BlockSpec(memory_space=pl.ANY)
WIDTH = 1152
HALF = 576
FF = 4304
FF_HALF = 2152
TILES = 17
TILE = 128
FF_PAD = 2 * TILES * TILE
FIRST = 320
SECOND = 256


class Place:
    def __init__(self):
        self.core = lax.axis_index("group")
        chip = lax.axis_index("replica")
        self.chip = chip
        self.x = lax.rem(chip, 2)
        self.y = lax.rem(chip // 2, 2)
        self.z = chip // 4
        self.x_pair = chip + 1 - 2 * self.x
        self.y_pair = chip + 2 - 4 * self.y
        self.z_pair = chip + 4 - 8 * lax.rem(self.z, 2)
        self.inner = (self.z == 1) | (self.z == 2)
        self.outer = jnp.logical_not(self.inner)
        self.mid_pair = jnp.where(self.inner, chip + 12 - 8 * self.z, chip)
        self.z_half = lax.rem(self.z // 2, 2)

    def barrier(self):
        sem = pltpu.get_barrier_semaphore()

        def greet(core, chip):
            pl.semaphore_signal(sem, inc=1, device_id=(core, chip), device_id_type=MESH)

        greet(1 - self.core, self.chip)
        greet(self.core, self.x_pair)
        greet(self.core, self.y_pair)
        greet(self.core, self.z_pair)

        @pl.when(self.inner)
        def _():
            greet(self.core, self.mid_pair)
            pl.semaphore_wait(sem, 5)

        @pl.when(self.outer)
        def _():
            pl.semaphore_wait(sem, 4)

    def copy(self, source, target, sent, got, chip):
        return pltpu.make_async_remote_copy(
            source, target, sent, got, device_id=(self.core, chip), device_id_type=MESH
        )

    def copy_sibling(self, source, target, sent, got):
        return pltpu.make_async_remote_copy(
            source, target, sent, got, device_id=(1 - self.core, self.chip), device_id_type=MESH
        )


def aligned(value, unit):
    return pl.multiple_of(value, unit)


def landing(slots, chunk):
    return slots.at[lax.rem(chunk, slots.shape[0])]


def add_rows(total, landed, chunk, start, count):
    rows = pl.ds(start, count)
    slot = lax.rem(chunk, total.shape[0])
    total[slot, rows, :] = total[slot, rows, :] + landed[...]


class TreeFirst:
    steps = 9
    after = 0

    def __init__(self, place, total, final, spot, landing, sent, got, kept):
        self.at = place
        self.total = total
        self.final = final
        self.spot = spot
        self.kept = kept
        self.land = landing
        self.sent = sent
        self.got = got
        n = total.shape[1]
        self.n = n
        p = place
        self.own = [
            (0, n),
            (aligned(p.z_half * (n // 2), n // 2), n // 2),
        ]
        self.other = [None, (aligned((1 - p.z_half) * (n // 2), n // 2), n // 2)]
        for bit, part in ((p.y, n // 4), (p.x, n // 8)):
            base = self.own[-1][0]
            self.own.append((aligned(base + bit * part, part), part))
            self.other.append((aligned(base + (1 - bit) * part, part), part))
        self.peer = [p.z_pair, p.mid_pair, p.y_pair, p.x_pair]

    def flags(self, k, chunk):
        slot = lax.rem(chunk + self.after, self.sent.shape[1])
        return self.sent.at[k, slot], self.got.at[k, slot]

    def rows(self, chunk, span):
        return landing(self.total, chunk).at[pl.ds(span[0], span[1]), :]

    def ends(self, chunk, span):
        return self.final.at[self.spot(chunk), pl.ds(span[0], span[1]), :]

    def send(self, k, chunk):
        sent, got = self.flags(k, chunk)
        if k < 4:
            span = self.own[0] if k == 0 else self.other[k]
            return self.at.copy(
                self.rows(chunk, span), landing(self.land[k], chunk), sent, got, self.peer[k]
            )
        level = 7 - k
        target = self.ends(chunk, self.own[level])
        source = self.rows(chunk, self.own[3]) if k == 4 else target
        return self.at.copy(source, target, sent, got, self.peer[level])

    def keep(self, chunk):
        return pltpu.make_async_copy(
            self.rows(chunk, self.own[3]), self.ends(chunk, self.own[3]), landing(self.kept, chunk)
        )

    def arrive(self, k, chunk):
        if k < 4:
            landed = landing(self.land[k], chunk)
        else:
            level = 7 - k
            landed = self.ends(chunk, self.own[0] if level == 0 else self.other[level])
        self.at.copy(landed, landed, *self.flags(k, chunk), self.at.z_pair).wait_recv()

    def step(self, k, chunk):
        at = self.at
        if k == 0:

            @pl.when(at.outer)
            def _():
                self.send(0, chunk).start()

        elif k <= 7:

            @pl.when(at.inner)
            def _():
                self.arrive(k - 1, chunk)
                if k <= 4:
                    add_rows(self.total, landing(self.land[k - 1], chunk), chunk, *self.own[k - 1])
                if k == 4:
                    self.keep(chunk).start()
                if k == 5:
                    self.keep(chunk).wait()
                self.send(k, chunk).start()

        else:

            @pl.when(at.inner)
            def _():
                for j in range(1, 8):
                    self.send(j, chunk).wait_send()

            @pl.when(at.outer)
            def _():
                self.arrive(7, chunk)
                self.send(0, chunk).wait_send()


class PlaneFirst:
    steps = 8

    def __init__(
        self, place, total, final, spot, base, n, x_first, landing, sent, got, kept, after=0
    ):
        self.at = place
        self.after = after
        self.total = total
        self.final = final
        self.spot = spot
        self.kept = kept
        self.land = landing
        self.sent = sent
        self.got = got
        p = place
        if x_first:
            one, two = (p.x, p.x_pair), (p.y, p.y_pair)
        else:
            one, two = (p.y, p.y_pair), (p.x, p.x_pair)
        self.peer_one, self.peer_two = one[1], two[1]
        start = aligned(base + one[0] * (n // 2), 16)
        self.half = (start, n // 2)
        self.half_other = (aligned(base + (1 - one[0]) * (n // 2), 16), n // 2)
        self.quarter = (aligned(start + two[0] * (n // 4), 16), n // 4)
        self.quarter_other = (aligned(start + (1 - two[0]) * (n // 4), 16), n // 4)

    def flags(self, k, chunk):
        slot = lax.rem(chunk + self.after, self.sent.shape[1])
        return self.sent.at[k, slot], self.got.at[k, slot]

    def rows(self, chunk, span):
        return landing(self.total, chunk).at[pl.ds(span[0], span[1]), :]

    def ends(self, chunk, span):
        return self.final.at[self.spot(chunk), pl.ds(span[0], span[1]), :]

    def keep(self, chunk):
        return pltpu.make_async_copy(
            self.rows(chunk, self.quarter), self.ends(chunk, self.quarter), landing(self.kept, chunk + self.after)
        )

    def send(self, k, chunk):
        at = self.at
        quarter = self.rows(chunk, self.quarter)
        quarter_end = self.ends(chunk, self.quarter)
        half_end = self.ends(chunk, self.half)
        source, target, peer = (
            (self.rows(chunk, self.half_other), landing(self.land[0], chunk), self.peer_one),
            (self.rows(chunk, self.quarter_other), landing(self.land[1], chunk), self.peer_two),
            (quarter, landing(self.land[2], chunk), at.z_pair),
            (quarter, landing(self.land[3], chunk), at.mid_pair),
            (quarter, quarter_end, at.z_pair),
            (quarter_end, quarter_end, self.peer_two),
            (half_end, half_end, self.peer_one),
        )[k]
        return at.copy(source, target, *self.flags(k, chunk), peer)

    def arrive(self, k, chunk):
        if k < 4:
            landed = landing(self.land[k], chunk)
        else:
            landed = self.ends(
                chunk, (self.quarter, self.quarter_other, self.half_other)[k - 4]
            )
        self.at.copy(landed, landed, *self.flags(k, chunk), self.at.z_pair).wait_recv()

    def step(self, k, chunk):
        at = self.at
        if k == 0:
            self.send(0, chunk).start()
        elif k == 1:
            self.arrive(0, chunk)
            add_rows(self.total, landing(self.land[0], chunk), chunk, *self.half)
            self.send(1, chunk).start()
        elif k == 2:
            self.arrive(1, chunk)
            add_rows(self.total, landing(self.land[1], chunk), chunk, *self.quarter)

            @pl.when(at.outer)
            def _():
                self.send(2, chunk).start()

        elif k == 3:

            @pl.when(at.inner)
            def _():
                self.arrive(2, chunk)
                add_rows(self.total, landing(self.land[2], chunk), chunk, *self.quarter)
                self.send(3, chunk).start()

        elif k == 4:

            @pl.when(at.inner)
            def _():
                self.arrive(3, chunk)
                self.send(3, chunk).wait_send()
                add_rows(self.total, landing(self.land[3], chunk), chunk, *self.quarter)
                self.send(4, chunk).start()
                self.keep(chunk).start()

        elif k == 5:

            @pl.when(at.inner)
            def _():
                self.keep(chunk).wait()

            @pl.when(at.outer)
            def _():
                self.arrive(4, chunk)

            self.send(5, chunk).start()
        elif k == 6:
            self.arrive(5, chunk)
            self.send(6, chunk).start()
        else:
            self.arrive(6, chunk)
            for j in (0, 1, 5, 6):
                self.send(j, chunk).wait_send()

            @pl.when(at.inner)
            def _():
                self.send(4, chunk).wait_send()

            @pl.when(at.outer)
            def _():
                self.send(2, chunk).wait_send()


def tree_scratch(n, width):
    return [
        pltpu.VMEM((slots, n // part, width), bf16)
        for slots, part in ((10, 1), (3, 2), (3, 4), (3, 8))
    ] + flag_scratch(8, 10)


def plane_scratch(n, width):
    return [
        pltpu.VMEM((slots, n // part, width), bf16)
        for slots, part in ((3, 2), (3, 4), (4, 4), (3, 4))
    ]


def flag_scratch(copies, slots):
    return [
        pltpu.SemaphoreType.DMA((copies, slots)),
        pltpu.SemaphoreType.DMA((copies, slots)),
        pltpu.SemaphoreType.DMA((slots,)),
    ]


def dot(left, right, contract):
    return lax.dot_general(left, right, (contract, ((), ())), preferred_element_type=f32)


NN = ((1,), (0,))
NT = ((1,), (1,))
TN = ((0,), (0,))


def gelu_and_slope(u):
    c = 0.7978845608028654
    square = u * u
    t = jnp.tanh(c * u * (1.0 + 0.044715 * square))
    half = 0.5 * (1.0 + t)
    slope = half + 0.5 * u * (1.0 - t * t) * (c * (1.0 + 3 * 0.044715 * square))
    return u * half, slope


VECTORS = 8
LANES = 640
SCALE = 72**-0.5
HEAD = 72


def head_window(h):
    return slice(h * HEAD // 128 * 128, ((h + 1) * HEAD + 127) // 128 * 128)


def only_head(rows, h):
    lane = lax.broadcasted_iota(jnp.int32, rows.shape, 1) + head_window(h).start
    return jnp.where((lane >= h * HEAD) & (lane < (h + 1) * HEAD), rows, jnp.zeros_like(rows))


class Lanes:
    def __init__(self):
        self.tiles = [None] * (WIDTH // 128)

    def add(self, h, window):
        first = head_window(h).start // 128
        for j in range(window.shape[1] // 128):
            part = window[:, j * 128 : (j + 1) * 128]
            old = self.tiles[first + j]
            self.tiles[first + j] = part if old is None else old + part

    def joined(self, scale=None):
        tiles = self.tiles if scale is None else [t * scale for t in self.tiles]
        return jnp.concatenate([t.astype(bf16) for t in tiles], axis=1)


def normalise(rows, gain, shift):
    center = rows - jnp.mean(rows, axis=-1, keepdims=True)
    spread = jnp.mean(center * center, axis=-1, keepdims=True)
    return center * lax.rsqrt(spread + 1e-06) * gain + shift


def forward_kernel(
    tokens_ref,
    wq_ref,
    wk_ref,
    wv_ref,
    wo_ref,
    up_ref,
    down_ref,
    pack_ref,
    bup_ref,
    h1_ref,
    q_ref,
    k_ref,
    v_ref,
    ao_ref,
    probs_ref,
    x2_ref,
    h2_ref,
    w_ref,
    wup_ref,
    wdown_ref,
    vec_ref,
    bups_ref,
    x,
    h1,
    q,
    k,
    v,
    ao,
    probs,
    x2,
    h2,
    w,
    up,
    up_wide,
    down,
    zeros,
    pack,
    vec,
    local,
    wsem,
    psem,
    sent,
    got,
    bsem,
):
    at = Place()
    core = at.core
    own = pl.ds(aligned(core * HALF, HALF), HALF)
    ff_own = pl.ds(aligned(core * TILES * TILE, TILE), FF_HALF)
    shards = (wq_ref, wk_ref, wv_ref, wo_ref)
    load_x = pltpu.make_async_copy(tokens_ref, x, local.at[0])
    load_x.start()
    load_w = [pltpu.make_async_copy(s, w.at[j, own, :], local.at[1 + j]) for j, s in enumerate(shards)]
    load_pack = pltpu.make_async_copy(pack_ref, pack.at[core], local.at[5])
    load_bup = pltpu.make_async_copy(bup_ref, bups_ref.at[core], local.at[6])
    load_up = pltpu.make_async_copy(up_ref, up, local.at[7])
    load_down = pltpu.make_async_copy(down_ref, down, local.at[8])
    keep_down = pltpu.make_async_copy(down, wdown_ref.at[ff_own, :], wsem.at[4])
    for load in (load_pack, *load_w, load_bup, load_up, load_down):
        load.start()
    zeros[...] = jnp.zeros_like(zeros)
    gap = TILES * TILE - FF_HALF
    blanks = [
        pltpu.make_async_copy(
            zeros, wdown_ref.at[pl.ds(h * TILES * TILE + FF_HALF, gap), :], local.at[9 + h]
        )
        for h in (0, 1)
    ]
    for blank in blanks:
        blank.start()

    bar = pltpu.get_barrier_semaphore()
    pl.semaphore_signal(bar, inc=1, device_id=(1 - core, at.chip), device_id_type=MESH)
    pl.semaphore_wait(bar, 1)

    def share(j, source, target):
        return at.copy_sibling(source, target, sent.at[j], got.at[j])

    give_w = [share(j, s, w.at[j, own, :]) for j, s in enumerate(shards)]
    give_pack = share(4, pack_ref, pack.at[core])
    give_bup = share(5, bup_ref, bups_ref.at[core])
    give_down = share(6, down_ref, wdown_ref.at[ff_own, :])
    give_up = share(7, up_wide, wup_ref.at[own, :])
    keep_up = pltpu.make_async_copy(up_wide, wup_ref.at[own, :], local.at[11])
    give_pack.start()
    for give in give_w:
        give.start()
    give_bup.start()
    give_down.start()

    load_pack.wait()
    give_pack.wait()
    vec[...] = jnp.concatenate([pack[0, :, :HALF], pack[1, :, :HALF]], axis=1)
    load_x.wait()
    rows_of = [pl.ds(b * 512, 512) for b in range(2)]

    def first_norm(b, carry):
        rows = pl.ds(aligned(b * 128, 128), 128)
        h1[rows, :] = normalise(x[rows, :].astype(f32), vec[0:1, :], vec[1:2, :]).astype(bf16)
        return carry

    lax.fori_loop(0, 8, first_norm, 0)
    keep = [pltpu.make_async_copy(h1, h1_ref, local.at[0])]
    keep[0].start()

    def project(j, target, bias):
        load_w[j].wait()
        give_w[j].wait()
        for rows in rows_of:
            y = dot(h1[rows, :], w[j], NN)
            if bias is not None:
                y = y + vec[bias : bias + 1, :]
            target[rows, :] = y.astype(bf16)

    project(0, q, 2)
    project(1, k, None)
    project(2, v, 3)
    for j, (s, d) in enumerate(((q, q_ref), (k, k_ref), (v, v_ref))):
        keep.append(pltpu.make_async_copy(s, d, local.at[12 + j]))
        keep[-1].start()

    load_down.wait()
    keep_down.start()
    load_up.wait()

    def widen(b, carry):
        rows = pl.ds(aligned(b * 64, 64), 64)
        row = up[rows, :]
        none = jnp.zeros((64, gap), bf16)
        up_wide[rows, :] = jnp.concatenate([row[:, :FF_HALF], none, row[:, FF_HALF:], none], axis=1)
        return carry

    lax.fori_loop(0, HALF // 64, widen, 0)
    keep_up.start()
    give_up.start()

    def keep_probs(i):
        slot = lax.rem(i, 2)
        return pltpu.make_async_copy(probs.at[slot], probs_ref.at[i], psem.at[slot])

    def attention(i, carry):
        rows = pl.ds(aligned(i * 128, 128), 128)
        slot = lax.rem(i, 2)

        @pl.when(i >= 2)
        def _():
            keep_probs(i - 2).wait()

        qi, ki, vi = q[rows, :], k[rows, :], v[rows, :]
        mixed = Lanes()
        held = []
        for h in range(HEADS):
            cols = head_window(h)
            logits = dot(qi[:, cols], only_head(ki[:, cols], h), NT) * SCALE
            e = jnp.exp(logits - jnp.max(logits, axis=-1, keepdims=True))
            p = (e / jnp.sum(e, axis=-1, keepdims=True)).astype(bf16)
            held.append(p)
            mixed.add(h, dot(p, only_head(vi[:, cols], h), NN))
        ao[rows, :] = mixed.joined()
        probs[slot] = jnp.concatenate(held, axis=1)
        keep_probs(i).start()
        return carry

    lax.fori_loop(0, 8, attention, 0)
    keep_ao = pltpu.make_async_copy(ao, ao_ref, local.at[15])
    keep_ao.start()

    load_w[3].wait()
    give_w[3].wait()
    keep_w = pltpu.make_async_copy(w, w_ref, wsem.at[0])
    keep_w.start()
    keep_vec = pltpu.make_async_copy(vec, vec_ref, wsem.at[1])
    keep_vec.start()
    for rows in rows_of:
        x2[rows, :] = x[rows, :].astype(f32) + dot(ao[rows, :], w[3], NN) + vec[4:5, :]

    def second_norm(b, carry):
        rows = pl.ds(aligned(b * 128, 128), 128)
        h2[rows, :] = normalise(x2[rows, :], vec[5:6, :], vec[6:7, :]).astype(bf16)
        return carry

    lax.fori_loop(0, 8, second_norm, 0)
    keep_x2 = pltpu.make_async_copy(x2, x2_ref, wsem.at[2])
    keep_h2 = pltpu.make_async_copy(h2, h2_ref, wsem.at[3])
    for copy in (keep_x2, keep_h2):
        copy.start()
    for copy in (
        *keep,
        keep_probs(6),
        keep_probs(7),
        keep_ao,
        keep_w,
        keep_vec,
        load_bup,
        keep_down,
        *blanks,
        keep_up,
        keep_x2,
        keep_h2,
    ):
        copy.wait()
    for give in (give_bup, give_down, give_up):
        give.wait()


def forward(tokens, wq, wk, wv, wo, up, down, pack, bup):
    rows = tokens.shape[0]
    images = rows // PATCHES
    flat = jax.ShapeDtypeStruct((rows, WIDTH), bf16)
    return pl.pallas_call(
        forward_kernel,
        out_shape=(
            flat,
            flat,
            flat,
            flat,
            flat,
            jax.ShapeDtypeStruct((images, PATCHES, HEADS * PATCHES), bf16),
            jax.ShapeDtypeStruct((rows, WIDTH), f32),
            flat,
            jax.ShapeDtypeStruct((4, WIDTH, WIDTH), bf16),
            jax.ShapeDtypeStruct((WIDTH, FF_PAD), bf16),
            jax.ShapeDtypeStruct((FF_PAD, WIDTH), bf16),
            jax.ShapeDtypeStruct((VECTORS, WIDTH), f32),
            jax.ShapeDtypeStruct((2, TILES, 1, TILE), f32),
        ),
        in_specs=[ANY] * 9,
        out_specs=[ANY] * 13,
        scratch_shapes=[pltpu.VMEM((rows, WIDTH), bf16)] * 6
        + [
            pltpu.VMEM((2, PATCHES, HEADS * PATCHES), bf16),
            pltpu.VMEM((rows, WIDTH), f32),
            pltpu.VMEM((rows, WIDTH), bf16),
            pltpu.VMEM((4, WIDTH, WIDTH), bf16),
            pltpu.VMEM((HALF, FF), bf16),
            pltpu.VMEM((HALF, FF_PAD), bf16),
            pltpu.VMEM((FF_HALF, WIDTH), bf16),
            pltpu.VMEM((TILES * TILE - FF_HALF, WIDTH), bf16),
            pltpu.VMEM((2, VECTORS, LANES), f32),
            pltpu.VMEM((VECTORS, WIDTH), f32),
            pltpu.SemaphoreType.DMA((16,)),
            pltpu.SemaphoreType.DMA((5,)),
            pltpu.SemaphoreType.DMA((2,)),
            pltpu.SemaphoreType.DMA((8,)),
            pltpu.SemaphoreType.DMA((8,)),
            pltpu.SemaphoreType.DMA((1,)),
        ],
        compiler_params=pltpu.CompilerParams(
            collective_id=3, has_side_effects=True, vmem_limit_bytes=62 * 2**20
        ),
        name="forward",
    )(tokens, wq, wk, wv, wo, up, down, pack, bup)


CHUNKS = 9
TREE = TILES + CHUNKS
SMALL = TILES + 2 * CHUNKS + 1
BLOCK = 128
FF_TICKS = 15
NORM_TICK = 4
VALUE_TICK = 3


def rest_kernel(
    tokens_ref,
    og_ref,
    h1_ref,
    q_ref,
    k_ref,
    v_ref,
    ao_ref,
    probs_ref,
    x2_ref,
    h2_ref,
    w_ref,
    wup_ref,
    wdown_ref,
    vec_ref,
    bup_ref,
    out_ref,
    din_ref,
    g1_ref,
    g2_ref,
    h2,
    h2t,
    og,
    dh2,
    bup,
    vec,
    dbup,
    dvec,
    small,
    sib1,
    sib2,
    sib3,
    sum1,
    sum2,
    sum3,
    local,
    gsent,
    ggot,
    *comm,
):
    at = Place()
    rows_all = h2.shape[0]
    blocks = rows_all // BLOCK
    flags = comm[7:10], comm[10:13]
    planes = [comm[j : j + 4] for j in range(13, 29, 4)]

    def tree_spot(chunk):
        late = chunk - TILES
        value_or_query = jnp.where(late < 5, 2 * late, CHUNKS + 2 * late - 9)
        return jnp.where(chunk < TILES, chunk, TILES + value_or_query)

    def late_spot(chunk):
        return TILES + jnp.where(chunk < 4, 2 * chunk + 1, CHUNKS + 2 * chunk - 8)

    tree = TreeFirst(at, sum1, g1_ref, tree_spot, comm[:4], *comm[4:7])
    early = [
        PlaneFirst(at, sum2, g2_ref, lambda c: c, base, n, j == 0, planes[j], *flags[j])
        for j, base, n in ((0, 0, FIRST), (1, FIRST, SECOND))
    ]
    late = [
        PlaneFirst(
            at, sum3, g1_ref, late_spot, base, TILE // 2, j == 0, planes[2 + j], *flags[j], TILES
        )
        for j, base in ((0, 0), (1, TILE // 2))
    ]

    def advance(tick):
        for k in reversed(range(TreeFirst.steps)):
            chunk = tick - k

            @pl.when((chunk >= 0) & (chunk < TREE))
            def _():
                tree.step(k, chunk)

            if k < PlaneFirst.steps:

                @pl.when((chunk >= 0) & (chunk < TILES))
                def _():
                    for part in early:
                        part.step(k, chunk)

                @pl.when((chunk >= TILES) & (chunk <= TREE))
                def _():
                    for part in late:
                        part.step(k, chunk - TILES)

    def block(b):
        return pl.ds(aligned(b * BLOCK, BLOCK), BLOCK)

    loads = [
        pltpu.make_async_copy(s, d, local.at[j])
        for j, (s, d) in enumerate(
            ((h2_ref, h2), (og_ref, og), (bup_ref, bup), (vec_ref, vec))
        )
    ]
    for load in loads:
        load.start()
    dvec[...] = jnp.zeros_like(dvec)

    def feed_forward(out, staged, wu, wd, mine1, mine2, wsem):
        load_x2 = pltpu.make_async_copy(x2_ref, out, local.at[4])
        load_x2.start()

        def weights(i, slot):
            cols = [pl.ds(aligned(h * TILES * TILE + i * TILE, TILE), TILE) for h in (0, 1)]
            parts = []
            for h in (0, 1):
                here = pl.ds(h * TILE, TILE)
                parts.append(
                    pltpu.make_async_copy(
                        wup_ref.at[:, cols[h]], wu.at[slot, :, here], wsem.at[h, slot]
                    )
                )
                parts.append(
                    pltpu.make_async_copy(
                        wdown_ref.at[cols[h], :], wd.at[slot, here, :], wsem.at[2 + h, slot]
                    )
                )
            return parts

        for part in weights(0, 0):
            part.start()
        at.barrier()
        for load in loads:
            load.wait()
        load_x2.wait()
        for b in range(blocks):
            rows = pl.ds(b * BLOCK, BLOCK)
            h2t[:, rows] = h2[rows, :].T
        out[...] = out[...] + vec[7:8, :]
        dh2[...] = jnp.zeros_like(dh2)

        def to_sibling(slot):
            return [
                at.copy_sibling(m.at[slot, 1 - at.core], s.at[slot], gsent.at[j, slot], ggot.at[j, slot])
                for j, (m, s) in enumerate(((mine1, sib1), (mine2, sib2)))
            ]

        def meet(i):
            slot = lax.rem(i, 2)
            for copy in to_sibling(slot):
                copy.wait()
            sum1[i] = mine1[slot, at.core] + sib1[slot]
            sum2[i] = mine2[slot, at.core] + sib2[slot]

        def tile(i, carry):
            slot = lax.rem(i, 2)

            @pl.when(i >= 1)
            def _():
                meet(i - 1)

            turn = i * FF_TICKS // (TILES - 1)

            @pl.when(turn > (i - 1) * FF_TICKS // (TILES - 1))
            def _():
                advance(turn - 1)

            for part in weights(i, slot):
                part.wait()

            @pl.when(i + 1 < TILES)
            def _():
                for part in weights(i + 1, 1 - slot):
                    part.start()

            bias = jnp.concatenate([bup[0, i], bup[1, i]], axis=1)
            u = dot(h2[...], wu[slot], NN) + bias
            a, slope = gelu_and_slope(u)
            a = a.astype(bf16)
            out[...] += dot(a, wd[slot], NN)
            d_wd = dot(a, og[...], TN).astype(bf16)
            mine1[slot, 0] = d_wd[:TILE]
            mine1[slot, 1] = d_wd[TILE:]
            du = (dot(og[...], wd[slot], NT) * slope).astype(bf16)
            d_wu = dot(h2t[...], du, NN).astype(bf16)
            mine2[slot, 0] = d_wu[:HALF]
            mine2[slot, 1] = d_wu[HALF:]
            for copy in to_sibling(slot):
                copy.start()
            dh2[...] += dot(du, wu[slot], NT)
            dbup[i] = jnp.sum(du.astype(f32), axis=0, keepdims=True)
            return carry

        lax.fori_loop(0, TILES, tile, 0)
        meet(TILES - 1)

        def put(b):
            slot = lax.rem(b, 2)
            return pltpu.make_async_copy(staged.at[slot], out_ref.at[block(b), :], local.at[slot])

        def put_rows(b, carry):
            @pl.when(b >= 2)
            def _():
                put(b - 2).wait()

            staged[lax.rem(b, 2)] = out[block(b), :].astype(bf16)
            put(b).start()
            return carry

        lax.fori_loop(0, blocks, put_rows, 0)
        put(blocks - 2).wait()
        put(blocks - 1).wait()

    pl.run_scoped(
        feed_forward,
        pltpu.VMEM((rows_all, WIDTH), f32),
        pltpu.VMEM((2, BLOCK, WIDTH), bf16),
        pltpu.VMEM((2, WIDTH, 2 * TILE), bf16),
        pltpu.VMEM((2, 2 * TILE, WIDTH), bf16),
        pltpu.VMEM((2, 2, TILE, WIDTH), bf16),
        pltpu.VMEM((2, 2, HALF, 2 * TILE), bf16),
        pltpu.SemaphoreType.DMA((4, 2)),
    )

    def attention(aot, dq, dk, dv, w, image, pimage, wide, source, staged, mine3, wsem, isem):
        load_ao = pltpu.make_async_copy(ao_ref, dq, wsem.at[0])
        load_h1 = pltpu.make_async_copy(h1_ref, dk, wsem.at[1])

        def load_w(j, slot):
            return pltpu.make_async_copy(w_ref.at[j], w.at[slot], wsem.at[2 + slot])

        def load_x2(b):
            slot = lax.rem(b, 2)
            return pltpu.make_async_copy(x2_ref.at[block(b), :], wide.at[slot], isem.at[4, slot])

        def load_x(b):
            slot = lax.rem(b, 2)
            return pltpu.make_async_copy(
                tokens_ref.at[pair(b), :], source.at[slot], isem.at[0, slot]
            )

        def put(b):
            slot = lax.rem(b, 2)
            return pltpu.make_async_copy(staged.at[slot], din_ref.at[pair(b), :], isem.at[4, slot])

        def pair(b):
            return pl.ds(aligned(b * 2 * BLOCK, 2 * BLOCK), 2 * BLOCK)

        def load_probs(i):
            slot = lax.rem(i, 2)
            return pltpu.make_async_copy(probs_ref.at[i], pimage.at[slot], isem.at[3, slot])

        def load_image(i):
            slot = lax.rem(i, 2)
            return [
                pltpu.make_async_copy(s.at[block(i), :], image.at[j, slot], isem.at[j, slot])
                for j, s in enumerate((q_ref, k_ref, v_ref))
            ] + [load_probs(i)]

        load_x2(0).start()
        load_w(3, 0).start()
        load_ao.start()
        load_h1.start()
        load_w(1, 1).start()
        load_w(2, 2).start()
        load_probs(0).start()

        def column_sum(j, value):
            dvec[j : j + 1, :] += jnp.sum(value, axis=0, keepdims=True)

        def norm_back(source, gain, incoming):
            center = source - jnp.mean(source, axis=-1, keepdims=True)
            rate = lax.rsqrt(jnp.mean(center * center, axis=-1, keepdims=True) + 1e-06)
            n = center * rate
            scaled = incoming * gain
            first = jnp.mean(scaled, axis=-1, keepdims=True)
            second = jnp.mean(scaled * n, axis=-1, keepdims=True)
            return n, (scaled - first - n * second) * rate

        def second_norm(b, carry):
            @pl.when(b == NORM_TICK)
            def _():
                advance(FF_TICKS)

            load_x2(b).wait()

            @pl.when(b + 1 < blocks)
            def _():
                load_x2(b + 1).start()

            rows = block(b)
            e = dh2[rows, :]
            n, dn = norm_back(wide[lax.rem(b, 2)], vec[5:6, :], e)
            g = og[rows, :].astype(f32)
            dx2 = g + dn
            dt = dx2.astype(bf16)
            dh2[rows, :] = dx2
            h2[rows, :] = dt
            column_sum(5, e * n)
            column_sum(6, e)
            column_sum(7, g)
            column_sum(4, dt.astype(f32))
            return carry

        lax.fori_loop(0, blocks, second_norm, 0)
        load_ao.wait()
        load_h1.wait()
        for b in range(blocks):
            rows = pl.ds(b * BLOCK, BLOCK)
            aot[:, rows] = dq[rows, :].T
            h2t[:, rows] = dk[rows, :].T
        load_w(3, 0).wait()
        for b in range(2):
            rows = pl.ds(b * (rows_all // 2), rows_all // 2)
            og[rows, :] = dot(h2[rows, :], w[0], NT).astype(bf16)
        load_w(0, 0).start()

        def values(i, carry):
            @pl.when(i == VALUE_TICK)
            def _():
                advance(FF_TICKS + 1)

            slot = lax.rem(i, 2)
            load_probs(i).wait()

            @pl.when(i + 1 < blocks)
            def _():
                load_probs(i + 1).start()

            rows = block(i)
            gi = og[rows, :]
            total = Lanes()
            for h in range(HEADS):
                low = pimage[slot, :, h * PATCHES : (h + 1) * PATCHES]
                total.add(h, dot(low, only_head(gi[:, head_window(h)], h), TN))
            dvi = total.joined()
            dv[rows, :] = dvi
            column_sum(3, dvi.astype(f32))
            return carry

        lax.fori_loop(0, blocks, values, 0)
        for copy in load_image(0):
            copy.start()

        def to_sibling(slot):
            return [
                at.copy_sibling(
                    mine3.at[slot, j, 1 - at.core],
                    sib3.at[slot, j],
                    gsent.at[2 + j, slot],
                    ggot.at[2 + j, slot],
                )
                for j in (0, 1)
            ]

        def meet(i):
            slot = lax.rem(i, 2)
            for copy in to_sibling(slot):
                copy.wait()
            for j, (s, c) in enumerate(((sum1, i + TILES), (sum3, i))):
                c = lax.rem(c, s.shape[0])
                s[c] = mine3[slot, j, at.core] + sib3[slot, j]

        def weight_rows(left, right, start, count):
            rows = [left[pl.ds(aligned(h * HALF + start, 64), count), :] for h in (0, 1)]
            return dot(jnp.concatenate(rows, axis=0), right[...], NN).astype(bf16)

        def produce(m, start, one, two):
            slot = lax.rem(m, 2)
            one = weight_rows(*one, start, TILE)
            two = weight_rows(*two, start, TILE)
            for h in (0, 1):
                for j in (0, 1):
                    part = slice(h * TILE + j * 64, h * TILE + j * 64 + 64)
                    mine3[slot, j, h] = jnp.concatenate([one[part], two[part]], axis=0)
            for copy in to_sibling(slot):
                copy.start()

        def heads(i, carry):
            @pl.when(lax.rem(i, 2) == 0)
            def _():
                produce(i // 2, i * 64, (h2t, dv), (aot, h2))

            slot = lax.rem(i, 2)
            for copy in load_image(i):
                copy.wait()

            @pl.when(i + 1 < blocks)
            def _():
                for copy in load_image(i + 1):
                    copy.start()

            @pl.when(lax.rem(i, 2) == 1)
            def _():
                meet(i // 2)
                advance(TILES + i // 2)

            rows = block(i)
            qi, ki, vi, gi = image[0, slot], image[1, slot], image[2, slot], og[rows, :]
            sums = Lanes(), Lanes()
            for h in range(HEADS):
                cols = head_window(h)
                p = pimage[slot, :, h * PATCHES : (h + 1) * PATCHES].astype(f32)
                dp = dot(gi[:, cols], only_head(vi[:, cols], h), NT)
                ds = (p * (dp - jnp.sum(p * dp, axis=-1, keepdims=True))).astype(bf16)
                sums[0].add(h, dot(ds, only_head(ki[:, cols], h), NN))
                sums[1].add(h, dot(ds, only_head(qi[:, cols], h), TN))
            dqi, dki = sums[0].joined(SCALE), sums[1].joined(SCALE)
            dq[rows, :] = dqi
            dk[rows, :] = dki
            column_sum(2, dqi.astype(f32))
            return carry

        lax.fori_loop(0, blocks, heads, 0)
        for j in range(3):
            load_w(j, j).wait()
        load_x(0).start()

        vo = weight_rows(h2t, dv, 512, 64), weight_rows(aot, h2, 512, 64)
        qk = weight_rows(h2t, dq, 0, 64), weight_rows(h2t, dk, 0, 64)
        for h in (0, 1):
            part = slice(h * 64, h * 64 + 64)
            for j, (one, two) in enumerate((vo, qk)):
                mine3[0, j, h] = jnp.concatenate([one[part], two[part]], axis=0)
        for copy in to_sibling(0):
            copy.start()

        def weight_gradients(j, carry):
            meet(j - 1)

            @pl.when(j < CHUNKS)
            def _():
                produce(j, (j - 5) * TILE + 64, (h2t, dq), (h2t, dk))

            advance(TILES - 1 + j)

            @pl.when(j < CHUNKS)
            def _():
                b = j - 5
                load_x(b).wait()

                @pl.when(b + 1 < 4)
                def _():
                    load_x(b + 1).start()

                @pl.when(b >= 2)
                def _():
                    put(b - 2).wait()

                rows = pair(b)
                e = dot(dq[rows, :], w[0], NT) + dot(dk[rows, :], w[1], NT)
                e = e + dot(dv[rows, :], w[2], NT)
                x = source[lax.rem(b, 2)].astype(f32)
                n, dn = norm_back(x, vec[0:1, :], e)
                staged[lax.rem(b, 2)] = (dh2[rows, :] + dn).astype(bf16)
                put(b).start()
                column_sum(0, e * n)
                column_sum(1, e)

            return carry

        lax.fori_loop(5, CHUNKS + 1, weight_gradients, 0)
        put(2).wait()
        put(3).wait()

        small[...] = jnp.zeros_like(small)
        small[0:VECTORS, :] = dvec[...]
        for i in range(TILES):
            small[VECTORS + i : VECTORS + i + 1, : 2 * TILE] = dbup[i]
        mine3[1, 1, 0] = jnp.concatenate(
            [small[...].astype(bf16), jnp.zeros((TILE - small.shape[0], WIDTH), bf16)], axis=0
        )
        trade = at.copy_sibling(mine3.at[1, 1, 0], sib3.at[1, 1], gsent.at[3, 1], ggot.at[3, 1])
        trade.start()
        trade.wait()
        sum3[CHUNKS] = mine3[1, 1, 0] + sib3[1, 1]

    flat = pltpu.VMEM((rows_all, WIDTH), bf16)
    pl.run_scoped(
        attention,
        pltpu.VMEM((WIDTH, rows_all), bf16),
        flat,
        flat,
        flat,
        pltpu.VMEM((3, WIDTH, WIDTH), bf16),
        pltpu.VMEM((3, 2, BLOCK, WIDTH), bf16),
        pltpu.VMEM((2, PATCHES, HEADS * PATCHES), bf16),
        pltpu.VMEM((2, BLOCK, WIDTH), f32),
        pltpu.VMEM((2, 2 * BLOCK, WIDTH), bf16),
        pltpu.VMEM((2, 2 * BLOCK, WIDTH), bf16),
        pltpu.VMEM((2, 2, 2, TILE, WIDTH), bf16),
        pltpu.SemaphoreType.DMA((5,)),
        pltpu.SemaphoreType.DMA((5, 2)),
    )

    def drain(tick, carry):
        advance(tick)
        return carry

    lax.fori_loop(TREE, TREE + 8, drain, 0)


def rest_of_layer(tokens, og, h1, q, k, v, ao, probs, x2, h2, w, wup, wdown, vec, bup):
    rows = h2.shape[0]
    flat = jax.ShapeDtypeStruct((rows, WIDTH), bf16)
    return pl.pallas_call(
        rest_kernel,
        out_shape=(
            flat,
            flat,
            jax.ShapeDtypeStruct((SMALL + 1, TILE, WIDTH), bf16),
            jax.ShapeDtypeStruct((TILES, HALF, 2 * TILE), bf16),
        ),
        in_specs=[ANY] * 15,
        out_specs=[ANY] * 4,
        scratch_shapes=[
            pltpu.VMEM((rows, WIDTH), bf16),
            pltpu.VMEM((WIDTH, rows), bf16),
            pltpu.VMEM((rows, WIDTH), bf16),
            pltpu.VMEM((rows, WIDTH), f32),
            pltpu.VMEM((2, TILES, 1, TILE), f32),
            pltpu.VMEM((VECTORS, WIDTH), f32),
            pltpu.VMEM((TILES, 1, 2 * TILE), f32),
            pltpu.VMEM((VECTORS, WIDTH), f32),
            pltpu.VMEM((32, WIDTH), f32),
            pltpu.VMEM((2, TILE, WIDTH), bf16),
            pltpu.VMEM((2, HALF, 2 * TILE), bf16),
            pltpu.VMEM((2, 2, TILE, WIDTH), bf16),
            pltpu.VMEM((TILES + 1, TILE, WIDTH), bf16),
            pltpu.VMEM((TILES, HALF, 2 * TILE), bf16),
            pltpu.VMEM((CHUNKS + 1, TILE, WIDTH), bf16),
            pltpu.SemaphoreType.DMA((5,)),
            pltpu.SemaphoreType.DMA((4, 2)),
            pltpu.SemaphoreType.DMA((4, 2)),
        ]
        + tree_scratch(TILE, WIDTH)
        + flag_scratch(7, 8) * 2
        + plane_scratch(FIRST, 2 * TILE)
        + plane_scratch(SECOND, 2 * TILE)
        + plane_scratch(TILE // 2, WIDTH) * 2,
        compiler_params=pltpu.CompilerParams(
            collective_id=1, has_side_effects=True, vmem_limit_bytes=62 * 2**20
        ),
        name="rest_of_layer",
    )(tokens, og, h1, q, k, v, ao, probs, x2, h2, w, wup, wdown, vec, bup)


def finish_kernel(
    g1_ref, q_ref, k_ref, g2_ref, v_ref, o_ref, d1_ref, d2_ref, dq_ref, dk_ref, dv_ref, do_ref
):
    d1_ref[...] = g1_ref[0].astype(f32)
    parts = []
    for h in (0, 1):
        for i in range(TILES):
            wide = TILE if i < TILES - 1 else FF_HALF - (TILES - 1) * TILE
            parts.append(g2_ref[i, :, h * TILE : h * TILE + wide].astype(f32))
    d2_ref[...] = jnp.concatenate(parts, axis=1)
    for s, d in ((q_ref, dq_ref), (k_ref, dk_ref), (v_ref, dv_ref), (o_ref, do_ref)):
        d[...] = s[0].astype(f32)


def finish(g1, g2):
    steps = HALF // 32
    square = jax.ShapeDtypeStruct((HALF, WIDTH), f32)
    last = TILES - 1

    def quarter(first, offset):
        return pl.BlockSpec((1, 32, WIDTH), lambda i: (first + i // 2, offset + i % 2, 0))

    return pl.pallas_call(
        finish_kernel,
        grid=(steps,),
        out_shape=(
            jax.ShapeDtypeStruct((FF_HALF, WIDTH), f32),
            jax.ShapeDtypeStruct((HALF, FF), f32),
        )
        + (square,) * 4,
        in_specs=[
            pl.BlockSpec((1, TILE, WIDTH), lambda i: (jnp.minimum(i, last), 0, 0)),
            quarter(TREE, 0),
            quarter(TREE, 2),
            pl.BlockSpec((TILES, 32, 2 * TILE), lambda i: (0, i, 0)),
            quarter(TILES, 0),
            quarter(TILES, 2),
        ],
        out_specs=[
            pl.BlockSpec((TILE, WIDTH), lambda i: (jnp.minimum(i, last), 0)),
            pl.BlockSpec((32, FF), lambda i: (i, 0)),
        ]
        + [pl.BlockSpec((32, WIDTH), lambda i: (i, 0))] * 4,
        compiler_params=pltpu.CompilerParams(vmem_limit_bytes=48 * 2**20),
        name="finish",
    )(g1, g1, g1, g2, g1, g1)


def fast_shards(
    tokens,
    out_grad,
    ln1_gain,
    ln1_bias,
    q_weight,
    q_bias,
    k_weight,
    v_weight,
    v_bias,
    o_weight,
    o_bias,
    ln2_gain,
    ln2_bias,
    up_weight,
    up_bias,
    down_weight,
    down_bias,
):
    small = [ln1_gain, ln1_bias, q_bias, v_bias, o_bias, ln2_gain, ln2_bias, down_bias]
    pack = jnp.concatenate([jnp.pad(v.astype(f32), (0, LANES - HALF)) for v in small])
    pack = pack.reshape(VECTORS, LANES)
    gap = TILES * TILE - FF_HALF
    bup = jnp.pad(up_bias.astype(f32), (0, gap)).reshape(TILES, 1, TILE)
    saved = forward(
        tokens, q_weight, k_weight, v_weight, o_weight, up_weight, down_weight, pack, bup
    )
    output, d_input, g1, g2 = rest_of_layer(tokens, out_grad, *saved)
    d_down, d_up, d_q, d_k, d_v, d_o = finish(g1, g2)
    core = lax.axis_index("group")
    vectors = lax.dynamic_slice(g1[SMALL, :VECTORS], (0, core * HALF), (VECTORS, HALF)).astype(f32)
    d_bup = lax.dynamic_slice(
        g1[SMALL, VECTORS : VECTORS + TILES], (0, core * TILE), (TILES, TILE)
    )
    d_bup = d_bup.reshape(TILES * TILE)[:FF_HALF].astype(f32)
    return (
        output,
        d_input,
        vectors[0],
        vectors[1],
        d_q,
        vectors[2],
        d_k,
        d_v,
        vectors[3],
        d_o,
        vectors[4],
        vectors[5],
        vectors[6],
        d_up,
        d_bup,
        d_down,
        vectors[7],
    )


def solution(mesh):
    placed = (
        P(("group", "replica"), None),
        P(("group", "replica"), None),
        P("group"),
        P("group"),
        P("group", None),
        P("group"),
        P("group", None),
        P("group", None),
        P("group"),
        P("group", None),
        P("group"),
        P("group"),
        P("group"),
        P("group", None),
        P("group"),
        P("group", None),
        P("group"),
    )
    fast = mesh.shape["group"] == 2 and mesh.shape["replica"] == 16
    return jax.shard_map(
        fast_shards if fast else shards,
        mesh=mesh,
        in_specs=placed,
        out_specs=(
            P(("group", "replica"), None),
            P(("group", "replica"), None),
            P("group"),
            P("group"),
            P("group", None),
            P("group"),
            P("group", None),
            P("group", None),
            P("group"),
            P("group", None),
            P("group"),
            P("group"),
            P("group"),
            P("group", None),
            P("group"),
            P("group", None),
            P("group"),
        ),
        check_vma=False,
    )
```

```python
import functools

import jax
import jax.numpy as jnp
from jax import lax
from jax.experimental import pallas as pl
from jax.experimental.pallas import tpu as pltpu
from jax.sharding import PartitionSpec as P

HEADS = 16
PATCHES = 128


def layer_norm(values, gain, shift):
    center = values - jnp.mean(values, axis=-1, keepdims=True)
    spread = jnp.mean(center * center, axis=-1, keepdims=True)
    return center * lax.rsqrt(spread + 1e-06) * gain + shift


def gelu_tanh(values):
    return jax.nn.gelu(values, approximate=True)


def split_heads(rows):
    return rows.reshape(-1, PATCHES, HEADS, rows.shape[-1] // HEADS)


def head_logits(query, key_rows):
    factor = (query.shape[-1] // HEADS) ** (-0.5)
    query_h = split_heads(query)
    key_h = split_heads(key_rows)
    logits = (
        jnp.einsum("isha,itha->ihst", query_h, key_h, preferred_element_type=jnp.float32) * factor
    )
    return (logits, query_h, key_h, factor)


def attend(query, key_rows, value_rows):
    logits, query_h, key_h, factor = head_logits(query, key_rows)
    peak = jnp.max(logits, axis=-1, keepdims=True)
    log_total = peak + jnp.log(jnp.sum(jnp.exp(logits - peak), axis=-1, keepdims=True))
    weights_low = jnp.exp(logits - log_total).astype(jnp.bfloat16)
    mixed = jnp.einsum(
        "ihst,itha->isha", weights_low, split_heads(value_rows), preferred_element_type=jnp.float32
    )
    return (mixed.reshape(query.shape), log_total)


def attend_back(query, key_rows, value_rows, log_total, d_mixed):
    logits, query_h, key_h, factor = head_logits(query, key_rows)
    weights = jnp.exp(logits - log_total)
    weights_low = weights.astype(jnp.bfloat16)
    value_h = split_heads(value_rows)
    d_mix_h = split_heads(d_mixed)
    d_weights = jnp.einsum("isha,itha->ihst", d_mix_h, value_h, preferred_element_type=jnp.float32)
    d_logits = weights * (d_weights - jnp.sum(weights * d_weights, axis=-1, keepdims=True))
    d_low = d_logits.astype(jnp.bfloat16)
    d_query = (
        jnp.einsum("ihst,itha->isha", d_low, key_h, preferred_element_type=jnp.float32) * factor
    ).astype(jnp.bfloat16)
    d_key = (
        jnp.einsum("ihst,isha->itha", d_low, query_h, preferred_element_type=jnp.float32) * factor
    ).astype(jnp.bfloat16)
    d_value = jnp.einsum(
        "ihst,isha->itha", weights_low, d_mix_h, preferred_element_type=jnp.float32
    ).astype(jnp.bfloat16)
    return (d_query.reshape(query.shape), d_key.reshape(query.shape), d_value.reshape(query.shape))


def outer_rows(left, right):
    return jnp.einsum("ra,rb->ab", left, right, preferred_element_type=jnp.float32)


def back_rows(grads, weight):
    return jnp.einsum("rb,ab->ra", grads, weight, preferred_element_type=jnp.float32)


def column_sums(grads):
    return jnp.sum(grads.astype(jnp.float32), axis=0)


def shards(
    tokens,
    out_grad,
    ln1_gain,
    ln1_bias,
    q_weight,
    q_bias,
    k_weight,
    v_weight,
    v_bias,
    o_weight,
    o_bias,
    ln2_gain,
    ln2_bias,
    up_weight,
    up_bias,
    down_weight,
    down_bias,
):
    attn_full = tuple(lax.all_gather(v, "group", axis=0, tiled=True) for v in (
        ln1_gain, ln1_bias, q_weight, q_bias, k_weight, v_weight, v_bias, o_weight, o_bias,
    ))
    gain_one, shift_one, wq_full, bq_full, wk_full, wv_full, bv_full, wo_full, bo_full = attn_full
    input_f = tokens.astype(jnp.float32)
    gain_one_f = gain_one.astype(jnp.float32)
    shift_one_f = shift_one.astype(jnp.float32)
    normed1 = layer_norm(input_f, gain_one_f, shift_one_f).astype(jnp.bfloat16)
    query = (
        jnp.dot(normed1, wq_full, preferred_element_type=jnp.float32) + bq_full.astype(jnp.float32)
    ).astype(jnp.bfloat16)
    key_rows = jnp.dot(normed1, wk_full, preferred_element_type=jnp.float32).astype(jnp.bfloat16)
    value_rows = (
        jnp.dot(normed1, wv_full, preferred_element_type=jnp.float32) + bv_full.astype(jnp.float32)
    ).astype(jnp.bfloat16)
    mixed, log_total = attend(query, key_rows, value_rows)
    attn_in = mixed.astype(jnp.bfloat16)
    residual = (
        input_f
        + jnp.dot(attn_in, wo_full, preferred_element_type=jnp.float32)
        + bo_full.astype(jnp.float32)
    )
    mlp_full = tuple(lax.all_gather(v, "group", axis=0, tiled=True) for v in (
        ln2_gain, ln2_bias, up_weight, up_bias, down_weight, down_bias,
    ))
    gain_two, shift_two, wup_full, bup_full, wdown_full, bdown_full = mlp_full
    gain_two_f = gain_two.astype(jnp.float32)
    shift_two_f = shift_two.astype(jnp.float32)
    normed2 = layer_norm(residual, gain_two_f, shift_two_f).astype(jnp.bfloat16)
    pre_act = jnp.dot(normed2, wup_full, preferred_element_type=jnp.float32) + bup_full.astype(
        jnp.float32
    )
    hidden = gelu_tanh(pre_act).astype(jnp.bfloat16)
    output = (
        residual
        + jnp.dot(hidden, wdown_full, preferred_element_type=jnp.float32)
        + bdown_full.astype(jnp.float32)
    )
    mlp_back = tuple(lax.all_gather(v, "group", axis=0, tiled=True) for v in (
        ln2_gain, ln2_bias, up_weight, up_bias, down_weight, down_bias,
    ))
    wup_back = mlp_back[2]
    wdown_back = mlp_back[4]
    grad_out = out_grad.astype(jnp.float32)
    d_wdown = outer_rows(hidden, out_grad)
    d_bdown = column_sums(out_grad)
    d_hidden = back_rows(out_grad, wdown_back)
    unused_act, gelu_back = jax.vjp(gelu_tanh, pre_act)
    d_pre = gelu_back(d_hidden)[0].astype(jnp.bfloat16)
    d_wup = outer_rows(normed2, d_pre)
    d_bup = column_sums(d_pre)
    d_normed2 = back_rows(d_pre, wup_back)
    unused_two, norm_back_two = jax.vjp(layer_norm, residual, gain_two_f, shift_two_f)
    d_res_norm, d_gain_two, d_shift_two = norm_back_two(d_normed2)
    d_residual = grad_out + d_res_norm
    mlp_grads = tuple(
        lax.psum_scatter(v.astype(jnp.bfloat16), "group", scatter_dimension=0, tiled=True).astype(jnp.float32)
        for v in (d_gain_two, d_shift_two, d_wup, d_bup, d_wdown, d_bdown)
    )
    attn_back = tuple(lax.all_gather(v, "group", axis=0, tiled=True) for v in (
        ln1_gain, ln1_bias, q_weight, q_bias, k_weight, v_weight, v_bias, o_weight, o_bias,
    ))
    wq_back = attn_back[2]
    wk_back = attn_back[4]
    wv_back = attn_back[5]
    wo_back = attn_back[7]
    d_attn = d_residual.astype(jnp.bfloat16)
    d_wout = outer_rows(attn_in, d_attn)
    d_bout = column_sums(d_attn)
    d_mixed = back_rows(d_attn, wo_back).astype(jnp.bfloat16)
    d_query, d_key, d_value = attend_back(query, key_rows, value_rows, log_total, d_mixed)
    d_wquery = outer_rows(normed1, d_query)
    d_bquery = column_sums(d_query)
    d_wkey = outer_rows(normed1, d_key)
    d_wvalue = outer_rows(normed1, d_value)
    d_bvalue = column_sums(d_value)
    d_normed1 = (
        back_rows(d_query, wq_back) + back_rows(d_key, wk_back) + back_rows(d_value, wv_back)
    )
    unused_one, norm_back_one = jax.vjp(layer_norm, input_f, gain_one_f, shift_one_f)
    d_in_norm, d_gain_one, d_shift_one = norm_back_one(d_normed1)
    d_input = (d_residual + d_in_norm).astype(jnp.bfloat16)
    attn_grads = tuple(
        lax.psum_scatter(v.astype(jnp.bfloat16), "group", scatter_dimension=0, tiled=True).astype(jnp.float32)
        for v in (d_gain_one, d_shift_one, d_wquery, d_bquery, d_wkey, d_wvalue, d_bvalue, d_wout, d_bout)
    )
    summed = tuple(
        lax.psum(v.astype(jnp.bfloat16), "replica").astype(jnp.float32) for v in attn_grads + mlp_grads
    )
    attn_grads = tuple(summed[:9])
    mlp_grads = tuple(summed[9:])
    return (output.astype(jnp.bfloat16), d_input) + tuple(attn_grads) + tuple(mlp_grads)


MESH = pl.DeviceIdType.MESH
bf16 = jnp.bfloat16
f32 = jnp.float32
ANY = pl.BlockSpec(memory_space=pl.ANY)
WIDTH = 1152
HALF = 576
FF = 4304
FF_HALF = 2152
TILES = 17
TILE = 128
FF_PAD = 2 * TILES * TILE
FIRST = 320
SECOND = 256


class Place:
    def __init__(self):
        self.core = lax.axis_index("group")
        chip = lax.axis_index("replica")
        self.chip = chip
        self.x = lax.rem(chip, 2)
        self.y = lax.rem(chip // 2, 2)
        self.z = chip // 4
        self.x_pair = chip + 1 - 2 * self.x
        self.y_pair = chip + 2 - 4 * self.y
        self.z_pair = chip + 4 - 8 * lax.rem(self.z, 2)
        self.inner = (self.z == 1) | (self.z == 2)
        self.outer = jnp.logical_not(self.inner)
        self.mid_pair = jnp.where(self.inner, chip + 12 - 8 * self.z, chip)
        self.z_half = lax.rem(self.z // 2, 2)

    def barrier(self):
        sem = pltpu.get_barrier_semaphore()

        def greet(core, chip):
            pl.semaphore_signal(sem, inc=1, device_id=(core, chip), device_id_type=MESH)

        greet(1 - self.core, self.chip)
        greet(self.core, self.x_pair)
        greet(self.core, self.y_pair)
        greet(self.core, self.z_pair)

        @pl.when(self.inner)
        def _():
            greet(self.core, self.mid_pair)
            pl.semaphore_wait(sem, 5)

        @pl.when(self.outer)
        def _():
            pl.semaphore_wait(sem, 4)

    def copy(self, source, target, sent, got, chip):
        return pltpu.make_async_remote_copy(
            source, target, sent, got, device_id=(self.core, chip), device_id_type=MESH
        )

    def copy_sibling(self, source, target, sent, got):
        return pltpu.make_async_remote_copy(
            source, target, sent, got, device_id=(1 - self.core, self.chip), device_id_type=MESH
        )


def aligned(value, unit):
    return pl.multiple_of(value, unit)


def landing(slots, chunk):
    return slots.at[lax.rem(chunk, slots.shape[0])]


def add_rows(total, landed, chunk, start, count):
    rows = pl.ds(start, count)
    slot = lax.rem(chunk, total.shape[0])
    total[slot, rows, :] = total[slot, rows, :] + landed[...]


class TreeFirst:
    steps = 9
    after = 0

    def __init__(self, place, total, final, spot, landing, sent, got, kept):
        self.at = place
        self.total = total
        self.final = final
        self.spot = spot
        self.kept = kept
        self.land = landing
        self.sent = sent
        self.got = got
        n = total.shape[1]
        self.n = n
        p = place
        self.own = [
            (0, n),
            (aligned(p.z_half * (n // 2), n // 2), n // 2),
        ]
        self.other = [None, (aligned((1 - p.z_half) * (n // 2), n // 2), n // 2)]
        for bit, part in ((p.y, n // 4), (p.x, n // 8)):
            base = self.own[-1][0]
            self.own.append((aligned(base + bit * part, part), part))
            self.other.append((aligned(base + (1 - bit) * part, part), part))
        self.peer = [p.z_pair, p.mid_pair, p.y_pair, p.x_pair]

    def flags(self, k, chunk):
        slot = lax.rem(chunk + self.after, self.sent.shape[1])
        return self.sent.at[k, slot], self.got.at[k, slot]

    def rows(self, chunk, span):
        return landing(self.total, chunk).at[pl.ds(span[0], span[1]), :]

    def ends(self, chunk, span):
        return self.final.at[self.spot(chunk), pl.ds(span[0], span[1]), :]

    def send(self, k, chunk):
        sent, got = self.flags(k, chunk)
        if k < 4:
            span = self.own[0] if k == 0 else self.other[k]
            return self.at.copy(
                self.rows(chunk, span), landing(self.land[k], chunk), sent, got, self.peer[k]
            )
        level = 7 - k
        target = self.ends(chunk, self.own[level])
        source = self.rows(chunk, self.own[3]) if k == 4 else target
        return self.at.copy(source, target, sent, got, self.peer[level])

    def keep(self, chunk):
        return pltpu.make_async_copy(
            self.rows(chunk, self.own[3]), self.ends(chunk, self.own[3]), landing(self.kept, chunk)
        )

    def arrive(self, k, chunk):
        if k < 4:
            landed = landing(self.land[k], chunk)
        else:
            level = 7 - k
            landed = self.ends(chunk, self.own[0] if level == 0 else self.other[level])
        self.at.copy(landed, landed, *self.flags(k, chunk), self.at.z_pair).wait_recv()

    def step(self, k, chunk):
        at = self.at
        if k == 0:

            @pl.when(at.outer)
            def _():
                self.send(0, chunk).start()

        elif k <= 7:

            @pl.when(at.inner)
            def _():
                self.arrive(k - 1, chunk)
                if k <= 4:
                    add_rows(self.total, landing(self.land[k - 1], chunk), chunk, *self.own[k - 1])
                if k == 4:
                    self.keep(chunk).start()
                if k == 5:
                    self.keep(chunk).wait()
                self.send(k, chunk).start()

        else:

            @pl.when(at.inner)
            def _():
                for j in range(1, 8):
                    self.send(j, chunk).wait_send()

            @pl.when(at.outer)
            def _():
                self.arrive(7, chunk)
                self.send(0, chunk).wait_send()


class PlaneFirst:
    steps = 8

    def __init__(
        self, place, total, final, spot, base, n, x_first, landing, sent, got, kept, after=0
    ):
        self.at = place
        self.after = after
        self.total = total
        self.final = final
        self.spot = spot
        self.kept = kept
        self.land = landing
        self.sent = sent
        self.got = got
        p = place
        if x_first:
            one, two = (p.x, p.x_pair), (p.y, p.y_pair)
        else:
            one, two = (p.y, p.y_pair), (p.x, p.x_pair)
        self.peer_one, self.peer_two = one[1], two[1]
        start = aligned(base + one[0] * (n // 2), 16)
        self.half = (start, n // 2)
        self.half_other = (aligned(base + (1 - one[0]) * (n // 2), 16), n // 2)
        self.quarter = (aligned(start + two[0] * (n // 4), 16), n // 4)
        self.quarter_other = (aligned(start + (1 - two[0]) * (n // 4), 16), n // 4)

    def flags(self, k, chunk):
        slot = lax.rem(chunk + self.after, self.sent.shape[1])
        return self.sent.at[k, slot], self.got.at[k, slot]

    def rows(self, chunk, span):
        return landing(self.total, chunk).at[pl.ds(span[0], span[1]), :]

    def ends(self, chunk, span):
        return self.final.at[self.spot(chunk), pl.ds(span[0], span[1]), :]

    def keep(self, chunk):
        return pltpu.make_async_copy(
            self.rows(chunk, self.quarter), self.ends(chunk, self.quarter), landing(self.kept, chunk + self.after)
        )

    def send(self, k, chunk):
        at = self.at
        quarter = self.rows(chunk, self.quarter)
        quarter_end = self.ends(chunk, self.quarter)
        half_end = self.ends(chunk, self.half)
        source, target, peer = (
            (self.rows(chunk, self.half_other), landing(self.land[0], chunk), self.peer_one),
            (self.rows(chunk, self.quarter_other), landing(self.land[1], chunk), self.peer_two),
            (quarter, landing(self.land[2], chunk), at.z_pair),
            (quarter, landing(self.land[3], chunk), at.mid_pair),
            (quarter, quarter_end, at.z_pair),
            (quarter_end, quarter_end, self.peer_two),
            (half_end, half_end, self.peer_one),
        )[k]
        return at.copy(source, target, *self.flags(k, chunk), peer)

    def arrive(self, k, chunk):
        if k < 4:
            landed = landing(self.land[k], chunk)
        else:
            landed = self.ends(
                chunk, (self.quarter, self.quarter_other, self.half_other)[k - 4]
            )
        self.at.copy(landed, landed, *self.flags(k, chunk), self.at.z_pair).wait_recv()

    def step(self, k, chunk):
        at = self.at
        if k == 0:
            self.send(0, chunk).start()
        elif k == 1:
            self.arrive(0, chunk)
            add_rows(self.total, landing(self.land[0], chunk), chunk, *self.half)
            self.send(1, chunk).start()
        elif k == 2:
            self.arrive(1, chunk)
            add_rows(self.total, landing(self.land[1], chunk), chunk, *self.quarter)

            @pl.when(at.outer)
            def _():
                self.send(2, chunk).start()

        elif k == 3:

            @pl.when(at.inner)
            def _():
                self.arrive(2, chunk)
                add_rows(self.total, landing(self.land[2], chunk), chunk, *self.quarter)
                self.send(3, chunk).start()

        elif k == 4:

            @pl.when(at.inner)
            def _():
                self.arrive(3, chunk)
                self.send(3, chunk).wait_send()
                add_rows(self.total, landing(self.land[3], chunk), chunk, *self.quarter)
                self.send(4, chunk).start()
                self.keep(chunk).start()

        elif k == 5:

            @pl.when(at.inner)
            def _():
                self.keep(chunk).wait()

            @pl.when(at.outer)
            def _():
                self.arrive(4, chunk)

            self.send(5, chunk).start()
        elif k == 6:
            self.arrive(5, chunk)
            self.send(6, chunk).start()
        else:
            self.arrive(6, chunk)
            for j in (0, 1, 5, 6):
                self.send(j, chunk).wait_send()

            @pl.when(at.inner)
            def _():
                self.send(4, chunk).wait_send()

            @pl.when(at.outer)
            def _():
                self.send(2, chunk).wait_send()


def tree_scratch(n, width):
    return [
        pltpu.VMEM((slots, n // part, width), bf16)
        for slots, part in ((10, 1), (3, 2), (3, 4), (3, 8))
    ] + flag_scratch(8, 10)


def plane_scratch(n, width):
    return [
        pltpu.VMEM((slots, n // part, width), bf16)
        for slots, part in ((3, 2), (3, 4), (4, 4), (3, 4))
    ]


def flag_scratch(copies, slots):
    return [
        pltpu.SemaphoreType.DMA((copies, slots)),
        pltpu.SemaphoreType.DMA((copies, slots)),
        pltpu.SemaphoreType.DMA((slots,)),
    ]


def dot(left, right, contract):
    return lax.dot_general(left, right, (contract, ((), ())), preferred_element_type=f32)


NN = ((1,), (0,))
NT = ((1,), (1,))
TN = ((0,), (0,))


def gelu_and_slope(u):
    c = 0.7978845608028654
    square = u * u
    t = jnp.tanh(c * u * (1.0 + 0.044715 * square))
    half = 0.5 * (1.0 + t)
    slope = half + 0.5 * u * (1.0 - t * t) * (c * (1.0 + 3 * 0.044715 * square))
    return u * half, slope


VECTORS = 8
LANES = 640
SCALE = 72**-0.5
HEAD = 72


def head_window(h):
    return slice(h * HEAD // 128 * 128, ((h + 1) * HEAD + 127) // 128 * 128)


def only_head(rows, h):
    lane = lax.broadcasted_iota(jnp.int32, rows.shape, 1) + head_window(h).start
    return jnp.where((lane >= h * HEAD) & (lane < (h + 1) * HEAD), rows, jnp.zeros_like(rows))


class Lanes:
    def __init__(self):
        self.tiles = [None] * (WIDTH // 128)

    def add(self, h, window):
        first = head_window(h).start // 128
        for j in range(window.shape[1] // 128):
            part = window[:, j * 128 : (j + 1) * 128]
            old = self.tiles[first + j]
            self.tiles[first + j] = part if old is None else old + part

    def joined(self, scale=None):
        tiles = self.tiles if scale is None else [t * scale for t in self.tiles]
        return jnp.concatenate([t.astype(bf16) for t in tiles], axis=1)


def normalise(rows, gain, shift):
    center = rows - jnp.mean(rows, axis=-1, keepdims=True)
    spread = jnp.mean(center * center, axis=-1, keepdims=True)
    return center * lax.rsqrt(spread + 1e-06) * gain + shift


def forward_kernel(
    tokens_ref,
    wq_ref,
    wk_ref,
    wv_ref,
    wo_ref,
    up_ref,
    down_ref,
    pack_ref,
    bup_ref,
    h1_ref,
    q_ref,
    k_ref,
    v_ref,
    ao_ref,
    probs_ref,
    x2_ref,
    h2_ref,
    w_ref,
    wup_ref,
    wdown_ref,
    vec_ref,
    bups_ref,
    x,
    h1,
    q,
    k,
    v,
    ao,
    probs,
    x2,
    h2,
    w,
    up,
    up_wide,
    down,
    zeros,
    pack,
    vec,
    local,
    wsem,
    psem,
    sent,
    got,
    bsem,
):
    at = Place()
    core = at.core
    own = pl.ds(aligned(core * HALF, HALF), HALF)
    ff_own = pl.ds(aligned(core * TILES * TILE, TILE), FF_HALF)
    shards = (wq_ref, wk_ref, wv_ref, wo_ref)
    load_x = pltpu.make_async_copy(tokens_ref, x, local.at[0])
    load_x.start()
    load_w = [pltpu.make_async_copy(s, w.at[j, own, :], local.at[1 + j]) for j, s in enumerate(shards)]
    load_pack = pltpu.make_async_copy(pack_ref, pack.at[core], local.at[5])
    load_bup = pltpu.make_async_copy(bup_ref, bups_ref.at[core], local.at[6])
    load_up = pltpu.make_async_copy(up_ref, up, local.at[7])
    load_down = pltpu.make_async_copy(down_ref, down, local.at[8])
    keep_down = pltpu.make_async_copy(down, wdown_ref.at[ff_own, :], wsem.at[4])
    for load in (load_pack, *load_w, load_bup, load_up, load_down):
        load.start()
    zeros[...] = jnp.zeros_like(zeros)
    gap = TILES * TILE - FF_HALF
    blanks = [
        pltpu.make_async_copy(
            zeros, wdown_ref.at[pl.ds(h * TILES * TILE + FF_HALF, gap), :], local.at[9 + h]
        )
        for h in (0, 1)
    ]
    for blank in blanks:
        blank.start()

    bar = pltpu.get_barrier_semaphore()
    pl.semaphore_signal(bar, inc=1, device_id=(1 - core, at.chip), device_id_type=MESH)
    pl.semaphore_wait(bar, 1)

    def share(j, source, target):
        return at.copy_sibling(source, target, sent.at[j], got.at[j])

    give_w = [share(j, s, w.at[j, own, :]) for j, s in enumerate(shards)]
    give_pack = share(4, pack_ref, pack.at[core])
    give_bup = share(5, bup_ref, bups_ref.at[core])
    give_down = share(6, down_ref, wdown_ref.at[ff_own, :])
    give_up = share(7, up_wide, wup_ref.at[own, :])
    keep_up = pltpu.make_async_copy(up_wide, wup_ref.at[own, :], local.at[11])
    give_pack.start()
    for give in give_w:
        give.start()
    give_bup.start()
    give_down.start()

    load_pack.wait()
    give_pack.wait()
    vec[...] = jnp.concatenate([pack[0, :, :HALF], pack[1, :, :HALF]], axis=1)
    load_x.wait()
    rows_of = [pl.ds(b * 512, 512) for b in range(2)]

    def first_norm(b, carry):
        rows = pl.ds(aligned(b * 128, 128), 128)
        h1[rows, :] = normalise(x[rows, :].astype(f32), vec[0:1, :], vec[1:2, :]).astype(bf16)
        return carry

    lax.fori_loop(0, 8, first_norm, 0)
    keep = [pltpu.make_async_copy(h1, h1_ref, local.at[0])]
    keep[0].start()

    def project(j, target, bias):
        load_w[j].wait()
        give_w[j].wait()
        for rows in rows_of:
            y = dot(h1[rows, :], w[j], NN)
            if bias is not None:
                y = y + vec[bias : bias + 1, :]
            target[rows, :] = y.astype(bf16)

    project(0, q, 2)
    project(1, k, None)
    project(2, v, 3)
    for j, (s, d) in enumerate(((q, q_ref), (k, k_ref), (v, v_ref))):
        keep.append(pltpu.make_async_copy(s, d, local.at[12 + j]))
        keep[-1].start()

    load_down.wait()
    keep_down.start()
    load_up.wait()

    def widen(b, carry):
        rows = pl.ds(aligned(b * 64, 64), 64)
        row = up[rows, :]
        none = jnp.zeros((64, gap), bf16)
        up_wide[rows, :] = jnp.concatenate([row[:, :FF_HALF], none, row[:, FF_HALF:], none], axis=1)
        return carry

    lax.fori_loop(0, HALF // 64, widen, 0)
    keep_up.start()
    give_up.start()

    def keep_probs(i):
        slot = lax.rem(i, 2)
        return pltpu.make_async_copy(probs.at[slot], probs_ref.at[i], psem.at[slot])

    def attention(i, carry):
        rows = pl.ds(aligned(i * 128, 128), 128)
        slot = lax.rem(i, 2)

        @pl.when(i >= 2)
        def _():
            keep_probs(i - 2).wait()

        qi, ki, vi = q[rows, :], k[rows, :], v[rows, :]
        mixed = Lanes()
        held = []
        for h in range(HEADS):
            cols = head_window(h)
            logits = dot(only_head(ki[:, cols], h), qi[:, cols], NT) * SCALE
            e = jnp.exp(logits - jnp.max(logits, axis=0, keepdims=True))
            p = (e / jnp.sum(e, axis=0, keepdims=True)).astype(bf16)
            held.append(p)
            mixed.add(h, dot(p, only_head(vi[:, cols], h), TN))
        ao[rows, :] = mixed.joined()
        probs[slot] = jnp.concatenate(held, axis=1)
        keep_probs(i).start()
        return carry

    lax.fori_loop(0, 8, attention, 0)
    keep_ao = pltpu.make_async_copy(ao, ao_ref, local.at[15])
    keep_ao.start()

    load_w[3].wait()
    give_w[3].wait()
    keep_w = pltpu.make_async_copy(w, w_ref, wsem.at[0])
    keep_w.start()
    keep_vec = pltpu.make_async_copy(vec, vec_ref, wsem.at[1])
    keep_vec.start()
    for rows in rows_of:
        x2[rows, :] = x[rows, :].astype(f32) + dot(ao[rows, :], w[3], NN) + vec[4:5, :]

    def second_norm(b, carry):
        rows = pl.ds(aligned(b * 128, 128), 128)
        h2[rows, :] = normalise(x2[rows, :], vec[5:6, :], vec[6:7, :]).astype(bf16)
        return carry

    lax.fori_loop(0, 8, second_norm, 0)
    keep_x2 = pltpu.make_async_copy(x2, x2_ref, wsem.at[2])
    keep_h2 = pltpu.make_async_copy(h2, h2_ref, wsem.at[3])
    for copy in (keep_x2, keep_h2):
        copy.start()
    for copy in (
        *keep,
        keep_probs(6),
        keep_probs(7),
        keep_ao,
        keep_w,
        keep_vec,
        load_bup,
        keep_down,
        *blanks,
        keep_up,
        keep_x2,
        keep_h2,
    ):
        copy.wait()
    for give in (give_bup, give_down, give_up):
        give.wait()


def forward(tokens, wq, wk, wv, wo, up, down, pack, bup):
    rows = tokens.shape[0]
    images = rows // PATCHES
    flat = jax.ShapeDtypeStruct((rows, WIDTH), bf16)
    return pl.pallas_call(
        forward_kernel,
        out_shape=(
            flat,
            flat,
            flat,
            flat,
            flat,
            jax.ShapeDtypeStruct((images, PATCHES, HEADS * PATCHES), bf16),
            jax.ShapeDtypeStruct((rows, WIDTH), f32),
            flat,
            jax.ShapeDtypeStruct((4, WIDTH, WIDTH), bf16),
            jax.ShapeDtypeStruct((WIDTH, FF_PAD), bf16),
            jax.ShapeDtypeStruct((FF_PAD, WIDTH), bf16),
            jax.ShapeDtypeStruct((VECTORS, WIDTH), f32),
            jax.ShapeDtypeStruct((2, TILES, 1, TILE), f32),
        ),
        in_specs=[ANY] * 9,
        out_specs=[ANY] * 13,
        scratch_shapes=[pltpu.VMEM((rows, WIDTH), bf16)] * 6
        + [
            pltpu.VMEM((2, PATCHES, HEADS * PATCHES), bf16),
            pltpu.VMEM((rows, WIDTH), f32),
            pltpu.VMEM((rows, WIDTH), bf16),
            pltpu.VMEM((4, WIDTH, WIDTH), bf16),
            pltpu.VMEM((HALF, FF), bf16),
            pltpu.VMEM((HALF, FF_PAD), bf16),
            pltpu.VMEM((FF_HALF, WIDTH), bf16),
            pltpu.VMEM((TILES * TILE - FF_HALF, WIDTH), bf16),
            pltpu.VMEM((2, VECTORS, LANES), f32),
            pltpu.VMEM((VECTORS, WIDTH), f32),
            pltpu.SemaphoreType.DMA((16,)),
            pltpu.SemaphoreType.DMA((5,)),
            pltpu.SemaphoreType.DMA((2,)),
            pltpu.SemaphoreType.DMA((8,)),
            pltpu.SemaphoreType.DMA((8,)),
            pltpu.SemaphoreType.DMA((1,)),
        ],
        compiler_params=pltpu.CompilerParams(
            collective_id=3, has_side_effects=True, vmem_limit_bytes=62 * 2**20
        ),
        name="forward",
    )(tokens, wq, wk, wv, wo, up, down, pack, bup)


CHUNKS = 9
TREE = TILES + CHUNKS
SMALL = TILES + 2 * CHUNKS + 1
BLOCK = 128
FF_TICKS = 15
NORM_TICK = 4
VALUE_TICK = 3


def rest_kernel(
    tokens_ref,
    og_ref,
    h1_ref,
    q_ref,
    k_ref,
    v_ref,
    ao_ref,
    probs_ref,
    x2_ref,
    h2_ref,
    w_ref,
    wup_ref,
    wdown_ref,
    vec_ref,
    bup_ref,
    out_ref,
    din_ref,
    g1_ref,
    g2_ref,
    h2,
    h2t,
    og,
    dh2,
    bup,
    vec,
    dbup,
    dvec,
    small,
    sib1,
    sib2,
    sib3,
    sum1,
    sum2,
    sum3,
    local,
    gsent,
    ggot,
    *comm,
):
    at = Place()
    rows_all = h2.shape[0]
    blocks = rows_all // BLOCK
    flags = comm[7:10], comm[10:13]
    planes = [comm[j : j + 4] for j in range(13, 29, 4)]

    def tree_spot(chunk):
        late = chunk - TILES
        value_or_query = jnp.where(late < 5, 2 * late, CHUNKS + 2 * late - 9)
        return jnp.where(chunk < TILES, chunk, TILES + value_or_query)

    def late_spot(chunk):
        return TILES + jnp.where(chunk < 4, 2 * chunk + 1, CHUNKS + 2 * chunk - 8)

    tree = TreeFirst(at, sum1, g1_ref, tree_spot, comm[:4], *comm[4:7])
    early = [
        PlaneFirst(at, sum2, g2_ref, lambda c: c, base, n, j == 0, planes[j], *flags[j])
        for j, base, n in ((0, 0, FIRST), (1, FIRST, SECOND))
    ]
    late = [
        PlaneFirst(
            at, sum3, g1_ref, late_spot, base, TILE // 2, j == 0, planes[2 + j], *flags[j], TILES
        )
        for j, base in ((0, 0), (1, TILE // 2))
    ]

    def advance(tick):
        for k in reversed(range(TreeFirst.steps)):
            chunk = tick - k

            @pl.when((chunk >= 0) & (chunk < TREE))
            def _():
                tree.step(k, chunk)

            if k < PlaneFirst.steps:

                @pl.when((chunk >= 0) & (chunk < TILES))
                def _():
                    for part in early:
                        part.step(k, chunk)

                @pl.when((chunk >= TILES) & (chunk <= TREE))
                def _():
                    late[0].step(k, chunk - TILES)

                @pl.when((chunk >= TILES) & (chunk < TREE))
                def _():
                    late[1].step(k, chunk - TILES)

    def block(b):
        return pl.ds(aligned(b * BLOCK, BLOCK), BLOCK)

    loads = [
        pltpu.make_async_copy(s, d, local.at[j])
        for j, (s, d) in enumerate(
            ((h2_ref, h2), (og_ref, og), (bup_ref, bup), (vec_ref, vec))
        )
    ]
    for load in loads:
        load.start()
    dvec[...] = jnp.zeros_like(dvec)

    def feed_forward(out, staged, wu, wd, mine1, mine2, wsem):
        load_x2 = pltpu.make_async_copy(x2_ref, out, local.at[4])
        load_x2.start()

        def weights(i, slot):
            cols = [pl.ds(aligned(h * TILES * TILE + i * TILE, TILE), TILE) for h in (0, 1)]
            parts = []
            for h in (0, 1):
                here = pl.ds(h * TILE, TILE)
                parts.append(
                    pltpu.make_async_copy(
                        wup_ref.at[:, cols[h]], wu.at[slot, :, here], wsem.at[h, slot]
                    )
                )
                parts.append(
                    pltpu.make_async_copy(
                        wdown_ref.at[cols[h], :], wd.at[slot, here, :], wsem.at[2 + h, slot]
                    )
                )
            return parts

        for part in weights(0, 0):
            part.start()
        at.barrier()
        for load in loads:
            load.wait()
        load_x2.wait()
        for b in range(blocks):
            rows = pl.ds(b * BLOCK, BLOCK)
            h2t[:, rows] = h2[rows, :].T
        out[...] = out[...] + vec[7:8, :]
        dh2[...] = jnp.zeros_like(dh2)

        def to_sibling(slot):
            return [
                at.copy_sibling(m.at[slot, 1 - at.core], s.at[slot], gsent.at[j, slot], ggot.at[j, slot])
                for j, (m, s) in enumerate(((mine1, sib1), (mine2, sib2)))
            ]

        def meet(i):
            slot = lax.rem(i, 2)
            for copy in to_sibling(slot):
                copy.wait()
            sum1[i] = mine1[slot, at.core] + sib1[slot]
            sum2[i] = mine2[slot, at.core] + sib2[slot]

        def tile(i, carry):
            slot = lax.rem(i, 2)

            @pl.when(i >= 1)
            def _():
                meet(i - 1)

            turn = i * FF_TICKS // (TILES - 1)

            @pl.when(turn > (i - 1) * FF_TICKS // (TILES - 1))
            def _():
                advance(turn - 1)

            for part in weights(i, slot):
                part.wait()

            @pl.when(i + 1 < TILES)
            def _():
                for part in weights(i + 1, 1 - slot):
                    part.start()

            bias = jnp.concatenate([bup[0, i], bup[1, i]], axis=1)
            u = dot(h2[...], wu[slot], NN) + bias
            a, slope = gelu_and_slope(u)
            a = a.astype(bf16)
            out[...] += dot(a, wd[slot], NN)
            d_wd = dot(a, og[...], TN).astype(bf16)
            mine1[slot, 0] = d_wd[:TILE]
            mine1[slot, 1] = d_wd[TILE:]
            du = (dot(og[...], wd[slot], NT) * slope).astype(bf16)
            d_wu = dot(h2t[...], du, NN).astype(bf16)
            mine2[slot, 0] = d_wu[:HALF]
            mine2[slot, 1] = d_wu[HALF:]
            for copy in to_sibling(slot):
                copy.start()
            dh2[...] += dot(du, wu[slot], NT)
            dbup[i] = jnp.sum(du.astype(f32), axis=0, keepdims=True)
            return carry

        lax.fori_loop(0, TILES, tile, 0)
        meet(TILES - 1)

        def put(b):
            slot = lax.rem(b, 2)
            return pltpu.make_async_copy(staged.at[slot], out_ref.at[block(b), :], local.at[slot])

        def put_rows(b, carry):
            @pl.when(b >= 2)
            def _():
                put(b - 2).wait()

            staged[lax.rem(b, 2)] = out[block(b), :].astype(bf16)
            put(b).start()
            return carry

        lax.fori_loop(0, blocks, put_rows, 0)
        put(blocks - 2).wait()
        put(blocks - 1).wait()

    pl.run_scoped(
        feed_forward,
        pltpu.VMEM((rows_all, WIDTH), f32),
        pltpu.VMEM((2, BLOCK, WIDTH), bf16),
        pltpu.VMEM((2, WIDTH, 2 * TILE), bf16),
        pltpu.VMEM((2, 2 * TILE, WIDTH), bf16),
        pltpu.VMEM((2, 2, TILE, WIDTH), bf16),
        pltpu.VMEM((2, 2, HALF, 2 * TILE), bf16),
        pltpu.SemaphoreType.DMA((4, 2)),
    )

    def attention(aot, dq, dk, dv, w, image, pimage, wide, source, staged, mine3, wsem, isem):
        load_ao = pltpu.make_async_copy(ao_ref, dq, wsem.at[0])
        load_h1 = pltpu.make_async_copy(h1_ref, dk, wsem.at[1])

        def load_w(j, slot):
            return pltpu.make_async_copy(w_ref.at[j], w.at[slot], wsem.at[2 + slot])

        def load_x2(b):
            slot = lax.rem(b, 2)
            return pltpu.make_async_copy(x2_ref.at[block(b), :], wide.at[slot], isem.at[4, slot])

        def load_x(b):
            slot = lax.rem(b, 2)
            return pltpu.make_async_copy(
                tokens_ref.at[pair(b), :], source.at[slot], isem.at[0, slot]
            )

        def put(b):
            slot = lax.rem(b, 2)
            return pltpu.make_async_copy(staged.at[slot], din_ref.at[pair(b), :], isem.at[4, slot])

        def pair(b):
            return pl.ds(aligned(b * 2 * BLOCK, 2 * BLOCK), 2 * BLOCK)

        def load_probs(i):
            slot = lax.rem(i, 2)
            return pltpu.make_async_copy(probs_ref.at[i], pimage.at[slot], isem.at[3, slot])

        def load_image(i):
            slot = lax.rem(i, 2)
            return [
                pltpu.make_async_copy(s.at[block(i), :], image.at[j, slot], isem.at[j, slot])
                for j, s in enumerate((q_ref, k_ref, v_ref))
            ] + [load_probs(i)]

        load_x2(0).start()
        load_w(3, 0).start()
        load_ao.start()
        load_h1.start()
        load_w(1, 1).start()
        load_w(2, 2).start()
        load_probs(0).start()

        def column_sum(j, value):
            dvec[j : j + 1, :] += jnp.sum(value, axis=0, keepdims=True)

        def norm_back(source, gain, incoming):
            center = source - jnp.mean(source, axis=-1, keepdims=True)
            rate = lax.rsqrt(jnp.mean(center * center, axis=-1, keepdims=True) + 1e-06)
            n = center * rate
            scaled = incoming * gain
            first = jnp.mean(scaled, axis=-1, keepdims=True)
            second = jnp.mean(scaled * n, axis=-1, keepdims=True)
            return n, (scaled - first - n * second) * rate

        def second_norm(b, carry):
            @pl.when(b == NORM_TICK)
            def _():
                advance(FF_TICKS)

            load_x2(b).wait()

            @pl.when(b + 1 < blocks)
            def _():
                load_x2(b + 1).start()

            rows = block(b)
            e = dh2[rows, :]
            n, dn = norm_back(wide[lax.rem(b, 2)], vec[5:6, :], e)
            g = og[rows, :].astype(f32)
            dx2 = g + dn
            dt = dx2.astype(bf16)
            dh2[rows, :] = dx2
            h2[rows, :] = dt
            column_sum(5, e * n)
            column_sum(6, e)
            column_sum(7, g)
            column_sum(4, dt.astype(f32))
            return carry

        lax.fori_loop(0, blocks, second_norm, 0)
        load_ao.wait()
        load_h1.wait()
        for b in range(blocks):
            rows = pl.ds(b * BLOCK, BLOCK)
            aot[:, rows] = dq[rows, :].T
            h2t[:, rows] = dk[rows, :].T
        load_w(3, 0).wait()
        for b in range(2):
            rows = pl.ds(b * (rows_all // 2), rows_all // 2)
            og[rows, :] = dot(h2[rows, :], w[0], NT).astype(bf16)
        load_w(0, 0).start()

        def values(i, carry):
            @pl.when(i == VALUE_TICK)
            def _():
                advance(FF_TICKS + 1)

            slot = lax.rem(i, 2)
            load_probs(i).wait()

            @pl.when(i + 1 < blocks)
            def _():
                load_probs(i + 1).start()

            rows = block(i)
            gi = og[rows, :]
            total = Lanes()
            for h in range(HEADS):
                low = pimage[slot, :, h * PATCHES : (h + 1) * PATCHES]
                total.add(h, dot(low, only_head(gi[:, head_window(h)], h), NN))
            dvi = total.joined()
            dv[rows, :] = dvi
            column_sum(3, dvi.astype(f32))
            return carry

        lax.fori_loop(0, blocks, values, 0)
        for copy in load_image(0):
            copy.start()

        def to_sibling(slot):
            return [
                at.copy_sibling(
                    mine3.at[slot, j, 1 - at.core],
                    sib3.at[slot, j],
                    gsent.at[2 + j, slot],
                    ggot.at[2 + j, slot],
                )
                for j in (0, 1)
            ]

        def meet(i):
            slot = lax.rem(i, 2)
            for copy in to_sibling(slot):
                copy.wait()
            for j, (s, c) in enumerate(((sum1, i + TILES), (sum3, i))):
                c = lax.rem(c, s.shape[0])
                s[c] = mine3[slot, j, at.core] + sib3[slot, j]

        def weight_rows(left, right, start, count):
            rows = [left[pl.ds(aligned(h * HALF + start, 64), count), :] for h in (0, 1)]
            return dot(jnp.concatenate(rows, axis=0), right[...], NN).astype(bf16)

        def produce(m, start, one, two):
            slot = lax.rem(m, 2)
            one = weight_rows(*one, start, TILE)
            two = weight_rows(*two, start, TILE)
            for h in (0, 1):
                for j in (0, 1):
                    part = slice(h * TILE + j * 64, h * TILE + j * 64 + 64)
                    mine3[slot, j, h] = jnp.concatenate([one[part], two[part]], axis=0)
            for copy in to_sibling(slot):
                copy.start()

        def heads(i, carry):
            @pl.when(lax.rem(i, 2) == 0)
            def _():
                produce(i // 2, i * 64, (h2t, dv), (aot, h2))

            slot = lax.rem(i, 2)
            for copy in load_image(i):
                copy.wait()

            @pl.when(i + 1 < blocks)
            def _():
                for copy in load_image(i + 1):
                    copy.start()

            @pl.when(lax.rem(i, 2) == 1)
            def _():
                meet(i // 2)
                advance(TILES + i // 2)

            rows = block(i)
            qi, ki, vi, gi = image[0, slot], image[1, slot], image[2, slot], og[rows, :]
            sums = Lanes(), Lanes()
            for h in range(HEADS):
                cols = head_window(h)
                p = pimage[slot, :, h * PATCHES : (h + 1) * PATCHES].astype(f32)
                dp = dot(only_head(vi[:, cols], h), gi[:, cols], NT)
                ds = (p * (dp - jnp.sum(p * dp, axis=0, keepdims=True))).astype(bf16)
                sums[0].add(h, dot(ds, only_head(ki[:, cols], h), TN))
                sums[1].add(h, dot(ds, only_head(qi[:, cols], h), NN))
            dqi, dki = sums[0].joined(SCALE), sums[1].joined(SCALE)
            dq[rows, :] = dqi
            dk[rows, :] = dki
            column_sum(2, dqi.astype(f32))
            return carry

        lax.fori_loop(0, blocks, heads, 0)
        for j in range(3):
            load_w(j, j).wait()
        load_x(0).start()

        vo = weight_rows(h2t, dv, 512, 64), weight_rows(aot, h2, 512, 64)
        qk = weight_rows(h2t, dq, 0, 64), weight_rows(h2t, dk, 0, 64)
        for h in (0, 1):
            part = slice(h * 64, h * 64 + 64)
            for j, (one, two) in enumerate((vo, qk)):
                mine3[0, j, h] = jnp.concatenate([one[part], two[part]], axis=0)
        for copy in to_sibling(0):
            copy.start()

        def weight_gradients(j, carry):
            meet(j - 1)

            @pl.when(j < CHUNKS)
            def _():
                produce(j, (j - 5) * TILE + 64, (h2t, dq), (h2t, dk))

            advance(TILES - 1 + j)

            @pl.when(j < CHUNKS)
            def _():
                b = j - 5
                load_x(b).wait()

                @pl.when(b + 1 < 4)
                def _():
                    load_x(b + 1).start()

                @pl.when(b >= 2)
                def _():
                    put(b - 2).wait()

                rows = pair(b)
                e = dot(dq[rows, :], w[0], NT) + dot(dk[rows, :], w[1], NT)
                e = e + dot(dv[rows, :], w[2], NT)
                x = source[lax.rem(b, 2)].astype(f32)
                n, dn = norm_back(x, vec[0:1, :], e)
                staged[lax.rem(b, 2)] = (dh2[rows, :] + dn).astype(bf16)
                put(b).start()
                column_sum(0, e * n)
                column_sum(1, e)

            return carry

        lax.fori_loop(5, CHUNKS + 1, weight_gradients, 0)
        put(2).wait()
        put(3).wait()

        small[...] = jnp.zeros_like(small)
        small[0:VECTORS, :] = dvec[...]
        for i in range(TILES):
            small[VECTORS + i : VECTORS + i + 1, : 2 * TILE] = dbup[i]
        mine3[1, 1, 0] = jnp.concatenate(
            [small[...].astype(bf16), jnp.zeros((TILE - small.shape[0], WIDTH), bf16)], axis=0
        )
        trade = at.copy_sibling(mine3.at[1, 1, 0], sib3.at[1, 1], gsent.at[3, 1], ggot.at[3, 1])
        trade.start()
        trade.wait()
        sum3[CHUNKS] = mine3[1, 1, 0] + sib3[1, 1]

    flat = pltpu.VMEM((rows_all, WIDTH), bf16)
    pl.run_scoped(
        attention,
        pltpu.VMEM((WIDTH, rows_all), bf16),
        flat,
        flat,
        flat,
        pltpu.VMEM((3, WIDTH, WIDTH), bf16),
        pltpu.VMEM((3, 2, BLOCK, WIDTH), bf16),
        pltpu.VMEM((2, PATCHES, HEADS * PATCHES), bf16),
        pltpu.VMEM((2, BLOCK, WIDTH), f32),
        pltpu.VMEM((2, 2 * BLOCK, WIDTH), bf16),
        pltpu.VMEM((2, 2 * BLOCK, WIDTH), bf16),
        pltpu.VMEM((2, 2, 2, TILE, WIDTH), bf16),
        pltpu.SemaphoreType.DMA((5,)),
        pltpu.SemaphoreType.DMA((5, 2)),
    )

    def drain(tick, carry):
        advance(tick)
        return carry

    lax.fori_loop(TREE, TREE + 8, drain, 0)


def rest_of_layer(tokens, og, h1, q, k, v, ao, probs, x2, h2, w, wup, wdown, vec, bup):
    rows = h2.shape[0]
    flat = jax.ShapeDtypeStruct((rows, WIDTH), bf16)
    return pl.pallas_call(
        rest_kernel,
        out_shape=(
            flat,
            flat,
            jax.ShapeDtypeStruct((SMALL + 1, TILE, WIDTH), bf16),
            jax.ShapeDtypeStruct((TILES, HALF, 2 * TILE), bf16),
        ),
        in_specs=[ANY] * 15,
        out_specs=[ANY] * 4,
        scratch_shapes=[
            pltpu.VMEM((rows, WIDTH), bf16),
            pltpu.VMEM((WIDTH, rows), bf16),
            pltpu.VMEM((rows, WIDTH), bf16),
            pltpu.VMEM((rows, WIDTH), f32),
            pltpu.VMEM((2, TILES, 1, TILE), f32),
            pltpu.VMEM((VECTORS, WIDTH), f32),
            pltpu.VMEM((TILES, 1, 2 * TILE), f32),
            pltpu.VMEM((VECTORS, WIDTH), f32),
            pltpu.VMEM((32, WIDTH), f32),
            pltpu.VMEM((2, TILE, WIDTH), bf16),
            pltpu.VMEM((2, HALF, 2 * TILE), bf16),
            pltpu.VMEM((2, 2, TILE, WIDTH), bf16),
            pltpu.VMEM((TILES + 1, TILE, WIDTH), bf16),
            pltpu.VMEM((TILES, HALF, 2 * TILE), bf16),
            pltpu.VMEM((CHUNKS + 1, TILE, WIDTH), bf16),
            pltpu.SemaphoreType.DMA((5,)),
            pltpu.SemaphoreType.DMA((4, 2)),
            pltpu.SemaphoreType.DMA((4, 2)),
        ]
        + tree_scratch(TILE, WIDTH)
        + flag_scratch(7, 8) * 2
        + plane_scratch(FIRST, 2 * TILE)
        + plane_scratch(SECOND, 2 * TILE)
        + plane_scratch(TILE // 2, WIDTH) * 2,
        compiler_params=pltpu.CompilerParams(
            collective_id=1, has_side_effects=True, vmem_limit_bytes=62 * 2**20
        ),
        name="rest_of_layer",
    )(tokens, og, h1, q, k, v, ao, probs, x2, h2, w, wup, wdown, vec, bup)


def finish_kernel(
    g1_ref, q_ref, k_ref, g2_ref, v_ref, o_ref, d1_ref, d2_ref, dq_ref, dk_ref, dv_ref, do_ref
):
    d1_ref[...] = g1_ref[0].astype(f32)
    parts = []
    for h in (0, 1):
        for i in range(TILES):
            wide = TILE if i < TILES - 1 else FF_HALF - (TILES - 1) * TILE
            parts.append(g2_ref[i, :, h * TILE : h * TILE + wide].astype(f32))
    d2_ref[...] = jnp.concatenate(parts, axis=1)
    for s, d in ((q_ref, dq_ref), (k_ref, dk_ref), (v_ref, dv_ref), (o_ref, do_ref)):
        d[...] = s[0].astype(f32)


def finish(g1, g2):
    steps = HALF // 32
    square = jax.ShapeDtypeStruct((HALF, WIDTH), f32)
    last = TILES - 1

    def quarter(first, offset):
        return pl.BlockSpec((1, 32, WIDTH), lambda i: (first + i // 2, offset + i % 2, 0))

    return pl.pallas_call(
        finish_kernel,
        grid=(steps,),
        out_shape=(
            jax.ShapeDtypeStruct((FF_HALF, WIDTH), f32),
            jax.ShapeDtypeStruct((HALF, FF), f32),
        )
        + (square,) * 4,
        in_specs=[
            pl.BlockSpec((1, TILE, WIDTH), lambda i: (jnp.minimum(i, last), 0, 0)),
            quarter(TREE, 0),
            quarter(TREE, 2),
            pl.BlockSpec((TILES, 32, 2 * TILE), lambda i: (0, i, 0)),
            quarter(TILES, 0),
            quarter(TILES, 2),
        ],
        out_specs=[
            pl.BlockSpec((TILE, WIDTH), lambda i: (jnp.minimum(i, last), 0)),
            pl.BlockSpec((32, FF), lambda i: (i, 0)),
        ]
        + [pl.BlockSpec((32, WIDTH), lambda i: (i, 0))] * 4,
        compiler_params=pltpu.CompilerParams(vmem_limit_bytes=62 * 2**20),
        name="finish",
    )(g1, g1, g1, g2, g1, g1)


def stack_kernel(*refs):
    rows = [r[...].astype(f32).reshape(1, HALF) for r in refs[:-1]]
    rows = jnp.concatenate(rows, axis=0)
    refs[-1][...] = jnp.concatenate([rows, jnp.zeros((VECTORS, LANES - HALF), f32)], axis=1)


def fast_shards(
    tokens,
    out_grad,
    ln1_gain,
    ln1_bias,
    q_weight,
    q_bias,
    k_weight,
    v_weight,
    v_bias,
    o_weight,
    o_bias,
    ln2_gain,
    ln2_bias,
    up_weight,
    up_bias,
    down_weight,
    down_bias,
):
    small = [ln1_gain, ln1_bias, q_bias, v_bias, o_bias, ln2_gain, ln2_bias, down_bias]
    pack = pl.pallas_call(
        stack_kernel, out_shape=jax.ShapeDtypeStruct((VECTORS, LANES), f32), name="stack"
    )(*small)
    gap = TILES * TILE - FF_HALF
    bup = jnp.pad(up_bias.astype(f32), (0, gap)).reshape(TILES, 1, TILE)
    saved = forward(
        tokens, q_weight, k_weight, v_weight, o_weight, up_weight, down_weight, pack, bup
    )
    output, d_input, g1, g2 = rest_of_layer(tokens, out_grad, *saved)
    d_down, d_up, d_q, d_k, d_v, d_o = finish(g1, g2)
    core = lax.axis_index("group")
    vectors = lax.dynamic_slice(g1[SMALL, :VECTORS], (0, core * HALF), (VECTORS, HALF)).astype(f32)
    d_bup = lax.dynamic_slice(
        g1[SMALL, VECTORS : VECTORS + TILES], (0, core * TILE), (TILES, TILE)
    )
    d_bup = d_bup.reshape(TILES * TILE)[:FF_HALF].astype(f32)
    return (
        output,
        d_input,
        vectors[0],
        vectors[1],
        d_q,
        vectors[2],
        d_k,
        d_v,
        vectors[3],
        d_o,
        vectors[4],
        vectors[5],
        vectors[6],
        d_up,
        d_bup,
        d_down,
        vectors[7],
    )


def solution(mesh):
    placed = (
        P(("group", "replica"), None),
        P(("group", "replica"), None),
        P("group"),
        P("group"),
        P("group", None),
        P("group"),
        P("group", None),
        P("group", None),
        P("group"),
        P("group", None),
        P("group"),
        P("group"),
        P("group"),
        P("group", None),
        P("group"),
        P("group", None),
        P("group"),
    )
    fast = mesh.shape["group"] == 2 and mesh.shape["replica"] == 16
    return jax.shard_map(
        fast_shards if fast else shards,
        mesh=mesh,
        in_specs=placed,
        out_specs=(
            P(("group", "replica"), None),
            P(("group", "replica"), None),
            P("group"),
            P("group"),
            P("group", None),
            P("group"),
            P("group", None),
            P("group", None),
            P("group"),
            P("group", None),
            P("group"),
            P("group"),
            P("group"),
            P("group", None),
            P("group"),
            P("group", None),
            P("group"),
        ),
        check_vma=False,
    )
```

```python
import functools

import jax
import jax.numpy as jnp
from jax import lax
from jax.experimental import pallas as pl
from jax.experimental.pallas import tpu as pltpu
from jax.sharding import PartitionSpec as P

HEADS = 16
PATCHES = 128


def layer_norm(values, gain, shift):
    center = values - jnp.mean(values, axis=-1, keepdims=True)
    spread = jnp.mean(center * center, axis=-1, keepdims=True)
    return center * lax.rsqrt(spread + 1e-06) * gain + shift


def gelu_tanh(values):
    return jax.nn.gelu(values, approximate=True)


def split_heads(rows):
    return rows.reshape(-1, PATCHES, HEADS, rows.shape[-1] // HEADS)


def head_logits(query, key_rows):
    factor = (query.shape[-1] // HEADS) ** (-0.5)
    query_h = split_heads(query)
    key_h = split_heads(key_rows)
    logits = (
        jnp.einsum("isha,itha->ihst", query_h, key_h, preferred_element_type=jnp.float32) * factor
    )
    return (logits, query_h, key_h, factor)


def attend(query, key_rows, value_rows):
    logits, query_h, key_h, factor = head_logits(query, key_rows)
    peak = jnp.max(logits, axis=-1, keepdims=True)
    log_total = peak + jnp.log(jnp.sum(jnp.exp(logits - peak), axis=-1, keepdims=True))
    weights_low = jnp.exp(logits - log_total).astype(jnp.bfloat16)
    mixed = jnp.einsum(
        "ihst,itha->isha", weights_low, split_heads(value_rows), preferred_element_type=jnp.float32
    )
    return (mixed.reshape(query.shape), log_total)


def attend_back(query, key_rows, value_rows, log_total, d_mixed):
    logits, query_h, key_h, factor = head_logits(query, key_rows)
    weights = jnp.exp(logits - log_total)
    weights_low = weights.astype(jnp.bfloat16)
    value_h = split_heads(value_rows)
    d_mix_h = split_heads(d_mixed)
    d_weights = jnp.einsum("isha,itha->ihst", d_mix_h, value_h, preferred_element_type=jnp.float32)
    d_logits = weights * (d_weights - jnp.sum(weights * d_weights, axis=-1, keepdims=True))
    d_low = d_logits.astype(jnp.bfloat16)
    d_query = (
        jnp.einsum("ihst,itha->isha", d_low, key_h, preferred_element_type=jnp.float32) * factor
    ).astype(jnp.bfloat16)
    d_key = (
        jnp.einsum("ihst,isha->itha", d_low, query_h, preferred_element_type=jnp.float32) * factor
    ).astype(jnp.bfloat16)
    d_value = jnp.einsum(
        "ihst,isha->itha", weights_low, d_mix_h, preferred_element_type=jnp.float32
    ).astype(jnp.bfloat16)
    return (d_query.reshape(query.shape), d_key.reshape(query.shape), d_value.reshape(query.shape))


def outer_rows(left, right):
    return jnp.einsum("ra,rb->ab", left, right, preferred_element_type=jnp.float32)


def back_rows(grads, weight):
    return jnp.einsum("rb,ab->ra", grads, weight, preferred_element_type=jnp.float32)


def column_sums(grads):
    return jnp.sum(grads.astype(jnp.float32), axis=0)


def shards(
    tokens,
    out_grad,
    ln1_gain,
    ln1_bias,
    q_weight,
    q_bias,
    k_weight,
    v_weight,
    v_bias,
    o_weight,
    o_bias,
    ln2_gain,
    ln2_bias,
    up_weight,
    up_bias,
    down_weight,
    down_bias,
):
    attn_full = tuple(lax.all_gather(v, "group", axis=0, tiled=True) for v in (
        ln1_gain, ln1_bias, q_weight, q_bias, k_weight, v_weight, v_bias, o_weight, o_bias,
    ))
    gain_one, shift_one, wq_full, bq_full, wk_full, wv_full, bv_full, wo_full, bo_full = attn_full
    input_f = tokens.astype(jnp.float32)
    gain_one_f = gain_one.astype(jnp.float32)
    shift_one_f = shift_one.astype(jnp.float32)
    normed1 = layer_norm(input_f, gain_one_f, shift_one_f).astype(jnp.bfloat16)
    query = (
        jnp.dot(normed1, wq_full, preferred_element_type=jnp.float32) + bq_full.astype(jnp.float32)
    ).astype(jnp.bfloat16)
    key_rows = jnp.dot(normed1, wk_full, preferred_element_type=jnp.float32).astype(jnp.bfloat16)
    value_rows = (
        jnp.dot(normed1, wv_full, preferred_element_type=jnp.float32) + bv_full.astype(jnp.float32)
    ).astype(jnp.bfloat16)
    mixed, log_total = attend(query, key_rows, value_rows)
    attn_in = mixed.astype(jnp.bfloat16)
    residual = (
        input_f
        + jnp.dot(attn_in, wo_full, preferred_element_type=jnp.float32)
        + bo_full.astype(jnp.float32)
    )
    mlp_full = tuple(lax.all_gather(v, "group", axis=0, tiled=True) for v in (
        ln2_gain, ln2_bias, up_weight, up_bias, down_weight, down_bias,
    ))
    gain_two, shift_two, wup_full, bup_full, wdown_full, bdown_full = mlp_full
    gain_two_f = gain_two.astype(jnp.float32)
    shift_two_f = shift_two.astype(jnp.float32)
    normed2 = layer_norm(residual, gain_two_f, shift_two_f).astype(jnp.bfloat16)
    pre_act = jnp.dot(normed2, wup_full, preferred_element_type=jnp.float32) + bup_full.astype(
        jnp.float32
    )
    hidden = gelu_tanh(pre_act).astype(jnp.bfloat16)
    output = (
        residual
        + jnp.dot(hidden, wdown_full, preferred_element_type=jnp.float32)
        + bdown_full.astype(jnp.float32)
    )
    mlp_back = tuple(lax.all_gather(v, "group", axis=0, tiled=True) for v in (
        ln2_gain, ln2_bias, up_weight, up_bias, down_weight, down_bias,
    ))
    wup_back = mlp_back[2]
    wdown_back = mlp_back[4]
    grad_out = out_grad.astype(jnp.float32)
    d_wdown = outer_rows(hidden, out_grad)
    d_bdown = column_sums(out_grad)
    d_hidden = back_rows(out_grad, wdown_back)
    unused_act, gelu_back = jax.vjp(gelu_tanh, pre_act)
    d_pre = gelu_back(d_hidden)[0].astype(jnp.bfloat16)
    d_wup = outer_rows(normed2, d_pre)
    d_bup = column_sums(d_pre)
    d_normed2 = back_rows(d_pre, wup_back)
    unused_two, norm_back_two = jax.vjp(layer_norm, residual, gain_two_f, shift_two_f)
    d_res_norm, d_gain_two, d_shift_two = norm_back_two(d_normed2)
    d_residual = grad_out + d_res_norm
    mlp_grads = tuple(
        lax.psum_scatter(v.astype(jnp.bfloat16), "group", scatter_dimension=0, tiled=True).astype(jnp.float32)
        for v in (d_gain_two, d_shift_two, d_wup, d_bup, d_wdown, d_bdown)
    )
    attn_back = tuple(lax.all_gather(v, "group", axis=0, tiled=True) for v in (
        ln1_gain, ln1_bias, q_weight, q_bias, k_weight, v_weight, v_bias, o_weight, o_bias,
    ))
    wq_back = attn_back[2]
    wk_back = attn_back[4]
    wv_back = attn_back[5]
    wo_back = attn_back[7]
    d_attn = d_residual.astype(jnp.bfloat16)
    d_wout = outer_rows(attn_in, d_attn)
    d_bout = column_sums(d_attn)
    d_mixed = back_rows(d_attn, wo_back).astype(jnp.bfloat16)
    d_query, d_key, d_value = attend_back(query, key_rows, value_rows, log_total, d_mixed)
    d_wquery = outer_rows(normed1, d_query)
    d_bquery = column_sums(d_query)
    d_wkey = outer_rows(normed1, d_key)
    d_wvalue = outer_rows(normed1, d_value)
    d_bvalue = column_sums(d_value)
    d_normed1 = (
        back_rows(d_query, wq_back) + back_rows(d_key, wk_back) + back_rows(d_value, wv_back)
    )
    unused_one, norm_back_one = jax.vjp(layer_norm, input_f, gain_one_f, shift_one_f)
    d_in_norm, d_gain_one, d_shift_one = norm_back_one(d_normed1)
    d_input = (d_residual + d_in_norm).astype(jnp.bfloat16)
    attn_grads = tuple(
        lax.psum_scatter(v.astype(jnp.bfloat16), "group", scatter_dimension=0, tiled=True).astype(jnp.float32)
        for v in (d_gain_one, d_shift_one, d_wquery, d_bquery, d_wkey, d_wvalue, d_bvalue, d_wout, d_bout)
    )
    summed = tuple(
        lax.psum(v.astype(jnp.bfloat16), "replica").astype(jnp.float32) for v in attn_grads + mlp_grads
    )
    attn_grads = tuple(summed[:9])
    mlp_grads = tuple(summed[9:])
    return (output.astype(jnp.bfloat16), d_input) + tuple(attn_grads) + tuple(mlp_grads)


MESH = pl.DeviceIdType.MESH
bf16 = jnp.bfloat16
f32 = jnp.float32
ANY = pl.BlockSpec(memory_space=pl.ANY)
WIDTH = 1152
HALF = 576
FF = 4304
FF_HALF = 2152
TILES = 17
TILE = 128
FF_PAD = 2 * TILES * TILE
FIRST = 320
SECOND = 256


class Place:
    def __init__(self):
        self.core = lax.axis_index("group")
        chip = lax.axis_index("replica")
        self.chip = chip
        self.x = lax.rem(chip, 2)
        self.y = lax.rem(chip // 2, 2)
        self.z = chip // 4
        self.x_pair = chip + 1 - 2 * self.x
        self.y_pair = chip + 2 - 4 * self.y
        self.z_pair = chip + 4 - 8 * lax.rem(self.z, 2)
        self.inner = (self.z == 1) | (self.z == 2)
        self.outer = jnp.logical_not(self.inner)
        self.mid_pair = jnp.where(self.inner, chip + 12 - 8 * self.z, chip)
        self.z_half = lax.rem(self.z // 2, 2)

    def barrier(self):
        sem = pltpu.get_barrier_semaphore()

        def greet(core, chip):
            pl.semaphore_signal(sem, inc=1, device_id=(core, chip), device_id_type=MESH)

        greet(1 - self.core, self.chip)
        greet(self.core, self.x_pair)
        greet(self.core, self.y_pair)
        greet(self.core, self.z_pair)

        @pl.when(self.inner)
        def _():
            greet(self.core, self.mid_pair)
            pl.semaphore_wait(sem, 5)

        @pl.when(self.outer)
        def _():
            pl.semaphore_wait(sem, 4)

    def copy(self, source, target, sent, got, chip):
        return pltpu.make_async_remote_copy(
            source, target, sent, got, device_id=(self.core, chip), device_id_type=MESH
        )

    def copy_sibling(self, source, target, sent, got):
        return pltpu.make_async_remote_copy(
            source, target, sent, got, device_id=(1 - self.core, self.chip), device_id_type=MESH
        )


def aligned(value, unit):
    return pl.multiple_of(value, unit)


def landing(slots, chunk):
    return slots.at[lax.rem(chunk, slots.shape[0])]


def add_rows(total, landed, chunk, start, count):
    rows = pl.ds(start, count)
    slot = lax.rem(chunk, total.shape[0])
    total[slot, rows, :] = total[slot, rows, :] + landed[...]


class TreeFirst:
    steps = 9
    after = 0

    def __init__(self, place, total, final, spot, landing, sent, got, kept):
        self.at = place
        self.total = total
        self.final = final
        self.spot = spot
        self.kept = kept
        self.land = landing
        self.sent = sent
        self.got = got
        n = total.shape[1]
        self.n = n
        p = place
        self.own = [
            (0, n),
            (aligned(p.z_half * (n // 2), n // 2), n // 2),
        ]
        self.other = [None, (aligned((1 - p.z_half) * (n // 2), n // 2), n // 2)]
        for bit, part in ((p.y, n // 4), (p.x, n // 8)):
            base = self.own[-1][0]
            self.own.append((aligned(base + bit * part, part), part))
            self.other.append((aligned(base + (1 - bit) * part, part), part))
        self.peer = [p.z_pair, p.mid_pair, p.y_pair, p.x_pair]

    def flags(self, k, chunk):
        slot = lax.rem(chunk + self.after, self.sent.shape[1])
        return self.sent.at[k, slot], self.got.at[k, slot]

    def rows(self, chunk, span):
        return landing(self.total, chunk).at[pl.ds(span[0], span[1]), :]

    def ends(self, chunk, span):
        return self.final.at[self.spot(chunk), pl.ds(span[0], span[1]), :]

    def send(self, k, chunk):
        sent, got = self.flags(k, chunk)
        if k < 4:
            span = self.own[0] if k == 0 else self.other[k]
            return self.at.copy(
                self.rows(chunk, span), landing(self.land[k], chunk), sent, got, self.peer[k]
            )
        level = 7 - k
        target = self.ends(chunk, self.own[level])
        source = self.rows(chunk, self.own[3]) if k == 4 else target
        return self.at.copy(source, target, sent, got, self.peer[level])

    def keep(self, chunk):
        return pltpu.make_async_copy(
            self.rows(chunk, self.own[3]), self.ends(chunk, self.own[3]), landing(self.kept, chunk)
        )

    def arrive(self, k, chunk):
        if k < 4:
            landed = landing(self.land[k], chunk)
        else:
            level = 7 - k
            landed = self.ends(chunk, self.own[0] if level == 0 else self.other[level])
        self.at.copy(landed, landed, *self.flags(k, chunk), self.at.z_pair).wait_recv()

    def step(self, k, chunk):
        at = self.at
        if k == 0:

            @pl.when(at.outer)
            def _():
                self.send(0, chunk).start()

        elif k <= 7:

            @pl.when(at.inner)
            def _():
                self.arrive(k - 1, chunk)
                if k <= 4:
                    add_rows(self.total, landing(self.land[k - 1], chunk), chunk, *self.own[k - 1])
                if k == 4:
                    self.keep(chunk).start()
                if k == 5:
                    self.keep(chunk).wait()
                self.send(k, chunk).start()

        else:

            @pl.when(at.inner)
            def _():
                for j in range(1, 8):
                    self.send(j, chunk).wait_send()

            @pl.when(at.outer)
            def _():
                self.arrive(7, chunk)
                self.send(0, chunk).wait_send()


class PlaneFirst:
    steps = 8

    def __init__(
        self, place, total, final, spot, base, n, x_first, landing, sent, got, kept, after=0
    ):
        self.at = place
        self.after = after
        self.total = total
        self.final = final
        self.spot = spot
        self.kept = kept
        self.land = landing
        self.sent = sent
        self.got = got
        p = place
        if x_first:
            one, two = (p.x, p.x_pair), (p.y, p.y_pair)
        else:
            one, two = (p.y, p.y_pair), (p.x, p.x_pair)
        self.peer_one, self.peer_two = one[1], two[1]
        start = aligned(base + one[0] * (n // 2), 16)
        self.half = (start, n // 2)
        self.half_other = (aligned(base + (1 - one[0]) * (n // 2), 16), n // 2)
        self.quarter = (aligned(start + two[0] * (n // 4), 16), n // 4)
        self.quarter_other = (aligned(start + (1 - two[0]) * (n // 4), 16), n // 4)

    def flags(self, k, chunk):
        slot = lax.rem(chunk + self.after, self.sent.shape[1])
        return self.sent.at[k, slot], self.got.at[k, slot]

    def rows(self, chunk, span):
        return landing(self.total, chunk).at[pl.ds(span[0], span[1]), :]

    def ends(self, chunk, span):
        return self.final.at[self.spot(chunk), pl.ds(span[0], span[1]), :]

    def keep(self, chunk):
        return pltpu.make_async_copy(
            self.rows(chunk, self.quarter), self.ends(chunk, self.quarter), landing(self.kept, chunk + self.after)
        )

    def send(self, k, chunk):
        at = self.at
        quarter = self.rows(chunk, self.quarter)
        quarter_end = self.ends(chunk, self.quarter)
        half_end = self.ends(chunk, self.half)
        source, target, peer = (
            (self.rows(chunk, self.half_other), landing(self.land[0], chunk), self.peer_one),
            (self.rows(chunk, self.quarter_other), landing(self.land[1], chunk), self.peer_two),
            (quarter, landing(self.land[2], chunk), at.z_pair),
            (quarter, landing(self.land[3], chunk), at.mid_pair),
            (quarter, quarter_end, at.z_pair),
            (quarter_end, quarter_end, self.peer_two),
            (half_end, half_end, self.peer_one),
        )[k]
        return at.copy(source, target, *self.flags(k, chunk), peer)

    def arrive(self, k, chunk):
        if k < 4:
            landed = landing(self.land[k], chunk)
        else:
            landed = self.ends(
                chunk, (self.quarter, self.quarter_other, self.half_other)[k - 4]
            )
        self.at.copy(landed, landed, *self.flags(k, chunk), self.at.z_pair).wait_recv()

    def step(self, k, chunk):
        at = self.at
        if k == 0:
            self.send(0, chunk).start()
        elif k == 1:
            self.arrive(0, chunk)
            add_rows(self.total, landing(self.land[0], chunk), chunk, *self.half)
            self.send(1, chunk).start()
        elif k == 2:
            self.arrive(1, chunk)
            add_rows(self.total, landing(self.land[1], chunk), chunk, *self.quarter)

            @pl.when(at.outer)
            def _():
                self.send(2, chunk).start()

        elif k == 3:

            @pl.when(at.inner)
            def _():
                self.arrive(2, chunk)
                add_rows(self.total, landing(self.land[2], chunk), chunk, *self.quarter)
                self.send(3, chunk).start()

        elif k == 4:

            @pl.when(at.inner)
            def _():
                self.arrive(3, chunk)
                self.send(3, chunk).wait_send()
                add_rows(self.total, landing(self.land[3], chunk), chunk, *self.quarter)
                self.send(4, chunk).start()
                self.keep(chunk).start()

        elif k == 5:

            @pl.when(at.inner)
            def _():
                self.keep(chunk).wait()

            @pl.when(at.outer)
            def _():
                self.arrive(4, chunk)

            self.send(5, chunk).start()
        elif k == 6:
            self.arrive(5, chunk)
            self.send(6, chunk).start()
        else:
            self.arrive(6, chunk)
            for j in (0, 1, 5, 6):
                self.send(j, chunk).wait_send()

            @pl.when(at.inner)
            def _():
                self.send(4, chunk).wait_send()

            @pl.when(at.outer)
            def _():
                self.send(2, chunk).wait_send()


def tree_scratch(n, width):
    return [
        pltpu.VMEM((slots, n // part, width), bf16)
        for slots, part in ((10, 1), (3, 2), (3, 4), (3, 8))
    ] + flag_scratch(8, 10)


def plane_scratch(n, width):
    return [
        pltpu.VMEM((slots, n // part, width), bf16)
        for slots, part in ((3, 2), (3, 4), (4, 4), (3, 4))
    ]


def flag_scratch(copies, slots):
    return [
        pltpu.SemaphoreType.DMA((copies, slots)),
        pltpu.SemaphoreType.DMA((copies, slots)),
        pltpu.SemaphoreType.DMA((slots,)),
    ]


def dot(left, right, contract):
    return lax.dot_general(left, right, (contract, ((), ())), preferred_element_type=f32)


NN = ((1,), (0,))
NT = ((1,), (1,))
TN = ((0,), (0,))


def gelu_and_slope(u):
    c = 0.7978845608028654
    square = u * u
    t = jnp.tanh(c * u * (1.0 + 0.044715 * square))
    half = 0.5 * (1.0 + t)
    slope = half + 0.5 * u * (1.0 - t * t) * (c * (1.0 + 3 * 0.044715 * square))
    return u * half, slope


VECTORS = 8
LANES = 640
SCALE = 72**-0.5
HEAD = 72


def head_window(h):
    return slice(h * HEAD // 128 * 128, ((h + 1) * HEAD + 127) // 128 * 128)


def only_head(rows, h):
    lane = lax.broadcasted_iota(jnp.int32, rows.shape, 1) + head_window(h).start
    return jnp.where((lane >= h * HEAD) & (lane < (h + 1) * HEAD), rows, jnp.zeros_like(rows))


class Lanes:
    def __init__(self):
        self.tiles = [None] * (WIDTH // 128)

    def add(self, h, window):
        first = head_window(h).start // 128
        for j in range(window.shape[1] // 128):
            part = window[:, j * 128 : (j + 1) * 128]
            old = self.tiles[first + j]
            self.tiles[first + j] = part if old is None else old + part

    def joined(self, scale=None):
        tiles = self.tiles if scale is None else [t * scale for t in self.tiles]
        return jnp.concatenate([t.astype(bf16) for t in tiles], axis=1)


def normalise(rows, gain, shift):
    center = rows - jnp.mean(rows, axis=-1, keepdims=True)
    spread = jnp.mean(center * center, axis=-1, keepdims=True)
    return center * lax.rsqrt(spread + 1e-06) * gain + shift


def forward_kernel(
    tokens_ref,
    wq_ref,
    wk_ref,
    wv_ref,
    wo_ref,
    up_ref,
    down_ref,
    pack_ref,
    bup_ref,
    h1_ref,
    q_ref,
    k_ref,
    v_ref,
    ao_ref,
    probs_ref,
    x2_ref,
    h2_ref,
    w_ref,
    wup_ref,
    wdown_ref,
    vec_ref,
    bups_ref,
    x,
    h1,
    q,
    k,
    v,
    ao,
    probs,
    x2,
    h2,
    w,
    up,
    up_wide,
    down,
    zeros,
    pack,
    vec,
    local,
    wsem,
    psem,
    sent,
    got,
    bsem,
):
    at = Place()
    core = at.core
    own = pl.ds(aligned(core * HALF, HALF), HALF)
    ff_own = pl.ds(aligned(core * TILES * TILE, TILE), FF_HALF)
    shards = (wq_ref, wk_ref, wv_ref, wo_ref)
    load_x = pltpu.make_async_copy(tokens_ref, x, local.at[0])
    load_x.start()
    load_w = [pltpu.make_async_copy(s, w.at[j, own, :], local.at[1 + j]) for j, s in enumerate(shards)]
    load_pack = pltpu.make_async_copy(pack_ref, pack.at[core], local.at[5])
    load_bup = pltpu.make_async_copy(bup_ref, bups_ref.at[core], local.at[6])
    load_up = pltpu.make_async_copy(up_ref, up, local.at[7])
    load_down = pltpu.make_async_copy(down_ref, down, local.at[8])
    keep_down = pltpu.make_async_copy(down, wdown_ref.at[ff_own, :], wsem.at[4])
    for load in (load_pack, *load_w, load_bup, load_up, load_down):
        load.start()
    zeros[...] = jnp.zeros_like(zeros)
    gap = TILES * TILE - FF_HALF
    blanks = [
        pltpu.make_async_copy(
            zeros, wdown_ref.at[pl.ds(h * TILES * TILE + FF_HALF, gap), :], local.at[9 + h]
        )
        for h in (0, 1)
    ]
    for blank in blanks:
        blank.start()

    bar = pltpu.get_barrier_semaphore()
    pl.semaphore_signal(bar, inc=1, device_id=(1 - core, at.chip), device_id_type=MESH)
    pl.semaphore_wait(bar, 1)

    def share(j, source, target):
        return at.copy_sibling(source, target, sent.at[j], got.at[j])

    give_w = [share(j, s, w.at[j, own, :]) for j, s in enumerate(shards)]
    give_pack = share(4, pack_ref, pack.at[core])
    give_bup = share(5, bup_ref, bups_ref.at[core])
    give_down = share(6, down_ref, wdown_ref.at[ff_own, :])
    give_up = share(7, up_wide, wup_ref.at[own, :])
    keep_up = pltpu.make_async_copy(up_wide, wup_ref.at[own, :], local.at[11])
    give_pack.start()
    for give in give_w:
        give.start()
    give_bup.start()
    give_down.start()

    load_pack.wait()
    give_pack.wait()
    vec[...] = jnp.concatenate([pack[0, :, :HALF], pack[1, :, :HALF]], axis=1)
    load_x.wait()
    rows_of = [pl.ds(b * 512, 512) for b in range(2)]

    def first_norm(b, carry):
        rows = pl.ds(aligned(b * 128, 128), 128)
        h1[rows, :] = normalise(x[rows, :].astype(f32), vec[0:1, :], vec[1:2, :]).astype(bf16)
        return carry

    lax.fori_loop(0, 8, first_norm, 0)
    keep = [pltpu.make_async_copy(h1, h1_ref, local.at[0])]
    keep[0].start()

    def project(j, target, bias):
        load_w[j].wait()
        give_w[j].wait()
        for rows in rows_of:
            y = dot(h1[rows, :], w[j], NN)
            if bias is not None:
                y = y + vec[bias : bias + 1, :]
            target[rows, :] = y.astype(bf16)

    project(0, q, 2)
    project(1, k, None)
    project(2, v, 3)
    for j, (s, d) in enumerate(((q, q_ref), (k, k_ref), (v, v_ref))):
        keep.append(pltpu.make_async_copy(s, d, local.at[12 + j]))
        keep[-1].start()

    load_down.wait()
    keep_down.start()
    load_up.wait()

    def widen(b, carry):
        rows = pl.ds(aligned(b * 64, 64), 64)
        row = up[rows, :]
        none = jnp.zeros((64, gap), bf16)
        up_wide[rows, :] = jnp.concatenate([row[:, :FF_HALF], none, row[:, FF_HALF:], none], axis=1)
        return carry

    lax.fori_loop(0, HALF // 64, widen, 0)
    keep_up.start()
    give_up.start()

    def keep_probs(i):
        slot = lax.rem(i, 2)
        return pltpu.make_async_copy(probs.at[slot], probs_ref.at[i], psem.at[slot])

    def attention(i, carry):
        rows = pl.ds(aligned(i * 128, 128), 128)
        slot = lax.rem(i, 2)

        @pl.when(i >= 2)
        def _():
            keep_probs(i - 2).wait()

        qi, ki, vi = q[rows, :], k[rows, :], v[rows, :]
        mixed = Lanes()
        held = []
        for h in range(HEADS):
            cols = head_window(h)
            logits = dot(only_head(ki[:, cols], h), qi[:, cols], NT) * SCALE
            e = jnp.exp(logits - jnp.max(logits, axis=0, keepdims=True))
            p = (e / jnp.sum(e, axis=0, keepdims=True)).astype(bf16)
            held.append(p)
            mixed.add(h, dot(p, only_head(vi[:, cols], h), TN))
        ao[rows, :] = mixed.joined()
        probs[slot] = jnp.concatenate(held, axis=1)
        keep_probs(i).start()
        return carry

    load_w[3].wait()
    give_w[3].wait()
    keep_w = pltpu.make_async_copy(w, w_ref, wsem.at[0])
    keep_w.start()
    keep_vec = pltpu.make_async_copy(vec, vec_ref, wsem.at[1])
    keep_vec.start()
    lax.fori_loop(0, 8, attention, 0)
    keep_ao = pltpu.make_async_copy(ao, ao_ref, local.at[15])
    keep_ao.start()

    def second_norm(b, carry):
        rows = pl.ds(aligned(b * 128, 128), 128)
        h2[rows, :] = normalise(x2[rows, :], vec[5:6, :], vec[6:7, :]).astype(bf16)
        return carry

    keep_rows = []
    for b, rows in enumerate(rows_of):
        x2[rows, :] = x[rows, :].astype(f32) + dot(ao[rows, :], w[3], NN) + vec[4:5, :]
        keep_rows.append(
            pltpu.make_async_copy(x2.at[rows, :], x2_ref.at[rows, :], wsem.at[2 + b])
        )
        keep_rows[-1].start()
        lax.fori_loop(4 * b, 4 * b + 4, second_norm, 0)
        keep_rows.append(
            pltpu.make_async_copy(h2.at[rows, :], h2_ref.at[rows, :], wsem.at[5 + b])
        )
        keep_rows[-1].start()
    for copy in (
        *keep,
        keep_probs(6),
        keep_probs(7),
        keep_ao,
        keep_w,
        keep_vec,
        load_bup,
        keep_down,
        *blanks,
        keep_up,
        *keep_rows,
    ):
        copy.wait()
    for give in (give_bup, give_down, give_up):
        give.wait()


def forward(tokens, wq, wk, wv, wo, up, down, pack, bup):
    rows = tokens.shape[0]
    images = rows // PATCHES
    flat = jax.ShapeDtypeStruct((rows, WIDTH), bf16)
    return pl.pallas_call(
        forward_kernel,
        out_shape=(
            flat,
            flat,
            flat,
            flat,
            flat,
            jax.ShapeDtypeStruct((images, PATCHES, HEADS * PATCHES), bf16),
            jax.ShapeDtypeStruct((rows, WIDTH), f32),
            flat,
            jax.ShapeDtypeStruct((4, WIDTH, WIDTH), bf16),
            jax.ShapeDtypeStruct((WIDTH, FF_PAD), bf16),
            jax.ShapeDtypeStruct((FF_PAD, WIDTH), bf16),
            jax.ShapeDtypeStruct((VECTORS, WIDTH), f32),
            jax.ShapeDtypeStruct((2, TILES, 1, TILE), f32),
        ),
        in_specs=[ANY] * 9,
        out_specs=[ANY] * 13,
        scratch_shapes=[pltpu.VMEM((rows, WIDTH), bf16)] * 6
        + [
            pltpu.VMEM((2, PATCHES, HEADS * PATCHES), bf16),
            pltpu.VMEM((rows, WIDTH), f32),
            pltpu.VMEM((rows, WIDTH), bf16),
            pltpu.VMEM((4, WIDTH, WIDTH), bf16),
            pltpu.VMEM((HALF, FF), bf16),
            pltpu.VMEM((HALF, FF_PAD), bf16),
            pltpu.VMEM((FF_HALF, WIDTH), bf16),
            pltpu.VMEM((TILES * TILE - FF_HALF, WIDTH), bf16),
            pltpu.VMEM((2, VECTORS, LANES), f32),
            pltpu.VMEM((VECTORS, WIDTH), f32),
            pltpu.SemaphoreType.DMA((16,)),
            pltpu.SemaphoreType.DMA((7,)),
            pltpu.SemaphoreType.DMA((2,)),
            pltpu.SemaphoreType.DMA((8,)),
            pltpu.SemaphoreType.DMA((8,)),
            pltpu.SemaphoreType.DMA((1,)),
        ],
        compiler_params=pltpu.CompilerParams(
            collective_id=3, has_side_effects=True, vmem_limit_bytes=62 * 2**20
        ),
        name="forward",
    )(tokens, wq, wk, wv, wo, up, down, pack, bup)


CHUNKS = 9
TREE = TILES + CHUNKS
SMALL = TILES + 2 * CHUNKS + 1
BLOCK = 128
FF_TICKS = 15
NORM_TICK = 4
VALUE_TICK = 3


def rest_kernel(
    tokens_ref,
    og_ref,
    h1_ref,
    q_ref,
    k_ref,
    v_ref,
    ao_ref,
    probs_ref,
    x2_ref,
    h2_ref,
    w_ref,
    wup_ref,
    wdown_ref,
    vec_ref,
    bup_ref,
    out_ref,
    din_ref,
    g1_ref,
    g2_ref,
    h2,
    h2t,
    og,
    dh2,
    bup,
    vec,
    dbup,
    dvec,
    small,
    sib1,
    sib2,
    sib3,
    sum1,
    sum2,
    sum3,
    local,
    gsent,
    ggot,
    *comm,
):
    at = Place()
    rows_all = h2.shape[0]
    blocks = rows_all // BLOCK
    flags = comm[7:10], comm[10:13]
    planes = [comm[j : j + 4] for j in range(13, 29, 4)]

    def tree_spot(chunk):
        late = chunk - TILES
        value_or_query = jnp.where(late < 5, 2 * late, CHUNKS + 2 * late - 9)
        return jnp.where(chunk < TILES, chunk, TILES + value_or_query)

    def late_spot(chunk):
        return TILES + jnp.where(chunk < 4, 2 * chunk + 1, CHUNKS + 2 * chunk - 8)

    tree = TreeFirst(at, sum1, g1_ref, tree_spot, comm[:4], *comm[4:7])
    early = [
        PlaneFirst(at, sum2, g2_ref, lambda c: c, base, n, j == 0, planes[j], *flags[j])
        for j, base, n in ((0, 0, FIRST), (1, FIRST, SECOND))
    ]
    late = [
        PlaneFirst(
            at, sum3, g1_ref, late_spot, base, TILE // 2, j == 0, planes[2 + j], *flags[j], TILES
        )
        for j, base in ((0, 0), (1, TILE // 2))
    ]

    def advance(tick):
        for k in reversed(range(TreeFirst.steps)):
            chunk = tick - k

            @pl.when((chunk >= 0) & (chunk < TREE))
            def _():
                tree.step(k, chunk)

            if k < PlaneFirst.steps:

                @pl.when((chunk >= 0) & (chunk < TILES))
                def _():
                    for part in early:
                        part.step(k, chunk)

                @pl.when((chunk >= TILES) & (chunk <= TREE))
                def _():
                    late[0].step(k, chunk - TILES)

                @pl.when((chunk >= TILES) & (chunk < TREE))
                def _():
                    late[1].step(k, chunk - TILES)

    def block(b):
        return pl.ds(aligned(b * BLOCK, BLOCK), BLOCK)

    loads = [
        pltpu.make_async_copy(s, d, local.at[j])
        for j, (s, d) in enumerate(
            ((h2_ref, h2), (og_ref, og), (bup_ref, bup), (vec_ref, vec))
        )
    ]
    for load in loads:
        load.start()
    dvec[...] = jnp.zeros_like(dvec)

    def feed_forward(out, staged, wu, wd, mine1, mine2, wsem):
        load_x2 = pltpu.make_async_copy(x2_ref, out, local.at[4])
        load_x2.start()

        def weights(i, slot):
            cols = [pl.ds(aligned(h * TILES * TILE + i * TILE, TILE), TILE) for h in (0, 1)]
            parts = []
            for h in (0, 1):
                here = pl.ds(h * TILE, TILE)
                parts.append(
                    pltpu.make_async_copy(
                        wup_ref.at[:, cols[h]], wu.at[slot, :, here], wsem.at[h, slot]
                    )
                )
                parts.append(
                    pltpu.make_async_copy(
                        wdown_ref.at[cols[h], :], wd.at[slot, here, :], wsem.at[2 + h, slot]
                    )
                )
            return parts

        for part in weights(0, 0):
            part.start()
        at.barrier()
        for load in loads:
            load.wait()
        load_x2.wait()
        for b in range(blocks):
            rows = pl.ds(b * BLOCK, BLOCK)
            h2t[:, rows] = h2[rows, :].T
        out[...] = out[...] + vec[7:8, :]
        dh2[...] = jnp.zeros_like(dh2)

        def to_sibling(slot):
            return [
                at.copy_sibling(m.at[slot, 1 - at.core], s.at[slot], gsent.at[j, slot], ggot.at[j, slot])
                for j, (m, s) in enumerate(((mine1, sib1), (mine2, sib2)))
            ]

        def meet(i):
            slot = lax.rem(i, 2)
            for copy in to_sibling(slot):
                copy.wait()
            sum1[i] = mine1[slot, at.core] + sib1[slot]
            sum2[i] = mine2[slot, at.core] + sib2[slot]

        def tile(i, carry):
            slot = lax.rem(i, 2)

            @pl.when(i >= 1)
            def _():
                meet(i - 1)

            turn = i * FF_TICKS // (TILES - 1)

            @pl.when(turn > (i - 1) * FF_TICKS // (TILES - 1))
            def _():
                advance(turn - 1)

            for part in weights(i, slot):
                part.wait()

            @pl.when(i + 1 < TILES)
            def _():
                for part in weights(i + 1, 1 - slot):
                    part.start()

            bias = jnp.concatenate([bup[0, i], bup[1, i]], axis=1)
            u = dot(h2[...], wu[slot], NN) + bias
            a, slope = gelu_and_slope(u)
            a = a.astype(bf16)
            out[...] += dot(a, wd[slot], NN)
            d_wd = dot(a, og[...], TN).astype(bf16)
            mine1[slot, 0] = d_wd[:TILE]
            mine1[slot, 1] = d_wd[TILE:]
            du = (dot(og[...], wd[slot], NT) * slope).astype(bf16)
            d_wu = dot(h2t[...], du, NN).astype(bf16)
            mine2[slot, 0] = d_wu[:HALF]
            mine2[slot, 1] = d_wu[HALF:]
            for copy in to_sibling(slot):
                copy.start()
            dh2[...] += dot(du, wu[slot], NT)
            dbup[i] = jnp.sum(du.astype(f32), axis=0, keepdims=True)
            return carry

        lax.fori_loop(0, TILES, tile, 0)
        meet(TILES - 1)

        def put(b):
            slot = lax.rem(b, 2)
            return pltpu.make_async_copy(staged.at[slot], out_ref.at[block(b), :], local.at[slot])

        def put_rows(b, carry):
            @pl.when(b >= 2)
            def _():
                put(b - 2).wait()

            staged[lax.rem(b, 2)] = out[block(b), :].astype(bf16)
            put(b).start()
            return carry

        lax.fori_loop(0, blocks, put_rows, 0)
        put(blocks - 2).wait()
        put(blocks - 1).wait()

    pl.run_scoped(
        feed_forward,
        pltpu.VMEM((rows_all, WIDTH), f32),
        pltpu.VMEM((2, BLOCK, WIDTH), bf16),
        pltpu.VMEM((2, WIDTH, 2 * TILE), bf16),
        pltpu.VMEM((2, 2 * TILE, WIDTH), bf16),
        pltpu.VMEM((2, 2, TILE, WIDTH), bf16),
        pltpu.VMEM((2, 2, HALF, 2 * TILE), bf16),
        pltpu.SemaphoreType.DMA((4, 2)),
    )

    def attention(aot, dq, dk, dv, w, image, pimage, wide, source, staged, mine3, wsem, isem):
        load_ao = pltpu.make_async_copy(ao_ref, dq, wsem.at[0])
        load_h1 = pltpu.make_async_copy(h1_ref, dk, wsem.at[1])

        def load_w(j, slot):
            return pltpu.make_async_copy(w_ref.at[j], w.at[slot], wsem.at[2 + slot])

        def load_x2(b):
            slot = lax.rem(b, 2)
            return pltpu.make_async_copy(x2_ref.at[block(b), :], wide.at[slot], isem.at[4, slot])

        def load_x(b):
            slot = lax.rem(b, 2)
            return pltpu.make_async_copy(
                tokens_ref.at[pair(b), :], source.at[slot], isem.at[0, slot]
            )

        def put(b):
            slot = lax.rem(b, 2)
            return pltpu.make_async_copy(staged.at[slot], din_ref.at[pair(b), :], isem.at[4, slot])

        def pair(b):
            return pl.ds(aligned(b * 2 * BLOCK, 2 * BLOCK), 2 * BLOCK)

        def load_probs(i):
            slot = lax.rem(i, 2)
            return pltpu.make_async_copy(probs_ref.at[i], pimage.at[slot], isem.at[3, slot])

        def load_image(i):
            slot = lax.rem(i, 2)
            return [
                pltpu.make_async_copy(s.at[block(i), :], image.at[j, slot], isem.at[j, slot])
                for j, s in enumerate((q_ref, k_ref, v_ref))
            ] + [load_probs(i)]

        load_x2(0).start()
        load_w(3, 0).start()
        load_ao.start()
        load_h1.start()
        load_w(1, 1).start()
        load_w(2, 2).start()
        load_probs(0).start()

        def column_sum(j, value):
            dvec[j : j + 1, :] += jnp.sum(value, axis=0, keepdims=True)

        def norm_back(source, gain, incoming):
            center = source - jnp.mean(source, axis=-1, keepdims=True)
            rate = lax.rsqrt(jnp.mean(center * center, axis=-1, keepdims=True) + 1e-06)
            n = center * rate
            scaled = incoming * gain
            first = jnp.mean(scaled, axis=-1, keepdims=True)
            second = jnp.mean(scaled * n, axis=-1, keepdims=True)
            return n, (scaled - first - n * second) * rate

        def second_norm(b, carry):
            @pl.when(b == NORM_TICK)
            def _():
                advance(FF_TICKS)

            load_x2(b).wait()

            @pl.when(b + 1 < blocks)
            def _():
                load_x2(b + 1).start()

            rows = block(b)
            e = dh2[rows, :]
            n, dn = norm_back(wide[lax.rem(b, 2)], vec[5:6, :], e)
            g = og[rows, :].astype(f32)
            dx2 = g + dn
            dt = dx2.astype(bf16)
            dh2[rows, :] = dx2
            h2[rows, :] = dt
            column_sum(5, e * n)
            column_sum(6, e)
            column_sum(7, g)
            column_sum(4, dt.astype(f32))
            return carry

        lax.fori_loop(0, blocks, second_norm, 0)
        load_ao.wait()
        load_h1.wait()
        for b in range(blocks):
            rows = pl.ds(b * BLOCK, BLOCK)
            aot[:, rows] = dq[rows, :].T
            h2t[:, rows] = dk[rows, :].T
        load_w(3, 0).wait()
        for b in range(2):
            rows = pl.ds(b * (rows_all // 2), rows_all // 2)
            og[rows, :] = dot(h2[rows, :], w[0], NT).astype(bf16)
        load_w(0, 0).start()

        def values(i, carry):
            @pl.when(i == VALUE_TICK)
            def _():
                advance(FF_TICKS + 1)

            slot = lax.rem(i, 2)
            load_probs(i).wait()

            @pl.when(i + 1 < blocks)
            def _():
                load_probs(i + 1).start()

            rows = block(i)
            gi = og[rows, :]
            total = Lanes()
            for h in range(HEADS):
                low = pimage[slot, :, h * PATCHES : (h + 1) * PATCHES]
                total.add(h, dot(low, only_head(gi[:, head_window(h)], h), NN))
            dvi = total.joined()
            dv[rows, :] = dvi
            column_sum(3, dvi.astype(f32))
            return carry

        lax.fori_loop(0, blocks, values, 0)
        for copy in load_image(0):
            copy.start()

        def to_sibling(slot):
            return [
                at.copy_sibling(
                    mine3.at[slot, j, 1 - at.core],
                    sib3.at[slot, j],
                    gsent.at[2 + j, slot],
                    ggot.at[2 + j, slot],
                )
                for j in (0, 1)
            ]

        def meet(i):
            slot = lax.rem(i, 2)
            for copy in to_sibling(slot):
                copy.wait()
            for j, (s, c) in enumerate(((sum1, i + TILES), (sum3, i))):
                c = lax.rem(c, s.shape[0])
                s[c] = mine3[slot, j, at.core] + sib3[slot, j]

        def weight_rows(left, right, start, count):
            rows = [left[pl.ds(aligned(h * HALF + start, 64), count), :] for h in (0, 1)]
            return dot(jnp.concatenate(rows, axis=0), right[...], NN).astype(bf16)

        def produce(m, start, one, two):
            slot = lax.rem(m, 2)
            one = weight_rows(*one, start, TILE)
            two = weight_rows(*two, start, TILE)
            for h in (0, 1):
                for j in (0, 1):
                    part = slice(h * TILE + j * 64, h * TILE + j * 64 + 64)
                    mine3[slot, j, h] = jnp.concatenate([one[part], two[part]], axis=0)
            for copy in to_sibling(slot):
                copy.start()

        def heads(i, carry):
            @pl.when(lax.rem(i, 2) == 0)
            def _():
                produce(i // 2, i * 64, (h2t, dv), (aot, h2))

            slot = lax.rem(i, 2)
            for copy in load_image(i):
                copy.wait()

            @pl.when(i + 1 < blocks)
            def _():
                for copy in load_image(i + 1):
                    copy.start()

            @pl.when(lax.rem(i, 2) == 1)
            def _():
                meet(i // 2)
                advance(TILES + i // 2)

            rows = block(i)
            qi, ki, vi, gi = image[0, slot], image[1, slot], image[2, slot], og[rows, :]
            sums = Lanes(), Lanes()
            for h in range(HEADS):
                cols = head_window(h)
                p = pimage[slot, :, h * PATCHES : (h + 1) * PATCHES].astype(f32)
                dp = dot(only_head(vi[:, cols], h), gi[:, cols], NT)
                ds = (p * (dp - jnp.sum(p * dp, axis=0, keepdims=True))).astype(bf16)
                sums[0].add(h, dot(ds, only_head(ki[:, cols], h), TN))
                sums[1].add(h, dot(ds, only_head(qi[:, cols], h), NN))
            dqi, dki = sums[0].joined(SCALE), sums[1].joined(SCALE)
            dq[rows, :] = dqi
            dk[rows, :] = dki
            column_sum(2, dqi.astype(f32))
            return carry

        lax.fori_loop(0, blocks, heads, 0)
        for j in range(3):
            load_w(j, j).wait()
        load_x(0).start()

        vo = weight_rows(h2t, dv, 512, 64), weight_rows(aot, h2, 512, 64)
        qk = weight_rows(h2t, dq, 0, 64), weight_rows(h2t, dk, 0, 64)
        for h in (0, 1):
            part = slice(h * 64, h * 64 + 64)
            for j, (one, two) in enumerate((vo, qk)):
                mine3[0, j, h] = jnp.concatenate([one[part], two[part]], axis=0)
        for copy in to_sibling(0):
            copy.start()

        def weight_gradients(j, carry):
            meet(j - 1)

            @pl.when(j < CHUNKS)
            def _():
                produce(j, (j - 5) * TILE + 64, (h2t, dq), (h2t, dk))

            advance(TILES - 1 + j)

            @pl.when(j < CHUNKS)
            def _():
                b = j - 5
                load_x(b).wait()

                @pl.when(b + 1 < 4)
                def _():
                    load_x(b + 1).start()

                @pl.when(b >= 2)
                def _():
                    put(b - 2).wait()

                rows = pair(b)
                e = dot(dq[rows, :], w[0], NT) + dot(dk[rows, :], w[1], NT)
                e = e + dot(dv[rows, :], w[2], NT)
                x = source[lax.rem(b, 2)].astype(f32)
                n, dn = norm_back(x, vec[0:1, :], e)
                staged[lax.rem(b, 2)] = (dh2[rows, :] + dn).astype(bf16)
                put(b).start()
                column_sum(0, e * n)
                column_sum(1, e)

            return carry

        lax.fori_loop(5, CHUNKS + 1, weight_gradients, 0)
        put(2).wait()
        put(3).wait()

        small[...] = jnp.zeros_like(small)
        small[0:VECTORS, :] = dvec[...]
        for i in range(TILES):
            small[VECTORS + i : VECTORS + i + 1, : 2 * TILE] = dbup[i]
        mine3[1, 1, 0] = jnp.concatenate(
            [small[...].astype(bf16), jnp.zeros((TILE - small.shape[0], WIDTH), bf16)], axis=0
        )
        trade = at.copy_sibling(mine3.at[1, 1, 0], sib3.at[1, 1], gsent.at[3, 1], ggot.at[3, 1])
        trade.start()
        trade.wait()
        sum3[CHUNKS] = mine3[1, 1, 0] + sib3[1, 1]

    flat = pltpu.VMEM((rows_all, WIDTH), bf16)
    pl.run_scoped(
        attention,
        pltpu.VMEM((WIDTH, rows_all), bf16),
        flat,
        flat,
        flat,
        pltpu.VMEM((3, WIDTH, WIDTH), bf16),
        pltpu.VMEM((3, 2, BLOCK, WIDTH), bf16),
        pltpu.VMEM((2, PATCHES, HEADS * PATCHES), bf16),
        pltpu.VMEM((2, BLOCK, WIDTH), f32),
        pltpu.VMEM((2, 2 * BLOCK, WIDTH), bf16),
        pltpu.VMEM((2, 2 * BLOCK, WIDTH), bf16),
        pltpu.VMEM((2, 2, 2, TILE, WIDTH), bf16),
        pltpu.SemaphoreType.DMA((5,)),
        pltpu.SemaphoreType.DMA((5, 2)),
    )

    def drain(tick, carry):
        advance(tick)
        return carry

    lax.fori_loop(TREE, TREE + 8, drain, 0)


def rest_of_layer(tokens, og, h1, q, k, v, ao, probs, x2, h2, w, wup, wdown, vec, bup):
    rows = h2.shape[0]
    flat = jax.ShapeDtypeStruct((rows, WIDTH), bf16)
    return pl.pallas_call(
        rest_kernel,
        out_shape=(
            flat,
            flat,
            jax.ShapeDtypeStruct((SMALL + 1, TILE, WIDTH), bf16),
            jax.ShapeDtypeStruct((TILES, HALF, 2 * TILE), bf16),
        ),
        in_specs=[ANY] * 15,
        out_specs=[ANY] * 4,
        scratch_shapes=[
            pltpu.VMEM((rows, WIDTH), bf16),
            pltpu.VMEM((WIDTH, rows), bf16),
            pltpu.VMEM((rows, WIDTH), bf16),
            pltpu.VMEM((rows, WIDTH), f32),
            pltpu.VMEM((2, TILES, 1, TILE), f32),
            pltpu.VMEM((VECTORS, WIDTH), f32),
            pltpu.VMEM((TILES, 1, 2 * TILE), f32),
            pltpu.VMEM((VECTORS, WIDTH), f32),
            pltpu.VMEM((32, WIDTH), f32),
            pltpu.VMEM((2, TILE, WIDTH), bf16),
            pltpu.VMEM((2, HALF, 2 * TILE), bf16),
            pltpu.VMEM((2, 2, TILE, WIDTH), bf16),
            pltpu.VMEM((TILES + 1, TILE, WIDTH), bf16),
            pltpu.VMEM((TILES, HALF, 2 * TILE), bf16),
            pltpu.VMEM((CHUNKS + 1, TILE, WIDTH), bf16),
            pltpu.SemaphoreType.DMA((5,)),
            pltpu.SemaphoreType.DMA((4, 2)),
            pltpu.SemaphoreType.DMA((4, 2)),
        ]
        + tree_scratch(TILE, WIDTH)
        + flag_scratch(7, 8) * 2
        + plane_scratch(FIRST, 2 * TILE)
        + plane_scratch(SECOND, 2 * TILE)
        + plane_scratch(TILE // 2, WIDTH) * 2,
        compiler_params=pltpu.CompilerParams(
            collective_id=1, has_side_effects=True, vmem_limit_bytes=62 * 2**20
        ),
        name="rest_of_layer",
    )(tokens, og, h1, q, k, v, ao, probs, x2, h2, w, wup, wdown, vec, bup)


def finish_kernel(
    g1_ref,
    q_ref,
    k_ref,
    g2_ref,
    v_ref,
    o_ref,
    out_ref,
    din_ref,
    d1_ref,
    d2_ref,
    dq_ref,
    dk_ref,
    dv_ref,
    do_ref,
    out_end,
    din_end,
):
    d1_ref[...] = g1_ref[...].reshape(2 * TILE, WIDTH).astype(f32)
    parts = []
    for h in (0, 1):
        for i in range(TILES):
            wide = TILE if i < TILES - 1 else FF_HALF - (TILES - 1) * TILE
            parts.append(g2_ref[i, :, h * TILE : h * TILE + wide].astype(f32))
    d2_ref[...] = jnp.concatenate(parts, axis=1)
    for s, d in ((q_ref, dq_ref), (k_ref, dk_ref), (v_ref, dv_ref), (o_ref, do_ref)):
        d[...] = s[0].astype(f32)
    out_end[...] = out_ref[...]
    din_end[...] = din_ref[...]


def finish(g1, g2, output, d_input):
    steps = HALF // 64
    square = jax.ShapeDtypeStruct((HALF, WIDTH), f32)
    blocks = output.shape[0] // BLOCK
    flat = pl.BlockSpec((BLOCK, WIDTH), lambda i: (jnp.minimum(i, blocks - 1), 0))

    def half_chunk(first, part):
        return pl.BlockSpec((1, 64, WIDTH), lambda i: (first + i, part, 0))

    return pl.pallas_call(
        finish_kernel,
        grid=(steps,),
        out_shape=(
            jax.ShapeDtypeStruct((FF_HALF, WIDTH), f32),
            jax.ShapeDtypeStruct((HALF, FF), f32),
        )
        + (square,) * 4
        + (jax.ShapeDtypeStruct(output.shape, bf16),) * 2,
        in_specs=[
            pl.BlockSpec((2, TILE, WIDTH), lambda i: (i, 0, 0)),
            half_chunk(TREE, 0),
            half_chunk(TREE, 1),
            pl.BlockSpec((TILES, 64, 2 * TILE), lambda i: (0, i, 0)),
            half_chunk(TILES, 0),
            half_chunk(TILES, 1),
            flat,
            flat,
        ],
        out_specs=[
            pl.BlockSpec((2 * TILE, WIDTH), lambda i: (i, 0)),
            pl.BlockSpec((64, FF), lambda i: (i, 0)),
        ]
        + [pl.BlockSpec((64, WIDTH), lambda i: (i, 0))] * 4
        + [flat] * 2,
        compiler_params=pltpu.CompilerParams(vmem_limit_bytes=62 * 2**20),
        name="finish",
    )(g1, g1, g1, g2, g1, g1, output, d_input)


def stack_kernel(*refs):
    rows = [r[...].astype(f32).reshape(1, HALF) for r in refs[:-1]]
    rows = jnp.concatenate(rows, axis=0)
    refs[-1][...] = jnp.concatenate([rows, jnp.zeros((VECTORS, LANES - HALF), f32)], axis=1)


def fast_shards(
    tokens,
    out_grad,
    ln1_gain,
    ln1_bias,
    q_weight,
    q_bias,
    k_weight,
    v_weight,
    v_bias,
    o_weight,
    o_bias,
    ln2_gain,
    ln2_bias,
    up_weight,
    up_bias,
    down_weight,
    down_bias,
):
    small = [ln1_gain, ln1_bias, q_bias, v_bias, o_bias, ln2_gain, ln2_bias, down_bias]
    pack = pl.pallas_call(
        stack_kernel, out_shape=jax.ShapeDtypeStruct((VECTORS, LANES), f32), name="stack"
    )(*small)
    gap = TILES * TILE - FF_HALF
    bup = jnp.pad(up_bias.astype(f32), (0, gap)).reshape(TILES, 1, TILE)
    saved = forward(
        tokens, q_weight, k_weight, v_weight, o_weight, up_weight, down_weight, pack, bup
    )
    output, d_input, g1, g2 = rest_of_layer(tokens, out_grad, *saved)
    d_down, d_up, d_q, d_k, d_v, d_o, output, d_input = finish(g1, g2, output, d_input)
    core = lax.axis_index("group")
    vectors = lax.dynamic_slice(g1[SMALL, :VECTORS], (0, core * HALF), (VECTORS, HALF)).astype(f32)
    d_bup = lax.dynamic_slice(
        g1[SMALL, VECTORS : VECTORS + TILES], (0, core * TILE), (TILES, TILE)
    )
    d_bup = d_bup.reshape(TILES * TILE)[:FF_HALF].astype(f32)
    return (
        output,
        d_input,
        vectors[0],
        vectors[1],
        d_q,
        vectors[2],
        d_k,
        d_v,
        vectors[3],
        d_o,
        vectors[4],
        vectors[5],
        vectors[6],
        d_up,
        d_bup,
        d_down,
        vectors[7],
    )


def solution(mesh):
    placed = (
        P(("group", "replica"), None),
        P(("group", "replica"), None),
        P("group"),
        P("group"),
        P("group", None),
        P("group"),
        P("group", None),
        P("group", None),
        P("group"),
        P("group", None),
        P("group"),
        P("group"),
        P("group"),
        P("group", None),
        P("group"),
        P("group", None),
        P("group"),
    )
    fast = mesh.shape["group"] == 2 and mesh.shape["replica"] == 16
    return jax.shard_map(
        fast_shards if fast else shards,
        mesh=mesh,
        in_specs=placed,
        out_specs=(
            P(("group", "replica"), None),
            P(("group", "replica"), None),
            P("group"),
            P("group"),
            P("group", None),
            P("group"),
            P("group", None),
            P("group", None),
            P("group"),
            P("group", None),
            P("group"),
            P("group"),
            P("group"),
            P("group", None),
            P("group"),
            P("group", None),
            P("group"),
        ),
        check_vma=False,
    )
```

```python
import functools

import jax
import jax.numpy as jnp
from jax import lax
from jax.experimental import pallas as pl
from jax.experimental.pallas import tpu as pltpu
from jax.sharding import PartitionSpec as P

HEADS = 16
PATCHES = 128


def layer_norm(values, gain, shift):
    center = values - jnp.mean(values, axis=-1, keepdims=True)
    spread = jnp.mean(center * center, axis=-1, keepdims=True)
    return center * lax.rsqrt(spread + 1e-06) * gain + shift


def gelu_tanh(values):
    return jax.nn.gelu(values, approximate=True)


def split_heads(rows):
    return rows.reshape(-1, PATCHES, HEADS, rows.shape[-1] // HEADS)


def head_logits(query, key_rows):
    factor = (query.shape[-1] // HEADS) ** (-0.5)
    query_h = split_heads(query)
    key_h = split_heads(key_rows)
    logits = (
        jnp.einsum("isha,itha->ihst", query_h, key_h, preferred_element_type=jnp.float32) * factor
    )
    return (logits, query_h, key_h, factor)


def attend(query, key_rows, value_rows):
    logits, query_h, key_h, factor = head_logits(query, key_rows)
    peak = jnp.max(logits, axis=-1, keepdims=True)
    log_total = peak + jnp.log(jnp.sum(jnp.exp(logits - peak), axis=-1, keepdims=True))
    weights_low = jnp.exp(logits - log_total).astype(jnp.bfloat16)
    mixed = jnp.einsum(
        "ihst,itha->isha", weights_low, split_heads(value_rows), preferred_element_type=jnp.float32
    )
    return (mixed.reshape(query.shape), log_total)


def attend_back(query, key_rows, value_rows, log_total, d_mixed):
    logits, query_h, key_h, factor = head_logits(query, key_rows)
    weights = jnp.exp(logits - log_total)
    weights_low = weights.astype(jnp.bfloat16)
    value_h = split_heads(value_rows)
    d_mix_h = split_heads(d_mixed)
    d_weights = jnp.einsum("isha,itha->ihst", d_mix_h, value_h, preferred_element_type=jnp.float32)
    d_logits = weights * (d_weights - jnp.sum(weights * d_weights, axis=-1, keepdims=True))
    d_low = d_logits.astype(jnp.bfloat16)
    d_query = (
        jnp.einsum("ihst,itha->isha", d_low, key_h, preferred_element_type=jnp.float32) * factor
    ).astype(jnp.bfloat16)
    d_key = (
        jnp.einsum("ihst,isha->itha", d_low, query_h, preferred_element_type=jnp.float32) * factor
    ).astype(jnp.bfloat16)
    d_value = jnp.einsum(
        "ihst,isha->itha", weights_low, d_mix_h, preferred_element_type=jnp.float32
    ).astype(jnp.bfloat16)
    return (d_query.reshape(query.shape), d_key.reshape(query.shape), d_value.reshape(query.shape))


def outer_rows(left, right):
    return jnp.einsum("ra,rb->ab", left, right, preferred_element_type=jnp.float32)


def back_rows(grads, weight):
    return jnp.einsum("rb,ab->ra", grads, weight, preferred_element_type=jnp.float32)


def column_sums(grads):
    return jnp.sum(grads.astype(jnp.float32), axis=0)


def shards(
    tokens,
    out_grad,
    ln1_gain,
    ln1_bias,
    q_weight,
    q_bias,
    k_weight,
    v_weight,
    v_bias,
    o_weight,
    o_bias,
    ln2_gain,
    ln2_bias,
    up_weight,
    up_bias,
    down_weight,
    down_bias,
):
    attn_full = tuple(lax.all_gather(v, "group", axis=0, tiled=True) for v in (
        ln1_gain, ln1_bias, q_weight, q_bias, k_weight, v_weight, v_bias, o_weight, o_bias,
    ))
    gain_one, shift_one, wq_full, bq_full, wk_full, wv_full, bv_full, wo_full, bo_full = attn_full
    input_f = tokens.astype(jnp.float32)
    gain_one_f = gain_one.astype(jnp.float32)
    shift_one_f = shift_one.astype(jnp.float32)
    normed1 = layer_norm(input_f, gain_one_f, shift_one_f).astype(jnp.bfloat16)
    query = (
        jnp.dot(normed1, wq_full, preferred_element_type=jnp.float32) + bq_full.astype(jnp.float32)
    ).astype(jnp.bfloat16)
    key_rows = jnp.dot(normed1, wk_full, preferred_element_type=jnp.float32).astype(jnp.bfloat16)
    value_rows = (
        jnp.dot(normed1, wv_full, preferred_element_type=jnp.float32) + bv_full.astype(jnp.float32)
    ).astype(jnp.bfloat16)
    mixed, log_total = attend(query, key_rows, value_rows)
    attn_in = mixed.astype(jnp.bfloat16)
    residual = (
        input_f
        + jnp.dot(attn_in, wo_full, preferred_element_type=jnp.float32)
        + bo_full.astype(jnp.float32)
    )
    mlp_full = tuple(lax.all_gather(v, "group", axis=0, tiled=True) for v in (
        ln2_gain, ln2_bias, up_weight, up_bias, down_weight, down_bias,
    ))
    gain_two, shift_two, wup_full, bup_full, wdown_full, bdown_full = mlp_full
    gain_two_f = gain_two.astype(jnp.float32)
    shift_two_f = shift_two.astype(jnp.float32)
    normed2 = layer_norm(residual, gain_two_f, shift_two_f).astype(jnp.bfloat16)
    pre_act = jnp.dot(normed2, wup_full, preferred_element_type=jnp.float32) + bup_full.astype(
        jnp.float32
    )
    hidden = gelu_tanh(pre_act).astype(jnp.bfloat16)
    output = (
        residual
        + jnp.dot(hidden, wdown_full, preferred_element_type=jnp.float32)
        + bdown_full.astype(jnp.float32)
    )
    mlp_back = tuple(lax.all_gather(v, "group", axis=0, tiled=True) for v in (
        ln2_gain, ln2_bias, up_weight, up_bias, down_weight, down_bias,
    ))
    wup_back = mlp_back[2]
    wdown_back = mlp_back[4]
    grad_out = out_grad.astype(jnp.float32)
    d_wdown = outer_rows(hidden, out_grad)
    d_bdown = column_sums(out_grad)
    d_hidden = back_rows(out_grad, wdown_back)
    unused_act, gelu_back = jax.vjp(gelu_tanh, pre_act)
    d_pre = gelu_back(d_hidden)[0].astype(jnp.bfloat16)
    d_wup = outer_rows(normed2, d_pre)
    d_bup = column_sums(d_pre)
    d_normed2 = back_rows(d_pre, wup_back)
    unused_two, norm_back_two = jax.vjp(layer_norm, residual, gain_two_f, shift_two_f)
    d_res_norm, d_gain_two, d_shift_two = norm_back_two(d_normed2)
    d_residual = grad_out + d_res_norm
    mlp_grads = tuple(
        lax.psum_scatter(v.astype(jnp.bfloat16), "group", scatter_dimension=0, tiled=True).astype(jnp.float32)
        for v in (d_gain_two, d_shift_two, d_wup, d_bup, d_wdown, d_bdown)
    )
    attn_back = tuple(lax.all_gather(v, "group", axis=0, tiled=True) for v in (
        ln1_gain, ln1_bias, q_weight, q_bias, k_weight, v_weight, v_bias, o_weight, o_bias,
    ))
    wq_back = attn_back[2]
    wk_back = attn_back[4]
    wv_back = attn_back[5]
    wo_back = attn_back[7]
    d_attn = d_residual.astype(jnp.bfloat16)
    d_wout = outer_rows(attn_in, d_attn)
    d_bout = column_sums(d_attn)
    d_mixed = back_rows(d_attn, wo_back).astype(jnp.bfloat16)
    d_query, d_key, d_value = attend_back(query, key_rows, value_rows, log_total, d_mixed)
    d_wquery = outer_rows(normed1, d_query)
    d_bquery = column_sums(d_query)
    d_wkey = outer_rows(normed1, d_key)
    d_wvalue = outer_rows(normed1, d_value)
    d_bvalue = column_sums(d_value)
    d_normed1 = (
        back_rows(d_query, wq_back) + back_rows(d_key, wk_back) + back_rows(d_value, wv_back)
    )
    unused_one, norm_back_one = jax.vjp(layer_norm, input_f, gain_one_f, shift_one_f)
    d_in_norm, d_gain_one, d_shift_one = norm_back_one(d_normed1)
    d_input = (d_residual + d_in_norm).astype(jnp.bfloat16)
    attn_grads = tuple(
        lax.psum_scatter(v.astype(jnp.bfloat16), "group", scatter_dimension=0, tiled=True).astype(jnp.float32)
        for v in (d_gain_one, d_shift_one, d_wquery, d_bquery, d_wkey, d_wvalue, d_bvalue, d_wout, d_bout)
    )
    summed = tuple(
        lax.psum(v.astype(jnp.bfloat16), "replica").astype(jnp.float32) for v in attn_grads + mlp_grads
    )
    attn_grads = tuple(summed[:9])
    mlp_grads = tuple(summed[9:])
    return (output.astype(jnp.bfloat16), d_input) + tuple(attn_grads) + tuple(mlp_grads)


MESH = pl.DeviceIdType.MESH
bf16 = jnp.bfloat16
f32 = jnp.float32
ANY = pl.BlockSpec(memory_space=pl.ANY)
WIDTH = 1152
HALF = 576
FF = 4304
FF_HALF = 2152
TILES = 17
TILE = 128
FF_PAD = 2 * TILES * TILE
FIRST = 320
SECOND = 256


class Place:
    def __init__(self):
        self.core = lax.axis_index("group")
        chip = lax.axis_index("replica")
        self.chip = chip
        self.x = lax.rem(chip, 2)
        self.y = lax.rem(chip // 2, 2)
        self.z = chip // 4
        self.x_pair = chip + 1 - 2 * self.x
        self.y_pair = chip + 2 - 4 * self.y
        self.z_pair = chip + 4 - 8 * lax.rem(self.z, 2)
        self.inner = (self.z == 1) | (self.z == 2)
        self.outer = jnp.logical_not(self.inner)
        self.mid_pair = jnp.where(self.inner, chip + 12 - 8 * self.z, chip)
        self.z_half = lax.rem(self.z // 2, 2)

    def barrier(self):
        sem = pltpu.get_barrier_semaphore()

        def greet(core, chip):
            pl.semaphore_signal(sem, inc=1, device_id=(core, chip), device_id_type=MESH)

        greet(1 - self.core, self.chip)
        greet(self.core, self.x_pair)
        greet(self.core, self.y_pair)
        greet(self.core, self.z_pair)

        @pl.when(self.inner)
        def _():
            greet(self.core, self.mid_pair)
            pl.semaphore_wait(sem, 5)

        @pl.when(self.outer)
        def _():
            pl.semaphore_wait(sem, 4)

    def copy(self, source, target, sent, got, chip):
        return pltpu.make_async_remote_copy(
            source, target, sent, got, device_id=(self.core, chip), device_id_type=MESH
        )

    def copy_sibling(self, source, target, sent, got):
        return pltpu.make_async_remote_copy(
            source, target, sent, got, device_id=(1 - self.core, self.chip), device_id_type=MESH
        )


def aligned(value, unit):
    return pl.multiple_of(value, unit)


def landing(slots, chunk):
    return slots.at[lax.rem(chunk, slots.shape[0])]


def add_rows(total, landed, chunk, start, count):
    rows = pl.ds(start, count)
    slot = lax.rem(chunk, total.shape[0])
    total[slot, rows, :] = total[slot, rows, :] + landed[...]


class TreeFirst:
    steps = 9
    after = 0

    def __init__(self, place, total, final, spot, landing, sent, got, kept):
        self.at = place
        self.total = total
        self.final = final
        self.spot = spot
        self.kept = kept
        self.land = landing
        self.sent = sent
        self.got = got
        n = total.shape[1]
        self.n = n
        p = place
        self.own = [
            (0, n),
            (aligned(p.z_half * (n // 2), n // 2), n // 2),
        ]
        self.other = [None, (aligned((1 - p.z_half) * (n // 2), n // 2), n // 2)]
        for bit, part in ((p.y, n // 4), (p.x, n // 8)):
            base = self.own[-1][0]
            self.own.append((aligned(base + bit * part, part), part))
            self.other.append((aligned(base + (1 - bit) * part, part), part))
        self.peer = [p.z_pair, p.mid_pair, p.y_pair, p.x_pair]

    def flags(self, k, chunk):
        slot = lax.rem(chunk + self.after, self.sent.shape[1])
        return self.sent.at[k, slot], self.got.at[k, slot]

    def rows(self, chunk, span):
        return landing(self.total, chunk).at[pl.ds(span[0], span[1]), :]

    def ends(self, chunk, span):
        return self.final.at[self.spot(chunk), pl.ds(span[0], span[1]), :]

    def send(self, k, chunk):
        sent, got = self.flags(k, chunk)
        if k < 4:
            span = self.own[0] if k == 0 else self.other[k]
            return self.at.copy(
                self.rows(chunk, span), landing(self.land[k], chunk), sent, got, self.peer[k]
            )
        level = 7 - k
        target = self.ends(chunk, self.own[level])
        source = self.rows(chunk, self.own[3]) if k == 4 else target
        return self.at.copy(source, target, sent, got, self.peer[level])

    def keep(self, chunk):
        return pltpu.make_async_copy(
            self.rows(chunk, self.own[3]), self.ends(chunk, self.own[3]), landing(self.kept, chunk)
        )

    def arrive(self, k, chunk):
        if k < 4:
            landed = landing(self.land[k], chunk)
        else:
            level = 7 - k
            landed = self.ends(chunk, self.own[0] if level == 0 else self.other[level])
        self.at.copy(landed, landed, *self.flags(k, chunk), self.at.z_pair).wait_recv()

    def step(self, k, chunk):
        at = self.at
        if k == 0:

            @pl.when(at.outer)
            def _():
                self.send(0, chunk).start()

        elif k <= 7:

            @pl.when(at.inner)
            def _():
                self.arrive(k - 1, chunk)
                if k <= 4:
                    add_rows(self.total, landing(self.land[k - 1], chunk), chunk, *self.own[k - 1])
                if k == 4:
                    self.keep(chunk).start()
                if k == 5:
                    self.keep(chunk).wait()
                self.send(k, chunk).start()

        else:

            @pl.when(at.inner)
            def _():
                for j in range(1, 8):
                    self.send(j, chunk).wait_send()

            @pl.when(at.outer)
            def _():
                self.arrive(7, chunk)
                self.send(0, chunk).wait_send()


class PlaneFirst:
    steps = 8

    def __init__(
        self, place, total, final, spot, base, n, x_first, landing, sent, got, kept, after=0
    ):
        self.at = place
        self.after = after
        self.total = total
        self.final = final
        self.spot = spot
        self.kept = kept
        self.land = landing
        self.sent = sent
        self.got = got
        p = place
        if x_first:
            one, two = (p.x, p.x_pair), (p.y, p.y_pair)
        else:
            one, two = (p.y, p.y_pair), (p.x, p.x_pair)
        self.peer_one, self.peer_two = one[1], two[1]
        start = aligned(base + one[0] * (n // 2), 16)
        self.half = (start, n // 2)
        self.half_other = (aligned(base + (1 - one[0]) * (n // 2), 16), n // 2)
        self.quarter = (aligned(start + two[0] * (n // 4), 16), n // 4)
        self.quarter_other = (aligned(start + (1 - two[0]) * (n // 4), 16), n // 4)

    def flags(self, k, chunk):
        slot = lax.rem(chunk + self.after, self.sent.shape[1])
        return self.sent.at[k, slot], self.got.at[k, slot]

    def rows(self, chunk, span):
        return landing(self.total, chunk).at[pl.ds(span[0], span[1]), :]

    def ends(self, chunk, span):
        return self.final.at[self.spot(chunk), pl.ds(span[0], span[1]), :]

    def keep(self, chunk):
        return pltpu.make_async_copy(
            self.rows(chunk, self.quarter), self.ends(chunk, self.quarter), landing(self.kept, chunk + self.after)
        )

    def send(self, k, chunk):
        at = self.at
        quarter = self.rows(chunk, self.quarter)
        quarter_end = self.ends(chunk, self.quarter)
        half_end = self.ends(chunk, self.half)
        source, target, peer = (
            (self.rows(chunk, self.half_other), landing(self.land[0], chunk), self.peer_one),
            (self.rows(chunk, self.quarter_other), landing(self.land[1], chunk), self.peer_two),
            (quarter, landing(self.land[2], chunk), at.z_pair),
            (quarter, landing(self.land[3], chunk), at.mid_pair),
            (quarter, quarter_end, at.z_pair),
            (quarter_end, quarter_end, self.peer_two),
            (half_end, half_end, self.peer_one),
        )[k]
        return at.copy(source, target, *self.flags(k, chunk), peer)

    def arrive(self, k, chunk):
        if k < 4:
            landed = landing(self.land[k], chunk)
        else:
            landed = self.ends(
                chunk, (self.quarter, self.quarter_other, self.half_other)[k - 4]
            )
        self.at.copy(landed, landed, *self.flags(k, chunk), self.at.z_pair).wait_recv()

    def step(self, k, chunk):
        at = self.at
        if k == 0:
            self.send(0, chunk).start()
        elif k == 1:
            self.arrive(0, chunk)
            add_rows(self.total, landing(self.land[0], chunk), chunk, *self.half)
            self.send(1, chunk).start()
        elif k == 2:
            self.arrive(1, chunk)
            add_rows(self.total, landing(self.land[1], chunk), chunk, *self.quarter)

            @pl.when(at.outer)
            def _():
                self.send(2, chunk).start()

        elif k == 3:

            @pl.when(at.inner)
            def _():
                self.arrive(2, chunk)
                add_rows(self.total, landing(self.land[2], chunk), chunk, *self.quarter)
                self.send(3, chunk).start()

        elif k == 4:

            @pl.when(at.inner)
            def _():
                self.arrive(3, chunk)
                self.send(3, chunk).wait_send()
                add_rows(self.total, landing(self.land[3], chunk), chunk, *self.quarter)
                self.send(4, chunk).start()
                self.keep(chunk).start()

        elif k == 5:

            @pl.when(at.inner)
            def _():
                self.keep(chunk).wait()

            @pl.when(at.outer)
            def _():
                self.arrive(4, chunk)

            self.send(5, chunk).start()
        elif k == 6:
            self.arrive(5, chunk)
            self.send(6, chunk).start()
        else:
            self.arrive(6, chunk)
            for j in (0, 1, 5, 6):
                self.send(j, chunk).wait_send()

            @pl.when(at.inner)
            def _():
                self.send(4, chunk).wait_send()

            @pl.when(at.outer)
            def _():
                self.send(2, chunk).wait_send()


def tree_scratch(n, width):
    return [
        pltpu.VMEM((slots, n // part, width), bf16)
        for slots, part in ((10, 1), (3, 2), (3, 4), (3, 8))
    ] + flag_scratch(8, 10)


def plane_scratch(n, width):
    return [
        pltpu.VMEM((slots, n // part, width), bf16)
        for slots, part in ((4, 2), (3, 4), (4, 4), (3, 4))
    ]


def flag_scratch(copies, slots):
    return [
        pltpu.SemaphoreType.DMA((copies, slots)),
        pltpu.SemaphoreType.DMA((copies, slots)),
        pltpu.SemaphoreType.DMA((slots,)),
    ]


def dot(left, right, contract):
    return lax.dot_general(left, right, (contract, ((), ())), preferred_element_type=f32)


NN = ((1,), (0,))
NT = ((1,), (1,))
TN = ((0,), (0,))


def gelu_and_slope(u):
    c = 0.7978845608028654
    square = u * u
    t = jnp.tanh(c * u * (1.0 + 0.044715 * square))
    half = 0.5 * (1.0 + t)
    slope = half + 0.5 * u * (1.0 - t * t) * (c * (1.0 + 3 * 0.044715 * square))
    return u * half, slope


VECTORS = 8
LANES = 640
SCALE = 72**-0.5
HEAD = 72


def head_window(h):
    return slice(h * HEAD // 128 * 128, ((h + 1) * HEAD + 127) // 128 * 128)


def only_head(rows, h):
    lane = lax.broadcasted_iota(jnp.int32, rows.shape, 1) + head_window(h).start
    return jnp.where((lane >= h * HEAD) & (lane < (h + 1) * HEAD), rows, jnp.zeros_like(rows))


class Lanes:
    def __init__(self):
        self.tiles = [None] * (WIDTH // 128)

    def add(self, h, window):
        first = head_window(h).start // 128
        for j in range(window.shape[1] // 128):
            part = window[:, j * 128 : (j + 1) * 128]
            old = self.tiles[first + j]
            self.tiles[first + j] = part if old is None else old + part

    def joined(self, scale=None):
        tiles = self.tiles if scale is None else [t * scale for t in self.tiles]
        return jnp.concatenate([t.astype(bf16) for t in tiles], axis=1)


def normalise(rows, gain, shift):
    center = rows - jnp.mean(rows, axis=-1, keepdims=True)
    spread = jnp.mean(center * center, axis=-1, keepdims=True)
    return center * lax.rsqrt(spread + 1e-06) * gain + shift


def forward_kernel(
    tokens_ref,
    wq_ref,
    wk_ref,
    wv_ref,
    wo_ref,
    up_ref,
    down_ref,
    pack_ref,
    bup_ref,
    h1_ref,
    q_ref,
    k_ref,
    v_ref,
    ao_ref,
    probs_ref,
    x2_ref,
    h2_ref,
    w_ref,
    wup_ref,
    wdown_ref,
    vec_ref,
    bups_ref,
    x,
    h1,
    q,
    k,
    v,
    ao,
    probs,
    x2,
    h2,
    w,
    up,
    up_wide,
    down,
    zeros,
    pack,
    vec,
    local,
    wsem,
    psem,
    sent,
    got,
    bsem,
):
    at = Place()
    core = at.core
    own = pl.ds(aligned(core * HALF, HALF), HALF)
    ff_own = pl.ds(aligned(core * TILES * TILE, TILE), FF_HALF)
    shards = (wq_ref, wk_ref, wv_ref, wo_ref)
    load_x = pltpu.make_async_copy(tokens_ref, x, local.at[0])
    load_x.start()
    load_w = [pltpu.make_async_copy(s, w.at[j, own, :], local.at[1 + j]) for j, s in enumerate(shards)]
    load_pack = pltpu.make_async_copy(pack_ref, pack.at[core], local.at[5])
    load_bup = pltpu.make_async_copy(bup_ref, bups_ref.at[core], local.at[6])
    load_up = pltpu.make_async_copy(up_ref, up, local.at[7])
    load_down = pltpu.make_async_copy(down_ref, down, local.at[8])
    keep_down = pltpu.make_async_copy(down, wdown_ref.at[ff_own, :], wsem.at[4])
    for load in (load_pack, *load_w, load_bup, load_up, load_down):
        load.start()
    zeros[...] = jnp.zeros_like(zeros)
    gap = TILES * TILE - FF_HALF
    blanks = [
        pltpu.make_async_copy(
            zeros, wdown_ref.at[pl.ds(h * TILES * TILE + FF_HALF, gap), :], local.at[9 + h]
        )
        for h in (0, 1)
    ]
    for blank in blanks:
        blank.start()

    bar = pltpu.get_barrier_semaphore()
    pl.semaphore_signal(bar, inc=1, device_id=(1 - core, at.chip), device_id_type=MESH)
    pl.semaphore_wait(bar, 1)

    def share(j, source, target):
        return at.copy_sibling(source, target, sent.at[j], got.at[j])

    give_w = [share(j, s, w.at[j, own, :]) for j, s in enumerate(shards)]
    give_pack = share(4, pack_ref, pack.at[core])
    give_bup = share(5, bup_ref, bups_ref.at[core])
    give_down = share(6, down_ref, wdown_ref.at[ff_own, :])
    give_up = share(7, up_wide, wup_ref.at[own, :])
    keep_up = pltpu.make_async_copy(up_wide, wup_ref.at[own, :], local.at[11])
    give_pack.start()
    for give in give_w:
        give.start()
    give_bup.start()
    give_down.start()

    load_pack.wait()
    give_pack.wait()
    vec[...] = jnp.concatenate([pack[0, :, :HALF], pack[1, :, :HALF]], axis=1)
    load_x.wait()
    rows_of = [pl.ds(b * 512, 512) for b in range(2)]

    def first_norm(b, carry):
        rows = pl.ds(aligned(b * 128, 128), 128)
        h1[rows, :] = normalise(x[rows, :].astype(f32), vec[0:1, :], vec[1:2, :]).astype(bf16)
        return carry

    lax.fori_loop(0, 8, first_norm, 0)
    keep = [pltpu.make_async_copy(h1, h1_ref, local.at[0])]
    keep[0].start()

    def project(j, target, bias):
        load_w[j].wait()
        give_w[j].wait()
        for rows in rows_of:
            y = dot(h1[rows, :], w[j], NN)
            if bias is not None:
                y = y + vec[bias : bias + 1, :]
            target[rows, :] = y.astype(bf16)

    project(0, q, 2)
    project(1, k, None)
    project(2, v, 3)
    for j, (s, d) in enumerate(((q, q_ref), (k, k_ref), (v, v_ref))):
        keep.append(pltpu.make_async_copy(s, d, local.at[12 + j]))
        keep[-1].start()

    load_down.wait()
    keep_down.start()
    load_up.wait()

    def widen(b, carry):
        rows = pl.ds(aligned(b * 64, 64), 64)
        row = up[rows, :]
        none = jnp.zeros((64, gap), bf16)
        up_wide[rows, :] = jnp.concatenate([row[:, :FF_HALF], none, row[:, FF_HALF:], none], axis=1)
        return carry

    lax.fori_loop(0, HALF // 64, widen, 0)
    keep_up.start()
    give_up.start()

    def keep_probs(i):
        slot = lax.rem(i, 2)
        return pltpu.make_async_copy(probs.at[slot], probs_ref.at[i], psem.at[slot])

    def attention(i, carry):
        rows = pl.ds(aligned(i * 128, 128), 128)
        slot = lax.rem(i, 2)

        @pl.when(i >= 2)
        def _():
            keep_probs(i - 2).wait()

        qi, ki, vi = q[rows, :], k[rows, :], v[rows, :]
        mixed = Lanes()
        held = []
        for h in range(HEADS):
            cols = head_window(h)
            logits = dot(only_head(ki[:, cols], h), qi[:, cols], NT) * SCALE
            e = jnp.exp(logits - jnp.max(logits, axis=0, keepdims=True))
            p = (e / jnp.sum(e, axis=0, keepdims=True)).astype(bf16)
            held.append(p)
            mixed.add(h, dot(p, only_head(vi[:, cols], h), TN))
        ao[rows, :] = mixed.joined()
        probs[slot] = jnp.concatenate(held, axis=1)
        keep_probs(i).start()
        return carry

    load_w[3].wait()
    give_w[3].wait()
    keep_w = pltpu.make_async_copy(w, w_ref, wsem.at[0])
    keep_w.start()
    keep_vec = pltpu.make_async_copy(vec, vec_ref, wsem.at[1])
    keep_vec.start()
    lax.fori_loop(0, 8, attention, 0)
    keep_ao = pltpu.make_async_copy(ao, ao_ref, local.at[15])
    keep_ao.start()

    def second_norm(b, carry):
        rows = pl.ds(aligned(b * 128, 128), 128)
        h2[rows, :] = normalise(x2[rows, :], vec[5:6, :], vec[6:7, :]).astype(bf16)
        return carry

    keep_rows = []
    for b, rows in enumerate(rows_of):
        x2[rows, :] = x[rows, :].astype(f32) + dot(ao[rows, :], w[3], NN) + vec[4:5, :]
        keep_rows.append(
            pltpu.make_async_copy(x2.at[rows, :], x2_ref.at[rows, :], wsem.at[2 + b])
        )
        keep_rows[-1].start()
        lax.fori_loop(4 * b, 4 * b + 4, second_norm, 0)
        keep_rows.append(
            pltpu.make_async_copy(h2.at[rows, :], h2_ref.at[rows, :], wsem.at[5 + b])
        )
        keep_rows[-1].start()
    for copy in (
        *keep,
        keep_probs(6),
        keep_probs(7),
        keep_ao,
        keep_w,
        keep_vec,
        load_bup,
        keep_down,
        *blanks,
        keep_up,
        *keep_rows,
    ):
        copy.wait()
    for give in (give_bup, give_down, give_up):
        give.wait()


def forward(tokens, wq, wk, wv, wo, up, down, pack, bup):
    rows = tokens.shape[0]
    images = rows // PATCHES
    flat = jax.ShapeDtypeStruct((rows, WIDTH), bf16)
    return pl.pallas_call(
        forward_kernel,
        out_shape=(
            flat,
            flat,
            flat,
            flat,
            flat,
            jax.ShapeDtypeStruct((images, PATCHES, HEADS * PATCHES), bf16),
            jax.ShapeDtypeStruct((rows, WIDTH), f32),
            flat,
            jax.ShapeDtypeStruct((4, WIDTH, WIDTH), bf16),
            jax.ShapeDtypeStruct((WIDTH, FF_PAD), bf16),
            jax.ShapeDtypeStruct((FF_PAD, WIDTH), bf16),
            jax.ShapeDtypeStruct((VECTORS, WIDTH), f32),
            jax.ShapeDtypeStruct((2, TILES, 1, TILE), f32),
        ),
        in_specs=[ANY] * 9,
        out_specs=[ANY] * 13,
        scratch_shapes=[pltpu.VMEM((rows, WIDTH), bf16)] * 6
        + [
            pltpu.VMEM((2, PATCHES, HEADS * PATCHES), bf16),
            pltpu.VMEM((rows, WIDTH), f32),
            pltpu.VMEM((rows, WIDTH), bf16),
            pltpu.VMEM((4, WIDTH, WIDTH), bf16),
            pltpu.VMEM((HALF, FF), bf16),
            pltpu.VMEM((HALF, FF_PAD), bf16),
            pltpu.VMEM((FF_HALF, WIDTH), bf16),
            pltpu.VMEM((TILES * TILE - FF_HALF, WIDTH), bf16),
            pltpu.VMEM((2, VECTORS, LANES), f32),
            pltpu.VMEM((VECTORS, WIDTH), f32),
            pltpu.SemaphoreType.DMA((16,)),
            pltpu.SemaphoreType.DMA((7,)),
            pltpu.SemaphoreType.DMA((2,)),
            pltpu.SemaphoreType.DMA((8,)),
            pltpu.SemaphoreType.DMA((8,)),
            pltpu.SemaphoreType.DMA((1,)),
        ],
        compiler_params=pltpu.CompilerParams(
            collective_id=3, has_side_effects=True, vmem_limit_bytes=62 * 2**20
        ),
        name="forward",
    )(tokens, wq, wk, wv, wo, up, down, pack, bup)


CHUNKS = 9
TREE = TILES + CHUNKS
SMALL = TILES + 2 * CHUNKS + 1
BLOCK = 128
FF_TICKS = 15
NORM_TICK = 4
VALUE_TICK = 3


def rest_kernel(
    tokens_ref,
    og_ref,
    h1_ref,
    q_ref,
    k_ref,
    v_ref,
    ao_ref,
    probs_ref,
    x2_ref,
    h2_ref,
    w_ref,
    wup_ref,
    wdown_ref,
    vec_ref,
    bup_ref,
    out_ref,
    din_ref,
    g1_ref,
    g2_ref,
    h2,
    h2t,
    og,
    dh2,
    bup,
    vec,
    dbup,
    dvec,
    small,
    sib1,
    sib2,
    sib3,
    sum1,
    sum2,
    sum3,
    local,
    gsent,
    ggot,
    *comm,
):
    at = Place()
    rows_all = h2.shape[0]
    blocks = rows_all // BLOCK
    flags = comm[7:10], comm[10:13]
    planes = [comm[j : j + 4] for j in range(13, 29, 4)]

    def tree_spot(chunk):
        late = chunk - TILES
        value_or_query = jnp.where(late < 5, 2 * late, CHUNKS + 2 * late - 9)
        return jnp.where(chunk < TILES, chunk, TILES + value_or_query)

    def late_spot(chunk):
        return TILES + jnp.where(chunk < 4, 2 * chunk + 1, CHUNKS + 2 * chunk - 8)

    tree = TreeFirst(at, sum1, g1_ref, tree_spot, comm[:4], *comm[4:7])
    early = [
        PlaneFirst(at, sum2, g2_ref, lambda c: c, base, n, j == 0, planes[j], *flags[j])
        for j, base, n in ((0, 0, FIRST), (1, FIRST, SECOND))
    ]
    late = [
        PlaneFirst(
            at, sum3, g1_ref, late_spot, base, TILE // 2, j == 0, planes[2 + j], *flags[j], TILES
        )
        for j, base in ((0, 0), (1, TILE // 2))
    ]

    def advance(tick):
        for k, j in ((0, 0), (7, 6), (6, 5), (5, 4), (4, 3), (3, 2), (2, 1), (1, None), (8, 7)):
            chunk = tick - k

            @pl.when((chunk >= 0) & (chunk < TREE))
            def _():
                tree.step(k, chunk)

            if j is not None:
                part = tick - j

                @pl.when((part >= 0) & (part < TILES))
                def _():
                    early[0].step(j, part)
                    early[1].step(j, part)

                @pl.when((part >= TILES) & (part <= TREE))
                def _():
                    late[0].step(j, part - TILES)

                @pl.when((part >= TILES) & (part < TREE))
                def _():
                    late[1].step(j, part - TILES)

    def block(b):
        return pl.ds(aligned(b * BLOCK, BLOCK), BLOCK)

    loads = [
        pltpu.make_async_copy(s, d, local.at[j])
        for j, (s, d) in enumerate(
            ((h2_ref, h2), (og_ref, og), (bup_ref, bup), (vec_ref, vec))
        )
    ]
    for load in loads:
        load.start()
    dvec[...] = jnp.zeros_like(dvec)

    def feed_forward(out, staged, wu, wd, mine1, mine2, wsem):
        load_x2 = pltpu.make_async_copy(x2_ref, out, local.at[4])
        load_x2.start()

        def weights(i, slot):
            cols = [pl.ds(aligned(h * TILES * TILE + i * TILE, TILE), TILE) for h in (0, 1)]
            parts = []
            for h in (0, 1):
                here = pl.ds(h * TILE, TILE)
                parts.append(
                    pltpu.make_async_copy(
                        wup_ref.at[:, cols[h]], wu.at[slot, :, here], wsem.at[h, slot]
                    )
                )
                parts.append(
                    pltpu.make_async_copy(
                        wdown_ref.at[cols[h], :], wd.at[slot, here, :], wsem.at[2 + h, slot]
                    )
                )
            return parts

        for part in weights(0, 0):
            part.start()
        at.barrier()
        for load in loads:
            load.wait()
        load_x2.wait()
        for b in range(blocks):
            rows = pl.ds(b * BLOCK, BLOCK)
            h2t[:, rows] = h2[rows, :].T
        out[...] = out[...] + vec[7:8, :]
        dh2[...] = jnp.zeros_like(dh2)

        def to_sibling(slot):
            return [
                at.copy_sibling(m.at[slot, 1 - at.core], s.at[slot], gsent.at[j, slot], ggot.at[j, slot])
                for j, (m, s) in enumerate(((mine1, sib1), (mine2, sib2)))
            ]

        def meet(i):
            slot = lax.rem(i, 2)
            for copy in to_sibling(slot):
                copy.wait()
            sum1[i] = mine1[slot, at.core] + sib1[slot]
            sum2[i] = mine2[slot, at.core] + sib2[slot]

        def tile(i, carry):
            slot = lax.rem(i, 2)

            @pl.when(i >= 1)
            def _():
                meet(i - 1)

            turn = i * FF_TICKS // (TILES - 1)

            @pl.when(turn > (i - 1) * FF_TICKS // (TILES - 1))
            def _():
                advance(turn - 1)

            for part in weights(i, slot):
                part.wait()

            @pl.when(i + 1 < TILES)
            def _():
                for part in weights(i + 1, 1 - slot):
                    part.start()

            bias = jnp.concatenate([bup[0, i], bup[1, i]], axis=1)
            u = dot(h2[...], wu[slot], NN) + bias
            a, slope = gelu_and_slope(u)
            a = a.astype(bf16)
            out[...] += dot(a, wd[slot], NN)
            d_wd = dot(a, og[...], TN).astype(bf16)
            mine1[slot, 0] = d_wd[:TILE]
            mine1[slot, 1] = d_wd[TILE:]
            du = (dot(og[...], wd[slot], NT) * slope).astype(bf16)
            d_wu = dot(h2t[...], du, NN).astype(bf16)
            mine2[slot, 0] = d_wu[:HALF]
            mine2[slot, 1] = d_wu[HALF:]
            for copy in to_sibling(slot):
                copy.start()
            dh2[...] += dot(du, wu[slot], NT)
            dbup[i] = jnp.sum(du.astype(f32), axis=0, keepdims=True)
            return carry

        lax.fori_loop(0, TILES, tile, 0)
        meet(TILES - 1)

        def put(b):
            slot = lax.rem(b, 2)
            return pltpu.make_async_copy(staged.at[slot], out_ref.at[block(b), :], local.at[slot])

        def put_rows(b, carry):
            @pl.when(b >= 2)
            def _():
                put(b - 2).wait()

            staged[lax.rem(b, 2)] = out[block(b), :].astype(bf16)
            put(b).start()
            return carry

        lax.fori_loop(0, blocks, put_rows, 0)
        put(blocks - 2).wait()
        put(blocks - 1).wait()

    pl.run_scoped(
        feed_forward,
        pltpu.VMEM((rows_all, WIDTH), f32),
        pltpu.VMEM((2, BLOCK, WIDTH), bf16),
        pltpu.VMEM((2, WIDTH, 2 * TILE), bf16),
        pltpu.VMEM((2, 2 * TILE, WIDTH), bf16),
        pltpu.VMEM((2, 2, TILE, WIDTH), bf16),
        pltpu.VMEM((2, 2, HALF, 2 * TILE), bf16),
        pltpu.SemaphoreType.DMA((4, 2)),
    )

    def attention(aot, dq, dk, dv, w, image, pimage, wide, source, staged, mine3, wsem, isem):
        load_ao = pltpu.make_async_copy(ao_ref, dq, wsem.at[0])
        load_h1 = pltpu.make_async_copy(h1_ref, dk, wsem.at[1])

        def load_w(j, slot):
            return pltpu.make_async_copy(w_ref.at[j], w.at[slot], wsem.at[2 + slot])

        def load_x2(b):
            slot = lax.rem(b, 2)
            return pltpu.make_async_copy(x2_ref.at[block(b), :], wide.at[slot], isem.at[4, slot])

        def load_x(b):
            slot = lax.rem(b, 2)
            return pltpu.make_async_copy(
                tokens_ref.at[pair(b), :], source.at[slot], isem.at[0, slot]
            )

        def put(b):
            slot = lax.rem(b, 2)
            return pltpu.make_async_copy(staged.at[slot], din_ref.at[pair(b), :], isem.at[4, slot])

        def pair(b):
            return pl.ds(aligned(b * 2 * BLOCK, 2 * BLOCK), 2 * BLOCK)

        def load_probs(i):
            slot = lax.rem(i, 2)
            return pltpu.make_async_copy(probs_ref.at[i], pimage.at[slot], isem.at[3, slot])

        def load_image(i):
            slot = lax.rem(i, 2)
            return [
                pltpu.make_async_copy(s.at[block(i), :], image.at[j, slot], isem.at[j, slot])
                for j, s in enumerate((q_ref, k_ref, v_ref))
            ] + [load_probs(i)]

        load_x2(0).start()
        load_w(3, 0).start()
        load_ao.start()
        load_h1.start()
        load_w(1, 1).start()
        load_w(2, 2).start()
        load_probs(0).start()

        def column_sum(j, value):
            dvec[j : j + 1, :] += jnp.sum(value, axis=0, keepdims=True)

        def norm_back(source, gain, incoming):
            center = source - jnp.mean(source, axis=-1, keepdims=True)
            rate = lax.rsqrt(jnp.mean(center * center, axis=-1, keepdims=True) + 1e-06)
            n = center * rate
            scaled = incoming * gain
            first = jnp.mean(scaled, axis=-1, keepdims=True)
            second = jnp.mean(scaled * n, axis=-1, keepdims=True)
            return n, (scaled - first - n * second) * rate

        def second_norm(b, carry):
            @pl.when(b == NORM_TICK)
            def _():
                advance(FF_TICKS)

            load_x2(b).wait()

            @pl.when(b + 1 < blocks)
            def _():
                load_x2(b + 1).start()

            rows = block(b)
            e = dh2[rows, :]
            n, dn = norm_back(wide[lax.rem(b, 2)], vec[5:6, :], e)
            g = og[rows, :].astype(f32)
            dx2 = g + dn
            dt = dx2.astype(bf16)
            dh2[rows, :] = dx2
            h2[rows, :] = dt
            column_sum(5, e * n)
            column_sum(6, e)
            column_sum(7, g)
            column_sum(4, dt.astype(f32))
            return carry

        lax.fori_loop(0, blocks, second_norm, 0)
        load_ao.wait()
        load_h1.wait()
        for b in range(blocks):
            rows = pl.ds(b * BLOCK, BLOCK)
            aot[:, rows] = dq[rows, :].T
            h2t[:, rows] = dk[rows, :].T
        load_w(3, 0).wait()
        for b in range(2):
            rows = pl.ds(b * (rows_all // 2), rows_all // 2)
            og[rows, :] = dot(h2[rows, :], w[0], NT).astype(bf16)
        load_w(0, 0).start()

        def values(i, carry):
            @pl.when(i == VALUE_TICK)
            def _():
                advance(FF_TICKS + 1)

            slot = lax.rem(i, 2)
            load_probs(i).wait()

            @pl.when(i + 1 < blocks)
            def _():
                load_probs(i + 1).start()

            rows = block(i)
            gi = og[rows, :]
            total = Lanes()
            for h in range(HEADS):
                low = pimage[slot, :, h * PATCHES : (h + 1) * PATCHES]
                total.add(h, dot(low, only_head(gi[:, head_window(h)], h), NN))
            dvi = total.joined()
            dv[rows, :] = dvi
            column_sum(3, dvi.astype(f32))
            return carry

        lax.fori_loop(0, blocks, values, 0)
        for copy in load_image(0):
            copy.start()

        def to_sibling(slot):
            return [
                at.copy_sibling(
                    mine3.at[slot, j, 1 - at.core],
                    sib3.at[slot, j],
                    gsent.at[2 + j, slot],
                    ggot.at[2 + j, slot],
                )
                for j in (0, 1)
            ]

        def meet(i):
            slot = lax.rem(i, 2)
            for copy in to_sibling(slot):
                copy.wait()
            for j, (s, c) in enumerate(((sum1, i + TILES), (sum3, i))):
                c = lax.rem(c, s.shape[0])
                s[c] = mine3[slot, j, at.core] + sib3[slot, j]

        def weight_rows(left, right, start, count):
            rows = [left[pl.ds(aligned(h * HALF + start, 64), count), :] for h in (0, 1)]
            return dot(jnp.concatenate(rows, axis=0), right[...], NN).astype(bf16)

        def produce(m, start, one, two):
            slot = lax.rem(m, 2)
            one = weight_rows(*one, start, TILE)
            two = weight_rows(*two, start, TILE)
            for h in (0, 1):
                for j in (0, 1):
                    part = slice(h * TILE + j * 64, h * TILE + j * 64 + 64)
                    mine3[slot, j, h] = jnp.concatenate([one[part], two[part]], axis=0)
            for copy in to_sibling(slot):
                copy.start()

        def heads(i, carry):
            @pl.when(lax.rem(i, 2) == 0)
            def _():
                produce(i // 2, i * 64, (h2t, dv), (aot, h2))

            slot = lax.rem(i, 2)
            for copy in load_image(i):
                copy.wait()

            @pl.when(i + 1 < blocks)
            def _():
                for copy in load_image(i + 1):
                    copy.start()

            @pl.when(lax.rem(i, 2) == 1)
            def _():
                meet(i // 2)
                advance(TILES + i // 2)

            rows = block(i)
            qi, ki, vi, gi = image[0, slot], image[1, slot], image[2, slot], og[rows, :]
            sums = Lanes(), Lanes()
            for h in range(HEADS):
                cols = head_window(h)
                p = pimage[slot, :, h * PATCHES : (h + 1) * PATCHES].astype(f32)
                dp = dot(only_head(vi[:, cols], h), gi[:, cols], NT)
                ds = (p * (dp - jnp.sum(p * dp, axis=0, keepdims=True))).astype(bf16)
                sums[0].add(h, dot(ds, only_head(ki[:, cols], h), TN))
                sums[1].add(h, dot(ds, only_head(qi[:, cols], h), NN))
            dqi, dki = sums[0].joined(SCALE), sums[1].joined(SCALE)
            dq[rows, :] = dqi
            dk[rows, :] = dki
            column_sum(2, dqi.astype(f32))
            return carry

        lax.fori_loop(0, blocks, heads, 0)
        for j in range(3):
            load_w(j, j).wait()
        load_x(0).start()

        vo = weight_rows(h2t, dv, 512, 64), weight_rows(aot, h2, 512, 64)
        qk = weight_rows(h2t, dq, 0, 64), weight_rows(h2t, dk, 0, 64)
        for h in (0, 1):
            part = slice(h * 64, h * 64 + 64)
            for j, (one, two) in enumerate((vo, qk)):
                mine3[0, j, h] = jnp.concatenate([one[part], two[part]], axis=0)
        for copy in to_sibling(0):
            copy.start()

        def weight_gradients(j, carry):
            meet(j - 1)

            @pl.when(j < CHUNKS)
            def _():
                produce(j, (j - 5) * TILE + 64, (h2t, dq), (h2t, dk))

            advance(TILES - 1 + j)

            @pl.when(j < CHUNKS)
            def _():
                b = j - 5
                load_x(b).wait()

                @pl.when(b + 1 < 4)
                def _():
                    load_x(b + 1).start()

                @pl.when(b >= 2)
                def _():
                    put(b - 2).wait()

                rows = pair(b)
                e = dot(dq[rows, :], w[0], NT) + dot(dk[rows, :], w[1], NT)
                e = e + dot(dv[rows, :], w[2], NT)
                x = source[lax.rem(b, 2)].astype(f32)
                n, dn = norm_back(x, vec[0:1, :], e)
                staged[lax.rem(b, 2)] = (dh2[rows, :] + dn).astype(bf16)
                put(b).start()
                column_sum(0, e * n)
                column_sum(1, e)

            return carry

        lax.fori_loop(5, CHUNKS + 1, weight_gradients, 0)
        put(2).wait()
        put(3).wait()

        small[...] = jnp.zeros_like(small)
        small[0:VECTORS, :] = dvec[...]
        for i in range(TILES):
            small[VECTORS + i : VECTORS + i + 1, : 2 * TILE] = dbup[i]
        mine3[1, 1, 0] = jnp.concatenate(
            [small[...].astype(bf16), jnp.zeros((TILE - small.shape[0], WIDTH), bf16)], axis=0
        )
        trade = at.copy_sibling(mine3.at[1, 1, 0], sib3.at[1, 1], gsent.at[3, 1], ggot.at[3, 1])
        trade.start()
        trade.wait()
        sum3[CHUNKS] = mine3[1, 1, 0] + sib3[1, 1]

    flat = pltpu.VMEM((rows_all, WIDTH), bf16)
    pl.run_scoped(
        attention,
        pltpu.VMEM((WIDTH, rows_all), bf16),
        flat,
        flat,
        flat,
        pltpu.VMEM((3, WIDTH, WIDTH), bf16),
        pltpu.VMEM((3, 2, BLOCK, WIDTH), bf16),
        pltpu.VMEM((2, PATCHES, HEADS * PATCHES), bf16),
        pltpu.VMEM((2, BLOCK, WIDTH), f32),
        pltpu.VMEM((2, 2 * BLOCK, WIDTH), bf16),
        pltpu.VMEM((2, 2 * BLOCK, WIDTH), bf16),
        pltpu.VMEM((2, 2, 2, TILE, WIDTH), bf16),
        pltpu.SemaphoreType.DMA((5,)),
        pltpu.SemaphoreType.DMA((5, 2)),
    )

    def drain(tick, carry):
        advance(tick)
        return carry

    lax.fori_loop(TREE, TREE + 8, drain, 0)


def rest_of_layer(tokens, og, h1, q, k, v, ao, probs, x2, h2, w, wup, wdown, vec, bup):
    rows = h2.shape[0]
    flat = jax.ShapeDtypeStruct((rows, WIDTH), bf16)
    return pl.pallas_call(
        rest_kernel,
        out_shape=(
            flat,
            flat,
            jax.ShapeDtypeStruct((SMALL + 1, TILE, WIDTH), bf16),
            jax.ShapeDtypeStruct((TILES, HALF, 2 * TILE), bf16),
        ),
        in_specs=[ANY] * 15,
        out_specs=[ANY] * 4,
        scratch_shapes=[
            pltpu.VMEM((rows, WIDTH), bf16),
            pltpu.VMEM((WIDTH, rows), bf16),
            pltpu.VMEM((rows, WIDTH), bf16),
            pltpu.VMEM((rows, WIDTH), f32),
            pltpu.VMEM((2, TILES, 1, TILE), f32),
            pltpu.VMEM((VECTORS, WIDTH), f32),
            pltpu.VMEM((TILES, 1, 2 * TILE), f32),
            pltpu.VMEM((VECTORS, WIDTH), f32),
            pltpu.VMEM((32, WIDTH), f32),
            pltpu.VMEM((2, TILE, WIDTH), bf16),
            pltpu.VMEM((2, HALF, 2 * TILE), bf16),
            pltpu.VMEM((2, 2, TILE, WIDTH), bf16),
            pltpu.VMEM((TILES + 1, TILE, WIDTH), bf16),
            pltpu.VMEM((TILES, HALF, 2 * TILE), bf16),
            pltpu.VMEM((CHUNKS + 1, TILE, WIDTH), bf16),
            pltpu.SemaphoreType.DMA((5,)),
            pltpu.SemaphoreType.DMA((4, 2)),
            pltpu.SemaphoreType.DMA((4, 2)),
        ]
        + tree_scratch(TILE, WIDTH)
        + flag_scratch(7, 8) * 2
        + plane_scratch(FIRST, 2 * TILE)
        + plane_scratch(SECOND, 2 * TILE)
        + plane_scratch(TILE // 2, WIDTH) * 2,
        compiler_params=pltpu.CompilerParams(
            collective_id=1, has_side_effects=True, vmem_limit_bytes=62 * 2**20
        ),
        name="rest_of_layer",
    )(tokens, og, h1, q, k, v, ao, probs, x2, h2, w, wup, wdown, vec, bup)


def finish_kernel(
    g1_ref,
    q_ref,
    k_ref,
    g2_ref,
    v_ref,
    o_ref,
    out_ref,
    din_ref,
    d1_ref,
    d2_ref,
    dq_ref,
    dk_ref,
    dv_ref,
    do_ref,
    out_end,
    din_end,
):
    d1_ref[...] = g1_ref[...].reshape(2 * TILE, WIDTH).astype(f32)
    parts = []
    for h in (0, 1):
        for i in range(TILES):
            wide = TILE if i < TILES - 1 else FF_HALF - (TILES - 1) * TILE
            parts.append(g2_ref[i, :, h * TILE : h * TILE + wide].astype(f32))
    d2_ref[...] = jnp.concatenate(parts, axis=1)
    for s, d in ((q_ref, dq_ref), (k_ref, dk_ref), (v_ref, dv_ref), (o_ref, do_ref)):
        d[...] = s[0].astype(f32)
    out_end[...] = out_ref[...]
    din_end[...] = din_ref[...]


def finish(g1, g2, output, d_input):
    steps = HALF // 64
    square = jax.ShapeDtypeStruct((HALF, WIDTH), f32)
    blocks = output.shape[0] // BLOCK
    flat = pl.BlockSpec((BLOCK, WIDTH), lambda i: (jnp.minimum(i, blocks - 1), 0))

    def half_chunk(first, part):
        return pl.BlockSpec((1, 64, WIDTH), lambda i: (first + i, part, 0))

    return pl.pallas_call(
        finish_kernel,
        grid=(steps,),
        out_shape=(
            jax.ShapeDtypeStruct((FF_HALF, WIDTH), f32),
            jax.ShapeDtypeStruct((HALF, FF), f32),
        )
        + (square,) * 4
        + (jax.ShapeDtypeStruct(output.shape, bf16),) * 2,
        in_specs=[
            pl.BlockSpec((2, TILE, WIDTH), lambda i: (i, 0, 0)),
            half_chunk(TREE, 0),
            half_chunk(TREE, 1),
            pl.BlockSpec((TILES, 64, 2 * TILE), lambda i: (0, i, 0)),
            half_chunk(TILES, 0),
            half_chunk(TILES, 1),
            flat,
            flat,
        ],
        out_specs=[
            pl.BlockSpec((2 * TILE, WIDTH), lambda i: (i, 0)),
            pl.BlockSpec((64, FF), lambda i: (i, 0)),
        ]
        + [pl.BlockSpec((64, WIDTH), lambda i: (i, 0))] * 4
        + [flat] * 2,
        compiler_params=pltpu.CompilerParams(vmem_limit_bytes=62 * 2**20),
        name="finish",
    )(g1, g1, g1, g2, g1, g1, output, d_input)


def stack_kernel(*refs):
    rows = [r[...].astype(f32).reshape(1, HALF) for r in refs[:-1]]
    rows = jnp.concatenate(rows, axis=0)
    refs[-1][...] = jnp.concatenate([rows, jnp.zeros((VECTORS, LANES - HALF), f32)], axis=1)


def fast_shards(
    tokens,
    out_grad,
    ln1_gain,
    ln1_bias,
    q_weight,
    q_bias,
    k_weight,
    v_weight,
    v_bias,
    o_weight,
    o_bias,
    ln2_gain,
    ln2_bias,
    up_weight,
    up_bias,
    down_weight,
    down_bias,
):
    small = [ln1_gain, ln1_bias, q_bias, v_bias, o_bias, ln2_gain, ln2_bias, down_bias]
    pack = pl.pallas_call(
        stack_kernel, out_shape=jax.ShapeDtypeStruct((VECTORS, LANES), f32), name="stack"
    )(*small)
    gap = TILES * TILE - FF_HALF
    bup = jnp.pad(up_bias.astype(f32), (0, gap)).reshape(TILES, 1, TILE)
    saved = forward(
        tokens, q_weight, k_weight, v_weight, o_weight, up_weight, down_weight, pack, bup
    )
    output, d_input, g1, g2 = rest_of_layer(tokens, out_grad, *saved)
    d_down, d_up, d_q, d_k, d_v, d_o, output, d_input = finish(g1, g2, output, d_input)
    core = lax.axis_index("group")
    vectors = lax.dynamic_slice(g1[SMALL, :VECTORS], (0, core * HALF), (VECTORS, HALF)).astype(f32)
    d_bup = lax.dynamic_slice(
        g1[SMALL, VECTORS : VECTORS + TILES], (0, core * TILE), (TILES, TILE)
    )
    d_bup = d_bup.reshape(TILES * TILE)[:FF_HALF].astype(f32)
    return (
        output,
        d_input,
        vectors[0],
        vectors[1],
        d_q,
        vectors[2],
        d_k,
        d_v,
        vectors[3],
        d_o,
        vectors[4],
        vectors[5],
        vectors[6],
        d_up,
        d_bup,
        d_down,
        vectors[7],
    )


def solution(mesh):
    placed = (
        P(("group", "replica"), None),
        P(("group", "replica"), None),
        P("group"),
        P("group"),
        P("group", None),
        P("group"),
        P("group", None),
        P("group", None),
        P("group"),
        P("group", None),
        P("group"),
        P("group"),
        P("group"),
        P("group", None),
        P("group"),
        P("group", None),
        P("group"),
    )
    fast = mesh.shape["group"] == 2 and mesh.shape["replica"] == 16
    return jax.shard_map(
        fast_shards if fast else shards,
        mesh=mesh,
        in_specs=placed,
        out_specs=(
            P(("group", "replica"), None),
            P(("group", "replica"), None),
            P("group"),
            P("group"),
            P("group", None),
            P("group"),
            P("group", None),
            P("group", None),
            P("group"),
            P("group", None),
            P("group"),
            P("group"),
            P("group"),
            P("group", None),
            P("group"),
            P("group", None),
            P("group"),
        ),
        check_vma=False,
    )
```
